32 devices in a mesh: grp: 4 (over x, core), seq: 8 (over z, y).
Axes of the slice: x: 2, y: 2, z: 4, core: 2. Of those that a mesh axis runs over, the one named last changes fastest.
Arguments:
- inputs: bfloat16 [4, 1024, 768], P('grp', 'seq'), may hold values from -6 to 6
- segment_ids: int32 [4, 1024], P('grp'), may hold values from 0 to 2, never falling along the last dimension, each value on 1 to 512 neighbouring positions
- padding: int32 [4, 1024], P('grp', 'seq'), may hold values 0 or 1
- cotangent: bfloat16 [4, 1024, 768], P('grp', 'seq'), may hold values from -6 to 6
- w_query: bfloat16 [768, 768], P(('grp', 'seq')), may hold values from -0.21875 to 0.21875
- b_query: bfloat16 [768], P(('grp', 'seq')), may hold values from -3 to 3
- w_key: bfloat16 [768, 768], P(('grp', 'seq')), may hold values from -0.21875 to 0.21875
- w_value: bfloat16 [768, 768], P(('grp', 'seq')), may hold values from -0.21875 to 0.21875
- b_value: bfloat16 [768], P(('grp', 'seq')), may hold values from -3 to 3
- w_out: bfloat16 [768, 768], P(('grp', 'seq')), may hold values from -3.5 to 3.5
- b_out: bfloat16 [768], P(('grp', 'seq')), may hold values from -2 to 2
- ln1_gain: bfloat16 [768], P(('grp', 'seq')), may hold values from 0.099609375 to 1.8984375
- ln1_shift: bfloat16 [768], P(('grp', 'seq')), may hold values from -2 to 2
- ln2_gain: bfloat16 [768], P(('grp', 'seq')), may hold values from 0.099609375 to 1.8984375
- ln2_shift: bfloat16 [768], P(('grp', 'seq')), may hold values from -2 to 2
- w_up: bfloat16 [768, 3072], P(('grp', 'seq')), may hold values from -0.21875 to 0.21875
- b_up: bfloat16 [3072], P(('grp', 'seq')), may hold values from -3 to 3
- w_down: bfloat16 [3072, 768], P(('grp', 'seq')), may hold values from -0.109375 to 0.109375
- b_down: bfloat16 [768], P(('grp', 'seq')), may hold values from -2 to 2
Outputs:
- output: bfloat16 [4, 1024, 768], P('grp', 'seq')
- grad_input: bfloat16 [4, 1024, 768], P('grp', 'seq')
- grad_w_query: float32 [768, 768], P(('grp', 'seq'))
- grad_b_query: float32 [768], P(('grp', 'seq'))
- grad_w_key: float32 [768, 768], P(('grp', 'seq'))
- grad_w_value: float32 [768, 768], P(('grp', 'seq'))
- grad_b_value: float32 [768], P(('grp', 'seq'))
- grad_w_out: float32 [768, 768], P(('grp', 'seq'))
- grad_b_out: float32 [768], P(('grp', 'seq'))
- grad_ln1_gain: float32 [768], P(('grp', 'seq'))
- grad_ln1_shift: float32 [768], P(('grp', 'seq'))
- grad_ln2_gain: float32 [768], P(('grp', 'seq'))
- grad_ln2_shift: float32 [768], P(('grp', 'seq'))
- grad_w_up: float32 [768, 3072], P(('grp', 'seq'))
- grad_b_up: float32 [3072], P(('grp', 'seq'))
- grad_w_down: float32 [3072, 768], P(('grp', 'seq'))
- grad_b_down: float32 [768], P(('grp', 'seq'))
The draws below stay inside these ranges and needn't reach their ends.
Inputs may be any that keep to these rules, and one draw needn't show every extreme that they name: `segment_ids`: per sequence the numbers never fall along the positions; a document spans at most 512 positions.
All inputs are finite; a program needn't handle non-finite values. No bound on the sum of `padding` on one device may be relied on, other than what follows from the above.
Results may differ from the reference program's by a relative error of at most 0.014.
Values may be sent and summed in bfloat16 or wider, within the bound.
No kernel may reach another device: no remote copies, remote signals or barrier semaphores. Data moves between devices by JAX's collectives and lax.ppermute only.
A program may use at most 192 MiB of HBM per device.

```python
import math
import jax
import jax.numpy as jnp
import numpy as np
from jax import lax

D = 768
HEADS = 12
HEAD_DIM = 64
FF = 3072
LENGTH = 1024
DOC_MAX = 512
SEQS = 4
DOCS = 3


def touch_ends(values, stream_key, least, largest):
    shape = values.shape
    spot = [jax.random.randint(jax.random.fold_in(stream_key, axis), (), 0, shape[axis]) for axis in range(len(shape))]
    values = values.at[tuple(spot)].set(least)
    longest = shape.index(max(shape))
    spot[longest] = (spot[longest] + 1) % shape[longest]
    return values.at[tuple(spot)].set(largest)


def block_scale(stream_key, dims, shards, smallest, largest):
    def one(position, parts):
        heights = jax.random.uniform(jax.random.fold_in(jax.random.fold_in(stream_key, 6), position), (parts,), jnp.float32, smallest / len(shards), largest / len(shards))
        return jnp.repeat(jnp.exp(heights), dims[position] // parts).reshape((-1,) + (1,) * (len(dims) - position - 1))

    level = one(*shards[0])
    for cut in shards[1:]:
        level = level * one(*cut)
    return level


def length_profile(number_of, total, bound, lean):
    loads = [(1 << 20) // math.isqrt(standing ** lean) + 1 for standing in range(2, number_of + 1)]
    rest, counts = total - bound - (number_of - 1), [1] * (number_of - 1)
    while rest > 0:
        candidates = [i for i in range(number_of - 1) if counts[i] < bound]
        whole, left = sum([loads[i] for i in candidates]), rest
        for i in candidates:
            extra = min(bound - counts[i], max(1, left * loads[i] // whole), rest)
            counts[i] = counts[i] + extra
            rest = rest - extra
    return np.array([bound] + counts)


def uneven(own_key, number_of, total, reach, slope):
    if number_of == 2:
        one = jax.random.randint(own_key, (), max(1, total - reach), min(reach, total - 1) + 1)
        return jnp.stack([one, total - one])
    sizes = jnp.asarray(length_profile(number_of, total, reach, slope), jnp.int32)
    couples = (number_of - 1) // 2
    donor, sink = sizes[1:1 + 2 * couples:2], sizes[2:2 + 2 * couples:2]
    room = jnp.minimum(donor - 1, reach - sink)
    moved = jax.random.randint(jax.random.fold_in(own_key, 1), (couples,), 0, 1 << 20) % (room + 1)
    sizes = sizes.at[1:1 + 2 * couples:2].set(donor - moved).at[2:2 + 2 * couples:2].set(sink + moved)
    return sizes[jax.random.permutation(jax.random.fold_in(own_key, 2), number_of)]


def normal_values(stream_key, extent, width, bound, shards=(), dtype=jnp.bfloat16):
    entries = jax.random.normal(stream_key, extent, jnp.float32) * width
    if len(shards) > 0:
        entries = block_scale(stream_key, extent, shards, -0.22, 0.18) * entries
    return jnp.clip(entries, min=-bound, max=bound).astype(dtype)


def setup_inputs(seed: int = 0) -> dict:
    streams_of = jax.random.split(jax.random.key(seed), 20)
    return {
        "inputs": normal_values(streams_of[0], (SEQS, LENGTH, D), 1.0, 6.0, ((0, 4), (1, 8))),
        "segment_ids": jax.vmap(lambda own: jnp.searchsorted(jnp.cumsum(uneven(own, DOCS, LENGTH, DOC_MAX, 0)), jnp.arange(LENGTH), side="right"))(jax.random.split(streams_of[1], SEQS)).reshape((SEQS, LENGTH)).astype(jnp.int32),
        "padding": touch_ends((jax.random.randint(streams_of[2], (SEQS, LENGTH), 0, 8) < 7).astype(jnp.int32), jax.random.fold_in(streams_of[2], 1), 0, 1),
        "cotangent": normal_values(streams_of[3], (SEQS, LENGTH, D), 1.0, 6.0, ((0, 4), (1, 8))),
        "w_query": normal_values(streams_of[4], (D, D), D ** -0.5, 0.21875, ((0, 32),)),
        "b_query": normal_values(streams_of[5], (D,), 0.5, 3.0, ((0, 32),)),
        "w_key": normal_values(streams_of[6], (D, D), D ** -0.5, 0.21875, ((0, 32),)),
        "w_value": normal_values(streams_of[7], (D, D), D ** -0.5, 0.21875, ((0, 32),)),
        "b_value": normal_values(streams_of[8], (D,), 0.5, 3.0, ((0, 32),)),
        "w_out": normal_values(streams_of[9], (D, D), (max(1, D // 256)) ** -0.5, 3.5, ((0, 32),)),
        "b_out": normal_values(streams_of[10], (D,), 0.3, 2.0, ((0, 32),)),
        "ln1_gain": jnp.clip(1.0 + 0.18 * jax.random.normal(streams_of[11], (D,), jnp.float32), 0.099609375, 1.8984375).astype(jnp.bfloat16),
        "ln1_shift": normal_values(streams_of[12], (D,), 0.3, 2.0, ((0, 32),)),
        "ln2_gain": jnp.clip(1.0 + 0.18 * jax.random.normal(streams_of[13], (D,), jnp.float32), 0.099609375, 1.8984375).astype(jnp.bfloat16),
        "ln2_shift": normal_values(streams_of[14], (D,), 0.3, 2.0, ((0, 32),)),
        "w_up": normal_values(streams_of[15], (D, FF), D ** -0.5, 0.21875, ((0, 32),)),
        "b_up": normal_values(streams_of[16], (FF,), 0.5, 3.0, ((0, 32),)),
        "w_down": normal_values(streams_of[17], (FF, D), FF ** -0.5, 0.109375, ((0, 32),)),
        "b_down": normal_values(streams_of[18], (D,), 0.3, 2.0, ((0, 32),)),
    }


highest = lax.Precision.HIGHEST
scaling = 0.125

@jax.custom_vjp
def low(v):
    return lax.optimization_barrier(v.astype(jnp.bfloat16)).astype(jnp.float32)

@jax.custom_vjp
def low_back(v):
    return v

def low_keep(v):
    return (low(v), None)

def low_pass(kept, grad):
    return (grad,)

def back_keep(v):
    return (v, None)

def back_low(kept, grad):
    return (low(grad),)
low.defvjp(low_keep, low_pass)
low_back.defvjp(back_keep, back_low)

def matmul(left, right):
    return jnp.dot(left, right, precision=highest)

def normalize(values, gain, shift):
    center = values - lax.optimization_barrier(jnp.mean(values, axis=-1, keepdims=True))
    variance = lax.optimization_barrier(jnp.mean(center * center, axis=-1, keepdims=True))
    return center * lax.rsqrt(variance + 1e-05) * gain + shift

def exact_gelu(values):
    return jax.nn.gelu(values, approximate=False)

def layer(values_in, docs, weights_in):
    w_query, b_query, w_key, w_value, b_value, w_out, b_out, gain_one, shift_one, gain_two, shift_two, w_up, b_up, w_down, b_down = weights_in
    length = values_in.shape[0]
    normed = low(normalize(values_in, gain_one, shift_one))
    queries = low(low_back(matmul(normed, w_query) + b_query))
    keys = low(low_back(matmul(normed, w_key)))
    values = low(low_back(matmul(normed, w_value) + b_value))
    key_heads = keys.reshape(length, HEADS, HEAD_DIM)
    value_heads = values.reshape(length, HEADS, HEAD_DIM)
    block_rows = min(512, length)
    blocks = length // block_rows

    def attend_block(packed):
        query_block, doc_block = packed
        scores = jnp.einsum('qhe,khe->hqk', query_block, key_heads, precision=highest) * scaling
        scores = low_back(scores)
        same_doc = doc_block[:, None] == docs[None, :]
        scores = jnp.where(same_doc[None], scores, -1e+30)
        shifted = scores - lax.optimization_barrier(jnp.max(scores, axis=-1, keepdims=True))
        exponent = jnp.exp(shifted)
        attn_probs = exponent / lax.optimization_barrier(jnp.sum(exponent, axis=-1, keepdims=True))
        return jnp.einsum('hqk,khe->qhe', low(attn_probs), value_heads, precision=highest)
    blocked = lax.map(jax.checkpoint(attend_block), (queries.reshape(blocks, block_rows, HEADS, HEAD_DIM), docs.reshape(blocks, block_rows)))
    mixed = low(low_back(blocked.reshape(length, HEADS * HEAD_DIM)))
    attended = low_back(matmul(mixed, w_out) + b_out)
    residual = values_in + attended
    normed_mlp = low(normalize(residual, gain_two, shift_two))
    pre_act = low_back(matmul(normed_mlp, w_up) + b_up)
    activated = low(exact_gelu(pre_act))
    branch = low_back(matmul(activated, w_down) + b_down)
    return residual + branch

def reference(inputs, segment_ids, padding, cotangent, w_query, b_query, w_key, w_value, b_value, w_out, b_out, ln1_gain, ln1_shift, ln2_gain, ln2_shift, w_up, b_up, w_down, b_down):
    params = (w_query.astype(jnp.float32), b_query.astype(jnp.float32), w_key.astype(jnp.float32), w_value.astype(jnp.float32), b_value.astype(jnp.float32), w_out.astype(jnp.float32), b_out.astype(jnp.float32), ln1_gain.astype(jnp.float32), ln1_shift.astype(jnp.float32), ln2_gain.astype(jnp.float32), ln2_shift.astype(jnp.float32), w_up.astype(jnp.float32), b_up.astype(jnp.float32), w_down.astype(jnp.float32), b_down.astype(jnp.float32))

    def one_sequence(totals, packed):
        seq_inputs, seq_docs, seq_padding, seq_cotangent = packed
        result, pull = jax.vjp(lambda values_in, weights_in: layer(values_in, seq_docs, weights_in), seq_inputs.astype(jnp.float32), params)
        grad_values, grad_params = pull(seq_cotangent.astype(jnp.float32) * seq_padding.astype(jnp.float32)[:, None])
        totals = jax.tree.map(lambda first, second: first + second, totals, grad_params)
        return (totals, (result.astype(jnp.bfloat16), grad_values.astype(jnp.bfloat16)))
    zeros = jax.tree.map(jnp.zeros_like, params)
    totals, (outputs, grads_in) = lax.scan(one_sequence, zeros, (inputs, segment_ids, padding, cotangent))
    return (outputs, grads_in, totals[0], totals[1], totals[2], totals[3], totals[4], totals[5], totals[6], totals[7], totals[8], totals[9], totals[10], totals[11], totals[12], totals[13], totals[14])
```

```python
import functools

import jax
import jax.numpy as jnp
from jax import lax
from jax.experimental import pallas as pl
from jax.experimental.pallas import tpu as pltpu
from jax.sharding import Mesh, PartitionSpec as P

HEADS = 12
HEAD_DIM = 64
TP = 4
HEADS_TP = HEADS // TP
EPS = 1e-05
NEG = -1e30
SCALE = 0.125
ALL = ("gx", "c", "sz", "sy")
SAME = ("gx", "sz", "sy")
SMALLS = 64
f32 = jnp.float32
bf16 = jnp.bfloat16


class Plan:
    def __init__(self, groups, blocks):
        if (groups, blocks) == (4, 8):
            self.shape = (2, 2, 4, 2)
            self.tp, self.half, self.rep = ("gx", "sy"), "c", ("c", "sz")
        else:
            self.shape = (groups // 2, 2, blocks // TP, TP)
            self.tp, self.half, self.rep = ("sy",), "sz", ("gx", "c", "sz")
        self.size = dict(zip(ALL, self.shape))
        self.devices = groups * blocks
        self.parts = self.size[self.half]
        self.copies = self.devices // TP
        self.route = []
        for src in range(self.devices):
            seq, block = divmod(src, blocks)
            part, member = divmod(block, TP)
            if self.tp == ("sy",):
                dst = src
            else:
                dst = (((member >> 1) * 2 + part) * 4 + seq) * 2 + (member & 1)
            self.route.append((src, dst))
        self.back = [(dst, src) for src, dst in self.route]

    def move(self, value, table):
        if all(a == b for a, b in table):
            return value
        return lax.ppermute(value, ALL, table)

    def shuffle(self, value, before, after):
        tail = value.shape[1:]
        dims = [self.size[a] for a in before]
        order = [before.index(a) for a in after]
        value = value.reshape(*dims, *tail)
        value = value.transpose(*order, *range(len(dims), len(dims) + len(tail)))
        return value.reshape(-1, *tail)


def dot(left, right, left_dim=1, right_dim=0):
    return lax.dot_general(
        left, right, (((left_dim,), (right_dim,)), ((), ())), preferred_element_type=f32
    )


def unit(values):
    center = values - jnp.mean(values, axis=-1, keepdims=True)
    variance = jnp.mean(center * center, axis=-1, keepdims=True)
    rstd = lax.rsqrt(variance + EPS)
    return center * rstd, rstd


def unit_back(grad_unit, units, rstd):
    first = jnp.mean(grad_unit, axis=-1, keepdims=True)
    second = jnp.mean(grad_unit * units, axis=-1, keepdims=True)
    return rstd * (grad_unit - first - units * second)


def params(limit=60 * 1024 * 1024, axes=1):
    return pltpu.CompilerParams(
        dimension_semantics=("arbitrary",) * axes, vmem_limit_bytes=limit
    )


def cost(flops, nbytes, trans=0):
    return pl.CostEstimate(flops=int(flops), bytes_accessed=int(nbytes), transcendentals=int(trans))


def whole(shape):
    zeros = (0,) * len(shape)
    return pl.BlockSpec(shape, lambda *_: zeros)


def head_lanes(value, head):
    lane = lax.broadcasted_iota(jnp.int32, value.shape, 1)
    keep = (lane >= head * HEAD_DIM) & (lane < (head + 1) * HEAD_DIM)
    return jnp.where(keep, value, jnp.zeros_like(value))


def qkv_kernel(x_ref, w_ref, vec_ref, bias_ref, h_ref, q_ref, kv_ref):
    units, _ = unit(x_ref[...].astype(f32))
    low = (units * vec_ref[3:4, :] + vec_ref[4:5, :]).astype(bf16)
    h_ref[...] = low
    cols = q_ref.shape[1]
    out = dot(low, w_ref[...])
    query = (out[:, :cols] + bias_ref[0:1, :]).astype(bf16)
    q_ref[...] = (query.astype(f32) * SCALE).astype(bf16)
    kv_ref[0] = out[:, cols : 2 * cols].astype(bf16)
    kv_ref[1] = (out[:, 2 * cols : 3 * cols] + bias_ref[1:2, :]).astype(bf16)


def qkv(x_all, w_qkv, vecs, bias):
    rows, width = x_all.shape
    cols = width // TP
    step = rows // TP
    return pl.pallas_call(
        qkv_kernel,
        grid=(TP,),
        in_specs=[
            pl.BlockSpec((step, width), lambda i: (i, 0)),
            whole(w_qkv.shape),
            whole(vecs.shape),
            whole(bias.shape),
        ],
        out_specs=[
            pl.BlockSpec((step, width), lambda i: (i, 0)),
            pl.BlockSpec((step, cols), lambda i: (i, 0)),
            pl.BlockSpec((2, step, cols), lambda i: (0, i, 0)),
        ],
        out_shape=[
            jax.ShapeDtypeStruct((rows, width), bf16),
            jax.ShapeDtypeStruct((rows, cols), bf16),
            jax.ShapeDtypeStruct((2, rows, cols), bf16),
        ],
        compiler_params=params(),
        cost_estimate=cost(2 * rows * width * 3 * cols, rows * width * 8),
        name="qkv",
    )(x_all, w_qkv, vecs, bias)


def fill_docs(ids_ref, part, parts, doc_ref):
    span, width = doc_ref.shape[1:]
    for j in range(parts):
        at = lax.rem(part + j, parts) * span
        row = ids_ref[0:1, pl.ds(pl.multiple_of(at, 512), span)]
        doc_ref[j] = jnp.broadcast_to(row, (width, span)).T


def fwd_kernel(parts, idx_ref, ids_ref, q_ref, *refs):
    kv_refs = refs[:parts]
    o_ref, lse_ref, turned, doc_ref = refs[parts:]
    step = pl.program_id(0)
    part = idx_ref[1]
    span = kv_refs[0].shape[1]
    width = q_ref.shape[0]

    @pl.when(step == 0)
    def _():
        fill_docs(ids_ref, part, parts, doc_ref)
        for j in range(parts):
            turned[j] = kv_refs[j][1].T

    at = part * span + step * width
    own = ids_ref[0:1, pl.ds(pl.multiple_of(at, 128), width)]
    query = q_ref[...]
    outs, lses = [], []
    for head in range(HEADS_TP):
        masked = head_lanes(query, head)
        scores = []
        for j in range(parts):
            raw = dot(kv_refs[j][0], masked, 1, 1)
            scores.append(jnp.where(doc_ref[j] == own, raw, NEG))
        peak = functools.reduce(
            jnp.maximum, [jnp.max(s, axis=0, keepdims=True) for s in scores]
        )
        exps = [jnp.exp(s - peak) for s in scores]
        total = functools.reduce(jnp.add, [jnp.sum(e, axis=0, keepdims=True) for e in exps])
        scale = 1.0 / total
        acc = None
        for j in range(parts):
            probs = (exps[j] * scale).astype(bf16)
            term = dot(turned[j, head * HEAD_DIM : (head + 1) * HEAD_DIM, :], probs)
            acc = term if acc is None else acc + term
        outs.append(acc)
        lses.append(peak + jnp.log(total))
    o_ref[...] = jnp.concatenate(outs, axis=0).T.astype(bf16)
    for head in range(HEADS_TP):
        lse_ref[head : head + 1, :] = lses[head]


def attend(idx, ids, q, kvs, width=256):
    rows, cols = q.shape
    parts = len(kvs)
    span = kvs[0].shape[1]
    return pl.pallas_call(
        functools.partial(fwd_kernel, parts),
        grid_spec=pltpu.PrefetchScalarGridSpec(
            num_scalar_prefetch=1,
            grid=(rows // width,),
            in_specs=[whole(ids.shape), pl.BlockSpec((width, cols), lambda i, *_: (i, 0))]
            + [whole(kv.shape) for kv in kvs],
            out_specs=[
                pl.BlockSpec((width, cols), lambda i, *_: (i, 0)),
                pl.BlockSpec((8, width), lambda i, *_: (0, i)),
            ],
            scratch_shapes=[
                pltpu.VMEM((parts, cols, span), bf16),
                pltpu.VMEM((parts, span, width), f32),
            ],
        ),
        out_shape=[
            jax.ShapeDtypeStruct((rows, cols), bf16),
            jax.ShapeDtypeStruct((8, rows), f32),
        ],
        compiler_params=params(),
        cost_estimate=cost(4 * rows * span * parts * cols, span * parts * cols * 4, rows * span * parts * HEADS_TP),
        name="attend",
    )(idx, ids, q, *kvs)


def bwd_kernel(parts, idx_ref, ids_ref, q_ref, da_ref, w_ref, lse_ref, *refs):
    kv_refs = refs[:parts]
    dq_ref, own_ref = refs[parts : parts + 2]
    other_refs = refs[parts + 2 : 2 * parts + 1]
    turned, doc_ref, key_acc, value_acc = refs[2 * parts + 1 :]
    step = pl.program_id(0)
    part = idx_ref[1]
    span = kv_refs[0].shape[1]
    width, cols = q_ref.shape

    @pl.when(step == 0)
    def _():
        fill_docs(ids_ref, part, parts, doc_ref)
        for j in range(parts):
            turned[j] = kv_refs[j][0].T
        key_acc[...] = jnp.zeros_like(key_acc)
        value_acc[...] = jnp.zeros_like(value_acc)

    at = part * span + step * width
    own = ids_ref[0:1, pl.ds(pl.multiple_of(at, 128), width)]
    query = q_ref[...]
    grad_mixed = dot(da_ref[...], w_ref[0], 1, 1).astype(bf16)
    turned_grads = []
    for head in range(HEADS_TP):
        masked_q = head_lanes(query, head)
        masked_g = head_lanes(grad_mixed, head)
        lse = lse_ref[head : head + 1, :]
        probs, grads = [], []
        for j in range(parts):
            raw = dot(kv_refs[j][0], masked_q, 1, 1)
            probs.append(jnp.exp(jnp.where(doc_ref[j] == own, raw, NEG) - lse))
            grads.append(dot(kv_refs[j][1], masked_g, 1, 1))
        delta = functools.reduce(
            jnp.add,
            [jnp.sum(p * g, axis=0, keepdims=True) for p, g in zip(probs, grads)],
        )
        acc = None
        for j in range(parts):
            grad_scores = (probs[j] * (grads[j] - delta)).astype(bf16)
            value_acc[j] += dot(probs[j].astype(bf16), masked_g)
            key_acc[j] += dot(grad_scores, masked_q)
            term = dot(turned[j, head * HEAD_DIM : (head + 1) * HEAD_DIM, :], grad_scores)
            acc = term if acc is None else acc + term
        turned_grads.append(acc)
    dq_ref[...] = (jnp.concatenate(turned_grads, axis=0).T * SCALE).astype(bf16)

    @pl.when(step == pl.num_programs(0) - 1)
    def _():
        own_ref[0] = key_acc[0]
        own_ref[1] = value_acc[0]
        for j in range(1, parts):
            other_refs[j - 1][0] = key_acc[j].astype(bf16)
            other_refs[j - 1][1] = value_acc[j].astype(bf16)


def attend_back(idx, ids, q, da_all, w_out, lse, kvs, width=256):
    rows, cols = q.shape
    model = da_all.shape[1]
    parts = len(kvs)
    span = kvs[0].shape[1]
    return pl.pallas_call(
        functools.partial(bwd_kernel, parts),
        grid_spec=pltpu.PrefetchScalarGridSpec(
            num_scalar_prefetch=1,
            grid=(rows // width,),
            in_specs=[
                whole(ids.shape),
                pl.BlockSpec((width, cols), lambda i, *_: (i, 0)),
                pl.BlockSpec((width, model), lambda i, *_: (i, 0)),
                pl.BlockSpec((1, cols, model), lambda i, idx: (idx[0], 0, 0)),
                pl.BlockSpec((8, width), lambda i, *_: (0, i)),
            ]
            + [whole(kv.shape) for kv in kvs],
            out_specs=[
                pl.BlockSpec((width, cols), lambda i, *_: (i, 0)),
                whole((2, span, cols)),
            ]
            + [whole((2, span, cols))] * (parts - 1),
            scratch_shapes=[
                pltpu.VMEM((parts, cols, span), bf16),
                pltpu.VMEM((parts, span, width), f32),
                pltpu.VMEM((parts, span, cols), f32),
                pltpu.VMEM((parts, span, cols), f32),
            ],
        ),
        out_shape=[
            jax.ShapeDtypeStruct((rows, cols), bf16),
            jax.ShapeDtypeStruct((2, span, cols), f32),
        ]
        + [jax.ShapeDtypeStruct((2, span, cols), bf16)] * (parts - 1),
        compiler_params=params(),
        cost_estimate=cost(10 * rows * span * parts * cols, span * parts * cols * 12, rows * span * parts * HEADS_TP),
        name="attend_back",
    )(idx, ids, q, da_all, w_out, lse, *kvs)


def mlp_kernel(
    x_ref, o_ref, dm_ref, wo_ref, wu_ref, wd_ref, vec_ref, bup_ref,
    r_ref, h_ref, a_ref, du_ref, out_ref, dh_ref, sum_ref, bsum_ref,
):
    step = pl.program_id(0)

    @pl.when(step == 0)
    def _():
        sum_ref[...] = jnp.zeros_like(sum_ref)
        bsum_ref[...] = jnp.zeros_like(bsum_ref)

    attended = dot(o_ref[0], wo_ref[0])
    for j in range(1, TP):
        attended += dot(o_ref[j], wo_ref[j])
    residual = x_ref[...].astype(f32) + (attended + vec_ref[2:3, :])
    r_ref[...] = residual
    units, _ = unit(residual)
    low = (units * vec_ref[5:6, :] + vec_ref[6:7, :]).astype(bf16)
    h_ref[...] = low
    pre = dot(low, wu_ref[...]) + bup_ref[...]
    normal = 0.5 * (1.0 + lax.erf(pre * 0.7071067811865476))
    act = (pre * normal).astype(bf16)
    a_ref[...] = act
    slope = normal + pre * (0.3989422804014327 * jnp.exp(-0.5 * pre * pre))
    out_ref[...] = dot(act, wd_ref[...]).astype(bf16)
    grad_pre = (dot(dm_ref[...], wd_ref[...], 1, 1) * slope).astype(bf16)
    du_ref[...] = grad_pre
    bsum_ref[0:1, :] += jnp.sum(grad_pre.astype(f32), axis=0, keepdims=True)
    grad = dot(grad_pre, wu_ref[...], 1, 1)
    dh_ref[...] = grad.astype(bf16)
    sum_ref[0:1, :] += jnp.sum(grad * units, axis=0, keepdims=True)
    sum_ref[1:2, :] += jnp.sum(grad, axis=0, keepdims=True)


def mlp(x_all, o_all, dm_all, w_out, w_up, w_down, vecs, b_up):
    rows, width = x_all.shape
    hidden = w_up.shape[1]
    cols = width // TP
    step = 128
    token = pl.BlockSpec((step, width), lambda i: (i, 0))
    inner = pl.BlockSpec((step, hidden), lambda i: (i, 0))
    return pl.pallas_call(
        mlp_kernel,
        grid=(rows // step,),
        in_specs=[
            token,
            pl.BlockSpec((TP, step, cols), lambda i: (0, i, 0)),
            token,
            whole(w_out.shape),
            whole(w_up.shape),
            whole(w_down.shape),
            whole(vecs.shape),
            whole(b_up.shape),
        ],
        out_specs=[token, token, inner, inner, token, token, whole((8, width)), whole((8, hidden))],
        out_shape=[
            jax.ShapeDtypeStruct((rows, width), f32),
            jax.ShapeDtypeStruct((rows, width), bf16),
            jax.ShapeDtypeStruct((rows, hidden), bf16),
            jax.ShapeDtypeStruct((rows, hidden), bf16),
            jax.ShapeDtypeStruct((rows, width), bf16),
            jax.ShapeDtypeStruct((rows, width), bf16),
            jax.ShapeDtypeStruct((8, width), f32),
            jax.ShapeDtypeStruct((8, hidden), f32),
        ],
        compiler_params=params(),
        cost_estimate=cost(2 * rows * width * (width + 4 * hidden), rows * width * 24, rows * hidden * 4),
        name="mlp",
    )(x_all, o_all, dm_all, w_out, w_up, w_down, vecs, b_up)


def pair_kernel(h_ref, du_ref, a_ref, dm_ref, up_ref, down_ref):
    up_ref[...] = dot(h_ref[...], du_ref[...], 0, 0).astype(bf16)
    down_ref[...] = dot(a_ref[...], dm_ref[...], 0, 0).astype(bf16)


def mlp_weight_grads(low, grad_pre, act, dm_all):
    rows, width = low.shape
    hidden = act.shape[1]
    step = 256
    return pl.pallas_call(
        pair_kernel,
        grid=(hidden // step,),
        in_specs=[
            whole((rows, width)),
            pl.BlockSpec((rows, step), lambda i: (0, i)),
            pl.BlockSpec((rows, step), lambda i: (0, i)),
            whole((rows, width)),
        ],
        out_specs=[
            pl.BlockSpec((width, step), lambda i: (0, i)),
            pl.BlockSpec((step, width), lambda i: (i, 0)),
        ],
        out_shape=[
            jax.ShapeDtypeStruct((width, hidden), bf16),
            jax.ShapeDtypeStruct((hidden, width), bf16),
        ],
        compiler_params=params(),
        cost_estimate=cost(4 * rows * width * hidden, width * hidden * 8),
        name="mlp_weight_grads",
    )(low, grad_pre, act, dm_all)


def resid_kernel(idx_ref, parts_ref, r_ref, dm_ref, vec_ref, dr_ref, da_ref, sum_ref):
    total = parts_ref[0].astype(f32)
    for j in range(1, TP):
        total += parts_ref[j].astype(f32)
    units, rstd = unit(r_ref[0])
    dm = dm_ref[...].astype(f32)
    dr = dm + unit_back(total * vec_ref[5:6, :], units, rstd)
    da = dr.astype(bf16)
    dr_ref[...] = dr
    da_ref[...] = da
    sum_ref[...] = jnp.zeros_like(sum_ref)
    sum_ref[0:1, :] = jnp.sum(da.astype(f32), axis=0, keepdims=True)
    sum_ref[1:2, :] = jnp.sum(dm, axis=0, keepdims=True)


def resid_back(idx, parts, r_all, dm, vecs):
    rows, width = dm.shape
    return pl.pallas_call(
        resid_kernel,
        grid_spec=pltpu.PrefetchScalarGridSpec(
            num_scalar_prefetch=1,
            grid=(1,),
            in_specs=[
                whole(parts.shape),
                pl.BlockSpec((1, rows, width), lambda i, idx: (idx[0], 0, 0)),
                whole(dm.shape),
                whole(vecs.shape),
            ],
            out_specs=[whole((rows, width)), whole((rows, width)), whole((8, width))],
        ),
        out_shape=[
            jax.ShapeDtypeStruct((rows, width), f32),
            jax.ShapeDtypeStruct((rows, width), bf16),
            jax.ShapeDtypeStruct((8, width), f32),
        ],
        compiler_params=params(),
        cost_estimate=cost(30 * rows * width, rows * width * 20),
        name="resid_back",
    )(idx, parts, r_all, dm, vecs)


def output_kernel(idx_ref, parts_ref, r_ref, vec_ref, out_ref):
    total = r_ref[0] + vec_ref[7:8, :]
    for j in range(TP):
        total += parts_ref[j].astype(f32)
    out_ref[...] = total.astype(bf16)


def finish_output(idx, parts, r_all, vecs):
    _, rows, width = parts.shape
    return pl.pallas_call(
        output_kernel,
        grid_spec=pltpu.PrefetchScalarGridSpec(
            num_scalar_prefetch=1,
            grid=(1,),
            in_specs=[
                whole(parts.shape),
                pl.BlockSpec((1, rows, width), lambda i, idx: (idx[0], 0, 0)),
                whole(vecs.shape),
            ],
            out_specs=whole((rows, width)),
        ),
        out_shape=jax.ShapeDtypeStruct((rows, width), bf16),
        compiler_params=params(),
        cost_estimate=cost(8 * rows * width, rows * width * 14),
        name="finish_output",
    )(idx, parts, r_all, vecs)


def input_kernel(parts_ref, x_ref, dr_ref, vec_ref, out_ref):
    total = parts_ref[0].astype(f32)
    for j in range(1, TP):
        total += parts_ref[j].astype(f32)
    units, rstd = unit(x_ref[...].astype(f32))
    out_ref[...] = (dr_ref[...] + unit_back(total * vec_ref[3:4, :], units, rstd)).astype(bf16)


def finish_input(parts, x, dr, vecs):
    return pl.pallas_call(
        input_kernel,
        out_shape=jax.ShapeDtypeStruct(x.shape, bf16),
        cost_estimate=cost(30 * x.size, x.size * 16),
        name="finish_input",
    )(parts, x, dr, vecs)


def normed_kernel(n_recv, x_ref, dq_ref, own_ref, *refs):
    recv_refs = refs[:n_recv]
    w_ref, d_ref, dh_ref, sum_ref = refs[n_recv:]
    step = pl.program_id(0)

    @pl.when(step == 0)
    def _():
        sum_ref[...] = jnp.zeros_like(sum_ref)

    cols = dq_ref.shape[1]
    width = x_ref.shape[1]
    grad_k, grad_v = own_ref[0], own_ref[1]
    for ref in recv_refs:
        grad_k += ref[0].astype(f32)
        grad_v += ref[1].astype(f32)
    d_ref[:, :cols] = dq_ref[...]
    d_ref[:, cols : 2 * cols] = grad_k.astype(bf16)
    d_ref[:, 2 * cols : 3 * cols] = grad_v.astype(bf16)
    d_ref[:, 3 * cols :] = jnp.zeros_like(d_ref[:, 3 * cols :])
    low = d_ref[...]
    grad = dot(low, w_ref[...], 1, 1)
    dh_ref[...] = grad.astype(bf16)
    units, _ = unit(x_ref[...].astype(f32))
    sum_ref[0:1, :width] += jnp.sum(grad * units, axis=0, keepdims=True)
    sum_ref[1:2, :width] += jnp.sum(grad, axis=0, keepdims=True)
    sum_ref[2:3, : low.shape[1]] += jnp.sum(low.astype(f32), axis=0, keepdims=True)


def normed_back(x_all, dq, own, recvs, w_qkv):
    rows, width = x_all.shape
    cols = dq.shape[1]
    wide = w_qkv.shape[1]
    step = 128
    pairs = pl.BlockSpec((2, step, cols), lambda i: (0, i, 0))
    return pl.pallas_call(
        functools.partial(normed_kernel, len(recvs)),
        grid=(rows // step,),
        in_specs=[
            pl.BlockSpec((step, width), lambda i: (i, 0)),
            pl.BlockSpec((step, cols), lambda i: (i, 0)),
            pairs,
        ]
        + [pairs] * len(recvs)
        + [whole(w_qkv.shape)],
        out_specs=[
            pl.BlockSpec((step, wide), lambda i: (i, 0)),
            pl.BlockSpec((step, width), lambda i: (i, 0)),
            whole((8, width)),
        ],
        out_shape=[
            jax.ShapeDtypeStruct((rows, wide), bf16),
            jax.ShapeDtypeStruct((rows, width), bf16),
            jax.ShapeDtypeStruct((8, width), f32),
        ],
        compiler_params=params(),
        cost_estimate=cost(2 * rows * width * wide, rows * width * 12),
        name="normed_back",
    )(x_all, dq, own, *recvs, w_qkv)


def proj_grads_kernel(h_ref, d_ref, o_ref, da_ref, v_ref, g_ref):
    wide = d_ref.shape[1]
    cols = da_ref.shape[1]
    g_ref[:, :wide] = dot(h_ref[...], d_ref[...], 0, 0).astype(bf16)
    for j in range(TP):
        at = j * cols
        part = dot(o_ref[j], da_ref[...], 0, 0)
        g_ref[at : at + cols, wide : wide + cols] = part.astype(bf16)
    turned = v_ref[...].T
    g_ref[:, wide + cols :] = turned[:, SMALLS:].astype(bf16)


def proj_grads(low, grads, o_all, da_cols, small):
    rows, width = low.shape
    wide = grads.shape[1] + da_cols.shape[1] + SMALLS
    return pl.pallas_call(
        proj_grads_kernel,
        out_shape=jax.ShapeDtypeStruct((width, wide), bf16),
        compiler_params=pltpu.CompilerParams(vmem_limit_bytes=60 * 1024 * 1024),
        cost_estimate=cost(2 * rows * width * wide, width * wide * 6),
        name="proj_grads",
    )(low, grads, o_all, da_cols, small)


def local(
    plan, inputs, segment_ids, padding, cotangent, w_query, b_query, w_key, w_value, b_value,
    w_out, b_out, ln1_gain, ln1_shift, ln2_gain, ln2_shift, w_up, b_up, w_down, b_down,
):
    x_own = inputs[0]
    rows, width = x_own.shape
    cols = width // TP
    length = segment_ids.shape[1]
    block = w_query.shape[0]
    hidden = w_up.shape[1]
    slab = b_up.shape[0]
    size = plan.size
    member = lax.axis_index(plan.tp)
    part = lax.axis_index(plan.half)
    core = lax.axis_index("c")
    idx = jnp.stack([member, part]).astype(jnp.int32)

    id_rows = jnp.pad(segment_ids[0].astype(bf16), (0, 8 * width - length)).reshape(8, width)
    moved = plan.move(jnp.concatenate([x_own, id_rows], axis=0), plan.route)
    x_mine = moved[:rows]
    ids = moved[rows:].reshape(1, -1)[:, :length].astype(f32)
    dm_own = (cotangent[0].astype(f32) * padding[0].astype(f32)[:, None]).astype(bf16)
    dm_mine = plan.move(dm_own, plan.route)

    small = jnp.stack(
        [b_query, b_value, b_out, ln1_gain, ln1_shift, ln2_gain, ln2_shift, b_down], axis=1
    )
    small = jnp.pad(small, ((0, 0), (0, SMALLS - small.shape[1])))
    split = [w.reshape(block, TP, cols).transpose(1, 0, 2) for w in (w_query, w_key, w_value)]
    chunk = jnp.concatenate(split + [jnp.broadcast_to(small, (TP, block, SMALLS))], axis=2)

    def spread(value):
        dims = [size[a] if a in plan.tp else 1 for a in SAME]
        tail = value.shape[1:]
        value = jnp.broadcast_to(value.reshape(*dims, *tail), (*[size[a] for a in SAME], *tail))
        return value.reshape(-1, *tail)

    got = lax.all_to_all(spread(chunk), SAME, 0, 0, tiled=True)
    both = lax.all_gather(got, "c", axis=0, tiled=True)
    table = plan.shuffle(both, ("c",) + SAME, ALL).reshape(width, -1)
    vecs = table[:, 3 * cols : 3 * cols + 8].T.astype(f32)
    w_qkv = table
    bias = lax.dynamic_slice(vecs, (0, member * cols), (2, cols))

    fields = w_up.reshape(block, plan.devices, slab).transpose(1, 0, 2)
    fields = plan.shuffle(fields, ALL, plan.tp + plan.rep)
    fields = fields.reshape(TP, plan.copies, block, slab).transpose(0, 2, 1, 3)
    fields = fields.reshape(TP, block, -1)
    fields = jnp.concatenate([fields, jnp.broadcast_to(w_out, (TP, block, width))], axis=1)
    fields = lax.all_to_all(fields, plan.tp, 0, 0, tiled=True)
    b_row = jnp.pad(b_up[None], ((0, 7), (0, width - slab)))
    bundle = jnp.concatenate(
        [
            fields[:, :block].reshape(TP * block, -1),
            fields[:, block:].reshape(TP * block, -1),
            w_down,
            b_row,
        ],
        axis=0,
    )
    bundle = lax.all_gather(bundle, plan.rep, axis=0, tiled=False)
    first = TP * block

    def by_row(value):
        value = value.reshape(plan.copies * TP, block, width)
        return plan.shuffle(value, plan.rep + plan.tp, ALL).reshape(width, width)

    up_mine = by_row(bundle[:, :first])
    out_full = by_row(bundle[:, first : 2 * first]).reshape(TP, cols, width)
    down_mine = bundle[:, 2 * first : 2 * first + slab].reshape(-1, width)
    b_up_mine = bundle[:, 2 * first + slab, :slab].reshape(1, -1).astype(f32)

    x_all = lax.all_gather(x_mine, plan.tp, axis=0, tiled=True)
    low_one, query, kv = qkv(x_all, w_qkv, vecs, bias)
    parts = plan.parts

    def turn(value, by):
        table = [(i, (i + by) % parts) for i in range(parts)]
        return lax.ppermute(value, plan.half, table)

    kvs = [kv] + [turn(kv, -j) for j in range(1, parts)]
    mixed, lse = attend(idx, ids, query, kvs)
    o_all = lax.all_gather(mixed, plan.tp, axis=0, tiled=False)
    dm_all = lax.all_gather(dm_mine, plan.tp, axis=0, tiled=True)
    r_all, low_two, act, grad_pre, out_part, dh_two, sum_two, sum_up = mlp(
        x_all, o_all, dm_all, out_full, up_mine, down_mine, vecs, b_up_mine
    )
    r_all = r_all.reshape(TP, rows, width)

    back_two = lax.all_to_all(dh_two.reshape(TP, rows, width), plan.tp, 0, 0, tiled=True)
    grad_up, grad_down = mlp_weight_grads(low_two, grad_pre, act, dm_all)
    dr, da, sum_own = resid_back(idx, back_two, r_all, dm_mine, vecs)
    da_all = lax.all_gather(da, plan.tp, axis=0, tiled=True)
    out_parts = lax.all_to_all(out_part.reshape(TP, rows, width), plan.tp, 0, 0, tiled=True)
    output = plan.move(finish_output(idx, out_parts, r_all, vecs), plan.back)

    grad_up = plan.shuffle(grad_up.reshape(plan.devices, block, -1), ALL, plan.rep + plan.tp)
    up_row = jnp.pad(
        sum_up[0].reshape(plan.copies, 1, slab).astype(bf16), ((0, 0), (0, 7), (0, width - slab))
    )
    summed = jnp.concatenate(
        [
            grad_up.reshape(plan.copies, first, width),
            grad_down.reshape(plan.copies, slab, width),
            up_row,
        ],
        axis=1,
    )
    summed = lax.psum_scatter(summed, plan.rep, scatter_dimension=0, tiled=False)
    g_w_down = summed[first : first + slab].astype(f32)
    g_b_up = summed[first + slab, :slab].astype(f32)
    ups = lax.all_to_all(summed[:first].reshape(TP, block, width), plan.tp, 0, 0, tiled=True)
    ups = ups.reshape(TP, block, plan.copies, slab).transpose(0, 2, 1, 3)
    ups = plan.shuffle(ups.reshape(plan.devices, block, slab), plan.tp + plan.rep, ALL)
    g_w_up = ups.transpose(1, 0, 2).reshape(block, hidden).astype(f32)

    results = attend_back(idx, ids, query, da_all, out_full, lse, kvs)
    grad_query, kv_own, kv_others = results[0], results[1], results[2:]
    recvs = [turn(kv_others[j - 1], j) for j in range(1, parts)]
    grads, dh_one, sum_one = normed_back(x_all, grad_query, kv_own, recvs, w_qkv)
    back_one = lax.all_to_all(dh_one.reshape(TP, rows, width), plan.tp, 0, 0, tiled=True)

    def placed(vector):
        return lax.dynamic_update_slice(jnp.zeros((width,), f32), vector, (member * cols,))

    vectors = [
        placed(sum_one[2, :cols]),
        placed(sum_one[2, 2 * cols : 3 * cols]),
        sum_own[0],
        sum_one[0],
        sum_one[1],
        sum_two[0],
        sum_two[1],
        sum_own[1],
    ]
    vectors = jnp.pad(jnp.stack(vectors), ((SMALLS, 2 * SMALLS - 8 - SMALLS), (0, 0)))
    da_cols = lax.dynamic_slice(da_all, (0, member * cols), (TP * rows, cols))
    chunk = proj_grads(low_one, grads, o_all, da_cols, vectors)
    chunk = chunk.reshape(size["gx"], 2, -1, block, chunk.shape[1])
    keep = lax.dynamic_index_in_dim(chunk, core, 1, keepdims=False)
    send = lax.dynamic_index_in_dim(chunk, 1 - core, 1, keepdims=False)
    other = lax.ppermute(send, "c", [(0, 1), (1, 0)])
    chunk = (keep.astype(f32) + other.astype(f32)).astype(bf16)
    chunk = chunk.reshape(-1, *chunk.shape[2:])
    chunk = lax.all_to_all(chunk, SAME, 0, 0, tiled=True).astype(f32)
    dims = [size[a] for a in SAME]
    chunk = chunk.reshape(*dims, *chunk.shape[1:])
    chunk = jnp.sum(chunk, axis=tuple(i for i, a in enumerate(SAME) if a not in plan.tp))
    chunk = chunk.reshape(TP, block, -1)

    def joined(at):
        return chunk[:, :, at : at + cols].transpose(1, 0, 2).reshape(block, width)

    wide = w_qkv.shape[1]
    vec = jnp.sum(chunk[:, :, wide + cols : wide + cols + 8], axis=0)

    grad_input = plan.move(finish_input(back_one, x_mine, dr, vecs), plan.back)
    return (
        output[None],
        grad_input[None],
        joined(0),
        vec[:, 0],
        joined(cols),
        joined(2 * cols),
        vec[:, 1],
        joined(wide),
        vec[:, 2],
        vec[:, 3],
        vec[:, 4],
        vec[:, 5],
        vec[:, 6],
        g_w_up,
        g_b_up,
        g_w_down,
        vec[:, 7],
    )


def solution(mesh):
    groups, blocks = mesh.shape["grp"], mesh.shape["seq"]
    plan = Plan(groups, blocks)
    fine = Mesh(mesh.devices.reshape(plan.shape), ALL)
    grp, seq = ("gx", "c"), ("sz", "sy")
    matrix, vector = P(ALL, None), P(ALL)
    token = P(grp, seq, None)
    return jax.shard_map(
        functools.partial(local, plan),
        mesh=fine,
        in_specs=(
            token, P(grp, None), P(grp, seq), token,
            matrix, vector, matrix, matrix, vector, matrix, vector,
            vector, vector, vector, vector, matrix, vector, matrix, vector,
        ),
        out_specs=(
            token, token,
            matrix, vector, matrix, matrix, vector, matrix, vector,
            vector, vector, vector, vector, matrix, vector, matrix, vector,
        ),
        check_vma=False,
    )
```

```python
import functools

import jax
import jax.numpy as jnp
from jax import lax
from jax.experimental import pallas as pl
from jax.experimental.pallas import tpu as pltpu
from jax.sharding import Mesh, PartitionSpec as P

HEADS = 12
HEAD_DIM = 64
TP = 4
HEADS_TP = HEADS // TP
EPS = 1e-05
NEG = -1e30
SCALE = 0.125
ALL = ("gx", "c", "sz", "sy")
SAME = ("gx", "sz", "sy")
SMALLS = 64
f32 = jnp.float32
bf16 = jnp.bfloat16


class Plan:
    def __init__(self, groups, blocks):
        if (groups, blocks) == (4, 8):
            self.shape = (2, 2, 4, 2)
            self.tp, self.half, self.rep = ("gx", "sy"), "c", ("c", "sz")
            self.fast = True
        else:
            self.shape = (groups // 2, 2, blocks // TP, TP)
            self.tp, self.half, self.rep = ("sy",), "sz", ("gx", "c", "sz")
            self.fast = False
        self.size = dict(zip(ALL, self.shape))
        self.devices = groups * blocks
        self.parts = self.size[self.half]
        self.copies = self.devices // TP
        self.lines = tuple(a for a in self.rep if a != "c")
        self.route = []
        for src in range(self.devices):
            seq, block = divmod(src, blocks)
            part, member = divmod(block, TP)
            if self.tp == ("sy",):
                dst = src
            else:
                dst = (((member >> 1) * 2 + part) * 4 + seq) * 2 + (member & 1)
            self.route.append((src, dst))
        self.back = [(dst, src) for src, dst in self.route]

    def swap(self, value):
        return lax.ppermute(value, "c", [(0, 1), (1, 0)])

    def partner(self, value, j):
        table = [(t, t ^ j) for t in range(TP)]
        return lax.ppermute(value, self.tp, table)

    def partners(self, value):
        return [value] + [self.partner(value, j) for j in range(1, TP)]

    def reduce(self, values):
        return [values[0]] + [self.partner(values[j], j) for j in range(1, TP)]

    def turn(self, value, axis, by):
        count = self.size[axis]
        return lax.ppermute(value, axis, [(i, (i + by) % count) for i in range(count)])

    def place(self, r):
        at, rest = {}, r
        for axis in reversed(ALL):
            rest, at[axis] = divmod(rest, self.size[axis])
        numbers = []
        for axes in (self.tp, self.rep):
            number = 0
            for axis in axes:
                number = number * self.size[axis] + at[axis]
            numbers.append(number)
        return tuple(numbers)

    def same(self, n):
        span = self.devices // 2 // self.size["gx"]
        gx, rest = divmod(n, span)
        return gx * 2 * span + rest

    def move(self, value, table):
        if all(a == b for a, b in table):
            return value
        return lax.ppermute(value, ALL, table)

    def shuffle(self, value, before, after):
        tail = value.shape[1:]
        dims = [self.size[a] for a in before]
        order = [before.index(a) for a in after]
        value = value.reshape(*dims, *tail)
        value = value.transpose(*order, *range(len(dims), len(dims) + len(tail)))
        return value.reshape(-1, *tail)


def dot(left, right, left_dim=1, right_dim=0):
    return lax.dot_general(
        left, right, (((left_dim,), (right_dim,)), ((), ())), preferred_element_type=f32
    )


def unit(values):
    center = values - jnp.mean(values, axis=-1, keepdims=True)
    variance = jnp.mean(center * center, axis=-1, keepdims=True)
    rstd = lax.rsqrt(variance + EPS)
    return center * rstd, rstd


def unit_back(grad_unit, units, rstd):
    first = jnp.mean(grad_unit, axis=-1, keepdims=True)
    second = jnp.mean(grad_unit * units, axis=-1, keepdims=True)
    return rstd * (grad_unit - first - units * second)


def params(limit=60 * 1024 * 1024, axes=1):
    return pltpu.CompilerParams(
        dimension_semantics=("arbitrary",) * axes, vmem_limit_bytes=limit
    )


def cost(flops, nbytes, trans=0):
    return pl.CostEstimate(flops=int(flops), bytes_accessed=int(nbytes), transcendentals=int(trans))


def whole(shape):
    zeros = (0,) * len(shape)
    return pl.BlockSpec(shape, lambda *_: zeros)


def head_lanes(value, head):
    lane = lax.broadcasted_iota(jnp.int32, value.shape, 1)
    keep = (lane >= head * HEAD_DIM) & (lane < (head + 1) * HEAD_DIM)
    return jnp.where(keep, value, jnp.zeros_like(value))


def member_cols(row, member, cols):
    out = jnp.zeros((row.shape[0], cols), row.dtype)
    for j in range(TP):
        out = jnp.where(member == j, row[:, j * cols : (j + 1) * cols], out)
    return out


def prep_kernel(rep_of, idx_ref, q_ref, k_ref, v_ref, small_ref, up_ref, *refs):
    chunk_refs, hold_ref = refs[:-1], refs[-1]
    block, width = q_ref.shape
    cols = width // TP
    wide = 3 * cols + SMALLS
    slab = up_ref.shape[1] // len(rep_of)
    for j in range(TP):
        at = slice(j * cols, (j + 1) * cols)
        hold_ref[j, :, :wide] = jnp.concatenate(
            [r[:, at].astype(f32) for r in (q_ref, k_ref, v_ref)] + [small_ref[...].astype(f32)],
            axis=1,
        )
    for r, (member, copy) in enumerate(rep_of):
        first = wide + copy * slab
        hold_ref[member, :, first : first + slab] = up_ref[:, r * slab : (r + 1) * slab].astype(f32)
    for j, ref in enumerate(chunk_refs):
        ref[...] = hold_ref[idx_ref[0] ^ j].astype(bf16)


def prepare(plan, idx, w_query, w_key, w_value, small, w_up):
    block, width = w_query.shape
    rep_of = [plan.place(r) for r in range(plan.devices)]
    shape = (block, 3 * width // TP + SMALLS + w_up.shape[1] // TP)
    return pl.pallas_call(
        functools.partial(prep_kernel, rep_of),
        in_specs=[pl.BlockSpec(memory_space=pltpu.SMEM)]
        + [pl.BlockSpec(memory_space=pltpu.VMEM)] * 5,
        out_shape=[jax.ShapeDtypeStruct(shape, bf16)] * TP,
        scratch_shapes=[pltpu.VMEM((TP, *shape), f32)],
        cost_estimate=cost(1000, 4 * w_up.size),
        name="prepare",
    )(idx, w_query, w_key, w_value, small, w_up)


def shards_kernel(idx_ref, *refs):
    part_refs, (proj_ref, up_ref, hold_ref) = refs[:TP], refs[TP:]
    for j, ref in enumerate(part_refs):
        hold_ref[idx_ref[0] ^ j] = ref[...].astype(f32)
    wide = proj_ref.shape[1]
    value = hold_ref[...].reshape(proj_ref.shape[0], -1).astype(bf16)
    proj_ref[...] = value[:, :wide]
    up_ref[...] = value[:, wide:]


def shards_of(idx, parts, wide):
    block, both = parts[0].shape
    return pl.pallas_call(
        shards_kernel,
        in_specs=[pl.BlockSpec(memory_space=pltpu.SMEM)]
        + [pl.BlockSpec(memory_space=pltpu.VMEM)] * TP,
        out_shape=[
            jax.ShapeDtypeStruct((TP * block, wide), bf16),
            jax.ShapeDtypeStruct((TP * block, both - wide), bf16),
        ],
        scratch_shapes=[pltpu.VMEM((TP, block, both), f32)],
        cost_estimate=cost(1000, 8 * TP * block * both),
        name="shards_of",
    )(idx, *parts)


def assemble_kernel(plan, idx_ref, *refs):
    lines = plan.copies // 2
    sides = refs[: 2 * (1 + lines + TP)]
    up_ref, out_ref, down_ref, row_ref, wide_ref = refs[2 * (1 + lines + TP) :]
    member, core, line = idx_ref[0], idx_ref[2], idx_ref[3]
    block = up_ref.shape[0] // plan.devices
    slab = down_ref.shape[2]
    pair = plan.size["sy"] * block
    for n, side in ((0, core), (1, 1 - core)):
        mine = sides[n * (1 + lines + TP) : (n + 1) * (1 + lines + TP)]
        raw_ref, up_refs, out_refs = mine[0], mine[1 : 1 + lines], mine[1 + lines :]
        for z in range(lines):
            down_ref[side, z] = raw_ref[z, block : block + slab, :]
            row_ref[side, z] = raw_ref[z, block + slab :, :]
        for j, ref in enumerate(up_refs):
            z = lax.rem(line + j, lines)
            value = ref[...].astype(f32)
            for gx in range(plan.size["gx"]):
                for sy in range(plan.size["sy"]):
                    at = gx * pair + sy * block
                    wide_ref[0, gx * 2 + side, z, sy] = value[at : at + block]
        for j, ref in enumerate(out_refs):
            other = member ^ j
            gx, sy = other // plan.size["sy"], lax.rem(other, plan.size["sy"])
            for z in range(lines):
                wide_ref[1, gx * 2 + side, z, sy] = ref[z].astype(f32)
    for ref, k in ((up_ref, 0), (out_ref, 1)):
        ref[...] = wide_ref[k].reshape(ref.shape).astype(bf16)


def assemble(plan, idx, own, other, block, slab):
    width = own[0].shape[2]
    lines = plan.copies // 2
    hidden = plan.copies * slab
    operands = [*own, *other]
    return pl.pallas_call(
        functools.partial(assemble_kernel, plan),
        in_specs=[pl.BlockSpec(memory_space=pltpu.SMEM)]
        + [pl.BlockSpec(memory_space=pltpu.VMEM)] * len(operands),
        out_shape=[
            jax.ShapeDtypeStruct((width, hidden), bf16),
            jax.ShapeDtypeStruct((width, width), bf16),
            jax.ShapeDtypeStruct((2, lines, slab, width), bf16),
            jax.ShapeDtypeStruct((2, lines, 8, width), bf16),
        ],
        scratch_shapes=[
            pltpu.VMEM((2, 2 * plan.size["gx"], lines, plan.size["sy"], block, width), f32)
        ],
        compiler_params=pltpu.CompilerParams(vmem_limit_bytes=60 * 1024 * 1024),
        cost_estimate=cost(1000, 12 * width * width),
        name="assemble",
    )(idx, *operands)


def qkv_kernel(plan, idx_ref, x_ref, *refs):
    fast = plan.fast
    if fast:
        own_ref, other_ref, h_ref, q_ref, kv_ref, w_ref, vec_ref, wide_ref = refs
    else:
        w_ref, vec_ref, h_ref, q_ref, kv_ref = refs
    cols = q_ref.shape[1]
    if fast:

        @pl.when(pl.program_id(0) == 0)
        def _():
            core = idx_ref[2]
            line = idx_ref[3]
            lines, rows, _ = own_ref.shape
            pair = rows // plan.size["gx"]
            for ref, side in ((own_ref, core), (other_ref, 1 - core)):
                for j in range(lines):
                    z = lax.rem(line + j, lines)
                    value = ref[j].astype(f32)
                    for gx in range(plan.size["gx"]):
                        wide_ref[gx * 2 + side, z] = value[gx * pair : (gx + 1) * pair, :]
            table = wide_ref[...].reshape(w_ref.shape)
            w_ref[...] = table.astype(bf16)
            vec_ref[...] = table[:, 512:640].T[64:72, :]

    units, _ = unit(x_ref[...].astype(f32))
    low = (units * vec_ref[3:4, :] + vec_ref[4:5, :]).astype(bf16)
    h_ref[...] = low
    out = dot(low, w_ref[...])
    bias = member_cols(vec_ref[0:2, :], idx_ref[0], cols)
    query = (out[:, :cols] + bias[0:1, :]).astype(bf16)
    q_ref[...] = (query.astype(f32) * SCALE).astype(bf16)
    kv_ref[0] = out[:, cols : 2 * cols].astype(bf16)
    kv_ref[1] = (out[:, 2 * cols : 3 * cols] + bias[1:2, :]).astype(bf16)


def qkv(plan, idx, x_all, *operands):
    rows, width = x_all.shape
    cols = width // TP
    step = rows // TP
    wide = 3 * cols + SMALLS
    out_specs = [
        pl.BlockSpec((step, width), lambda i, *_: (i, 0)),
        pl.BlockSpec((step, cols), lambda i, *_: (i, 0)),
        pl.BlockSpec((2, step, cols), lambda i, *_: (0, i, 0)),
    ]
    out_shape = [
        jax.ShapeDtypeStruct((rows, width), bf16),
        jax.ShapeDtypeStruct((rows, cols), bf16),
        jax.ShapeDtypeStruct((2, rows, cols), bf16),
    ]
    scratch = []
    if plan.fast:
        out_specs += [whole((width, wide)), whole((8, width))]
        out_shape += [
            jax.ShapeDtypeStruct((width, wide), bf16),
            jax.ShapeDtypeStruct((8, width), f32),
        ]
        lines = plan.copies // 2
        scratch = [pltpu.VMEM((2 * plan.size["gx"], lines, width // (2 * plan.size["gx"] * lines), wide), f32)]
    return pl.pallas_call(
        functools.partial(qkv_kernel, plan),
        grid_spec=pltpu.PrefetchScalarGridSpec(
            num_scalar_prefetch=1,
            grid=(TP,),
            in_specs=[pl.BlockSpec((step, width), lambda i, *_: (i, 0))]
            + [whole(v.shape) for v in operands],
            out_specs=out_specs,
            scratch_shapes=scratch,
        ),
        out_shape=out_shape,
        compiler_params=params(),
        cost_estimate=cost(2 * rows * width * 3 * cols, rows * width * 8),
        name="qkv",
    )(idx, x_all, *operands)


def fill_docs(ids_ref, part, parts, doc_ref):
    span, width = doc_ref.shape[1:]
    for j in range(parts):
        at = lax.rem(part + j, parts) * span
        row = ids_ref[0:1, pl.ds(pl.multiple_of(at, 512), span)]
        doc_ref[j] = jnp.broadcast_to(row, (width, span)).T


def fwd_kernel(parts, idx_ref, ids_ref, q_ref, *refs):
    kv_refs = refs[:parts]
    o_ref, lse_ref, turned, doc_ref = refs[parts:]
    step = pl.program_id(0)
    part = idx_ref[1]
    span = kv_refs[0].shape[1]
    width = q_ref.shape[0]

    @pl.when(step == 0)
    def _():
        fill_docs(ids_ref, part, parts, doc_ref)
        for j in range(parts):
            turned[j] = kv_refs[j][1].T

    at = part * span + step * width
    own = ids_ref[0:1, pl.ds(pl.multiple_of(at, 128), width)]
    query = q_ref[...]
    outs, lses = [], []
    for head in range(HEADS_TP):
        masked = head_lanes(query, head)
        scores = []
        for j in range(parts):
            raw = dot(kv_refs[j][0], masked, 1, 1)
            scores.append(jnp.where(doc_ref[j] == own, raw, NEG))
        peak = functools.reduce(
            jnp.maximum, [jnp.max(s, axis=0, keepdims=True) for s in scores]
        )
        exps = [jnp.exp(s - peak) for s in scores]
        total = functools.reduce(jnp.add, [jnp.sum(e, axis=0, keepdims=True) for e in exps])
        scale = 1.0 / total
        acc = None
        for j in range(parts):
            probs = (exps[j] * scale).astype(bf16)
            term = dot(turned[j, head * HEAD_DIM : (head + 1) * HEAD_DIM, :], probs)
            acc = term if acc is None else acc + term
        outs.append(acc)
        lses.append(peak + jnp.log(total))
    o_ref[...] = jnp.concatenate(outs, axis=0).T.astype(bf16)
    for head in range(HEADS_TP):
        lse_ref[head : head + 1, :] = lses[head]


def attend(idx, ids, q, kvs, width=256):
    rows, cols = q.shape
    parts = len(kvs)
    span = kvs[0].shape[1]
    return pl.pallas_call(
        functools.partial(fwd_kernel, parts),
        grid_spec=pltpu.PrefetchScalarGridSpec(
            num_scalar_prefetch=1,
            grid=(rows // width,),
            in_specs=[whole(ids.shape), pl.BlockSpec((width, cols), lambda i, *_: (i, 0))]
            + [whole(kv.shape) for kv in kvs],
            out_specs=[
                pl.BlockSpec((width, cols), lambda i, *_: (i, 0)),
                pl.BlockSpec((8, width), lambda i, *_: (0, i)),
            ],
            scratch_shapes=[
                pltpu.VMEM((parts, cols, span), bf16),
                pltpu.VMEM((parts, span, width), f32),
            ],
        ),
        out_shape=[
            jax.ShapeDtypeStruct((rows, cols), bf16),
            jax.ShapeDtypeStruct((8, rows), f32),
        ],
        compiler_params=params(),
        cost_estimate=cost(4 * rows * span * parts * cols, span * parts * cols * 4, rows * span * parts * HEADS_TP),
        name="attend",
    )(idx, ids, q, *kvs)


def bwd_kernel(parts, idx_ref, ids_ref, q_ref, w_ref, lse_ref, *refs):
    da_refs, refs = refs[:TP], refs[TP:]
    kv_refs = refs[:parts]
    dq_ref, own_ref, cols_ref = refs[parts : parts + 3]
    other_refs = refs[parts + 3 : 2 * parts + 2]
    turned, doc_ref, key_acc, value_acc, mixed_ref = refs[2 * parts + 2 :]
    step = pl.program_id(0)
    part = idx_ref[1]
    span = kv_refs[0].shape[1]
    width, cols = q_ref.shape

    @pl.when(step == 0)
    def _():
        fill_docs(ids_ref, part, parts, doc_ref)
        for j in range(parts):
            turned[j] = kv_refs[j][0].T
        key_acc[...] = jnp.zeros_like(key_acc)
        value_acc[...] = jnp.zeros_like(value_acc)
        member = idx_ref[0]
        for j in range(TP):
            da = da_refs[j][...]
            mixed_ref[member ^ j] = dot(da, w_ref[0], 1, 1).astype(bf16)
            cols_ref[member ^ j] = member_cols(da, member, cols)

    at = part * span + step * width
    own = ids_ref[0:1, pl.ds(pl.multiple_of(at, 128), width)]
    query = q_ref[...]
    group = width // mixed_ref.shape[1]
    grad_mixed = mixed_ref[pl.ds(step * group, group)].reshape(width, cols)
    turned_grads = []
    for head in range(HEADS_TP):
        masked_q = head_lanes(query, head)
        masked_g = head_lanes(grad_mixed, head)
        lse = lse_ref[head : head + 1, :]
        probs, grads = [], []
        for j in range(parts):
            raw = dot(kv_refs[j][0], masked_q, 1, 1)
            probs.append(jnp.exp(jnp.where(doc_ref[j] == own, raw, NEG) - lse))
            grads.append(dot(kv_refs[j][1], masked_g, 1, 1))
        delta = functools.reduce(
            jnp.add,
            [jnp.sum(p * g, axis=0, keepdims=True) for p, g in zip(probs, grads)],
        )
        acc = None
        for j in range(parts):
            grad_scores = (probs[j] * (grads[j] - delta)).astype(bf16)
            value_acc[j] += dot(probs[j].astype(bf16), masked_g)
            key_acc[j] += dot(grad_scores, masked_q)
            term = dot(turned[j, head * HEAD_DIM : (head + 1) * HEAD_DIM, :], grad_scores)
            acc = term if acc is None else acc + term
        turned_grads.append(acc)
    dq_ref[...] = (jnp.concatenate(turned_grads, axis=0).T * SCALE).astype(bf16)

    @pl.when(step == pl.num_programs(0) - 1)
    def _():
        own_ref[0] = key_acc[0]
        own_ref[1] = value_acc[0]
        for j in range(1, parts):
            other_refs[j - 1][0] = key_acc[j].astype(bf16)
            other_refs[j - 1][1] = value_acc[j].astype(bf16)


def attend_back(idx, ids, q, das, w_out, lse, kvs, width=256):
    rows, cols = q.shape
    step, model = das[0].shape
    parts = len(kvs)
    span = kvs[0].shape[1]
    return pl.pallas_call(
        functools.partial(bwd_kernel, parts),
        grid_spec=pltpu.PrefetchScalarGridSpec(
            num_scalar_prefetch=1,
            grid=(rows // width,),
            in_specs=[
                whole(ids.shape),
                pl.BlockSpec((width, cols), lambda i, *_: (i, 0)),
                pl.BlockSpec((1, cols, model), lambda i, idx: (idx[0], 0, 0)),
                pl.BlockSpec((8, width), lambda i, *_: (0, i)),
            ]
            + [whole((step, model))] * TP
            + [whole(kv.shape) for kv in kvs],
            out_specs=[
                pl.BlockSpec((width, cols), lambda i, *_: (i, 0)),
                whole((2, span, cols)),
                whole((TP, step, cols)),
            ]
            + [whole((2, span, cols))] * (parts - 1),
            scratch_shapes=[
                pltpu.VMEM((parts, cols, span), bf16),
                pltpu.VMEM((parts, span, width), f32),
                pltpu.VMEM((parts, span, cols), f32),
                pltpu.VMEM((parts, span, cols), f32),
                pltpu.VMEM((TP, step, cols), bf16),
            ],
        ),
        out_shape=[
            jax.ShapeDtypeStruct((rows, cols), bf16),
            jax.ShapeDtypeStruct((2, span, cols), f32),
            jax.ShapeDtypeStruct((TP, step, cols), bf16),
        ]
        + [jax.ShapeDtypeStruct((2, span, cols), bf16)] * (parts - 1),
        compiler_params=params(),
        cost_estimate=cost(10 * rows * span * parts * cols, span * parts * cols * 12, rows * span * parts * HEADS_TP),
        name="attend_back",
    )(idx, ids, q, w_out, lse, *das, *kvs)


def mlp_kernel(idx_ref, x_ref, *refs):
    o_refs, dm_refs, refs = refs[:TP], refs[TP : 2 * TP], refs[2 * TP :]
    wo_ref, wu_ref, wd_ref, vec_ref, bup_ref, r_ref, h_ref, a_ref, du_ref, dm_ref, sum_ref = refs[:11]
    dh_refs, dm_now, dh_now = refs[11 : 11 + TP], refs[-2], refs[-1]
    step = pl.program_id(0)
    member = idx_ref[0]

    @pl.when(step == 0)
    def _():
        sum_ref[...] = jnp.zeros_like(sum_ref)

    attended = dot(o_refs[0][...], wo_ref[member])
    for j in range(1, TP):
        attended += dot(o_refs[j][...], wo_ref[member ^ j])
    residual = x_ref[...].astype(f32) + (attended + vec_ref[2:3, :])

    for j in range(TP):

        @pl.when(step == j)
        def _(j=j):
            dm_now[...] = dm_refs[j][...]
            if j == 0:
                r_ref[...] = residual

    units, _ = unit(residual)
    low = (units * vec_ref[5:6, :] + vec_ref[6:7, :]).astype(bf16)
    h_ref[...] = low
    pre = dot(low, wu_ref[...]) + bup_ref[...]
    normal = 0.5 * (1.0 + lax.erf(pre * 0.7071067811865476))
    act = (pre * normal).astype(bf16)
    a_ref[...] = act
    slope = normal + pre * (0.3989422804014327 * jnp.exp(-0.5 * pre * pre))
    dm = dm_now[...]
    dm_ref[...] = dm
    grad_pre = (dot(dm, wd_ref[...], 1, 1) * slope).astype(bf16)
    du_ref[...] = grad_pre
    grad = dot(grad_pre, wu_ref[...], 1, 1)
    sum_ref[0:1, :] += jnp.sum(grad * units, axis=0, keepdims=True)
    sum_ref[1:2, :] += jnp.sum(grad, axis=0, keepdims=True)
    dh_now[...] = grad.astype(bf16)
    for j in range(TP):

        @pl.when(step == j)
        def _(j=j):
            dh_refs[j][...] = dh_now[...]


def mlp(idx, x_all, os, dms, w_out, w_up, w_down, vecs, b_up):
    rows, width = x_all.shape
    hidden = w_up.shape[1]
    cols = width // TP
    step = rows // TP
    token = pl.BlockSpec((step, width), lambda i, idx: (i ^ idx[0], 0))
    inner = pl.BlockSpec((step, hidden), lambda i, idx: (i ^ idx[0], 0))
    head = pl.BlockSpec((step, cols), lambda i, idx: (i ^ idx[0], 0))
    one = whole((step, width))
    return pl.pallas_call(
        mlp_kernel,
        grid_spec=pltpu.PrefetchScalarGridSpec(
            num_scalar_prefetch=1,
            grid=(TP,),
            in_specs=[token]
            + [head] * TP
            + [one] * TP
            + [whole(v.shape) for v in (w_out, w_up, w_down, vecs, b_up)],
            out_specs=[one, token, inner, inner, token, whole((8, width))] + [one] * TP,
            scratch_shapes=[pltpu.VMEM((step, width), bf16), pltpu.VMEM((step, width), bf16)],
        ),
        out_shape=[
            jax.ShapeDtypeStruct((step, width), f32),
            jax.ShapeDtypeStruct((rows, width), bf16),
            jax.ShapeDtypeStruct((rows, hidden), bf16),
            jax.ShapeDtypeStruct((rows, hidden), bf16),
            jax.ShapeDtypeStruct((rows, width), bf16),
            jax.ShapeDtypeStruct((8, width), f32),
        ]
        + [jax.ShapeDtypeStruct((step, width), bf16)] * TP,
        compiler_params=params(),
        cost_estimate=cost(2 * rows * width * (width + 3 * hidden), rows * width * 24, rows * hidden * 4),
        name="mlp",
    )(idx, x_all, *os, *dms, w_out, w_up, w_down, vecs, b_up)


def pair_kernel(plan, idx_ref, h_ref, du_ref, a_ref, dm_ref, wd_ref, near_ref, far_ref, *refs):
    out_refs, acc_ref, wide_ref = refs[:TP], refs[TP], refs[TP + 1]
    lines = plan.copies // 2
    step = pl.program_id(0)
    member, core = idx_ref[0], idx_ref[2]
    half = step ^ core
    grad_pre = du_ref[...]
    act = a_ref[...]
    width = h_ref.shape[1]
    block = width // plan.devices
    size = act.shape[1]
    slab = size // lines
    first = TP * block
    up = dot(h_ref[...], grad_pre, 0, 0)
    down = dot(act, dm_ref[...], 0, 0)
    bias = jnp.sum(grad_pre.astype(f32), axis=0, keepdims=True)
    term = dot(act, wd_ref[...])

    @pl.when(step == 0)
    def _():
        acc_ref[...] = term.reshape(acc_ref.shape)
        wide_ref[:, :size] = up

    @pl.when(step == 1)
    def _():
        acc_ref[...] += term.reshape(acc_ref.shape)
        for j in range(TP):
            out_refs[j][...] = acc_ref[member ^ j].astype(bf16)
        wide_ref[:, size:] = up
        pair = plan.size["sy"] * block
        for ref, owner in ((near_ref, core), (far_ref, 1 - core)):
            for z in range(lines):
                for gx in range(plan.size["gx"]):
                    at = ((gx * 2 + owner) * lines + z) * pair
                    value = wide_ref[pl.ds(pl.multiple_of(at, 16), pair), :]
                    ref[z, gx * pair : (gx + 1) * pair, :] = value.astype(bf16)

    def put(ref):
        for k in range(lines):
            at = k * slab
            row = jnp.concatenate(
                [bias[:, at : at + slab], jnp.zeros((1, width - slab), f32)], axis=1
            )
            ref[k, first : first + slab, :] = down[at : at + slab, :].astype(bf16)
            ref[k, first + slab :, :] = jnp.broadcast_to(row, (8, width)).astype(bf16)

    @pl.when(half == 0)
    def _():
        put(near_ref)

    @pl.when(half == 1)
    def _():
        put(far_ref)


def mlp_weight_grads(plan, idx, low, grad_pre, act, dm_all, w_down):
    rows, width = low.shape
    hidden = act.shape[1]
    step = hidden // 2
    lines = plan.copies // 2
    block = width // plan.devices
    slab = hidden // plan.copies
    bundle = (lines, TP * block + slab + 8, width)
    token = (rows // TP, width)
    return pl.pallas_call(
        functools.partial(pair_kernel, plan),
        grid_spec=pltpu.PrefetchScalarGridSpec(
            num_scalar_prefetch=1,
            grid=(2,),
            in_specs=[
                whole((rows, width)),
                pl.BlockSpec((rows, step), lambda i, idx: (0, i)),
                pl.BlockSpec((rows, step), lambda i, idx: (0, i)),
                whole((rows, width)),
                pl.BlockSpec((step, width), lambda i, idx: (i, 0)),
            ],
            out_specs=[whole(bundle)] * 2 + [whole(token)] * TP,
            scratch_shapes=[
                pltpu.VMEM((TP, *token), f32),
                pltpu.VMEM((width, hidden), f32),
            ],
        ),
        out_shape=[jax.ShapeDtypeStruct(bundle, bf16)] * 2
        + [jax.ShapeDtypeStruct(token, bf16)] * TP,
        compiler_params=params(),
        cost_estimate=cost(6 * rows * width * hidden, width * hidden * 12),
        name="mlp_weight_grads",
    )(idx, low, grad_pre, act, dm_all, w_down)


def add_kernel(*refs):
    *in_refs, out_ref = refs
    total = in_refs[0][...].astype(f32)
    for ref in in_refs[1:]:
        total += ref[...].astype(f32)
    out_ref[...] = total.astype(out_ref.dtype)


def add(*values, dtype=bf16):
    return pl.pallas_call(
        add_kernel,
        out_shape=jax.ShapeDtypeStruct(values[0].shape, dtype),
        compiler_params=pltpu.CompilerParams(vmem_limit_bytes=60 * 1024 * 1024),
        cost_estimate=cost(values[0].size * len(values), 2 * values[0].size * (len(values) + 1)),
        name="add",
    )(*values)


def rows_kernel(plan, idx_ref, *refs):
    term_ref, up_refs = refs[0], refs[1 : 1 + TP]
    down_ref, row_ref, total_ref = refs[1 + TP :]
    member = idx_ref[0]
    total = term_ref[0].astype(f32)
    for z in range(1, term_ref.shape[0]):
        total += term_ref[z].astype(f32)
    block = up_refs[0].shape[0]
    first, slab = TP * block, down_ref.shape[0]
    total_ref[...] = total[:first].reshape(total_ref.shape)
    for j in range(TP):
        up_refs[j][...] = total_ref[member ^ j].astype(bf16)
    down_ref[...] = total[first : first + slab]
    row_ref[...] = total[first + slab : first + slab + 1, :slab]


def sum_rows(plan, idx, terms, block, slab):
    lines, rows, width = terms.shape
    return pl.pallas_call(
        functools.partial(rows_kernel, plan),
        in_specs=[pl.BlockSpec(memory_space=pltpu.SMEM), pl.BlockSpec(memory_space=pltpu.VMEM)],
        out_shape=[jax.ShapeDtypeStruct((block, width), bf16)] * TP
        + [jax.ShapeDtypeStruct((slab, width), f32), jax.ShapeDtypeStruct((1, slab), f32)],
        scratch_shapes=[pltpu.VMEM((TP, block, width), f32)],
        cost_estimate=cost(lines * rows * width, 2 * lines * rows * width),
        name="sum_rows",
    )(idx, terms)


def up_kernel(plan, idx_ref, *refs):
    part_refs, out_ref, hold_ref = refs[:TP], refs[TP], refs[TP + 1]
    member = idx_ref[0]
    for j in range(TP):
        hold_ref[member ^ j] = part_refs[j][...].astype(f32)
    slab = out_ref.shape[1] // plan.devices
    for r in range(plan.devices):
        t, copy = plan.place(r)
        out_ref[:, r * slab : (r + 1) * slab] = hold_ref[t, :, copy * slab : (copy + 1) * slab]


def join_up(plan, idx, parts, hidden):
    block, width = parts[0].shape
    return pl.pallas_call(
        functools.partial(up_kernel, plan),
        in_specs=[pl.BlockSpec(memory_space=pltpu.SMEM)]
        + [pl.BlockSpec(memory_space=pltpu.VMEM)] * TP,
        out_shape=jax.ShapeDtypeStruct((block, hidden), f32),
        scratch_shapes=[pltpu.VMEM((TP, block, width), f32)],
        cost_estimate=cost(block * hidden, 6 * block * hidden),
        name="join_up",
    )(idx, *parts)


def resid_kernel(r_ref, dm_ref, vec_ref, *refs):
    part_refs, (dr_ref, da_ref, sum_ref) = refs[:TP], refs[TP:]
    total = part_refs[0][...].astype(f32)
    for j in range(1, TP):
        total += part_refs[j][...].astype(f32)
    units, rstd = unit(r_ref[...])
    dm = dm_ref[...].astype(f32)
    dr = dm + unit_back(total * vec_ref[5:6, :], units, rstd)
    da = dr.astype(bf16)
    dr_ref[...] = dr
    da_ref[...] = da
    sum_ref[...] = jnp.zeros_like(sum_ref)
    sum_ref[0:1, :] = jnp.sum(da.astype(f32), axis=0, keepdims=True)
    sum_ref[1:2, :] = jnp.sum(dm, axis=0, keepdims=True)


def resid_back(parts, r_own, dm, vecs):
    rows, width = dm.shape
    return pl.pallas_call(
        resid_kernel,
        out_shape=[
            jax.ShapeDtypeStruct((rows, width), f32),
            jax.ShapeDtypeStruct((rows, width), bf16),
            jax.ShapeDtypeStruct((8, width), f32),
        ],
        cost_estimate=cost(30 * rows * width, rows * width * 20),
        name="resid_back",
    )(r_own, dm, vecs, *parts)


def output_kernel(r_ref, vec_ref, *refs):
    total = r_ref[...] + vec_ref[7:8, :]
    for ref in refs[:TP]:
        total += ref[...].astype(f32)
    refs[TP][...] = total.astype(bf16)


def finish_output(parts, r_own, vecs):
    return pl.pallas_call(
        output_kernel,
        out_shape=jax.ShapeDtypeStruct(r_own.shape, bf16),
        cost_estimate=cost(8 * r_own.size, r_own.size * 14),
        name="finish_output",
    )(r_own, vecs, *parts)


def input_kernel(x_ref, dr_ref, vec_ref, *refs):
    total = refs[0][...].astype(f32)
    for ref in refs[1:TP]:
        total += ref[...].astype(f32)
    units, rstd = unit(x_ref[...].astype(f32))
    grad = dr_ref[...] + unit_back(total * vec_ref[3:4, :], units, rstd)
    refs[TP][...] = grad.astype(bf16)


def finish_input(parts, x, dr, vecs):
    return pl.pallas_call(
        input_kernel,
        out_shape=jax.ShapeDtypeStruct(x.shape, bf16),
        cost_estimate=cost(30 * x.size, x.size * 16),
        name="finish_input",
    )(x, dr, vecs, *parts)


def normed_kernel(n_recv, idx_ref, x_ref, dq_ref, own_ref, *refs):
    recv_refs = refs[:n_recv]
    w_ref, d_ref, sum_ref = refs[n_recv : n_recv + 3]
    dh_refs, dh_now = refs[n_recv + 3 : -1], refs[-1]
    step = pl.program_id(0)

    @pl.when(step == 0)
    def _():
        sum_ref[...] = jnp.zeros_like(sum_ref)

    cols = dq_ref.shape[1]
    width = x_ref.shape[1]
    grad_k, grad_v = own_ref[0], own_ref[1]
    for ref in recv_refs:
        grad_k += ref[0].astype(f32)
        grad_v += ref[1].astype(f32)
    d_ref[:, :cols] = dq_ref[...]
    d_ref[:, cols : 2 * cols] = grad_k.astype(bf16)
    d_ref[:, 2 * cols : 3 * cols] = grad_v.astype(bf16)
    d_ref[:, 3 * cols :] = jnp.zeros_like(d_ref[:, 3 * cols :])
    low = d_ref[...]
    grad = dot(low, w_ref[...], 1, 1)
    dh_now[...] = grad.astype(bf16)
    for j in range(TP):

        @pl.when(step == j)
        def _(j=j):
            dh_refs[j][...] = dh_now[...]

    units, _ = unit(x_ref[...].astype(f32))
    sum_ref[0:1, :width] += jnp.sum(grad * units, axis=0, keepdims=True)
    sum_ref[1:2, :width] += jnp.sum(grad, axis=0, keepdims=True)
    sum_ref[2:3, : low.shape[1]] += jnp.sum(low.astype(f32), axis=0, keepdims=True)


def normed_back(idx, x_all, dq, own, recvs, w_qkv):
    rows, width = x_all.shape
    cols = dq.shape[1]
    wide = w_qkv.shape[1]
    step = rows // TP
    pairs = pl.BlockSpec((2, step, cols), lambda i, idx: (0, i ^ idx[0], 0))
    return pl.pallas_call(
        functools.partial(normed_kernel, len(recvs)),
        grid_spec=pltpu.PrefetchScalarGridSpec(
            num_scalar_prefetch=1,
            grid=(TP,),
            in_specs=[
                pl.BlockSpec((step, width), lambda i, idx: (i ^ idx[0], 0)),
                pl.BlockSpec((step, cols), lambda i, idx: (i ^ idx[0], 0)),
                pairs,
            ]
            + [pairs] * len(recvs)
            + [whole(w_qkv.shape)],
            out_specs=[
                pl.BlockSpec((step, wide), lambda i, idx: (i ^ idx[0], 0)),
                whole((8, width)),
            ]
            + [whole((step, width))] * TP,
            scratch_shapes=[pltpu.VMEM((step, width), bf16)],
        ),
        out_shape=[
            jax.ShapeDtypeStruct((rows, wide), bf16),
            jax.ShapeDtypeStruct((8, width), f32),
        ]
        + [jax.ShapeDtypeStruct((step, width), bf16)] * TP,
        compiler_params=params(),
        cost_estimate=cost(2 * rows * width * wide, rows * width * 12),
        name="normed_back",
    )(idx, x_all, dq, own, *recvs, w_qkv)


def proj_grads_kernel(plan, idx_ref, h_ref, d_ref, sum_ref, own_ref, two_ref, da_ref, *refs):
    o_refs, refs = refs[:TP], refs[TP:]
    fast = plan.fast
    acc_ref, out_acc, vec_ref = refs[-3:]
    wide = d_ref.shape[1]
    cols = o_refs[0].shape[1]
    rows, width = h_ref.shape
    member = idx_ref[0]
    acc_ref[:, :wide] = dot(h_ref[...], d_ref[...], 0, 0)
    da = da_ref[...].reshape(rows, cols)
    for j in range(TP):
        out_acc[member ^ j] = dot(o_refs[j][...], da, 0, 0)
    acc_ref[:, wide : wide + cols] = out_acc[...].reshape(width, cols)
    bias_q, bias_v = sum_ref[2:3, :cols], sum_ref[2:3, 2 * cols : 3 * cols]
    zero = jnp.zeros_like(bias_q)
    vec_ref[...] = jnp.zeros_like(vec_ref)
    rows_of = [
        jnp.concatenate([jnp.where(member == j, b, zero) for j in range(TP)], axis=1)
        for b in (bias_q, bias_v)
    ]
    rows_of += [own_ref[0:1, :], sum_ref[0:1, :], sum_ref[1:2, :], two_ref[0:1, :], two_ref[1:2, :], own_ref[1:2, :]]
    for j, row in enumerate(rows_of):
        vec_ref[SMALLS + j : SMALLS + j + 1, :] = row
    acc_ref[:, wide + cols :] = vec_ref[...].T[:, SMALLS:]
    if not fast:
        refs[0][...] = acc_ref[...].astype(bf16)
        return
    core = idx_ref[2]
    keep_ref, send_ref = refs[:2]
    near, block, _ = keep_ref.shape
    span = near // plan.size["gx"]
    for ref, owner in ((keep_ref, core), (send_ref, 1 - core)):
        for n in range(near):
            gx, rest = divmod(n, span)
            at = ((gx * 2 + owner) * span + rest) * block
            ref[n] = acc_ref[pl.ds(pl.multiple_of(at, 8), block), :].astype(bf16)


def proj_grads(plan, idx, low, grads, sums, sum_own, sum_two, da_cols, os):
    rows, width = low.shape
    cols = os[0].shape[1]
    wide = grads.shape[1] + cols + SMALLS
    near = plan.devices // 2
    if plan.fast:
        out_shape = [jax.ShapeDtypeStruct((near, width // plan.devices, wide), bf16)] * 2
    else:
        out_shape = jax.ShapeDtypeStruct((width, wide), bf16)
    operands = (low, grads, sums, sum_own, sum_two, da_cols, *os)
    return pl.pallas_call(
        functools.partial(proj_grads_kernel, plan),
        in_specs=[pl.BlockSpec(memory_space=pltpu.SMEM)]
        + [pl.BlockSpec(memory_space=pltpu.VMEM)] * len(operands),
        out_shape=out_shape,
        scratch_shapes=[
            pltpu.VMEM((width, wide), f32),
            pltpu.VMEM((TP, cols, cols), f32),
            pltpu.VMEM((2 * SMALLS, width), f32),
        ],
        compiler_params=pltpu.CompilerParams(vmem_limit_bytes=60 * 1024 * 1024),
        cost_estimate=cost(2 * rows * width * wide, width * wide * 6),
        name="proj_grads",
    )(idx, *operands)


def join_kernel(keep, cols, wide, in_ref, *out_refs):
    *mats, vec_ref = out_refs
    groups = {}
    for n in range(in_ref.shape[0]):
        value = in_ref[n].astype(f32)
        key = keep[n]
        groups[key] = value if key not in groups else groups[key] + value
    for j in range(TP):
        for ref, at in zip(mats, (0, cols, 2 * cols, wide)):
            ref[:, j * cols : (j + 1) * cols] = groups[j][:, at : at + cols]
    total = functools.reduce(jnp.add, [groups[j] for j in range(TP)])
    vec_ref[...] = total[:, wide + cols :]


def join_grads(plan, got, cols, wide):
    near, block, _ = got.shape
    dims = [plan.size[a] for a in SAME]
    members = []
    for n in range(near):
        place = dict(zip(SAME, (n // (dims[1] * dims[2]), n // dims[2] % dims[1], n % dims[2])))
        member = 0
        for axis in plan.tp:
            member = member * plan.size[axis] + place[axis]
        members.append(member)
    width = cols * TP
    return pl.pallas_call(
        functools.partial(join_kernel, members, cols, wide),
        out_shape=[jax.ShapeDtypeStruct((block, width), f32)] * 4
        + [jax.ShapeDtypeStruct((block, SMALLS), f32)],
        compiler_params=pltpu.CompilerParams(vmem_limit_bytes=60 * 1024 * 1024),
        cost_estimate=cost(got.size, got.size * 2),
        name="join_grads",
    )(got)


def local(
    plan, inputs, segment_ids, padding, cotangent, w_query, b_query, w_key, w_value, b_value,
    w_out, b_out, ln1_gain, ln1_shift, ln2_gain, ln2_shift, w_up, b_up, w_down, b_down,
):
    x_own = inputs[0]
    rows, width = x_own.shape
    cols = width // TP
    length = segment_ids.shape[1]
    block = w_query.shape[0]
    hidden = w_up.shape[1]
    slab = b_up.shape[0]
    size = plan.size
    member = lax.axis_index(plan.tp)
    part = lax.axis_index(plan.half)
    core = lax.axis_index("c")
    idx = jnp.stack([member, part, core, lax.axis_index("sz")]).astype(jnp.int32)
    lines = plan.copies // 2
    fast = plan.fast

    id_rows = jnp.pad(segment_ids[0].astype(bf16), (0, 8 * width - length)).reshape(8, width)
    moved = plan.move(jnp.concatenate([x_own, id_rows], axis=0), plan.route)
    x_mine = moved[:rows]
    ids = moved[rows:].reshape(1, -1)[:, :length].astype(f32)
    dm_own = (cotangent[0].astype(f32) * padding[0].astype(f32)[:, None]).astype(bf16)
    dm_mine = plan.move(dm_own, plan.route)
    x_all = lax.all_gather(x_mine, plan.tp, axis=0, tiled=True)

    small = [b_query, b_value, b_out, ln1_gain, ln1_shift, ln2_gain, ln2_shift, b_down]
    small = jnp.stack(small, axis=1)
    b_row = jnp.pad(b_up[None], ((0, 7), (0, width - slab)))
    if fast:
        small = jnp.pad(small, ((0, 0), (0, SMALLS - small.shape[1])))
        raw = jnp.concatenate([w_out, w_down, b_row], axis=0)
        raw = jnp.broadcast_to(raw, (lines, *raw.shape))
        raw = lax.all_to_all(raw, "sz", 0, 0, tiled=True)
        chunks = prepare(plan, idx, w_query, w_key, w_value, small, w_up)
        proj, up = shards_of(idx, plan.reduce(chunks), 3 * cols + SMALLS)
        projs = [proj] + [plan.turn(proj, "sz", -j) for j in range(1, lines)]
        projs, x_all = lax.optimization_barrier((projs, x_all))
        projs = jnp.stack(projs)
        low_one, query, kv, w_qkv, vecs = qkv(plan, idx, x_all, projs, plan.swap(projs))
        ups = [up] + [plan.turn(up, "sz", -j) for j in range(1, lines)]
        outs = plan.partners(raw[:, :block])
        ups, outs, query = lax.optimization_barrier((ups, outs, query))
    else:
        table = [w_query, w_key, w_value, w_out, small]
        table = lax.all_gather(jnp.concatenate(table, axis=1), ALL, axis=0, tiled=True)
        vecs = table[:, 4 * width :].T.astype(f32)
        split = [lax.dynamic_slice(table, (0, i * width + member * cols), (width, cols)) for i in range(3)]
        w_qkv = jnp.concatenate([*split, jnp.zeros((width, SMALLS), bf16)], axis=1)
        out_full = table[:, 3 * width : 4 * width].reshape(TP, cols, width)
        low_one, query, kv = qkv(plan, idx, x_all, w_qkv, vecs)
        up_mine = lax.all_gather(w_up, ALL, axis=0, tiled=True)
        up_mine = up_mine.reshape(width, plan.devices, slab).transpose(1, 0, 2)
        up_mine = plan.shuffle(up_mine, ALL, plan.tp + plan.rep).reshape(TP, plan.copies, width, slab)
        up_mine = lax.dynamic_index_in_dim(up_mine, member, 0, keepdims=False)
        up_mine = up_mine.transpose(1, 0, 2).reshape(width, -1)
        downs = jnp.concatenate([w_down, b_row], axis=0)
        downs = lax.all_gather(downs, plan.rep, axis=0, tiled=False)
        down_mine = downs[:, :slab].reshape(-1, width)
        b_up_mine = downs[:, slab, :slab].reshape(1, -1).astype(f32)

    parts = plan.parts
    kvs = [kv] + [plan.turn(kv, plan.half, -j) for j in range(1, parts)]
    mixed, lse = attend(idx, ids, query, kvs)
    if fast:
        raw, ups, outs, mixed = lax.optimization_barrier((raw, ups, outs, mixed))
        own = [raw, *ups, *outs]
        other = [plan.swap(v) for v in own]
        up_mine, out_full, down_mine, row = assemble(plan, idx, own, other, block, slab)
        out_full = out_full.reshape(TP, cols, width)
        down_mine = down_mine.reshape(-1, width)
        b_up_mine = row[:, :, 0, :slab].reshape(1, -1).astype(f32)
    os = plan.partners(mixed)
    dms = plan.partners(dm_mine)
    r_own, low_two, act, grad_pre, dm_all, sum_two, *dh_two = mlp(
        idx, x_all, os, dms, out_full, up_mine, down_mine, vecs, b_up_mine
    )

    back_two = plan.reduce(dh_two)
    if fast:
        near_terms, far_terms, *out_terms = mlp_weight_grads(
            plan, idx, low_two, grad_pre, act, dm_all, down_mine
        )
        back_two, out_terms, far_terms = lax.optimization_barrier((back_two, out_terms, far_terms))
    else:
        up_terms = dot(low_two, grad_pre, 0, 0).astype(bf16)
        down_terms = dot(act, dm_all, 0, 0).astype(bf16)
        row = jnp.sum(grad_pre.astype(f32), axis=0).astype(bf16)
        out_terms = dot(act, down_mine).astype(bf16).reshape(TP, rows, width)
        out_terms = [
            lax.dynamic_index_in_dim(out_terms, member ^ j, 0, keepdims=False) for j in range(TP)
        ]
    dr, da, sum_own = resid_back(back_two, r_own, dm_mine, vecs)
    das = plan.partners(da)
    das, out_terms = lax.optimization_barrier((das, out_terms))
    out_parts = plan.reduce(out_terms)
    output = finish_output(out_parts, r_own, vecs)

    if fast:
        terms = add(near_terms, plan.swap(far_terms))
        das, terms = lax.optimization_barrier((das, terms))
        terms = lax.all_to_all(terms, "sz", 0, 0, tiled=True)
        *ups, g_w_down, g_b_up = sum_rows(plan, idx, terms, block, slab)
    else:
        row = jnp.pad(row.reshape(plan.copies, 1, slab), ((0, 0), (0, 7), (0, width - slab)))
        downs = jnp.concatenate([down_terms.reshape(plan.copies, slab, width), row], axis=1)
        downs = lax.psum_scatter(downs, plan.rep, scatter_dimension=0, tiled=False)
        g_w_down = downs[:slab].astype(f32)
        g_b_up = downs[slab, :slab].astype(f32)
        ups = plan.shuffle(up_terms.reshape(plan.devices, block, -1), ALL, plan.rep + plan.tp)
        ups = ups.reshape(plan.copies, TP * block, -1)
        ups = lax.psum_scatter(ups, plan.rep, scatter_dimension=0, tiled=False)
        ups = lax.all_to_all(ups.reshape(TP, block, -1), plan.tp, 0, 0, tiled=True).astype(f32)
    grad_query, kv_own, da_cols, *kv_others = attend_back(idx, ids, query, das, out_full, lse, kvs)
    recvs = [plan.turn(kv_others[j - 1], plan.half, j) for j in range(1, parts)]
    recvs, output = lax.optimization_barrier((recvs, output))
    grads, sum_one, *dh_one = normed_back(idx, x_all, grad_query, kv_own, recvs, w_qkv)
    back_one = plan.reduce(dh_one)
    output, sum_one = lax.optimization_barrier((output, sum_one))
    output = plan.move(output, plan.back)
    terms = proj_grads(plan, idx, low_one, grads, sum_one, sum_own, sum_two, da_cols, os)
    if fast:
        keep, send = terms
        terms = add(keep, plan.swap(send))
        terms, back_one, ups = lax.optimization_barrier((terms, back_one, ups))
        got = lax.all_to_all(terms, SAME, 0, 0, tiled=True)
    else:
        terms = plan.shuffle(terms.reshape(plan.devices, block, -1), ALL, ("c",) + SAME)
        terms = terms.reshape(2, -1, *terms.shape[1:])
        keep, send = jnp.where(core == 0, terms, terms[::-1])
        got = lax.all_to_all(add(keep, plan.swap(send)), SAME, 0, 0, tiled=True)
    if fast:
        g_w_up = join_up(plan, idx, plan.reduce(ups), hidden)
        g_b_up = g_b_up[0]
    else:
        ups = ups.reshape(TP, block, plan.copies, slab).transpose(0, 2, 1, 3)
        ups = plan.shuffle(ups.reshape(plan.devices, block, slab), plan.tp + plan.rep, ALL)
        g_w_up = ups.transpose(1, 0, 2).reshape(block, hidden)
    g_query, g_key, g_value, g_out, vec = join_grads(plan, got, cols, w_qkv.shape[1])

    grad_input = plan.move(finish_input(back_one, x_mine, dr, vecs), plan.back)
    return (
        output[None],
        grad_input[None],
        g_query,
        vec[:, 0],
        g_key,
        g_value,
        vec[:, 1],
        g_out,
        vec[:, 2],
        vec[:, 3],
        vec[:, 4],
        vec[:, 5],
        vec[:, 6],
        g_w_up,
        g_b_up,
        g_w_down,
        vec[:, 7],
    )


def solution(mesh):
    groups, blocks = mesh.shape["grp"], mesh.shape["seq"]
    plan = Plan(groups, blocks)
    fine = Mesh(mesh.devices.reshape(plan.shape), ALL)
    grp, seq = ("gx", "c"), ("sz", "sy")
    matrix, vector = P(ALL, None), P(ALL)
    token = P(grp, seq, None)
    return jax.shard_map(
        functools.partial(local, plan),
        mesh=fine,
        in_specs=(
            token, P(grp, None), P(grp, seq), token,
            matrix, vector, matrix, matrix, vector, matrix, vector,
            vector, vector, vector, vector, matrix, vector, matrix, vector,
        ),
        out_specs=(
            token, token,
            matrix, vector, matrix, matrix, vector, matrix, vector,
            vector, vector, vector, vector, matrix, vector, matrix, vector,
        ),
        check_vma=False,
    )
```

```python
import functools

import jax
import jax.numpy as jnp
from jax import lax
from jax.experimental import pallas as pl
from jax.experimental.pallas import tpu as pltpu
from jax.sharding import Mesh, PartitionSpec as P

HEADS = 12
HEAD_DIM = 64
TP = 4
HEADS_TP = HEADS // TP
EPS = 1e-05
NEG = -1e30
SCALE = 0.125
ALL = ("gx", "c", "sz", "sy")
SAME = ("gx", "sz", "sy")
SMALLS = 64
f32 = jnp.float32
bf16 = jnp.bfloat16


class Plan:
    def __init__(self, groups, blocks):
        if (groups, blocks) == (4, 8):
            self.shape = (2, 2, 4, 2)
            self.tp, self.half, self.rep = ("gx", "sy"), "c", ("c", "sz")
            self.fast = True
        else:
            self.shape = (groups // 2, 2, blocks // TP, TP)
            self.tp, self.half, self.rep = ("sy",), "sz", ("gx", "c", "sz")
            self.fast = False
        self.size = dict(zip(ALL, self.shape))
        self.devices = groups * blocks
        self.parts = self.size[self.half]
        self.copies = self.devices // TP
        self.lines = tuple(a for a in self.rep if a != "c")
        self.route = []
        for src in range(self.devices):
            seq, block = divmod(src, blocks)
            part, member = divmod(block, TP)
            if self.tp == ("sy",):
                dst = src
            else:
                dst = (((member >> 1) * 2 + part) * 4 + seq) * 2 + (member & 1)
            self.route.append((src, dst))
        self.back = [(dst, src) for src, dst in self.route]

    def swap(self, value):
        return lax.ppermute(value, "c", [(0, 1), (1, 0)])

    def gather(self, value):
        return lax.all_to_all(
            jnp.broadcast_to(value, (TP, *value.shape)), self.tp, 0, 0, tiled=True
        )

    def partner(self, value, j):
        table = [(t, t ^ j) for t in range(TP)]
        return lax.ppermute(value, self.tp, table)

    def partners(self, value):
        return [value] + [self.partner(value, j) for j in range(1, TP)]

    def reduce(self, values):
        return [values[0]] + [self.partner(values[j], j) for j in range(1, TP)]

    def turn(self, value, axis, by):
        count = self.size[axis]
        return lax.ppermute(value, axis, [(i, (i + by) % count) for i in range(count)])

    def place(self, r):
        at, rest = {}, r
        for axis in reversed(ALL):
            rest, at[axis] = divmod(rest, self.size[axis])
        numbers = []
        for axes in (self.tp, self.rep):
            number = 0
            for axis in axes:
                number = number * self.size[axis] + at[axis]
            numbers.append(number)
        return tuple(numbers)

    def same(self, n):
        span = self.devices // 2 // self.size["gx"]
        gx, rest = divmod(n, span)
        return gx * 2 * span + rest

    def move(self, value, table):
        if all(a == b for a, b in table):
            return value
        return lax.ppermute(value, ALL, table)

    def shuffle(self, value, before, after):
        tail = value.shape[1:]
        dims = [self.size[a] for a in before]
        order = [before.index(a) for a in after]
        value = value.reshape(*dims, *tail)
        value = value.transpose(*order, *range(len(dims), len(dims) + len(tail)))
        return value.reshape(-1, *tail)


def dot(left, right, left_dim=1, right_dim=0):
    return lax.dot_general(
        left, right, (((left_dim,), (right_dim,)), ((), ())), preferred_element_type=f32
    )


def unit(values):
    center = values - jnp.mean(values, axis=-1, keepdims=True)
    variance = jnp.mean(center * center, axis=-1, keepdims=True)
    rstd = lax.rsqrt(variance + EPS)
    return center * rstd, rstd


def unit_back(grad_unit, units, rstd):
    first = jnp.mean(grad_unit, axis=-1, keepdims=True)
    second = jnp.mean(grad_unit * units, axis=-1, keepdims=True)
    return rstd * (grad_unit - first - units * second)


def params(limit=60 * 1024 * 1024, axes=1):
    return pltpu.CompilerParams(
        dimension_semantics=("arbitrary",) * axes, vmem_limit_bytes=limit
    )


def cost(flops, nbytes, trans=0):
    return pl.CostEstimate(flops=int(flops), bytes_accessed=int(nbytes), transcendentals=int(trans))


def whole(shape):
    zeros = (0,) * len(shape)
    return pl.BlockSpec(shape, lambda *_: zeros)


def head_lanes(value, head):
    lane = lax.broadcasted_iota(jnp.int32, value.shape, 1)
    keep = (lane >= head * HEAD_DIM) & (lane < (head + 1) * HEAD_DIM)
    return jnp.where(keep, value, jnp.zeros_like(value))


def member_cols(row, member, cols):
    out = jnp.zeros((row.shape[0], cols), row.dtype)
    for j in range(TP):
        out = jnp.where(member == j, row[:, j * cols : (j + 1) * cols], out)
    return out


def prep_kernel(rep_of, q_ref, k_ref, v_ref, small_ref, up_ref, out_ref, chunk_ref, turn_ref):
    block, width = q_ref.shape
    cols = width // TP
    wide = 3 * cols + SMALLS
    slab = up_ref.shape[1] // len(rep_of)
    turn_ref[...] = jnp.zeros_like(turn_ref)
    turn_ref[: small_ref.shape[0], :block] = small_ref[...].astype(f32)
    small = turn_ref[...].T[:block, :SMALLS]
    for j in range(TP):
        at = slice(j * cols, (j + 1) * cols)
        chunk_ref[j, :, :wide] = jnp.concatenate(
            [r[:, at].astype(f32) for r in (q_ref, k_ref, v_ref)] + [small], axis=1
        ).astype(bf16)
        chunk_ref[j, :, wide + width :] = out_ref[...]
    for r, (member, copy) in enumerate(rep_of):
        first = wide + copy * slab
        chunk_ref[member, :, first : first + slab] = up_ref[:, r * slab : (r + 1) * slab]


def prepare(plan, w_query, w_key, w_value, small, w_up, w_out):
    block, width = w_query.shape
    rep_of = [plan.place(r) for r in range(plan.devices)]
    wide = 3 * width // TP + SMALLS
    return pl.pallas_call(
        functools.partial(prep_kernel, rep_of),
        out_shape=jax.ShapeDtypeStruct((TP, block, wide + w_up.shape[1] // TP + width), bf16),
        scratch_shapes=[pltpu.VMEM((128, 128), f32)],
        cost_estimate=cost(1000, 4 * w_up.size),
        name="prepare",
    )(w_query, w_key, w_value, small, w_up, w_out)


def shards_kernel(wide, got_ref, down_ref, row_ref, proj_ref, shard_ref):
    block = got_ref.shape[1]
    slab, width = down_ref.shape
    first = TP * block
    for t in range(TP):
        at = t * block
        proj_ref[at : at + block, :] = got_ref[t, :, :wide]
        up = got_ref[t, :, wide : wide + width]
        out = got_ref[t, :, wide + width :]
        for n in range(shard_ref.shape[0]):
            shard_ref[n, at : at + block, :] = up
            shard_ref[n, first + at : first + at + block, :] = out
    row = jnp.concatenate([row_ref[...].astype(f32), jnp.zeros((1, width - slab), f32)], axis=1)
    row = jnp.broadcast_to(row, (8, width)).astype(bf16)
    for n in range(shard_ref.shape[0]):
        shard_ref[n, 2 * first : 2 * first + slab, :] = down_ref[...]
        shard_ref[n, 2 * first + slab :, :] = row


def shards_of(got, w_down, b_row, wide, lines):
    _, block, _ = got.shape
    slab, width = w_down.shape
    return pl.pallas_call(
        functools.partial(shards_kernel, wide),
        out_shape=[
            jax.ShapeDtypeStruct((TP * block, wide), bf16),
            jax.ShapeDtypeStruct((lines, 2 * TP * block + slab + 8, width), bf16),
        ],
        cost_estimate=cost(1000, 4 * lines * slab * width),
        name="shards_of",
    )(got, w_down, b_row)


def assemble_kernel(plan, idx_ref, own_ref, other_ref, up_ref, out_ref, down_ref, row_ref, wide_ref):
    core = idx_ref[2]
    slab = down_ref.shape[2]
    first = TP * up_ref.shape[0] // plan.devices
    pair = first // plan.size["gx"]
    for ref, side in ((own_ref, core), (other_ref, 1 - core)):
        for z in range(ref.shape[0]):
            value = ref[z, : 2 * first, :].astype(f32)
            for gx in range(plan.size["gx"]):
                at = gx * pair
                wide_ref[0, gx * 2 + side, z] = value[at : at + pair]
                wide_ref[1, gx * 2 + side, z] = value[first + at : first + at + pair]
            down_ref[side, z] = ref[z, 2 * first : 2 * first + slab, :]
            row_ref[side, z] = ref[z, 2 * first + slab :, :]
    for ref, k in ((up_ref, 0), (out_ref, 1)):
        ref[...] = wide_ref[k].reshape(ref.shape).astype(bf16)


def assemble(plan, idx, own, other, slab):
    lines, _, width = own.shape
    hidden = plan.copies * slab
    pair = plan.size["sy"] * width // plan.devices
    return pl.pallas_call(
        functools.partial(assemble_kernel, plan),
        in_specs=[pl.BlockSpec(memory_space=pltpu.SMEM)]
        + [pl.BlockSpec(memory_space=pltpu.VMEM)] * 2,
        out_shape=[
            jax.ShapeDtypeStruct((width, hidden), bf16),
            jax.ShapeDtypeStruct((width, width), bf16),
            jax.ShapeDtypeStruct((2, lines, slab, width), bf16),
            jax.ShapeDtypeStruct((2, lines, 8, width), bf16),
        ],
        scratch_shapes=[pltpu.VMEM((2, 2 * plan.size["gx"], lines, pair, width), f32)],
        compiler_params=pltpu.CompilerParams(vmem_limit_bytes=60 * 1024 * 1024),
        cost_estimate=cost(1000, 12 * width * width),
        name="assemble",
    )(idx, own, other)


def qkv_kernel(plan, idx_ref, x_ref, *refs):
    fast = plan.fast
    if fast:
        own_ref, other_ref, h_ref, q_ref, kv_ref, w_ref, vec_ref, wide_ref = refs
    else:
        w_ref, vec_ref, h_ref, q_ref, kv_ref = refs
    cols = q_ref.shape[1]
    if fast:

        @pl.when(pl.program_id(0) == 0)
        def _():
            core = idx_ref[2]
            line = idx_ref[3]
            lines, rows, _ = own_ref.shape
            pair = rows // plan.size["gx"]
            for ref, side in ((own_ref, core), (other_ref, 1 - core)):
                for j in range(lines):
                    z = lax.rem(line + j, lines)
                    value = ref[j].astype(f32)
                    for gx in range(plan.size["gx"]):
                        wide_ref[gx * 2 + side, z] = value[gx * pair : (gx + 1) * pair, :]
            table = wide_ref[...].reshape(w_ref.shape)
            w_ref[...] = table.astype(bf16)
            vec_ref[...] = table[:, 512:640].T[64:72, :]

    units, _ = unit(x_ref[...].astype(f32))
    low = (units * vec_ref[3:4, :] + vec_ref[4:5, :]).astype(bf16)
    h_ref[...] = low
    out = dot(low, w_ref[...])
    bias = member_cols(vec_ref[0:2, :], idx_ref[0], cols)
    query = (out[:, :cols] + bias[0:1, :]).astype(bf16)
    q_ref[...] = (query.astype(f32) * SCALE).astype(bf16)
    kv_ref[0] = out[:, cols : 2 * cols].astype(bf16)
    kv_ref[1] = (out[:, 2 * cols : 3 * cols] + bias[1:2, :]).astype(bf16)


def qkv(plan, idx, x_all, *operands):
    rows, width = x_all.shape
    cols = width // TP
    step = rows // 2
    wide = 3 * cols + SMALLS
    out_specs = [
        pl.BlockSpec((step, width), lambda i, *_: (i, 0)),
        pl.BlockSpec((step, cols), lambda i, *_: (i, 0)),
        pl.BlockSpec((2, step, cols), lambda i, *_: (0, i, 0)),
    ]
    out_shape = [
        jax.ShapeDtypeStruct((rows, width), bf16),
        jax.ShapeDtypeStruct((rows, cols), bf16),
        jax.ShapeDtypeStruct((2, rows, cols), bf16),
    ]
    scratch = []
    if plan.fast:
        out_specs += [whole((width, wide)), whole((8, width))]
        out_shape += [
            jax.ShapeDtypeStruct((width, wide), bf16),
            jax.ShapeDtypeStruct((8, width), f32),
        ]
        lines = plan.copies // 2
        scratch = [pltpu.VMEM((2 * plan.size["gx"], lines, width // (2 * plan.size["gx"] * lines), wide), f32)]
    return pl.pallas_call(
        functools.partial(qkv_kernel, plan),
        grid_spec=pltpu.PrefetchScalarGridSpec(
            num_scalar_prefetch=1,
            grid=(2,),
            in_specs=[pl.BlockSpec((step, width), lambda i, *_: (i, 0))]
            + [whole(v.shape) for v in operands],
            out_specs=out_specs,
            scratch_shapes=scratch,
        ),
        out_shape=out_shape,
        compiler_params=params(),
        cost_estimate=cost(2 * rows * width * 3 * cols, rows * width * 8),
        name="qkv",
    )(idx, x_all, *operands)


def fill_docs(ids_ref, part, parts, doc_ref):
    span, width = doc_ref.shape[1:]
    for j in range(parts):
        at = lax.rem(part + j, parts) * span
        row = ids_ref[0:1, pl.ds(pl.multiple_of(at, 512), span)]
        doc_ref[j] = jnp.broadcast_to(row, (width, span)).T


def fwd_kernel(parts, idx_ref, ids_ref, q_ref, *refs):
    kv_refs = refs[:parts]
    o_ref, lse_ref, turned, doc_ref = refs[parts:]
    step = pl.program_id(0)
    part = idx_ref[1]
    span = kv_refs[0].shape[1]
    width = q_ref.shape[0]

    @pl.when(step == 0)
    def _():
        fill_docs(ids_ref, part, parts, doc_ref)
        for j in range(parts):
            turned[j] = kv_refs[j][1].T

    at = part * span + step * width
    own = ids_ref[0:1, pl.ds(pl.multiple_of(at, 128), width)]
    query = q_ref[...]
    outs, lses = [], []
    for head in range(HEADS_TP):
        masked = head_lanes(query, head)
        scores = []
        for j in range(parts):
            raw = dot(kv_refs[j][0], masked, 1, 1)
            scores.append(jnp.where(doc_ref[j] == own, raw, NEG))
        peak = functools.reduce(
            jnp.maximum, [jnp.max(s, axis=0, keepdims=True) for s in scores]
        )
        exps = [jnp.exp(s - peak) for s in scores]
        total = functools.reduce(jnp.add, [jnp.sum(e, axis=0, keepdims=True) for e in exps])
        scale = 1.0 / total
        acc = None
        for j in range(parts):
            probs = (exps[j] * scale).astype(bf16)
            term = dot(turned[j, head * HEAD_DIM : (head + 1) * HEAD_DIM, :], probs)
            acc = term if acc is None else acc + term
        outs.append(acc)
        lses.append(peak + jnp.log(total))
    o_ref[...] = jnp.concatenate(outs, axis=0).T.astype(bf16)
    for head in range(HEADS_TP):
        lse_ref[head : head + 1, :] = lses[head]


def attend(idx, ids, q, kvs, width=256):
    rows, cols = q.shape
    parts = len(kvs)
    span = kvs[0].shape[1]
    return pl.pallas_call(
        functools.partial(fwd_kernel, parts),
        grid_spec=pltpu.PrefetchScalarGridSpec(
            num_scalar_prefetch=1,
            grid=(rows // width,),
            in_specs=[whole(ids.shape), pl.BlockSpec((width, cols), lambda i, *_: (i, 0))]
            + [whole(kv.shape) for kv in kvs],
            out_specs=[
                pl.BlockSpec((width, cols), lambda i, *_: (i, 0)),
                pl.BlockSpec((8, width), lambda i, *_: (0, i)),
            ],
            scratch_shapes=[
                pltpu.VMEM((parts, cols, span), bf16),
                pltpu.VMEM((parts, span, width), f32),
            ],
        ),
        out_shape=[
            jax.ShapeDtypeStruct((rows, cols), bf16),
            jax.ShapeDtypeStruct((8, rows), f32),
        ],
        compiler_params=params(),
        cost_estimate=cost(4 * rows * span * parts * cols, span * parts * cols * 4, rows * span * parts * HEADS_TP),
        name="attend",
    )(idx, ids, q, *kvs)


def bwd_kernel(parts, idx_ref, ids_ref, q_ref, w_ref, lse_ref, *refs):
    da_refs, refs = refs[:TP], refs[TP:]
    kv_refs = refs[:parts]
    dq_ref, own_ref, cols_ref = refs[parts : parts + 3]
    other_refs = refs[parts + 3 : 2 * parts + 2]
    turned, doc_ref, key_acc, value_acc, mixed_ref = refs[2 * parts + 2 :]
    step = pl.program_id(0)
    part = idx_ref[1]
    span = kv_refs[0].shape[1]
    width, cols = q_ref.shape

    @pl.when(step == 0)
    def _():
        fill_docs(ids_ref, part, parts, doc_ref)
        for j in range(parts):
            turned[j] = kv_refs[j][0].T
        key_acc[...] = jnp.zeros_like(key_acc)
        value_acc[...] = jnp.zeros_like(value_acc)
        member = idx_ref[0]
        for j in range(TP):
            da = da_refs[j][...]
            mixed_ref[member ^ j] = dot(da, w_ref[0], 1, 1).astype(bf16)
            cols_ref[member ^ j] = member_cols(da, member, cols)

    at = part * span + step * width
    own = ids_ref[0:1, pl.ds(pl.multiple_of(at, 128), width)]
    query = q_ref[...]
    group = width // mixed_ref.shape[1]
    grad_mixed = mixed_ref[pl.ds(step * group, group)].reshape(width, cols)
    turned_grads = []
    for head in range(HEADS_TP):
        masked_q = head_lanes(query, head)
        masked_g = head_lanes(grad_mixed, head)
        lse = lse_ref[head : head + 1, :]
        probs, grads = [], []
        for j in range(parts):
            raw = dot(kv_refs[j][0], masked_q, 1, 1)
            probs.append(jnp.exp(jnp.where(doc_ref[j] == own, raw, NEG) - lse))
            grads.append(dot(kv_refs[j][1], masked_g, 1, 1))
        delta = functools.reduce(
            jnp.add,
            [jnp.sum(p * g, axis=0, keepdims=True) for p, g in zip(probs, grads)],
        )
        acc = None
        for j in range(parts):
            grad_scores = (probs[j] * (grads[j] - delta)).astype(bf16)
            value_acc[j] += dot(probs[j].astype(bf16), masked_g)
            key_acc[j] += dot(grad_scores, masked_q)
            term = dot(turned[j, head * HEAD_DIM : (head + 1) * HEAD_DIM, :], grad_scores)
            acc = term if acc is None else acc + term
        turned_grads.append(acc)
    dq_ref[...] = (jnp.concatenate(turned_grads, axis=0).T * SCALE).astype(bf16)

    @pl.when(step == pl.num_programs(0) - 1)
    def _():
        own_ref[0] = key_acc[0]
        own_ref[1] = value_acc[0]
        for j in range(1, parts):
            other_refs[j - 1][0] = key_acc[j].astype(bf16)
            other_refs[j - 1][1] = value_acc[j].astype(bf16)


def attend_back(idx, ids, q, das, w_out, lse, kvs, width=256):
    rows, cols = q.shape
    step, model = das[0].shape
    parts = len(kvs)
    span = kvs[0].shape[1]
    return pl.pallas_call(
        functools.partial(bwd_kernel, parts),
        grid_spec=pltpu.PrefetchScalarGridSpec(
            num_scalar_prefetch=1,
            grid=(rows // width,),
            in_specs=[
                whole(ids.shape),
                pl.BlockSpec((width, cols), lambda i, *_: (i, 0)),
                pl.BlockSpec((1, cols, model), lambda i, idx: (idx[0], 0, 0)),
                pl.BlockSpec((8, width), lambda i, *_: (0, i)),
            ]
            + [whole((step, model))] * TP
            + [whole(kv.shape) for kv in kvs],
            out_specs=[
                pl.BlockSpec((width, cols), lambda i, *_: (i, 0)),
                whole((2, span, cols)),
                whole((TP, step, cols)),
            ]
            + [whole((2, span, cols))] * (parts - 1),
            scratch_shapes=[
                pltpu.VMEM((parts, cols, span), bf16),
                pltpu.VMEM((parts, span, width), f32),
                pltpu.VMEM((parts, span, cols), f32),
                pltpu.VMEM((parts, span, cols), f32),
                pltpu.VMEM((TP, step, cols), bf16),
            ],
        ),
        out_shape=[
            jax.ShapeDtypeStruct((rows, cols), bf16),
            jax.ShapeDtypeStruct((2, span, cols), f32),
            jax.ShapeDtypeStruct((TP, step, cols), bf16),
        ]
        + [jax.ShapeDtypeStruct((2, span, cols), bf16)] * (parts - 1),
        compiler_params=params(),
        cost_estimate=cost(10 * rows * span * parts * cols, span * parts * cols * 12, rows * span * parts * HEADS_TP),
        name="attend_back",
    )(idx, ids, q, w_out, lse, *das, *kvs)


def mlp_kernel(idx_ref, x_ref, o_ref, *refs):
    dm_refs, refs = refs[:TP], refs[TP:]
    wo_ref, wu_ref, wd_ref, vec_ref, bup_ref, r_ref, h_ref, a_ref, du_ref, dm_ref, sum_ref = refs[:11]
    dh_refs, dm_now, r_now, dh_now = refs[11 : 11 + TP], refs[-3], refs[-2], refs[-1]
    step = pl.program_id(0)
    side = lax.rem(idx_ref[0], 2)

    @pl.when(step == 0)
    def _():
        sum_ref[...] = jnp.zeros_like(sum_ref)

    attended = dot(o_ref[0], wo_ref[0])
    for j in range(1, TP):
        attended += dot(o_ref[j], wo_ref[j])
    residual = x_ref[...].astype(f32) + (attended + vec_ref[2:3, :])

    for i in range(2):

        @pl.when(step == i)
        def _(i=i):
            for b in range(2):
                dm_now[side ^ b] = dm_refs[2 * i + b][...]
            if i == 0:
                r_now[...] = residual.reshape(r_now.shape)
                r_ref[...] = r_now[side]

    units, _ = unit(residual)
    low = (units * vec_ref[5:6, :] + vec_ref[6:7, :]).astype(bf16)
    h_ref[...] = low
    pre = dot(low, wu_ref[...]) + bup_ref[...]
    normal = 0.5 * (1.0 + lax.erf(pre * 0.7071067811865476))
    act = (pre * normal).astype(bf16)
    a_ref[...] = act
    slope = normal + pre * (0.3989422804014327 * jnp.exp(-0.5 * pre * pre))
    dm = dm_now[...].reshape(x_ref.shape)
    dm_ref[...] = dm
    grad_pre = (dot(dm, wd_ref[...], 1, 1) * slope).astype(bf16)
    du_ref[...] = grad_pre
    grad = dot(grad_pre, wu_ref[...], 1, 1)
    sum_ref[0:1, :] += jnp.sum(grad * units, axis=0, keepdims=True)
    sum_ref[1:2, :] += jnp.sum(grad, axis=0, keepdims=True)
    dh_now[...] = grad.astype(bf16).reshape(dh_now.shape)
    for i in range(2):

        @pl.when(step == i)
        def _(i=i):
            for b in range(2):
                dh_refs[2 * i + b][...] = dh_now[side ^ b]


def mlp(idx, x_all, o_all, dms, w_out, w_up, w_down, vecs, b_up):
    rows, width = x_all.shape
    hidden = w_up.shape[1]
    cols = width // TP
    step = rows // 2

    def block(i, idx):
        return (i ^ (idx[0] // 2), 0)

    token = pl.BlockSpec((step, width), block)
    inner = pl.BlockSpec((step, hidden), block)
    one = whole((rows // TP, width))
    now = (2, rows // TP, width)
    return pl.pallas_call(
        mlp_kernel,
        grid_spec=pltpu.PrefetchScalarGridSpec(
            num_scalar_prefetch=1,
            grid=(2,),
            in_specs=[token, pl.BlockSpec((TP, step, cols), lambda i, idx: (0, i ^ (idx[0] // 2), 0))]
            + [one] * TP
            + [whole(v.shape) for v in (w_out, w_up, w_down, vecs, b_up)],
            out_specs=[one, token, inner, inner, token, whole((8, width))] + [one] * TP,
            scratch_shapes=[pltpu.VMEM(now, bf16), pltpu.VMEM(now, f32), pltpu.VMEM(now, bf16)],
        ),
        out_shape=[
            jax.ShapeDtypeStruct((rows // TP, width), f32),
            jax.ShapeDtypeStruct((rows, width), bf16),
            jax.ShapeDtypeStruct((rows, hidden), bf16),
            jax.ShapeDtypeStruct((rows, hidden), bf16),
            jax.ShapeDtypeStruct((rows, width), bf16),
            jax.ShapeDtypeStruct((8, width), f32),
        ]
        + [jax.ShapeDtypeStruct((rows // TP, width), bf16)] * TP,
        compiler_params=params(),
        cost_estimate=cost(2 * rows * width * (width + 3 * hidden), rows * width * 24, rows * hidden * 4),
        name="mlp",
    )(idx, x_all, o_all, *dms, w_out, w_up, w_down, vecs, b_up)


def pair_kernel(plan, idx_ref, h_ref, du_ref, a_ref, dm_ref, wd_ref, near_ref, far_ref, *refs):
    out_refs, acc_ref, wide_ref = refs[:TP], refs[TP], refs[TP + 1]
    lines = plan.copies // 2
    step = pl.program_id(0)
    member, core = idx_ref[0], idx_ref[2]
    half = step ^ core
    grad_pre = du_ref[...]
    act = a_ref[...]
    width = h_ref.shape[1]
    block = width // plan.devices
    size = act.shape[1]
    slab = size // lines
    first = TP * block
    up = dot(h_ref[...], grad_pre, 0, 0)
    down = dot(act, dm_ref[...], 0, 0)
    bias = jnp.sum(grad_pre.astype(f32), axis=0, keepdims=True)
    term = dot(act, wd_ref[...])

    @pl.when(step == 0)
    def _():
        acc_ref[...] = term.reshape(acc_ref.shape)
        wide_ref[:, :size] = up

    @pl.when(step == 1)
    def _():
        acc_ref[...] += term.reshape(acc_ref.shape)
        for j in range(TP):
            out_refs[j][...] = acc_ref[member ^ j].astype(bf16)
        wide_ref[:, size:] = up
        pair = plan.size["sy"] * block
        for ref, owner in ((near_ref, core), (far_ref, 1 - core)):
            for z in range(lines):
                for gx in range(plan.size["gx"]):
                    at = ((gx * 2 + owner) * lines + z) * pair
                    value = wide_ref[pl.ds(pl.multiple_of(at, 16), pair), :]
                    ref[z, gx * pair : (gx + 1) * pair, :] = value.astype(bf16)

    def put(ref):
        for k in range(lines):
            at = k * slab
            row = jnp.concatenate(
                [bias[:, at : at + slab], jnp.zeros((1, width - slab), f32)], axis=1
            )
            ref[k, first : first + slab, :] = down[at : at + slab, :].astype(bf16)
            ref[k, first + slab :, :] = jnp.broadcast_to(row, (8, width)).astype(bf16)

    @pl.when(half == 0)
    def _():
        put(near_ref)

    @pl.when(half == 1)
    def _():
        put(far_ref)


def mlp_weight_grads(plan, idx, low, grad_pre, act, dm_all, w_down):
    rows, width = low.shape
    hidden = act.shape[1]
    step = hidden // 2
    lines = plan.copies // 2
    block = width // plan.devices
    slab = hidden // plan.copies
    bundle = (lines, TP * block + slab + 8, width)
    token = (rows // TP, width)
    return pl.pallas_call(
        functools.partial(pair_kernel, plan),
        grid_spec=pltpu.PrefetchScalarGridSpec(
            num_scalar_prefetch=1,
            grid=(2,),
            in_specs=[
                whole((rows, width)),
                pl.BlockSpec((rows, step), lambda i, idx: (0, i)),
                pl.BlockSpec((rows, step), lambda i, idx: (0, i)),
                whole((rows, width)),
                pl.BlockSpec((step, width), lambda i, idx: (i, 0)),
            ],
            out_specs=[whole(bundle)] * 2 + [whole(token)] * TP,
            scratch_shapes=[
                pltpu.VMEM((TP, *token), f32),
                pltpu.VMEM((width, hidden), f32),
            ],
        ),
        out_shape=[jax.ShapeDtypeStruct(bundle, bf16)] * 2
        + [jax.ShapeDtypeStruct(token, bf16)] * TP,
        compiler_params=params(),
        cost_estimate=cost(6 * rows * width * hidden, width * hidden * 12),
        name="mlp_weight_grads",
    )(idx, low, grad_pre, act, dm_all, w_down)


def add_kernel(*refs):
    *in_refs, out_ref = refs
    total = in_refs[0][...].astype(f32)
    for ref in in_refs[1:]:
        total += ref[...].astype(f32)
    out_ref[...] = total.astype(out_ref.dtype)


def add(*values, dtype=bf16):
    return pl.pallas_call(
        add_kernel,
        out_shape=jax.ShapeDtypeStruct(values[0].shape, dtype),
        compiler_params=pltpu.CompilerParams(vmem_limit_bytes=60 * 1024 * 1024),
        cost_estimate=cost(values[0].size * len(values), 2 * values[0].size * (len(values) + 1)),
        name="add",
    )(*values)


def rows_kernel(plan, idx_ref, *refs):
    term_ref, up_refs = refs[0], refs[1 : 1 + TP]
    down_ref, row_ref, total_ref = refs[1 + TP :]
    member = idx_ref[0]
    total = term_ref[0].astype(f32)
    for z in range(1, term_ref.shape[0]):
        total += term_ref[z].astype(f32)
    block = up_refs[0].shape[0]
    first, slab = TP * block, down_ref.shape[0]
    total_ref[...] = total[:first].reshape(total_ref.shape)
    for j in range(TP):
        up_refs[j][...] = total_ref[member ^ j].astype(bf16)
    down_ref[...] = total[first : first + slab]
    row_ref[...] = total[first + slab : first + slab + 1, :slab]


def sum_rows(plan, idx, terms, block, slab):
    lines, rows, width = terms.shape
    return pl.pallas_call(
        functools.partial(rows_kernel, plan),
        in_specs=[pl.BlockSpec(memory_space=pltpu.SMEM), pl.BlockSpec(memory_space=pltpu.VMEM)],
        out_shape=[jax.ShapeDtypeStruct((block, width), bf16)] * TP
        + [jax.ShapeDtypeStruct((slab, width), f32), jax.ShapeDtypeStruct((1, slab), f32)],
        scratch_shapes=[pltpu.VMEM((TP, block, width), f32)],
        cost_estimate=cost(lines * rows * width, 2 * lines * rows * width),
        name="sum_rows",
    )(idx, terms)


def up_kernel(plan, idx_ref, *refs):
    part_refs, out_ref, hold_ref = refs[:TP], refs[TP], refs[TP + 1]
    member = idx_ref[0]
    for j in range(TP):
        hold_ref[member ^ j] = part_refs[j][...].astype(f32)
    slab = out_ref.shape[1] // plan.devices
    for r in range(plan.devices):
        t, copy = plan.place(r)
        out_ref[:, r * slab : (r + 1) * slab] = hold_ref[t, :, copy * slab : (copy + 1) * slab]


def join_up(plan, idx, parts, hidden):
    block, width = parts[0].shape
    return pl.pallas_call(
        functools.partial(up_kernel, plan),
        in_specs=[pl.BlockSpec(memory_space=pltpu.SMEM)]
        + [pl.BlockSpec(memory_space=pltpu.VMEM)] * TP,
        out_shape=jax.ShapeDtypeStruct((block, hidden), f32),
        scratch_shapes=[pltpu.VMEM((TP, block, width), f32)],
        cost_estimate=cost(block * hidden, 6 * block * hidden),
        name="join_up",
    )(idx, *parts)


def resid_kernel(r_ref, dm_ref, vec_ref, *refs):
    part_refs, (dr_ref, da_ref, sum_ref) = refs[:TP], refs[TP:]
    total = part_refs[0][...].astype(f32)
    for j in range(1, TP):
        total += part_refs[j][...].astype(f32)
    units, rstd = unit(r_ref[...])
    dm = dm_ref[...].astype(f32)
    dr = dm + unit_back(total * vec_ref[5:6, :], units, rstd)
    da = dr.astype(bf16)
    dr_ref[...] = dr
    da_ref[...] = da
    sum_ref[...] = jnp.zeros_like(sum_ref)
    sum_ref[0:1, :] = jnp.sum(da.astype(f32), axis=0, keepdims=True)
    sum_ref[1:2, :] = jnp.sum(dm, axis=0, keepdims=True)


def resid_back(parts, r_own, dm, vecs):
    rows, width = dm.shape
    return pl.pallas_call(
        resid_kernel,
        out_shape=[
            jax.ShapeDtypeStruct((rows, width), f32),
            jax.ShapeDtypeStruct((rows, width), bf16),
            jax.ShapeDtypeStruct((8, width), f32),
        ],
        cost_estimate=cost(30 * rows * width, rows * width * 20),
        name="resid_back",
    )(r_own, dm, vecs, *parts)


def finish_kernel(r_ref, x_ref, dr_ref, vec_ref, *refs):
    rows = r_ref.shape[0]
    total = refs[0][...].astype(f32)
    for ref in refs[1:TP]:
        total += ref[...].astype(f32)
    units, rstd = unit(x_ref[...].astype(f32))
    grad = dr_ref[...] + unit_back(total[:rows] * vec_ref[3:4, :], units, rstd)
    refs[TP][:rows, :] = (r_ref[...] + vec_ref[7:8, :] + total[rows:]).astype(bf16)
    refs[TP][rows:, :] = grad.astype(bf16)


def finish(parts, r_own, x, dr, vecs):
    rows, width = x.shape
    return pl.pallas_call(
        finish_kernel,
        out_shape=jax.ShapeDtypeStruct((2 * rows, width), bf16),
        cost_estimate=cost(40 * x.size, x.size * 30),
        name="finish",
    )(r_own, x, dr, vecs, *parts)


def normed_kernel(n_recv, idx_ref, x_ref, dq_ref, own_ref, *refs):
    out_refs, refs = refs[:TP], refs[TP:]
    recv_refs = refs[:n_recv]
    w_ref, d_ref, sum_ref = refs[n_recv : n_recv + 3]
    dh_refs, dh_now = refs[n_recv + 3 : -1], refs[-1]
    step = pl.program_id(0)

    @pl.when(step == 0)
    def _():
        sum_ref[...] = jnp.zeros_like(sum_ref)

    cols = dq_ref.shape[1]
    width = x_ref.shape[1]
    grad_k, grad_v = own_ref[0], own_ref[1]
    for ref in recv_refs:
        grad_k += ref[0].astype(f32)
        grad_v += ref[1].astype(f32)
    d_ref[:, :cols] = dq_ref[...]
    d_ref[:, cols : 2 * cols] = grad_k.astype(bf16)
    d_ref[:, 2 * cols : 3 * cols] = grad_v.astype(bf16)
    d_ref[:, 3 * cols :] = jnp.zeros_like(d_ref[:, 3 * cols :])
    low = d_ref[...]
    grad = dot(low, w_ref[...], 1, 1)
    dh_now[...] = grad.astype(bf16).reshape(dh_now.shape)
    side = lax.rem(idx_ref[0], 2)
    for i in range(2):

        @pl.when(step == i)
        def _(i=i):
            for b in range(2):
                rows = dh_now.shape[1]
                dh_refs[2 * i + b][:rows, :] = dh_now[side ^ b]
                dh_refs[2 * i + b][rows:, :] = out_refs[2 * i + b][...]

    units, _ = unit(x_ref[...].astype(f32))
    sum_ref[0:1, :width] += jnp.sum(grad * units, axis=0, keepdims=True)
    sum_ref[1:2, :width] += jnp.sum(grad, axis=0, keepdims=True)
    sum_ref[2:3, : low.shape[1]] += jnp.sum(low.astype(f32), axis=0, keepdims=True)


def normed_back(idx, x_all, dq, own, recvs, w_qkv, out_terms):
    rows, width = x_all.shape
    cols = dq.shape[1]
    wide = w_qkv.shape[1]
    step = rows // 2
    one = (rows // TP, width)
    pairs = pl.BlockSpec((2, step, cols), lambda i, idx: (0, i ^ (idx[0] // 2), 0))
    return pl.pallas_call(
        functools.partial(normed_kernel, len(recvs)),
        grid_spec=pltpu.PrefetchScalarGridSpec(
            num_scalar_prefetch=1,
            grid=(2,),
            in_specs=[
                pl.BlockSpec((step, width), lambda i, idx: (i ^ (idx[0] // 2), 0)),
                pl.BlockSpec((step, cols), lambda i, idx: (i ^ (idx[0] // 2), 0)),
                pairs,
            ]
            + [whole(one)] * TP
            + [pairs] * len(recvs)
            + [whole(w_qkv.shape)],
            out_specs=[
                pl.BlockSpec((step, wide), lambda i, idx: (i ^ (idx[0] // 2), 0)),
                whole((8, width)),
            ]
            + [whole((2 * one[0], width))] * TP,
            scratch_shapes=[pltpu.VMEM((2, *one), bf16)],
        ),
        out_shape=[
            jax.ShapeDtypeStruct((rows, wide), bf16),
            jax.ShapeDtypeStruct((8, width), f32),
        ]
        + [jax.ShapeDtypeStruct((2 * one[0], width), bf16)] * TP,
        compiler_params=params(),
        cost_estimate=cost(2 * rows * width * wide, rows * width * 12),
        name="normed_back",
    )(idx, x_all, dq, own, *out_terms, *recvs, w_qkv)


def proj_grads_kernel(plan, idx_ref, h_ref, d_ref, sum_ref, own_ref, two_ref, da_ref, o_ref, *refs):
    fast = plan.fast
    acc_ref, vec_ref = refs[-2:]
    wide = d_ref.shape[1]
    cols = o_ref.shape[2]
    rows, width = h_ref.shape
    member = idx_ref[0]
    acc_ref[:, :wide] = dot(h_ref[...], d_ref[...], 0, 0)
    da = da_ref[...].reshape(rows, cols)
    for j in range(TP):
        at = j * cols
        acc_ref[at : at + cols, wide : wide + cols] = dot(o_ref[j], da, 0, 0)
    bias_q, bias_v = sum_ref[2:3, :cols], sum_ref[2:3, 2 * cols : 3 * cols]
    zero = jnp.zeros_like(bias_q)
    vec_ref[...] = jnp.zeros_like(vec_ref)
    rows_of = [
        jnp.concatenate([jnp.where(member == j, b, zero) for j in range(TP)], axis=1)
        for b in (bias_q, bias_v)
    ]
    rows_of += [own_ref[0:1, :], sum_ref[0:1, :], sum_ref[1:2, :], two_ref[0:1, :], two_ref[1:2, :], own_ref[1:2, :]]
    for j, row in enumerate(rows_of):
        vec_ref[SMALLS + j : SMALLS + j + 1, :] = row
    acc_ref[:, wide + cols :] = vec_ref[...].T[:, SMALLS:]
    if not fast:
        refs[0][...] = acc_ref[...].astype(bf16)
        return
    core = idx_ref[2]
    keep_ref, send_ref = refs[:2]
    near, block, _ = keep_ref.shape
    span = near // plan.size["gx"]
    for ref, owner in ((keep_ref, core), (send_ref, 1 - core)):
        for n in range(near):
            gx, rest = divmod(n, span)
            at = ((gx * 2 + owner) * span + rest) * block
            ref[n] = acc_ref[pl.ds(pl.multiple_of(at, 8), block), :].astype(bf16)


def proj_grads(plan, idx, low, grads, sums, sum_own, sum_two, da_cols, o_all):
    rows, width = low.shape
    cols = o_all.shape[2]
    wide = grads.shape[1] + cols + SMALLS
    near = plan.devices // 2
    if plan.fast:
        out_shape = [jax.ShapeDtypeStruct((near, width // plan.devices, wide), bf16)] * 2
    else:
        out_shape = jax.ShapeDtypeStruct((width, wide), bf16)
    operands = (low, grads, sums, sum_own, sum_two, da_cols, o_all)
    return pl.pallas_call(
        functools.partial(proj_grads_kernel, plan),
        in_specs=[pl.BlockSpec(memory_space=pltpu.SMEM)]
        + [pl.BlockSpec(memory_space=pltpu.VMEM)] * len(operands),
        out_shape=out_shape,
        scratch_shapes=[
            pltpu.VMEM((width, wide), f32),
            pltpu.VMEM((2 * SMALLS, width), f32),
        ],
        compiler_params=pltpu.CompilerParams(vmem_limit_bytes=60 * 1024 * 1024),
        cost_estimate=cost(2 * rows * width * wide, width * wide * 6),
        name="proj_grads",
    )(idx, *operands)


def join_kernel(keep, cols, wide, in_ref, both_ref, *refs):
    mats, vec_refs = refs[:4], refs[4:12]
    output_ref, input_ref, turn_ref = refs[12:]
    rows = output_ref.shape[0]
    output_ref[...] = both_ref[:rows, :]
    input_ref[...] = both_ref[rows:, :]
    groups = {}
    for n in range(in_ref.shape[0]):
        value = in_ref[n].astype(f32)
        key = keep[n]
        groups[key] = value if key not in groups else groups[key] + value
    for j in range(TP):
        for ref, at in zip(mats, (0, cols, 2 * cols, wide)):
            ref[:, j * cols : (j + 1) * cols] = groups[j][:, at : at + cols]
    total = functools.reduce(jnp.add, [groups[j] for j in range(TP)])
    block = in_ref.shape[1]
    turn_ref[...] = jnp.zeros_like(turn_ref)
    turn_ref[:block, :SMALLS] = total[:, wide + cols :]
    turned = turn_ref[...].T
    for j, ref in enumerate(vec_refs):
        ref[...] = turned[j : j + 1, :block]


def join_grads(plan, got, both, cols, wide):
    near, block, _ = got.shape
    members = [plan.place(plan.same(n))[0] for n in range(near)]
    width = cols * TP
    return pl.pallas_call(
        functools.partial(join_kernel, members, cols, wide),
        out_shape=[jax.ShapeDtypeStruct((block, width), f32)] * 4
        + [jax.ShapeDtypeStruct((1, block), f32)] * 8
        + [jax.ShapeDtypeStruct((both.shape[0] // 2, both.shape[1]), bf16)] * 2,
        scratch_shapes=[pltpu.VMEM((128, 128), f32)],
        compiler_params=pltpu.CompilerParams(vmem_limit_bytes=60 * 1024 * 1024),
        cost_estimate=cost(got.size, got.size * 2),
        name="join_grads",
    )(got, both)


def local(
    plan, inputs, segment_ids, padding, cotangent, w_query, b_query, w_key, w_value, b_value,
    w_out, b_out, ln1_gain, ln1_shift, ln2_gain, ln2_shift, w_up, b_up, w_down, b_down,
):
    x_own = inputs[0]
    rows, width = x_own.shape
    cols = width // TP
    length = segment_ids.shape[1]
    block = w_query.shape[0]
    hidden = w_up.shape[1]
    slab = b_up.shape[0]
    size = plan.size
    member = lax.axis_index(plan.tp)
    part = lax.axis_index(plan.half)
    core = lax.axis_index("c")
    idx = jnp.stack([member, part, core, lax.axis_index("sz")]).astype(jnp.int32)
    lines = plan.copies // 2
    fast = plan.fast

    id_rows = jnp.pad(segment_ids[0].astype(bf16), (0, 8 * width - length)).reshape(8, width)
    moved = plan.move(jnp.concatenate([x_own, id_rows], axis=0), plan.route)
    x_mine = moved[:rows]
    ids = moved[rows:].reshape(1, -1)[:, :length].astype(f32)
    dm_own = (cotangent[0].astype(f32) * padding[0].astype(f32)[:, None]).astype(bf16)
    dm_mine = plan.move(dm_own, plan.route)

    small = [b_query, b_value, b_out, ln1_gain, ln1_shift, ln2_gain, ln2_shift, b_down]
    if fast:
        small = jnp.stack(small, axis=0)
        chunk = prepare(plan, w_query, w_key, w_value, small, w_up, w_out)
        got = lax.all_to_all(chunk, plan.tp, 0, 0, tiled=True)
        got, x_mine = lax.optimization_barrier((got, x_mine))
        x_all = lax.all_gather(x_mine, plan.tp, axis=0, tiled=True)
        proj, shard = shards_of(got, w_down, b_up[None], 3 * cols + SMALLS, lines)
        projs = [proj] + [plan.turn(proj, "sz", -j) for j in range(1, lines)]
        projs, x_all, shard, dm_mine = lax.optimization_barrier((projs, x_all, shard, dm_mine))
        shard = lax.all_to_all(shard, "sz", 0, 0, tiled=True)
        projs = jnp.stack(projs)
        low_one, query, kv, w_qkv, vecs = qkv(plan, idx, x_all, projs, plan.swap(projs))
    else:
        small = jnp.stack(small, axis=1)
        x_all = lax.all_gather(x_mine, plan.tp, axis=0, tiled=True)
        b_row = jnp.pad(b_up[None], ((0, 7), (0, width - slab)))
        table = [w_query, w_key, w_value, w_out, small]
        table = lax.all_gather(jnp.concatenate(table, axis=1), ALL, axis=0, tiled=True)
        vecs = table[:, 4 * width :].T.astype(f32)
        split = [lax.dynamic_slice(table, (0, i * width + member * cols), (width, cols)) for i in range(3)]
        w_qkv = jnp.concatenate([*split, jnp.zeros((width, SMALLS), bf16)], axis=1)
        out_full = table[:, 3 * width : 4 * width].reshape(TP, cols, width)
        low_one, query, kv = qkv(plan, idx, x_all, w_qkv, vecs)
        up_mine = lax.all_gather(w_up, ALL, axis=0, tiled=True)
        up_mine = up_mine.reshape(width, plan.devices, slab).transpose(1, 0, 2)
        up_mine = plan.shuffle(up_mine, ALL, plan.tp + plan.rep).reshape(TP, plan.copies, width, slab)
        up_mine = lax.dynamic_index_in_dim(up_mine, member, 0, keepdims=False)
        up_mine = up_mine.transpose(1, 0, 2).reshape(width, -1)
        downs = jnp.concatenate([w_down, b_row], axis=0)
        downs = lax.all_gather(downs, plan.rep, axis=0, tiled=False)
        down_mine = downs[:, :slab].reshape(-1, width)
        b_up_mine = downs[:, slab, :slab].reshape(1, -1).astype(f32)

    parts = plan.parts
    kvs = [kv] + [plan.turn(kv, plan.half, -j) for j in range(1, parts)]
    mixed, lse = attend(idx, ids, query, kvs)
    o_all = lax.all_gather(mixed, plan.tp, axis=0, tiled=False)
    dms = plan.partners(dm_mine)
    if fast:
        shard, o_all, dms = lax.optimization_barrier((shard, o_all, dms))
        up_mine, out_full, down_mine, row = assemble(plan, idx, shard, plan.swap(shard), slab)
        out_full = out_full.reshape(TP, cols, width)
        down_mine = down_mine.reshape(-1, width)
        b_up_mine = row[:, :, 0, :slab].reshape(1, -1).astype(f32)
    r_own, low_two, act, grad_pre, dm_all, sum_two, *dh_two = mlp(
        idx, x_all, o_all, dms, out_full, up_mine, down_mine, vecs, b_up_mine
    )

    back_two = plan.reduce(dh_two)
    if fast:
        near_terms, far_terms, *out_terms = mlp_weight_grads(
            plan, idx, low_two, grad_pre, act, dm_all, down_mine
        )
        back_two, out_terms, far_terms = lax.optimization_barrier((back_two, out_terms, far_terms))
    else:
        up_terms = dot(low_two, grad_pre, 0, 0).astype(bf16)
        down_terms = dot(act, dm_all, 0, 0).astype(bf16)
        row = jnp.sum(grad_pre.astype(f32), axis=0).astype(bf16)
        out_terms = dot(act, down_mine).astype(bf16).reshape(TP, rows, width)
        out_terms = [
            lax.dynamic_index_in_dim(out_terms, member ^ j, 0, keepdims=False) for j in range(TP)
        ]
    dr, da, sum_own = resid_back(back_two, r_own, dm_mine, vecs)
    if fast:
        terms = add(near_terms, plan.swap(far_terms))
        das = [da, plan.partner(da, 1), plan.partner(da, 2)]
        terms, da = lax.optimization_barrier((terms, da))
        das += [plan.partner(da, 3)]
        terms = lax.all_to_all(terms, "sz", 0, 0, tiled=True)
        *ups, g_w_down, g_b_up = sum_rows(plan, idx, terms, block, slab)
    else:
        das = plan.partners(da)
        row = jnp.pad(row.reshape(plan.copies, 1, slab), ((0, 0), (0, 7), (0, width - slab)))
        downs = jnp.concatenate([down_terms.reshape(plan.copies, slab, width), row], axis=1)
        downs = lax.psum_scatter(downs, plan.rep, scatter_dimension=0, tiled=False)
        g_w_down = downs[:slab].astype(f32)
        g_b_up = downs[slab, :slab].astype(f32)
        ups = plan.shuffle(up_terms.reshape(plan.devices, block, -1), ALL, plan.rep + plan.tp)
        ups = ups.reshape(plan.copies, TP * block, -1)
        ups = lax.psum_scatter(ups, plan.rep, scatter_dimension=0, tiled=False)
        ups = lax.all_to_all(ups.reshape(TP, block, -1), plan.tp, 0, 0, tiled=True).astype(f32)
    grad_query, kv_own, da_cols, *kv_others = attend_back(idx, ids, query, das, out_full, lse, kvs)
    recvs = [plan.turn(kv_others[j - 1], plan.half, j) for j in range(1, parts)]
    grads, sum_one, *both = normed_back(idx, x_all, grad_query, kv_own, recvs, w_qkv, out_terms)
    both = plan.reduce(both)
    terms = proj_grads(plan, idx, low_one, grads, sum_one, sum_own, sum_two, da_cols, o_all)
    if fast:
        keep, send = terms
        terms = add(keep, plan.swap(send))
        terms, ups, both = lax.optimization_barrier((terms, ups, both))
        got = lax.all_to_all(terms, SAME, 0, 0, tiled=True)
    else:
        terms = plan.shuffle(terms.reshape(plan.devices, block, -1), ALL, ("c",) + SAME)
        terms = terms.reshape(2, -1, *terms.shape[1:])
        keep, send = jnp.where(core == 0, terms, terms[::-1])
        got = lax.all_to_all(add(keep, plan.swap(send)), SAME, 0, 0, tiled=True)
    if fast:
        g_w_up = join_up(plan, idx, plan.reduce(ups), hidden)
        g_b_up = g_b_up[0]
    else:
        ups = ups.reshape(TP, block, plan.copies, slab).transpose(0, 2, 1, 3)
        ups = plan.shuffle(ups.reshape(plan.devices, block, slab), plan.tp + plan.rep, ALL)
        g_w_up = ups.transpose(1, 0, 2).reshape(block, hidden)
    both = plan.move(finish(both, r_own, x_mine, dr, vecs), plan.back)
    joined = join_grads(plan, got, both, cols, w_qkv.shape[1])
    g_query, g_key, g_value, g_out, *vec, output, grad_input = joined
    vec = [v[0] for v in vec]
    return (
        output[None],
        grad_input[None],
        g_query,
        vec[0],
        g_key,
        g_value,
        vec[1],
        g_out,
        vec[2],
        vec[3],
        vec[4],
        vec[5],
        vec[6],
        g_w_up,
        g_b_up,
        g_w_down,
        vec[7],
    )


def solution(mesh):
    groups, blocks = mesh.shape["grp"], mesh.shape["seq"]
    plan = Plan(groups, blocks)
    fine = Mesh(mesh.devices.reshape(plan.shape), ALL)
    grp, seq = ("gx", "c"), ("sz", "sy")
    matrix, vector = P(ALL, None), P(ALL)
    token = P(grp, seq, None)
    return jax.shard_map(
        functools.partial(local, plan),
        mesh=fine,
        in_specs=(
            token, P(grp, None), P(grp, seq), token,
            matrix, vector, matrix, matrix, vector, matrix, vector,
            vector, vector, vector, vector, matrix, vector, matrix, vector,
        ),
        out_specs=(
            token, token,
            matrix, vector, matrix, matrix, vector, matrix, vector,
            vector, vector, vector, vector, matrix, vector, matrix, vector,
        ),
        check_vma=False,
    )
```

```python
import functools

import jax
import jax.numpy as jnp
from jax import lax
from jax.experimental import pallas as pl
from jax.experimental.pallas import tpu as pltpu
from jax.sharding import Mesh, PartitionSpec as P

HEADS = 12
HEAD_DIM = 64
TP = 4
HEADS_TP = HEADS // TP
EPS = 1e-05
NEG = -1e30
SCALE = 0.125
ALL = ("gx", "c", "sz", "sy")
SAME = ("gx", "sz", "sy")
SMALLS = 64
NORMED = 13.0
f32 = jnp.float32
bf16 = jnp.bfloat16


class Plan:
    def __init__(self, groups, blocks):
        if (groups, blocks) == (4, 8):
            self.shape = (2, 2, 4, 2)
            self.tp, self.half, self.rep = ("gx", "sy"), "c", ("c", "sz")
            self.fast = True
        else:
            self.shape = (groups // 2, 2, blocks // TP, TP)
            self.tp, self.half, self.rep = ("sy",), "sz", ("gx", "c", "sz")
            self.fast = False
        self.size = dict(zip(ALL, self.shape))
        self.devices = groups * blocks
        self.parts = self.size[self.half]
        self.copies = self.devices // TP
        self.lines = tuple(a for a in self.rep if a != "c")
        self.route = []
        for src in range(self.devices):
            seq, block = divmod(src, blocks)
            part, member = divmod(block, TP)
            if self.tp == ("sy",):
                dst = src
            else:
                dst = (((member >> 1) * 2 + part) * 4 + seq) * 2 + (member & 1)
            self.route.append((src, dst))
        self.back = [(dst, src) for src, dst in self.route]

    def swap(self, value):
        return lax.ppermute(value, "c", [(0, 1), (1, 0)])

    def gather(self, value):
        return lax.all_to_all(
            jnp.broadcast_to(value, (TP, *value.shape)), self.tp, 0, 0, tiled=True
        )

    def partner(self, value, j):
        table = [(t, t ^ j) for t in range(TP)]
        return lax.ppermute(value, self.tp, table)

    def partners(self, value):
        return [value] + [self.partner(value, j) for j in range(1, TP)]

    def reduce(self, values):
        return [values[0]] + [self.partner(values[j], j) for j in range(1, TP)]

    def turn(self, value, axis, by):
        count = self.size[axis]
        return lax.ppermute(value, axis, [(i, (i + by) % count) for i in range(count)])

    def place(self, r):
        at, rest = {}, r
        for axis in reversed(ALL):
            rest, at[axis] = divmod(rest, self.size[axis])
        numbers = []
        for axes in (self.tp, self.rep):
            number = 0
            for axis in axes:
                number = number * self.size[axis] + at[axis]
            numbers.append(number)
        return tuple(numbers)

    def same(self, n):
        span = self.devices // 2 // self.size["gx"]
        gx, rest = divmod(n, span)
        return gx * 2 * span + rest

    def move(self, value, table):
        if all(a == b for a, b in table):
            return value
        return lax.ppermute(value, ALL, table)

    def shuffle(self, value, before, after):
        tail = value.shape[1:]
        dims = [self.size[a] for a in before]
        order = [before.index(a) for a in after]
        value = value.reshape(*dims, *tail)
        value = value.transpose(*order, *range(len(dims), len(dims) + len(tail)))
        return value.reshape(-1, *tail)


def dot(left, right, left_dim=1, right_dim=0):
    return lax.dot_general(
        left, right, (((left_dim,), (right_dim,)), ((), ())), preferred_element_type=f32
    )


def unit(values):
    center = values - jnp.mean(values, axis=-1, keepdims=True)
    variance = jnp.mean(center * center, axis=-1, keepdims=True)
    rstd = lax.rsqrt(variance + EPS)
    return center * rstd, rstd


def unit_back(grad_unit, units, rstd):
    first = jnp.mean(grad_unit, axis=-1, keepdims=True)
    second = jnp.mean(grad_unit * units, axis=-1, keepdims=True)
    return rstd * (grad_unit - first - units * second)


def params(limit=60 * 1024 * 1024, axes=1):
    return pltpu.CompilerParams(
        dimension_semantics=("arbitrary",) * axes, vmem_limit_bytes=limit
    )


def takes(microseconds):
    return pl.CostEstimate(
        flops=0, bytes_accessed=int(microseconds * 3.69e6), transcendentals=0
    )


def whole(shape):
    zeros = (0,) * len(shape)
    return pl.BlockSpec(shape, lambda *_: zeros)


def head_lanes(value, head):
    lane = lax.broadcasted_iota(jnp.int32, value.shape, 1)
    keep = (lane >= head * HEAD_DIM) & (lane < (head + 1) * HEAD_DIM)
    return jnp.where(keep, value, jnp.zeros_like(value))


def member_cols(row, member, cols):
    out = jnp.zeros((row.shape[0], cols), row.dtype)
    for j in range(TP):
        out = jnp.where(member == j, row[:, j * cols : (j + 1) * cols], out)
    return out


def prep_kernel(rep_of, q_ref, k_ref, v_ref, up_ref, out_ref, *refs):
    small_refs, chunk_ref, turn_ref = refs[:-2], refs[-2], refs[-1]
    block, width = q_ref.shape
    cols = width // TP
    wide = 3 * cols + SMALLS
    slab = up_ref.shape[1] // len(rep_of)
    turn_ref[...] = jnp.zeros_like(turn_ref)
    for j, ref in enumerate(small_refs):
        turn_ref[j : j + 1, :block] = ref[...].astype(f32)
    small = turn_ref[...].T[:block, :SMALLS]
    for j in range(TP):
        at = slice(j * cols, (j + 1) * cols)
        chunk_ref[j, :, :wide] = jnp.concatenate(
            [r[:, at].astype(f32) for r in (q_ref, k_ref, v_ref)] + [small], axis=1
        ).astype(bf16)
        chunk_ref[j, :, wide + width :] = out_ref[...]
    for r, (member, copy) in enumerate(rep_of):
        first = wide + copy * slab
        chunk_ref[member, :, first : first + slab] = up_ref[:, r * slab : (r + 1) * slab]


def prepare(plan, w_query, w_key, w_value, small, w_up, w_out):
    block, width = w_query.shape
    rep_of = [plan.place(r) for r in range(plan.devices)]
    wide = 3 * width // TP + SMALLS
    return pl.pallas_call(
        functools.partial(prep_kernel, rep_of),
        out_shape=jax.ShapeDtypeStruct((TP, block, wide + w_up.shape[1] // TP + width), bf16),
        scratch_shapes=[pltpu.VMEM((128, 128), f32)],
        cost_estimate=takes(1.9),
        name="prepare",
    )(w_query, w_key, w_value, w_up, w_out, *[v[None] for v in small])


def shards_kernel(wide, got_ref, down_ref, row_ref, proj_ref, shard_ref):
    block = got_ref.shape[1]
    slab, width = down_ref.shape
    first = TP * block
    for t in range(TP):
        at = t * block
        proj_ref[at : at + block, :] = got_ref[t, :, :wide]
        up = got_ref[t, :, wide : wide + width]
        out = got_ref[t, :, wide + width :]
        for n in range(shard_ref.shape[0]):
            shard_ref[n, at : at + block, :] = up
            shard_ref[n, first + at : first + at + block, :] = out
    row = jnp.concatenate([row_ref[...].astype(f32), jnp.zeros((1, width - slab), f32)], axis=1)
    row = jnp.broadcast_to(row, (8, width)).astype(bf16)
    for n in range(shard_ref.shape[0]):
        shard_ref[n, 2 * first : 2 * first + slab, :] = down_ref[...]
        shard_ref[n, 2 * first + slab :, :] = row


def shards_of(got, w_down, b_row, wide, lines):
    _, block, _ = got.shape
    slab, width = w_down.shape
    return pl.pallas_call(
        functools.partial(shards_kernel, wide),
        out_shape=[
            jax.ShapeDtypeStruct((TP * block, wide), bf16),
            jax.ShapeDtypeStruct((lines, 2 * TP * block + slab + 8, width), bf16),
        ],
        cost_estimate=takes(2.4),
        name="shards_of",
    )(got, w_down, b_row)


def qkv_kernel(plan, idx_ref, x_ref, *refs):
    fast = plan.fast
    if fast:
        own_ref, other_ref, h_ref, q_ref, kv_ref, w_ref, vec_ref, wide_ref = refs
    else:
        w_ref, vec_ref, h_ref, q_ref, kv_ref = refs
    cols = q_ref.shape[1]
    if fast:

        @pl.when(pl.program_id(0) == 0)
        def _():
            core = idx_ref[2]
            line = idx_ref[3]
            lines, rows, _ = own_ref.shape
            pair = rows // plan.size["gx"]
            for ref, side in ((own_ref, core), (other_ref, 1 - core)):
                for j in range(lines):
                    z = lax.rem(line + j, lines)
                    value = ref[j].astype(f32)
                    for gx in range(plan.size["gx"]):
                        wide_ref[gx * 2 + side, z] = value[gx * pair : (gx + 1) * pair, :]
            table = wide_ref[...].reshape(w_ref.shape)
            w_ref[...] = table.astype(bf16)
            vec_ref[...] = table[:, 512:640].T[64:72, :]

    units, _ = unit(x_ref[...].astype(f32))
    low = (units * vec_ref[3:4, :] + vec_ref[4:5, :]).astype(bf16)
    h_ref[...] = low
    out = dot(low, w_ref[...])
    bias = member_cols(vec_ref[0:2, :], idx_ref[0], cols)
    query = (out[:, :cols] + bias[0:1, :]).astype(bf16)
    q_ref[...] = (query.astype(f32) * SCALE).astype(bf16)
    kv_ref[0] = out[:, cols : 2 * cols].astype(bf16)
    kv_ref[1] = (out[:, 2 * cols : 3 * cols] + bias[1:2, :]).astype(bf16)


def qkv(plan, idx, x_all, *operands):
    rows, width = x_all.shape
    cols = width // TP
    step = rows // 2
    wide = 3 * cols + SMALLS
    out_specs = [
        pl.BlockSpec((step, width), lambda i, *_: (i, 0)),
        pl.BlockSpec((step, cols), lambda i, *_: (i, 0)),
        pl.BlockSpec((2, step, cols), lambda i, *_: (0, i, 0)),
    ]
    out_shape = [
        jax.ShapeDtypeStruct((rows, width), bf16),
        jax.ShapeDtypeStruct((rows, cols), bf16),
        jax.ShapeDtypeStruct((2, rows, cols), bf16),
    ]
    scratch = []
    if plan.fast:
        out_specs += [whole((width, wide)), whole((8, width))]
        out_shape += [
            jax.ShapeDtypeStruct((width, wide), bf16),
            jax.ShapeDtypeStruct((8, width), f32),
        ]
        lines = plan.copies // 2
        scratch = [pltpu.VMEM((2 * plan.size["gx"], lines, width // (2 * plan.size["gx"] * lines), wide), f32)]
    return pl.pallas_call(
        functools.partial(qkv_kernel, plan),
        grid_spec=pltpu.PrefetchScalarGridSpec(
            num_scalar_prefetch=1,
            grid=(2,),
            in_specs=[pl.BlockSpec((step, width), lambda i, *_: (i, 0))]
            + [whole(v.shape) for v in operands],
            out_specs=out_specs,
            scratch_shapes=scratch,
        ),
        out_shape=out_shape,
        compiler_params=params(),
        cost_estimate=takes(4.8),
        name="qkv",
    )(idx, x_all, *operands)


def fill_docs(ids_ref, part, parts, doc_ref):
    span, width = doc_ref.shape[1:]
    for j in range(parts):
        at = lax.rem(part + j, parts) * span
        row = ids_ref[0:1, pl.ds(pl.multiple_of(at, 512), span)]
        doc_ref[j] = jnp.broadcast_to(row, (width, span)).T


def fwd_kernel(parts, idx_ref, ids_ref, q_ref, *refs):
    kv_refs = refs[:parts]
    o_ref, lse_ref, turned, doc_ref = refs[parts:]
    step = pl.program_id(0)
    part = idx_ref[1]
    span = kv_refs[0].shape[1]
    width = q_ref.shape[0]

    @pl.when(step == 0)
    def _():
        fill_docs(ids_ref, part, parts, doc_ref)
        for j in range(parts):
            turned[j] = kv_refs[j][1].T

    at = part * span + step * width
    own = ids_ref[0:1, pl.ds(pl.multiple_of(at, 128), width)]
    query = q_ref[...]
    outs, lses = [], []
    for head in range(HEADS_TP):
        masked = head_lanes(query, head)
        scores = []
        for j in range(parts):
            raw = dot(kv_refs[j][0], masked, 1, 1)
            scores.append(jnp.where(doc_ref[j] == own, raw, NEG))
        peak = functools.reduce(
            jnp.maximum, [jnp.max(s, axis=0, keepdims=True) for s in scores]
        )
        exps = [jnp.exp(s - peak) for s in scores]
        total = functools.reduce(jnp.add, [jnp.sum(e, axis=0, keepdims=True) for e in exps])
        scale = 1.0 / total
        acc = None
        for j in range(parts):
            probs = (exps[j] * scale).astype(bf16)
            term = dot(turned[j, head * HEAD_DIM : (head + 1) * HEAD_DIM, :], probs)
            acc = term if acc is None else acc + term
        outs.append(acc)
        lses.append(peak + jnp.log(total))
    o_ref[...] = jnp.concatenate(outs, axis=0).T.astype(bf16)
    for head in range(HEADS_TP):
        lse_ref[head : head + 1, :] = lses[head]


def attend(idx, ids, q, kvs, width=256):
    rows, cols = q.shape
    parts = len(kvs)
    span = kvs[0].shape[1]
    return pl.pallas_call(
        functools.partial(fwd_kernel, parts),
        grid_spec=pltpu.PrefetchScalarGridSpec(
            num_scalar_prefetch=1,
            grid=(rows // width,),
            in_specs=[whole(ids.shape), pl.BlockSpec((width, cols), lambda i, *_: (i, 0))]
            + [whole(kv.shape) for kv in kvs],
            out_specs=[
                pl.BlockSpec((width, cols), lambda i, *_: (i, 0)),
                pl.BlockSpec((8, width), lambda i, *_: (0, i)),
            ],
            scratch_shapes=[
                pltpu.VMEM((parts, cols, span), bf16),
                pltpu.VMEM((parts, span, width), f32),
            ],
        ),
        out_shape=[
            jax.ShapeDtypeStruct((rows, cols), bf16),
            jax.ShapeDtypeStruct((8, rows), f32),
        ],
        compiler_params=params(),
        cost_estimate=takes(7.1),
        name="attend",
    )(idx, ids, q, *kvs)


def bwd_kernel(parts, waits, idx_ref, ids_ref, q_ref, w_ref, lse_ref, *refs):
    da_refs, refs = refs[:TP], refs[TP + waits :]
    kv_refs = refs[:parts]
    dq_ref, own_ref, cols_ref = refs[parts : parts + 3]
    other_refs = refs[parts + 3 : 2 * parts + 2]
    turned, doc_ref, key_acc, value_acc, mixed_ref = refs[2 * parts + 2 :]
    step = pl.program_id(0)
    part = idx_ref[1]
    span = kv_refs[0].shape[1]
    width, cols = q_ref.shape

    @pl.when(step == 0)
    def _():
        fill_docs(ids_ref, part, parts, doc_ref)
        for j in range(parts):
            turned[j] = kv_refs[j][0].T
        key_acc[...] = jnp.zeros_like(key_acc)
        value_acc[...] = jnp.zeros_like(value_acc)
        member = idx_ref[0]
        for j in range(TP):
            da = da_refs[j][...]
            mixed_ref[member ^ j] = dot(da, w_ref[...], 1, 1).astype(bf16)
            cols_ref[member ^ j] = member_cols(da, member, cols)

    at = part * span + step * width
    own = ids_ref[0:1, pl.ds(pl.multiple_of(at, 128), width)]
    query = q_ref[...]
    group = width // mixed_ref.shape[1]
    grad_mixed = mixed_ref[pl.ds(step * group, group)].reshape(width, cols)
    turned_grads = []
    for head in range(HEADS_TP):
        masked_q = head_lanes(query, head)
        masked_g = head_lanes(grad_mixed, head)
        lse = lse_ref[head : head + 1, :]
        probs, grads = [], []
        for j in range(parts):
            raw = dot(kv_refs[j][0], masked_q, 1, 1)
            probs.append(jnp.exp(jnp.where(doc_ref[j] == own, raw, NEG) - lse))
            grads.append(dot(kv_refs[j][1], masked_g, 1, 1))
        delta = functools.reduce(
            jnp.add,
            [jnp.sum(p * g, axis=0, keepdims=True) for p, g in zip(probs, grads)],
        )
        acc = None
        for j in range(parts):
            grad_scores = (probs[j] * (grads[j] - delta)).astype(bf16)
            value_acc[j] += dot(probs[j].astype(bf16), masked_g)
            key_acc[j] += dot(grad_scores, masked_q)
            term = dot(turned[j, head * HEAD_DIM : (head + 1) * HEAD_DIM, :], grad_scores)
            acc = term if acc is None else acc + term
        turned_grads.append(acc)
    dq_ref[...] = (jnp.concatenate(turned_grads, axis=0).T * SCALE).astype(bf16)

    @pl.when(step == pl.num_programs(0) - 1)
    def _():
        own_ref[0] = key_acc[0]
        own_ref[1] = value_acc[0]
        for j in range(1, parts):
            other_refs[j - 1][0] = key_acc[j].astype(bf16)
            other_refs[j - 1][1] = value_acc[j].astype(bf16)


def attend_back(idx, ids, q, das, after, w_out, lse, kvs, width=256):
    rows, cols = q.shape
    step, model = das[0].shape
    parts = len(kvs)
    span = kvs[0].shape[1]
    return pl.pallas_call(
        functools.partial(bwd_kernel, parts, len(after)),
        grid_spec=pltpu.PrefetchScalarGridSpec(
            num_scalar_prefetch=1,
            grid=(rows // width,),
            in_specs=[
                whole(ids.shape),
                pl.BlockSpec((width, cols), lambda i, *_: (i, 0)),
                whole((cols, model)),
                pl.BlockSpec((8, width), lambda i, *_: (0, i)),
            ]
            + [whole((step, model))] * TP
            + [pl.BlockSpec(memory_space=pl.ANY)] * len(after)
            + [whole(kv.shape) for kv in kvs],
            out_specs=[
                pl.BlockSpec((width, cols), lambda i, *_: (i, 0)),
                whole((2, span, cols)),
                whole((TP, step, cols)),
            ]
            + [whole((2, span, cols))] * (parts - 1),
            scratch_shapes=[
                pltpu.VMEM((parts, cols, span), bf16),
                pltpu.VMEM((parts, span, width), f32),
                pltpu.VMEM((parts, span, cols), f32),
                pltpu.VMEM((parts, span, cols), f32),
                pltpu.VMEM((TP, step, cols), bf16),
            ],
        ),
        out_shape=[
            jax.ShapeDtypeStruct((rows, cols), bf16),
            jax.ShapeDtypeStruct((2, span, cols), f32),
            jax.ShapeDtypeStruct((TP, step, cols), bf16),
        ]
        + [jax.ShapeDtypeStruct((2, span, cols), bf16)] * (parts - 1),
        compiler_params=params(),
        cost_estimate=takes(10.7),
        name="attend_back",
    )(idx, ids, q, w_out, lse, *das, *after, *kvs)


def mlp_kernel(plan, idx_ref, x_ref, o_ref, vec_ref, *refs):
    dm_refs, refs = refs[:TP], refs[TP:]
    step = pl.program_id(0)
    side = lax.rem(idx_ref[0], 2)
    if plan.fast:
        own_ref, other_ref, r_ref, h_ref, a_ref, du_ref, dm_ref, sum_ref = refs[:8]
        dh_refs = refs[8 : 8 + TP]
        out_ref, down_ref, dm_now, r_now, dh_now, held, held_down, held_row = refs[8 + TP :]

        @pl.when(step == 0)
        def _():
            core = idx_ref[2]
            first = held.shape[3] * plan.size["gx"]
            pair = held.shape[3]
            slab = held_down.shape[2]
            rows = []
            for z in range(held.shape[2]):
                for ref, owner in ((own_ref, core), (other_ref, 1 - core)):
                    for gx in range(plan.size["gx"]):
                        at = gx * pair
                        held[0, gx * 2 + owner, z] = ref[z, at : at + pair, :]
                        held[1, gx * 2 + owner, z] = ref[z, first + at : first + at + pair, :]
                    held_down[owner, z] = ref[z, 2 * first : 2 * first + slab, :]
            for owner in range(2):
                for z in range(held.shape[2]):
                    at = 2 * first + slab
                    row = jnp.where(
                        core == owner,
                        own_ref[z, at : at + 8, :].astype(f32),
                        other_ref[z, at : at + 8, :].astype(f32),
                    )
                    rows.append(row[0:1, :slab])
            held_row[...] = jnp.concatenate(rows, axis=1)
            out = held[1, idx_ref[0]]
            out_ref[...] = out.reshape(out_ref.shape)
            down_ref[...] = held_down[...].reshape(down_ref.shape)

        width = held.shape[-1]
        w_up = held[0].reshape(-1, width)
        outs = [held[1, j].reshape(-1, width) for j in range(TP)]
        w_down = held_down[...].reshape(-1, width)
        b_up = held_row[...]
    else:
        wo_ref, wu_ref, wd_ref, bup_ref, r_ref, h_ref, a_ref, du_ref, dm_ref, sum_ref = refs[:10]
        dh_refs, dm_now, r_now, dh_now = refs[10 : 10 + TP], refs[-3], refs[-2], refs[-1]
        w_up, w_down, b_up = wu_ref[...], wd_ref[...], bup_ref[...]
        outs = [wo_ref[j] for j in range(TP)]

    @pl.when(step == 0)
    def _():
        sum_ref[...] = jnp.zeros_like(sum_ref)

    attended = dot(o_ref[0], outs[0])
    for j in range(1, TP):
        attended += dot(o_ref[j], outs[j])
    residual = x_ref[...].astype(f32) + (attended + vec_ref[2:3, :])

    for i in range(2):

        @pl.when(step == i)
        def _(i=i):
            for b in range(2):
                dm_now[side ^ b] = dm_refs[2 * i + b][...]
            if i == 0:
                r_now[...] = residual.reshape(r_now.shape)
                r_ref[...] = r_now[side]

    units, _ = unit(residual)
    low = (units * vec_ref[5:6, :] + vec_ref[6:7, :]).astype(bf16)
    h_ref[...] = low
    pre = dot(low, w_up) + b_up
    normal = 0.5 * (1.0 + lax.erf(pre * 0.7071067811865476))
    act = (pre * normal).astype(bf16)
    a_ref[...] = act
    slope = normal + pre * (0.3989422804014327 * jnp.exp(-0.5 * pre * pre))
    dm = dm_now[...].reshape(x_ref.shape)
    dm_ref[...] = dm
    grad_pre = (dot(dm, w_down, 1, 1) * slope).astype(bf16)
    du_ref[...] = grad_pre
    grad = dot(grad_pre, w_up, 1, 1)
    sum_ref[0:1, :] += jnp.sum(grad * units, axis=0, keepdims=True)
    sum_ref[1:2, :] += jnp.sum(grad, axis=0, keepdims=True)
    dh_now[...] = grad.astype(bf16).reshape(dh_now.shape)
    for i in range(2):

        @pl.when(step == i)
        def _(i=i):
            for b in range(2):
                dh_refs[2 * i + b][...] = dh_now[side ^ b]


def mlp(plan, idx, x_all, o_all, vecs, dms, weights, slab):
    rows, width = x_all.shape
    hidden = plan.copies * slab
    cols = width // TP
    step = rows // 2

    def block(i, idx):
        return (i ^ (idx[0] // 2), 0)

    token = pl.BlockSpec((step, width), block)
    inner = pl.BlockSpec((step, hidden), block)
    one = whole((rows // TP, width))
    now = (2, rows // TP, width)
    out_specs = [one, token, inner, inner, token, whole((8, width))] + [one] * TP
    out_shape = [
        jax.ShapeDtypeStruct((rows // TP, width), f32),
        jax.ShapeDtypeStruct((rows, width), bf16),
        jax.ShapeDtypeStruct((rows, hidden), bf16),
        jax.ShapeDtypeStruct((rows, hidden), bf16),
        jax.ShapeDtypeStruct((rows, width), bf16),
        jax.ShapeDtypeStruct((8, width), f32),
    ] + [jax.ShapeDtypeStruct((rows // TP, width), bf16)] * TP
    scratch = [pltpu.VMEM(now, bf16), pltpu.VMEM(now, f32), pltpu.VMEM(now, bf16)]
    if plan.fast:
        lines = plan.copies // 2
        gx = plan.size["gx"]
        out_specs += [whole((cols, width)), whole((hidden, width))]
        out_shape += [
            jax.ShapeDtypeStruct((cols, width), bf16),
            jax.ShapeDtypeStruct((hidden, width), bf16),
        ]
        scratch += [
            pltpu.VMEM((2, 2 * gx, lines, width // (2 * gx * lines), width), bf16),
            pltpu.VMEM((2, lines, slab, width), bf16),
            pltpu.VMEM((1, hidden), f32),
        ]
    return pl.pallas_call(
        functools.partial(mlp_kernel, plan),
        grid_spec=pltpu.PrefetchScalarGridSpec(
            num_scalar_prefetch=1,
            grid=(2,),
            in_specs=[
                token,
                pl.BlockSpec((TP, step, cols), lambda i, idx: (0, i ^ (idx[0] // 2), 0)),
                whole(vecs.shape),
            ]
            + [one] * TP
            + [whole(v.shape) for v in weights],
            out_specs=out_specs,
            scratch_shapes=scratch,
        ),
        out_shape=out_shape,
        compiler_params=params(),
        cost_estimate=takes(10.5),
        name="mlp",
    )(idx, x_all, o_all, vecs, *dms, *weights)


def pair_kernel(plan, idx_ref, h_ref, du_ref, a_ref, dm_ref, wd_ref, near_ref, far_ref, *refs):
    out_refs, acc_ref, wide_ref = refs[:TP], refs[TP], refs[TP + 1]
    lines = plan.copies // 2
    step = pl.program_id(0)
    member, core = idx_ref[0], idx_ref[2]
    half = step ^ core
    grad_pre = du_ref[...]
    act = a_ref[...]
    width = h_ref.shape[1]
    block = width // plan.devices
    size = act.shape[1]
    slab = size // lines
    first = TP * block
    up = dot(h_ref[...], grad_pre, 0, 0)
    down = dot(act, dm_ref[...], 0, 0)
    bias = jnp.sum(grad_pre.astype(f32), axis=0, keepdims=True)
    term = dot(act, wd_ref[...])

    @pl.when(step == 0)
    def _():
        acc_ref[...] = term.reshape(acc_ref.shape)
        wide_ref[:, :size] = up

    @pl.when(step == 1)
    def _():
        acc_ref[...] += term.reshape(acc_ref.shape)
        for j in range(TP):
            out_refs[j][...] = acc_ref[member ^ j].astype(bf16)
        wide_ref[:, size:] = up
        pair = plan.size["sy"] * block
        for ref, owner in ((near_ref, core), (far_ref, 1 - core)):
            for z in range(lines):
                for gx in range(plan.size["gx"]):
                    at = ((gx * 2 + owner) * lines + z) * pair
                    value = wide_ref[pl.ds(pl.multiple_of(at, 16), pair), :]
                    ref[z, gx * pair : (gx + 1) * pair, :] = value.astype(bf16)

    def put(ref):
        for k in range(lines):
            at = k * slab
            row = jnp.concatenate(
                [bias[:, at : at + slab], jnp.zeros((1, width - slab), f32)], axis=1
            )
            ref[k, first : first + slab, :] = down[at : at + slab, :].astype(bf16)
            ref[k, first + slab :, :] = jnp.broadcast_to(row, (8, width)).astype(bf16)

    @pl.when(half == 0)
    def _():
        put(near_ref)

    @pl.when(half == 1)
    def _():
        put(far_ref)


def mlp_weight_grads(plan, idx, low, grad_pre, act, dm_all, w_down):
    rows, width = low.shape
    hidden = act.shape[1]
    step = hidden // 2
    lines = plan.copies // 2
    block = width // plan.devices
    slab = hidden // plan.copies
    bundle = (lines, TP * block + slab + 8, width)
    token = (rows // TP, width)
    return pl.pallas_call(
        functools.partial(pair_kernel, plan),
        grid_spec=pltpu.PrefetchScalarGridSpec(
            num_scalar_prefetch=1,
            grid=(2,),
            in_specs=[
                whole((rows, width)),
                pl.BlockSpec((rows, step), lambda i, idx: (0, i)),
                pl.BlockSpec((rows, step), lambda i, idx: (0, i)),
                whole((rows, width)),
                pl.BlockSpec((step, width), lambda i, idx: (i, 0)),
            ],
            out_specs=[whole(bundle)] * 2 + [whole(token)] * TP,
            scratch_shapes=[
                pltpu.VMEM((TP, *token), f32),
                pltpu.VMEM((width, hidden), f32),
            ],
        ),
        out_shape=[jax.ShapeDtypeStruct(bundle, bf16)] * 2
        + [jax.ShapeDtypeStruct(token, bf16)] * TP,
        compiler_params=params(),
        cost_estimate=takes(7.6),
        name="mlp_weight_grads",
    )(idx, low, grad_pre, act, dm_all, w_down)


def add_kernel(count, *refs):
    total = refs[0][...].astype(f32)
    for ref in refs[1:count]:
        total += ref[...].astype(f32)
    refs[-1][...] = total.astype(bf16)


def add(*values, after=()):
    return pl.pallas_call(
        functools.partial(add_kernel, len(values)),
        in_specs=[pl.BlockSpec(memory_space=pltpu.VMEM)] * len(values)
        + [pl.BlockSpec(memory_space=pl.ANY)] * len(after),
        out_shape=jax.ShapeDtypeStruct(values[0].shape, bf16),
        compiler_params=pltpu.CompilerParams(vmem_limit_bytes=60 * 1024 * 1024),
        cost_estimate=takes(2.6),
        name="add",
    )(*values, *after)


def rows_kernel(plan, idx_ref, *refs):
    term_ref, up_refs = refs[0], refs[1 : 1 + TP]
    down_ref, row_ref, total_ref = refs[1 + TP :]
    member = idx_ref[0]
    total = term_ref[0].astype(f32)
    for z in range(1, term_ref.shape[0]):
        total += term_ref[z].astype(f32)
    block = up_refs[0].shape[0]
    first, slab = TP * block, down_ref.shape[0]
    total_ref[...] = total[:first].reshape(total_ref.shape)
    for j in range(TP):
        up_refs[j][...] = total_ref[member ^ j].astype(bf16)
    down_ref[...] = total[first : first + slab]
    row_ref[...] = total[first + slab : first + slab + 1, :slab]


def sum_rows(plan, idx, terms, block, slab):
    lines, rows, width = terms.shape
    return pl.pallas_call(
        functools.partial(rows_kernel, plan),
        in_specs=[pl.BlockSpec(memory_space=pltpu.SMEM), pl.BlockSpec(memory_space=pltpu.VMEM)],
        out_shape=[jax.ShapeDtypeStruct((block, width), bf16)] * TP
        + [jax.ShapeDtypeStruct((slab, width), f32), jax.ShapeDtypeStruct((1, slab), f32)],
        scratch_shapes=[pltpu.VMEM((TP, block, width), f32)],
        cost_estimate=takes(2.2),
        name="sum_rows",
    )(idx, terms)


def up_kernel(plan, idx_ref, *refs):
    part_refs, out_ref, hold_ref = refs[:TP], refs[TP], refs[TP + 1]
    member = idx_ref[0]
    for j in range(TP):
        hold_ref[member ^ j] = part_refs[j][...].astype(f32)
    slab = out_ref.shape[1] // plan.devices
    for r in range(plan.devices):
        t, copy = plan.place(r)
        out_ref[:, r * slab : (r + 1) * slab] = hold_ref[t, :, copy * slab : (copy + 1) * slab]


def join_up(plan, idx, parts, hidden):
    block, width = parts[0].shape
    return pl.pallas_call(
        functools.partial(up_kernel, plan),
        in_specs=[pl.BlockSpec(memory_space=pltpu.SMEM)]
        + [pl.BlockSpec(memory_space=pltpu.VMEM)] * TP,
        out_shape=jax.ShapeDtypeStruct((block, hidden), f32),
        scratch_shapes=[pltpu.VMEM((TP, block, width), f32)],
        cost_estimate=takes(1.7),
        name="join_up",
    )(idx, *parts)


def resid_kernel(r_ref, dm_ref, vec_ref, *refs):
    part_refs, (dr_ref, da_ref, sum_ref) = refs[:TP], refs[TP:]
    total = part_refs[0][...].astype(f32)
    for j in range(1, TP):
        total += part_refs[j][...].astype(f32)
    units, rstd = unit(r_ref[...])
    dm = dm_ref[...].astype(f32)
    dr = dm + unit_back(total * vec_ref[5:6, :], units, rstd)
    da = dr.astype(bf16)
    dr_ref[...] = dr
    da_ref[...] = da
    sum_ref[...] = jnp.zeros_like(sum_ref)
    sum_ref[0:1, :] = jnp.sum(da.astype(f32), axis=0, keepdims=True)
    sum_ref[1:2, :] = jnp.sum(dm, axis=0, keepdims=True)


def resid_back(parts, r_own, dm, vecs):
    rows, width = dm.shape
    return pl.pallas_call(
        resid_kernel,
        out_shape=[
            jax.ShapeDtypeStruct((rows, width), f32),
            jax.ShapeDtypeStruct((rows, width), bf16),
            jax.ShapeDtypeStruct((8, width), f32),
        ],
        cost_estimate=takes(2.7),
        name="resid_back",
    )(r_own, dm, vecs, *parts)


def output_kernel(r_ref, vec_ref, *refs):
    total = r_ref[...] + vec_ref[7:8, :]
    for ref in refs[:TP]:
        total += ref[...].astype(f32)
    refs[TP][...] = total.astype(bf16)


def finish_output(parts, r_own, vecs):
    return pl.pallas_call(
        output_kernel,
        out_shape=jax.ShapeDtypeStruct(r_own.shape, bf16),
        cost_estimate=takes(2.1),
        name="finish_output",
    )(r_own, vecs, *parts)


def input_kernel(x_ref, dr_ref, vec_ref, *refs):
    total = refs[0][...].astype(f32)
    for ref in refs[1:TP]:
        total += ref[...].astype(f32)
    units, rstd = unit(x_ref[...].astype(f32))
    grad = dr_ref[...] + unit_back(total * vec_ref[3:4, :], units, rstd)
    refs[TP][...] = grad.astype(bf16)


def finish_input(parts, x, dr, vecs):
    return pl.pallas_call(
        input_kernel,
        out_shape=jax.ShapeDtypeStruct(x.shape, bf16),
        cost_estimate=takes(2.4),
        name="finish_input",
    )(x, dr, vecs, *parts)


def normed_kernel(plan, n_recv, idx_ref, x_ref, dq_ref, own_ref, *refs):
    recv_refs, refs = refs[:n_recv], refs[n_recv:]
    w_ref, h_ref, o_ref, da_ref, own_sum_ref, two_ref = refs[:6]
    dh_refs, refs = refs[6 : 6 + TP], refs[6 + TP :]
    g_refs, (dh_now, low_ref, sum_ref, acc_ref, vec_ref) = refs[:-5], refs[-5:]
    step = pl.program_id(0)
    member, core = idx_ref[0], idx_ref[2]
    side = lax.rem(member, 2)
    cols = dq_ref.shape[1]
    rows, width = x_ref.shape

    @pl.when(step == 0)
    def _():
        sum_ref[...] = jnp.zeros_like(sum_ref)

    grad_k, grad_v = own_ref[0], own_ref[1]
    for ref in recv_refs:
        grad_k += ref[0].astype(f32)
        grad_v += ref[1].astype(f32)
    place = step ^ (member // 2)
    low_ref[place, :, :cols] = dq_ref[...]
    low_ref[place, :, cols : 2 * cols] = grad_k.astype(bf16)
    low_ref[place, :, 2 * cols : 3 * cols] = grad_v.astype(bf16)
    low_ref[place, :, 3 * cols :] = jnp.zeros((rows, SMALLS), bf16)
    low = low_ref[place]
    grad = dot(low, w_ref[...], 1, 1)
    dh_now[...] = grad.astype(bf16).reshape(dh_now.shape)
    for i in range(2):

        @pl.when(step == i)
        def _(i=i):
            for b in range(2):
                dh_refs[2 * i + b][...] = dh_now[side ^ b]

    units, _ = unit(x_ref[...].astype(f32))
    sum_ref[0:1, :width] += jnp.sum(grad * units, axis=0, keepdims=True)
    sum_ref[1:2, :width] += jnp.sum(grad, axis=0, keepdims=True)
    sum_ref[2:3, : low.shape[1]] += jnp.sum(low.astype(f32), axis=0, keepdims=True)

    @pl.when(step == 1)
    def _():
        wide = low_ref.shape[2]
        acc_ref[:, :wide] = dot(h_ref[...], low_ref[...].reshape(2 * rows, wide), 0, 0)
        da = da_ref[...].reshape(2 * rows, cols)
        for j in range(TP):
            at = j * cols
            acc_ref[at : at + cols, wide : wide + cols] = dot(o_ref[j], da, 0, 0)
        bias_q, bias_v = sum_ref[2:3, :cols], sum_ref[2:3, 2 * cols : 3 * cols]
        zero = jnp.zeros_like(bias_q)
        vec_ref[...] = jnp.zeros_like(vec_ref)
        vectors = [
            jnp.concatenate([jnp.where(member == j, b, zero) for j in range(TP)], axis=1)
            for b in (bias_q, bias_v)
        ]
        vectors += [
            own_sum_ref[0:1, :],
            sum_ref[0:1, :],
            sum_ref[1:2, :],
            two_ref[0:1, :],
            two_ref[1:2, :],
            own_sum_ref[1:2, :],
        ]
        for j, row in enumerate(vectors):
            vec_ref[SMALLS + j : SMALLS + j + 1, :] = row
        acc_ref[:, wide + cols :] = vec_ref[...].T[:, SMALLS:]
        if not plan.fast:
            g_refs[0][...] = acc_ref[...].astype(bf16)
            return
        near, block, _ = g_refs[0].shape
        span = near // plan.size["gx"]
        for ref, owner in ((g_refs[0], core), (g_refs[1], 1 - core)):
            for n in range(near):
                gx, rest = divmod(n, span)
                at = ((gx * 2 + owner) * span + rest) * block
                ref[n] = acc_ref[pl.ds(pl.multiple_of(at, 8), block), :].astype(bf16)


def normed_back(plan, idx, x_all, dq, own, recvs, w_qkv, low, o_all, da_cols, sum_own, sum_two):
    rows, width = x_all.shape
    cols = dq.shape[1]
    wide = w_qkv.shape[1]
    total = wide + cols + SMALLS
    step = rows // 2
    one = (rows // TP, width)
    near = plan.devices // 2

    def block(i, idx):
        return (i ^ (idx[0] // 2), 0)

    pairs = pl.BlockSpec((2, step, cols), lambda i, idx: (0, i ^ (idx[0] // 2), 0))
    if plan.fast:
        sums = [(near, width // plan.devices, total)] * 2
    else:
        sums = [(width, total)]
    constants = (w_qkv, low, o_all, da_cols, sum_own, sum_two)
    return pl.pallas_call(
        functools.partial(normed_kernel, plan, len(recvs)),
        grid_spec=pltpu.PrefetchScalarGridSpec(
            num_scalar_prefetch=1,
            grid=(2,),
            in_specs=[pl.BlockSpec((step, width), block), pl.BlockSpec((step, cols), block), pairs]
            + [pairs] * len(recvs)
            + [whole(v.shape) for v in constants],
            out_specs=[whole(one)] * TP + [whole(shape) for shape in sums],
            scratch_shapes=[
                pltpu.VMEM((2, *one), bf16),
                pltpu.VMEM((2, step, wide), bf16),
                pltpu.VMEM((8, width), f32),
                pltpu.VMEM((width, total), f32),
                pltpu.VMEM((2 * SMALLS, width), f32),
            ],
        ),
        out_shape=[jax.ShapeDtypeStruct(one, bf16)] * TP
        + [jax.ShapeDtypeStruct(shape, bf16) for shape in sums],
        compiler_params=params(),
        cost_estimate=takes(NORMED),
        name="normed_back",
    )(idx, x_all, dq, own, *recvs, *constants)


def join_kernel(keep, cols, wide, in_ref, first_ref, second_ref, *refs):
    mats, vec_refs = refs[:4], refs[4:12]
    output_ref, input_ref, turn_ref = refs[12:]
    output_ref[...] = first_ref[...]
    input_ref[...] = second_ref[...]
    groups = {}
    for n in range(in_ref.shape[0]):
        value = in_ref[n].astype(f32)
        key = keep[n]
        groups[key] = value if key not in groups else groups[key] + value
    for j in range(TP):
        for ref, at in zip(mats, (0, cols, 2 * cols, wide)):
            ref[:, j * cols : (j + 1) * cols] = groups[j][:, at : at + cols]
    total = functools.reduce(jnp.add, [groups[j] for j in range(TP)])
    block = in_ref.shape[1]
    turn_ref[...] = jnp.zeros_like(turn_ref)
    turn_ref[:block, :SMALLS] = total[:, wide + cols :]
    turned = turn_ref[...].T
    for j, ref in enumerate(vec_refs):
        ref[...] = turned[j : j + 1, :block]


def join_grads(plan, got, first, second, cols, wide):
    near, block, _ = got.shape
    members = [plan.place(plan.same(n))[0] for n in range(near)]
    width = cols * TP
    return pl.pallas_call(
        functools.partial(join_kernel, members, cols, wide),
        out_shape=[jax.ShapeDtypeStruct((block, width), f32)] * 4
        + [jax.ShapeDtypeStruct((1, block), f32)] * 8
        + [jax.ShapeDtypeStruct(first.shape, bf16)] * 2,
        scratch_shapes=[pltpu.VMEM((128, 128), f32)],
        compiler_params=pltpu.CompilerParams(vmem_limit_bytes=60 * 1024 * 1024),
        cost_estimate=takes(2.2),
        name="join_grads",
    )(got, first, second)


def local(
    plan, inputs, segment_ids, padding, cotangent, w_query, b_query, w_key, w_value, b_value,
    w_out, b_out, ln1_gain, ln1_shift, ln2_gain, ln2_shift, w_up, b_up, w_down, b_down,
):
    x_own = inputs[0]
    rows, width = x_own.shape
    cols = width // TP
    length = segment_ids.shape[1]
    block = w_query.shape[0]
    hidden = w_up.shape[1]
    slab = b_up.shape[0]
    size = plan.size
    member = lax.axis_index(plan.tp)
    part = lax.axis_index(plan.half)
    core = lax.axis_index("c")
    idx = jnp.stack([member, part, core, lax.axis_index("sz")]).astype(jnp.int32)
    lines = plan.copies // 2
    fast = plan.fast

    id_rows = jnp.pad(segment_ids[0].astype(bf16), (0, 8 * width - length)).reshape(8, width)
    packed = jnp.concatenate([x_own, id_rows], axis=0)
    dm_own = (cotangent[0].astype(f32) * padding[0].astype(f32)[:, None]).astype(bf16)
    dm_mine = plan.move(dm_own, plan.route)

    small = [b_query, b_value, b_out, ln1_gain, ln1_shift, ln2_gain, ln2_shift, b_down]
    if fast:
        chunk = prepare(plan, w_query, w_key, w_value, small, w_up, w_out)
        got = lax.all_to_all(chunk, plan.tp, 0, 0, tiled=True)
        moved = plan.move(packed, plan.route)
        got, moved = lax.optimization_barrier((got, moved))
        x_mine = moved[:rows]
        x_all = lax.all_gather(x_mine, plan.tp, axis=0, tiled=True)
        proj, shard = shards_of(got, w_down, b_up[None], 3 * cols + SMALLS, lines)
        projs = [proj] + [plan.turn(proj, "sz", -j) for j in range(1, lines)]
        projs, x_all, shard, dm_mine = lax.optimization_barrier((projs, x_all, shard, dm_mine))
        shard = lax.all_to_all(shard, "sz", 0, 0, tiled=True)
        projs = jnp.stack(projs)
        low_one, query, kv, w_qkv, vecs = qkv(plan, idx, x_all, projs, plan.swap(projs))
    else:
        small = jnp.stack(small, axis=1)
        moved = plan.move(packed, plan.route)
        x_mine = moved[:rows]
        x_all = lax.all_gather(x_mine, plan.tp, axis=0, tiled=True)
        b_row = jnp.pad(b_up[None], ((0, 7), (0, width - slab)))
        table = [w_query, w_key, w_value, w_out, small]
        table = lax.all_gather(jnp.concatenate(table, axis=1), ALL, axis=0, tiled=True)
        vecs = table[:, 4 * width :].T.astype(f32)
        split = [lax.dynamic_slice(table, (0, i * width + member * cols), (width, cols)) for i in range(3)]
        w_qkv = jnp.concatenate([*split, jnp.zeros((width, SMALLS), bf16)], axis=1)
        out_full = table[:, 3 * width : 4 * width].reshape(TP, cols, width)
        low_one, query, kv = qkv(plan, idx, x_all, w_qkv, vecs)
        up_mine = lax.all_gather(w_up, ALL, axis=0, tiled=True)
        up_mine = up_mine.reshape(width, plan.devices, slab).transpose(1, 0, 2)
        up_mine = plan.shuffle(up_mine, ALL, plan.tp + plan.rep).reshape(TP, plan.copies, width, slab)
        up_mine = lax.dynamic_index_in_dim(up_mine, member, 0, keepdims=False)
        up_mine = up_mine.transpose(1, 0, 2).reshape(width, -1)
        downs = jnp.concatenate([w_down, b_row], axis=0)
        downs = lax.all_gather(downs, plan.rep, axis=0, tiled=False)
        down_mine = downs[:, :slab].reshape(-1, width)
        b_up_mine = downs[:, slab, :slab].reshape(1, -1).astype(f32)

    ids = moved[rows:].reshape(1, -1)[:, :length].astype(f32)

    parts = plan.parts
    kvs = [kv] + [plan.turn(kv, plan.half, -j) for j in range(1, parts)]
    mixed, lse = attend(idx, ids, query, kvs)
    o_all = lax.all_gather(mixed, plan.tp, axis=0, tiled=False)
    dms = plan.partners(dm_mine)
    if fast:
        shard, o_all, dms = lax.optimization_barrier((shard, o_all, dms))
        weights = [shard, plan.swap(shard)]
    else:
        weights = [out_full, up_mine, down_mine, b_up_mine]
    results = mlp(plan, idx, x_all, o_all, vecs, dms, weights, slab)
    r_own, low_two, act, grad_pre, dm_all, sum_two = results[:6]
    dh_two = results[6 : 6 + TP]
    if fast:
        out_mine, down_mine = results[6 + TP :]
    else:
        out_mine = lax.dynamic_index_in_dim(out_full, member, 0, keepdims=False)

    back_two = plan.reduce(dh_two)
    if fast:
        near_terms, far_terms, *out_terms = mlp_weight_grads(
            plan, idx, low_two, grad_pre, act, dm_all, down_mine
        )
        back_two, out_terms, far_terms = lax.optimization_barrier((back_two, out_terms, far_terms))
    else:
        up_terms = dot(low_two, grad_pre, 0, 0).astype(bf16)
        down_terms = dot(act, dm_all, 0, 0).astype(bf16)
        row = jnp.sum(grad_pre.astype(f32), axis=0).astype(bf16)
        out_terms = dot(act, down_mine).astype(bf16).reshape(TP, rows, width)
        out_terms = [
            lax.dynamic_index_in_dim(out_terms, member ^ j, 0, keepdims=False) for j in range(TP)
        ]
    dr, da, sum_own = resid_back(back_two, r_own, dm_mine, vecs)
    if fast:
        terms = add(near_terms, plan.swap(far_terms), after=(da,))
        das = plan.partners(da)
        after = [terms]
        terms = lax.all_to_all(terms, "sz", 0, 0, tiled=True)
        *ups, g_w_down, g_b_up = sum_rows(plan, idx, terms, block, slab)
    else:
        das = plan.partners(da)
        after = []
        row = jnp.pad(row.reshape(plan.copies, 1, slab), ((0, 0), (0, 7), (0, width - slab)))
        downs = jnp.concatenate([down_terms.reshape(plan.copies, slab, width), row], axis=1)
        downs = lax.psum_scatter(downs, plan.rep, scatter_dimension=0, tiled=False)
        g_w_down = downs[:slab].astype(f32)
        g_b_up = downs[slab, :slab].astype(f32)
        ups = plan.shuffle(up_terms.reshape(plan.devices, block, -1), ALL, plan.rep + plan.tp)
        ups = ups.reshape(plan.copies, TP * block, -1)
        ups = lax.psum_scatter(ups, plan.rep, scatter_dimension=0, tiled=False)
        ups = lax.all_to_all(ups.reshape(TP, block, -1), plan.tp, 0, 0, tiled=True).astype(f32)
    grad_query, kv_own, da_cols, *kv_others = attend_back(
        idx, ids, query, das, after, out_mine, lse, kvs
    )
    kv_others, out_parts = lax.optimization_barrier((kv_others, plan.reduce(out_terms)))
    recvs = [plan.turn(kv_others[j - 1], plan.half, j) for j in range(1, parts)]
    results = normed_back(
        plan, idx, x_all, grad_query, kv_own, recvs, w_qkv, low_one, o_all, da_cols, sum_own, sum_two
    )
    back_one, terms = plan.reduce(results[:TP]), results[TP:]
    output = plan.move(finish_output(out_parts, r_own, vecs), plan.back)
    if fast:
        keep, send = terms
        terms = add(keep, plan.swap(send))
        terms, ups, back_one = lax.optimization_barrier((terms, ups, back_one))
        got = lax.all_to_all(terms, SAME, 0, 0, tiled=True)
    else:
        terms = plan.shuffle(terms[0].reshape(plan.devices, block, -1), ALL, ("c",) + SAME)
        terms = terms.reshape(2, -1, *terms.shape[1:])
        keep, send = jnp.where(core == 0, terms, terms[::-1])
        got = lax.all_to_all(add(keep, plan.swap(send)), SAME, 0, 0, tiled=True)
    if fast:
        g_w_up = join_up(plan, idx, plan.reduce(ups), hidden)
        g_b_up = g_b_up[0]
    else:
        ups = ups.reshape(TP, block, plan.copies, slab).transpose(0, 2, 1, 3)
        ups = plan.shuffle(ups.reshape(plan.devices, block, slab), plan.tp + plan.rep, ALL)
        g_w_up = ups.transpose(1, 0, 2).reshape(block, hidden)
    grad_input = plan.move(finish_input(back_one, x_mine, dr, vecs), plan.back)
    joined = join_grads(plan, got, output, grad_input, cols, w_qkv.shape[1])
    g_query, g_key, g_value, g_out, *vec, output, grad_input = joined
    vec = [v[0] for v in vec]
    return (
        output[None],
        grad_input[None],
        g_query,
        vec[0],
        g_key,
        g_value,
        vec[1],
        g_out,
        vec[2],
        vec[3],
        vec[4],
        vec[5],
        vec[6],
        g_w_up,
        g_b_up,
        g_w_down,
        vec[7],
    )


def solution(mesh):
    groups, blocks = mesh.shape["grp"], mesh.shape["seq"]
    plan = Plan(groups, blocks)
    fine = Mesh(mesh.devices.reshape(plan.shape), ALL)
    grp, seq = ("gx", "c"), ("sz", "sy")
    matrix, vector = P(ALL, None), P(ALL)
    token = P(grp, seq, None)
    return jax.shard_map(
        functools.partial(local, plan),
        mesh=fine,
        in_specs=(
            token, P(grp, None), P(grp, seq), token,
            matrix, vector, matrix, matrix, vector, matrix, vector,
            vector, vector, vector, vector, matrix, vector, matrix, vector,
        ),
        out_specs=(
            token, token,
            matrix, vector, matrix, matrix, vector, matrix, vector,
            vector, vector, vector, vector, matrix, vector, matrix, vector,
        ),
        check_vma=False,
    )
```

```python
import functools

import jax
import jax.numpy as jnp
from jax import lax
from jax.experimental import pallas as pl
from jax.experimental.pallas import tpu as pltpu
from jax.sharding import Mesh, PartitionSpec as P

HEADS = 12
HEAD_DIM = 64
TP = 4
HEADS_TP = HEADS // TP
EPS = 1e-05
NEG = -1e30
SCALE = 0.125
ALL = ("gx", "c", "sz", "sy")
SAME = ("gx", "sz", "sy")
SMALLS = 64
NORMED = 13.0
f32 = jnp.float32
bf16 = jnp.bfloat16


class Plan:
    def __init__(self, groups, blocks):
        if (groups, blocks) == (4, 8):
            self.shape = (2, 2, 4, 2)
            self.tp, self.half, self.rep = ("gx", "sy"), "c", ("c", "sz")
            self.fast = True
        else:
            self.shape = (groups // 2, 2, blocks // TP, TP)
            self.tp, self.half, self.rep = ("sy",), "sz", ("gx", "c", "sz")
            self.fast = False
        self.size = dict(zip(ALL, self.shape))
        self.devices = groups * blocks
        self.parts = self.size[self.half]
        self.copies = self.devices // TP
        self.lines = tuple(a for a in self.rep if a != "c")
        self.route = []
        for src in range(self.devices):
            seq, block = divmod(src, blocks)
            part, member = divmod(block, TP)
            if self.tp == ("sy",):
                dst = src
            else:
                dst = (((member >> 1) * 2 + part) * 4 + seq) * 2 + (member & 1)
            self.route.append((src, dst))
        self.back = [(dst, src) for src, dst in self.route]

    def swap(self, value):
        return lax.ppermute(value, "c", [(0, 1), (1, 0)])

    def gather(self, value):
        return lax.all_to_all(
            jnp.broadcast_to(value, (TP, *value.shape)), self.tp, 0, 0, tiled=True
        )

    def partner(self, value, j):
        table = [(t, t ^ j) for t in range(TP)]
        return lax.ppermute(value, self.tp, table)

    def partners(self, value):
        return [value] + [self.partner(value, j) for j in range(1, TP)]

    def reduce(self, values):
        return [values[0]] + [self.partner(values[j], j) for j in range(1, TP)]

    def turn(self, value, axis, by):
        count = self.size[axis]
        return lax.ppermute(value, axis, [(i, (i + by) % count) for i in range(count)])

    def place(self, r):
        at, rest = {}, r
        for axis in reversed(ALL):
            rest, at[axis] = divmod(rest, self.size[axis])
        numbers = []
        for axes in (self.tp, self.rep):
            number = 0
            for axis in axes:
                number = number * self.size[axis] + at[axis]
            numbers.append(number)
        return tuple(numbers)

    def same(self, n):
        span = self.devices // 2 // self.size["gx"]
        gx, rest = divmod(n, span)
        return gx * 2 * span + rest

    def move(self, value, table):
        if all(a == b for a, b in table):
            return value
        return lax.ppermute(value, ALL, table)

    def shuffle(self, value, before, after):
        tail = value.shape[1:]
        dims = [self.size[a] for a in before]
        order = [before.index(a) for a in after]
        value = value.reshape(*dims, *tail)
        value = value.transpose(*order, *range(len(dims), len(dims) + len(tail)))
        return value.reshape(-1, *tail)


def dot(left, right, left_dim=1, right_dim=0):
    return lax.dot_general(
        left, right, (((left_dim,), (right_dim,)), ((), ())), preferred_element_type=f32
    )


def unit(values):
    center = values - jnp.mean(values, axis=-1, keepdims=True)
    variance = jnp.mean(center * center, axis=-1, keepdims=True)
    rstd = lax.rsqrt(variance + EPS)
    return center * rstd, rstd


def unit_back(grad_unit, units, rstd):
    first = jnp.mean(grad_unit, axis=-1, keepdims=True)
    second = jnp.mean(grad_unit * units, axis=-1, keepdims=True)
    return rstd * (grad_unit - first - units * second)


def params(limit=14 * 1024 * 1024, axes=1):
    return pltpu.CompilerParams(
        dimension_semantics=("arbitrary",) * axes, vmem_limit_bytes=limit
    )


def small_params():
    return pltpu.CompilerParams(vmem_limit_bytes=8 * 1024 * 1024)


def takes(microseconds):
    return pl.CostEstimate(
        flops=0, bytes_accessed=int(microseconds * 3.69e6), transcendentals=0
    )


def whole(shape):
    zeros = (0,) * len(shape)
    return pl.BlockSpec(shape, lambda *_: zeros)


def here(shape):
    return pl.BlockSpec(memory_space=pltpu.VMEM)


def head_lanes(value, head):
    lane = lax.broadcasted_iota(jnp.int32, value.shape, 1)
    keep = (lane >= head * HEAD_DIM) & (lane < (head + 1) * HEAD_DIM)
    return jnp.where(keep, value, jnp.zeros_like(value))


def member_cols(row, member, cols):
    out = jnp.zeros((row.shape[0], cols), row.dtype)
    for j in range(TP):
        out = jnp.where(member == j, row[:, j * cols : (j + 1) * cols], out)
    return out


def prep_kernel(rep_of, q_ref, k_ref, v_ref, up_ref, out_ref, *refs):
    small_refs, chunk_ref, turn_ref = refs[:-2], refs[-2], refs[-1]
    block, width = q_ref.shape
    cols = width // TP
    wide = 3 * cols + SMALLS
    slab = up_ref.shape[1] // len(rep_of)
    turn_ref[...] = jnp.zeros_like(turn_ref)
    for j, ref in enumerate(small_refs):
        turn_ref[j : j + 1, :block] = ref[...].astype(f32)
    small = turn_ref[...].T[:block, :SMALLS]
    for j in range(TP):
        at = slice(j * cols, (j + 1) * cols)
        chunk_ref[j, :, :wide] = jnp.concatenate(
            [r[:, at].astype(f32) for r in (q_ref, k_ref, v_ref)] + [small], axis=1
        ).astype(bf16)
        chunk_ref[j, :, wide + width :] = out_ref[...]
    for r, (member, copy) in enumerate(rep_of):
        first = wide + copy * slab
        chunk_ref[member, :, first : first + slab] = up_ref[:, r * slab : (r + 1) * slab]


def prepare(plan, w_query, w_key, w_value, small, w_up, w_out):
    block, width = w_query.shape
    rep_of = [plan.place(r) for r in range(plan.devices)]
    wide = 3 * width // TP + SMALLS
    return pl.pallas_call(
        functools.partial(prep_kernel, rep_of),
        out_shape=jax.ShapeDtypeStruct((TP, block, wide + w_up.shape[1] // TP + width), bf16),
        scratch_shapes=[pltpu.VMEM((128, 128), f32)],
        cost_estimate=takes(1.9),
        name="prepare",
    )(w_query, w_key, w_value, w_up, w_out, *[v[None] for v in small])


def shards_kernel(wide, got_ref, down_ref, row_ref, proj_ref, shard_ref):
    block = got_ref.shape[1]
    slab, width = down_ref.shape
    first = TP * block
    for t in range(TP):
        at = t * block
        proj_ref[at : at + block, :] = got_ref[t, :, :wide]
        up = got_ref[t, :, wide : wide + width]
        out = got_ref[t, :, wide + width :]
        for n in range(shard_ref.shape[0]):
            shard_ref[n, at : at + block, :] = up
            shard_ref[n, first + at : first + at + block, :] = out
    row = jnp.concatenate([row_ref[...].astype(f32), jnp.zeros((1, width - slab), f32)], axis=1)
    row = jnp.broadcast_to(row, (8, width)).astype(bf16)
    for n in range(shard_ref.shape[0]):
        shard_ref[n, 2 * first : 2 * first + slab, :] = down_ref[...]
        shard_ref[n, 2 * first + slab :, :] = row


def shards_of(got, w_down, b_row, wide, lines):
    _, block, _ = got.shape
    slab, width = w_down.shape
    return pl.pallas_call(
        functools.partial(shards_kernel, wide),
        out_shape=[
            jax.ShapeDtypeStruct((TP * block, wide), bf16),
            jax.ShapeDtypeStruct((lines, 2 * TP * block + slab + 8, width), bf16),
        ],
        compiler_params=small_params(),
        cost_estimate=takes(2.4),
        name="shards_of",
    )(got, w_down, b_row)


def qkv_kernel(plan, idx_ref, x_ref, *refs):
    fast = plan.fast
    if fast:
        own_ref, other_ref, h_ref, q_ref, kv_ref, w_ref, vec_ref, wide_ref = refs
    else:
        w_ref, vec_ref, h_ref, q_ref, kv_ref = refs
    cols = q_ref.shape[1]
    if fast:

        @pl.when(pl.program_id(0) == 0)
        def _():
            core = idx_ref[2]
            line = idx_ref[3]
            lines, rows, _ = own_ref.shape
            pair = rows // plan.size["gx"]
            for ref, side in ((own_ref, core), (other_ref, 1 - core)):
                for j in range(lines):
                    z = lax.rem(line + j, lines)
                    value = ref[j].astype(f32)
                    for gx in range(plan.size["gx"]):
                        wide_ref[gx * 2 + side, z] = value[gx * pair : (gx + 1) * pair, :]
            table = wide_ref[...].reshape(w_ref.shape)
            w_ref[...] = table.astype(bf16)
            vec_ref[...] = table[:, 512:640].T[64:72, :]

    units, _ = unit(x_ref[...].astype(f32))
    low = (units * vec_ref[3:4, :] + vec_ref[4:5, :]).astype(bf16)
    h_ref[...] = low
    out = dot(low, w_ref[...])
    bias = member_cols(vec_ref[0:2, :], idx_ref[0], cols)
    query = (out[:, :cols] + bias[0:1, :]).astype(bf16)
    q_ref[...] = (query.astype(f32) * SCALE).astype(bf16)
    kv_ref[0] = out[:, cols : 2 * cols].astype(bf16)
    kv_ref[1] = (out[:, 2 * cols : 3 * cols] + bias[1:2, :]).astype(bf16)


def qkv(plan, idx, x_all, *operands):
    rows, width = x_all.shape
    cols = width // TP
    step = rows // 2
    wide = 3 * cols + SMALLS
    out_specs = [
        pl.BlockSpec((step, width), lambda i, *_: (i, 0)),
        pl.BlockSpec((step, cols), lambda i, *_: (i, 0)),
        pl.BlockSpec((2, step, cols), lambda i, *_: (0, i, 0)),
    ]
    out_shape = [
        jax.ShapeDtypeStruct((rows, width), bf16),
        jax.ShapeDtypeStruct((rows, cols), bf16),
        jax.ShapeDtypeStruct((2, rows, cols), bf16),
    ]
    scratch = []
    if plan.fast:
        out_specs += [here((width, wide)), here((8, width))]
        out_shape += [
            jax.ShapeDtypeStruct((width, wide), bf16),
            jax.ShapeDtypeStruct((8, width), f32),
        ]
        lines = plan.copies // 2
        scratch = [pltpu.VMEM((2 * plan.size["gx"], lines, width // (2 * plan.size["gx"] * lines), wide), f32)]
    return pl.pallas_call(
        functools.partial(qkv_kernel, plan),
        grid_spec=pltpu.PrefetchScalarGridSpec(
            num_scalar_prefetch=1,
            grid=(2,),
            in_specs=[pl.BlockSpec((step, width), lambda i, *_: (i, 0))]
            + [here(v.shape) for v in operands],
            out_specs=out_specs,
            scratch_shapes=scratch,
        ),
        out_shape=out_shape,
        compiler_params=params(),
        cost_estimate=takes(4.8),
        name="qkv",
    )(idx, x_all, *operands)


def fill_docs(ids_ref, part, parts, doc_ref):
    span, width = doc_ref.shape[1:]
    for j in range(parts):
        at = lax.rem(part + j, parts) * span
        row = ids_ref[0:1, pl.ds(pl.multiple_of(at, 512), span)]
        doc_ref[j] = jnp.broadcast_to(row, (width, span)).T


def fwd_kernel(parts, idx_ref, ids_ref, q_ref, *refs):
    kv_refs = refs[:parts]
    o_ref, lse_ref, turned, doc_ref = refs[parts:]
    step = pl.program_id(0)
    part = idx_ref[1]
    span = kv_refs[0].shape[1]
    width = q_ref.shape[0]

    @pl.when(step == 0)
    def _():
        fill_docs(ids_ref, part, parts, doc_ref)
        for j in range(parts):
            turned[j] = kv_refs[j][1].T

    at = part * span + step * width
    own = ids_ref[0:1, pl.ds(pl.multiple_of(at, 128), width)]
    query = q_ref[...]
    outs, lses = [], []
    for head in range(HEADS_TP):
        masked = head_lanes(query, head)
        scores = []
        for j in range(parts):
            raw = dot(kv_refs[j][0], masked, 1, 1)
            scores.append(jnp.where(doc_ref[j] == own, raw, NEG))
        peak = functools.reduce(
            jnp.maximum, [jnp.max(s, axis=0, keepdims=True) for s in scores]
        )
        exps = [jnp.exp(s - peak) for s in scores]
        total = functools.reduce(jnp.add, [jnp.sum(e, axis=0, keepdims=True) for e in exps])
        scale = 1.0 / total
        acc = None
        for j in range(parts):
            probs = (exps[j] * scale).astype(bf16)
            term = dot(turned[j, head * HEAD_DIM : (head + 1) * HEAD_DIM, :], probs)
            acc = term if acc is None else acc + term
        outs.append(acc)
        lses.append(peak + jnp.log(total))
    o_ref[...] = jnp.concatenate(outs, axis=0).T.astype(bf16)
    for head in range(HEADS_TP):
        lse_ref[head : head + 1, :] = lses[head]


def attend(idx, ids, q, kvs, width=256):
    rows, cols = q.shape
    parts = len(kvs)
    span = kvs[0].shape[1]
    return pl.pallas_call(
        functools.partial(fwd_kernel, parts),
        grid_spec=pltpu.PrefetchScalarGridSpec(
            num_scalar_prefetch=1,
            grid=(rows // width,),
            in_specs=[here(ids.shape), pl.BlockSpec((width, cols), lambda i, *_: (i, 0))]
            + [here(kv.shape) for kv in kvs],
            out_specs=[
                pl.BlockSpec((width, cols), lambda i, *_: (i, 0)),
                pl.BlockSpec((8, width), lambda i, *_: (0, i)),
            ],
            scratch_shapes=[
                pltpu.VMEM((parts, cols, span), bf16),
                pltpu.VMEM((parts, span, width), f32),
            ],
        ),
        out_shape=[
            jax.ShapeDtypeStruct((rows, cols), bf16),
            jax.ShapeDtypeStruct((8, rows), f32),
        ],
        compiler_params=params(),
        cost_estimate=takes(7.1),
        name="attend",
    )(idx, ids, q, *kvs)


def bwd_kernel(parts, waits, idx_ref, ids_ref, q_ref, w_ref, lse_ref, *refs):
    da_refs, refs = refs[:TP], refs[TP + waits :]
    kv_refs = refs[:parts]
    dq_ref, own_ref, cols_ref = refs[parts : parts + 3]
    other_refs = refs[parts + 3 : 2 * parts + 2]
    turned, doc_ref, key_acc, value_acc, mixed_ref = refs[2 * parts + 2 :]
    step = pl.program_id(0)
    part = idx_ref[1]
    span = kv_refs[0].shape[1]
    width, cols = q_ref.shape

    @pl.when(step == 0)
    def _():
        fill_docs(ids_ref, part, parts, doc_ref)
        for j in range(parts):
            turned[j] = kv_refs[j][0].T
        key_acc[...] = jnp.zeros_like(key_acc)
        value_acc[...] = jnp.zeros_like(value_acc)
        member = idx_ref[0]
        for j in range(TP):
            da = da_refs[j][...]
            mixed_ref[member ^ j] = dot(da, w_ref[...], 1, 1).astype(bf16)
            cols_ref[member ^ j] = member_cols(da, member, cols)

    at = part * span + step * width
    own = ids_ref[0:1, pl.ds(pl.multiple_of(at, 128), width)]
    query = q_ref[...]
    group = width // mixed_ref.shape[1]
    grad_mixed = mixed_ref[pl.ds(step * group, group)].reshape(width, cols)
    turned_grads = []
    for head in range(HEADS_TP):
        masked_q = head_lanes(query, head)
        masked_g = head_lanes(grad_mixed, head)
        lse = lse_ref[head : head + 1, :]
        probs, grads = [], []
        for j in range(parts):
            raw = dot(kv_refs[j][0], masked_q, 1, 1)
            probs.append(jnp.exp(jnp.where(doc_ref[j] == own, raw, NEG) - lse))
            grads.append(dot(kv_refs[j][1], masked_g, 1, 1))
        delta = functools.reduce(
            jnp.add,
            [jnp.sum(p * g, axis=0, keepdims=True) for p, g in zip(probs, grads)],
        )
        acc = None
        for j in range(parts):
            grad_scores = (probs[j] * (grads[j] - delta)).astype(bf16)
            value_acc[j] += dot(probs[j].astype(bf16), masked_g)
            key_acc[j] += dot(grad_scores, masked_q)
            term = dot(turned[j, head * HEAD_DIM : (head + 1) * HEAD_DIM, :], grad_scores)
            acc = term if acc is None else acc + term
        turned_grads.append(acc)
    dq_ref[...] = (jnp.concatenate(turned_grads, axis=0).T * SCALE).astype(bf16)

    @pl.when(step == pl.num_programs(0) - 1)
    def _():
        own_ref[0] = key_acc[0]
        own_ref[1] = value_acc[0]
        for j in range(1, parts):
            other_refs[j - 1][0] = key_acc[j].astype(bf16)
            other_refs[j - 1][1] = value_acc[j].astype(bf16)


def attend_back(idx, ids, q, das, after, w_out, lse, kvs, width=256):
    rows, cols = q.shape
    step, model = das[0].shape
    parts = len(kvs)
    span = kvs[0].shape[1]
    return pl.pallas_call(
        functools.partial(bwd_kernel, parts, len(after)),
        grid_spec=pltpu.PrefetchScalarGridSpec(
            num_scalar_prefetch=1,
            grid=(rows // width,),
            in_specs=[
                whole(ids.shape),
                pl.BlockSpec((width, cols), lambda i, *_: (i, 0)),
                whole((cols, model)),
                pl.BlockSpec((8, width), lambda i, *_: (0, i)),
            ]
            + [here((step, model))] * TP
            + [pl.BlockSpec(memory_space=pl.ANY)] * len(after)
            + [whole(kv.shape) for kv in kvs],
            out_specs=[
                pl.BlockSpec((width, cols), lambda i, *_: (i, 0)),
                here((2, span, cols)),
                here((TP, step, cols)),
            ]
            + [here((2, span, cols))] * (parts - 1),
            scratch_shapes=[
                pltpu.VMEM((parts, cols, span), bf16),
                pltpu.VMEM((parts, span, width), f32),
                pltpu.VMEM((parts, span, cols), f32),
                pltpu.VMEM((parts, span, cols), f32),
                pltpu.VMEM((TP, step, cols), bf16),
            ],
        ),
        out_shape=[
            jax.ShapeDtypeStruct((rows, cols), bf16),
            jax.ShapeDtypeStruct((2, span, cols), f32),
            jax.ShapeDtypeStruct((TP, step, cols), bf16),
        ]
        + [jax.ShapeDtypeStruct((2, span, cols), bf16)] * (parts - 1),
        compiler_params=params(),
        cost_estimate=takes(10.7),
        name="attend_back",
    )(idx, ids, q, w_out, lse, *das, *after, *kvs)


def mlp_kernel(plan, idx_ref, x_ref, o_ref, vec_ref, *refs):
    dm_refs, refs = refs[:TP], refs[TP:]
    step = pl.program_id(0)
    side = lax.rem(idx_ref[0], 2)
    if plan.fast:
        own_ref, other_ref, r_ref, h_ref, a_ref, du_ref, dm_ref, sum_ref = refs[:8]
        dh_refs = refs[8 : 8 + TP]
        out_ref, down_ref, dm_now, r_now, dh_now, held, held_down, held_row = refs[8 + TP :]

        @pl.when(step == 0)
        def _():
            core = idx_ref[2]
            first = held.shape[3] * plan.size["gx"]
            pair = held.shape[3]
            slab = held_down.shape[2]
            rows = []
            for z in range(held.shape[2]):
                for ref, owner in ((own_ref, core), (other_ref, 1 - core)):
                    for gx in range(plan.size["gx"]):
                        at = gx * pair
                        held[0, gx * 2 + owner, z] = ref[z, at : at + pair, :]
                        held[1, gx * 2 + owner, z] = ref[z, first + at : first + at + pair, :]
                    held_down[owner, z] = ref[z, 2 * first : 2 * first + slab, :]
            for owner in range(2):
                for z in range(held.shape[2]):
                    at = 2 * first + slab
                    row = jnp.where(
                        core == owner,
                        own_ref[z, at : at + 8, :].astype(f32),
                        other_ref[z, at : at + 8, :].astype(f32),
                    )
                    rows.append(row[0:1, :slab])
            held_row[...] = jnp.concatenate(rows, axis=1)
            out = held[1, idx_ref[0]]
            out_ref[...] = out.reshape(out_ref.shape)
            down_ref[...] = held_down[...].reshape(down_ref.shape)

        width = held.shape[-1]
        w_up = held[0].reshape(-1, width)
        outs = [held[1, j].reshape(-1, width) for j in range(TP)]
        w_down = held_down[...].reshape(-1, width)
        b_up = held_row[...]
    else:
        wo_ref, wu_ref, wd_ref, bup_ref, r_ref, h_ref, a_ref, du_ref, dm_ref, sum_ref = refs[:10]
        dh_refs, dm_now, r_now, dh_now = refs[10 : 10 + TP], refs[-3], refs[-2], refs[-1]
        w_up, w_down, b_up = wu_ref[...], wd_ref[...], bup_ref[...]
        outs = [wo_ref[j] for j in range(TP)]

    @pl.when(step == 0)
    def _():
        sum_ref[...] = jnp.zeros_like(sum_ref)

    attended = dot(o_ref[0], outs[0])
    for j in range(1, TP):
        attended += dot(o_ref[j], outs[j])
    residual = x_ref[...].astype(f32) + (attended + vec_ref[2:3, :])

    for i in range(2):

        @pl.when(step == i)
        def _(i=i):
            for b in range(2):
                dm_now[side ^ b] = dm_refs[2 * i + b][...]
            if i == 0:
                r_now[...] = residual.reshape(r_now.shape)
                r_ref[...] = r_now[side]

    units, _ = unit(residual)
    low = (units * vec_ref[5:6, :] + vec_ref[6:7, :]).astype(bf16)
    h_ref[...] = low
    pre = dot(low, w_up) + b_up
    normal = 0.5 * (1.0 + lax.erf(pre * 0.7071067811865476))
    act = (pre * normal).astype(bf16)
    a_ref[...] = act
    slope = normal + pre * (0.3989422804014327 * jnp.exp(-0.5 * pre * pre))
    dm = dm_now[...].reshape(x_ref.shape)
    dm_ref[...] = dm
    grad_pre = (dot(dm, w_down, 1, 1) * slope).astype(bf16)
    du_ref[...] = grad_pre
    grad = dot(grad_pre, w_up, 1, 1)
    sum_ref[0:1, :] += jnp.sum(grad * units, axis=0, keepdims=True)
    sum_ref[1:2, :] += jnp.sum(grad, axis=0, keepdims=True)
    dh_now[...] = grad.astype(bf16).reshape(dh_now.shape)
    for i in range(2):

        @pl.when(step == i)
        def _(i=i):
            for b in range(2):
                dh_refs[2 * i + b][...] = dh_now[side ^ b]


def mlp(plan, idx, x_all, o_all, vecs, dms, weights, slab):
    rows, width = x_all.shape
    hidden = plan.copies * slab
    cols = width // TP
    step = rows // 2

    def block(i, idx):
        return (i ^ (idx[0] // 2), 0)

    token = pl.BlockSpec((step, width), block)
    inner = pl.BlockSpec((step, hidden), block)
    one = here((rows // TP, width))
    now = (2, rows // TP, width)
    out_specs = [one, token, inner, inner, token, here((8, width))] + [one] * TP
    out_shape = [
        jax.ShapeDtypeStruct((rows // TP, width), f32),
        jax.ShapeDtypeStruct((rows, width), bf16),
        jax.ShapeDtypeStruct((rows, hidden), bf16),
        jax.ShapeDtypeStruct((rows, hidden), bf16),
        jax.ShapeDtypeStruct((rows, width), bf16),
        jax.ShapeDtypeStruct((8, width), f32),
    ] + [jax.ShapeDtypeStruct((rows // TP, width), bf16)] * TP
    scratch = [pltpu.VMEM(now, bf16), pltpu.VMEM(now, f32), pltpu.VMEM(now, bf16)]
    if plan.fast:
        lines = plan.copies // 2
        gx = plan.size["gx"]
        out_specs += [here((cols, width)), here((hidden, width))]
        out_shape += [
            jax.ShapeDtypeStruct((cols, width), bf16),
            jax.ShapeDtypeStruct((hidden, width), bf16),
        ]
        scratch += [
            pltpu.VMEM((2, 2 * gx, lines, width // (2 * gx * lines), width), bf16),
            pltpu.VMEM((2, lines, slab, width), bf16),
            pltpu.VMEM((1, hidden), f32),
        ]
    return pl.pallas_call(
        functools.partial(mlp_kernel, plan),
        grid_spec=pltpu.PrefetchScalarGridSpec(
            num_scalar_prefetch=1,
            grid=(2,),
            in_specs=[
                token,
                pl.BlockSpec((TP, step, cols), lambda i, idx: (0, i ^ (idx[0] // 2), 0)),
                here(vecs.shape),
            ]
            + [here(dms[0].shape)] * TP
            + [here(v.shape) for v in weights],
            out_specs=out_specs,
            scratch_shapes=scratch,
        ),
        out_shape=out_shape,
        compiler_params=params(),
        cost_estimate=takes(10.5),
        name="mlp",
    )(idx, x_all, o_all, vecs, *dms, *weights)


def pair_kernel(plan, idx_ref, h_ref, du_ref, a_ref, dm_ref, wd_ref, near_ref, far_ref, *refs):
    out_refs, acc_ref, wide_ref = refs[:TP], refs[TP], refs[TP + 1]
    lines = plan.copies // 2
    step = pl.program_id(0)
    member, core = idx_ref[0], idx_ref[2]
    half = step ^ core
    grad_pre = du_ref[...]
    act = a_ref[...]
    width = h_ref.shape[1]
    block = width // plan.devices
    size = act.shape[1]
    slab = size // lines
    first = TP * block
    up = dot(h_ref[...], grad_pre, 0, 0)
    down = dot(act, dm_ref[...], 0, 0)
    bias = jnp.sum(grad_pre.astype(f32), axis=0, keepdims=True)
    term = dot(act, wd_ref[...])

    @pl.when(step == 0)
    def _():
        acc_ref[...] = term.reshape(acc_ref.shape)
        wide_ref[:, :size] = up

    @pl.when(step == 1)
    def _():
        acc_ref[...] += term.reshape(acc_ref.shape)
        for j in range(TP):
            out_refs[j][...] = acc_ref[member ^ j].astype(bf16)
        wide_ref[:, size:] = up
        pair = plan.size["sy"] * block
        for ref, owner in ((near_ref, core), (far_ref, 1 - core)):
            for z in range(lines):
                for gx in range(plan.size["gx"]):
                    at = ((gx * 2 + owner) * lines + z) * pair
                    value = wide_ref[pl.ds(pl.multiple_of(at, 16), pair), :]
                    ref[z, gx * pair : (gx + 1) * pair, :] = value.astype(bf16)

    def put(ref):
        for k in range(lines):
            at = k * slab
            row = jnp.concatenate(
                [bias[:, at : at + slab], jnp.zeros((1, width - slab), f32)], axis=1
            )
            ref[k, first : first + slab, :] = down[at : at + slab, :].astype(bf16)
            ref[k, first + slab :, :] = jnp.broadcast_to(row, (8, width)).astype(bf16)

    @pl.when(half == 0)
    def _():
        put(near_ref)

    @pl.when(half == 1)
    def _():
        put(far_ref)


def mlp_weight_grads(plan, idx, low, grad_pre, act, dm_all, w_down):
    rows, width = low.shape
    hidden = act.shape[1]
    step = hidden // 2
    lines = plan.copies // 2
    block = width // plan.devices
    slab = hidden // plan.copies
    bundle = (lines, TP * block + slab + 8, width)
    token = (rows // TP, width)
    return pl.pallas_call(
        functools.partial(pair_kernel, plan),
        grid_spec=pltpu.PrefetchScalarGridSpec(
            num_scalar_prefetch=1,
            grid=(2,),
            in_specs=[
                here((rows, width)),
                pl.BlockSpec((rows, step), lambda i, idx: (0, i)),
                pl.BlockSpec((rows, step), lambda i, idx: (0, i)),
                here((rows, width)),
                pl.BlockSpec((step, width), lambda i, idx: (i, 0)),
            ],
            out_specs=[here(bundle)] * 2 + [here(token)] * TP,
            scratch_shapes=[
                pltpu.VMEM((TP, *token), f32),
                pltpu.VMEM((width, hidden), f32),
            ],
        ),
        out_shape=[jax.ShapeDtypeStruct(bundle, bf16)] * 2
        + [jax.ShapeDtypeStruct(token, bf16)] * TP,
        compiler_params=params(),
        cost_estimate=takes(7.6),
        name="mlp_weight_grads",
    )(idx, low, grad_pre, act, dm_all, w_down)


def add_kernel(count, *refs):
    total = refs[0][...].astype(f32)
    for ref in refs[1:count]:
        total += ref[...].astype(f32)
    refs[-1][...] = total.astype(bf16)


def add(*values, after=()):
    return pl.pallas_call(
        functools.partial(add_kernel, len(values)),
        in_specs=[pl.BlockSpec(memory_space=pltpu.VMEM)] * len(values)
        + [pl.BlockSpec(memory_space=pl.ANY)] * len(after),
        out_shape=jax.ShapeDtypeStruct(values[0].shape, bf16),
        compiler_params=small_params(),
        cost_estimate=takes(2.6),
        name="add",
    )(*values, *after)


def rows_kernel(plan, idx_ref, *refs):
    term_ref, up_refs = refs[0], refs[1 : 1 + TP]
    down_ref, row_ref, total_ref = refs[1 + TP :]
    member = idx_ref[0]
    total = term_ref[0].astype(f32)
    for z in range(1, term_ref.shape[0]):
        total += term_ref[z].astype(f32)
    block = up_refs[0].shape[0]
    first, slab = TP * block, down_ref.shape[0]
    total_ref[...] = total[:first].reshape(total_ref.shape)
    for j in range(TP):
        up_refs[j][...] = total_ref[member ^ j].astype(bf16)
    down_ref[...] = total[first : first + slab]
    row_ref[...] = total[first + slab : first + slab + 1, :slab]


def sum_rows(plan, idx, terms, block, slab):
    lines, rows, width = terms.shape
    return pl.pallas_call(
        functools.partial(rows_kernel, plan),
        in_specs=[pl.BlockSpec(memory_space=pltpu.SMEM), pl.BlockSpec(memory_space=pltpu.VMEM)],
        out_shape=[jax.ShapeDtypeStruct((block, width), bf16)] * TP
        + [jax.ShapeDtypeStruct((slab, width), f32), jax.ShapeDtypeStruct((1, slab), f32)],
        scratch_shapes=[pltpu.VMEM((TP, block, width), f32)],
        compiler_params=small_params(),
        cost_estimate=takes(2.2),
        name="sum_rows",
    )(idx, terms)


def up_kernel(plan, idx_ref, *refs):
    part_refs, out_ref, hold_ref = refs[:TP], refs[TP], refs[TP + 1]
    member = idx_ref[0]
    for j in range(TP):
        hold_ref[member ^ j] = part_refs[j][...].astype(f32)
    slab = out_ref.shape[1] // plan.devices
    for r in range(plan.devices):
        t, copy = plan.place(r)
        out_ref[:, r * slab : (r + 1) * slab] = hold_ref[t, :, copy * slab : (copy + 1) * slab]


def join_up(plan, idx, parts, hidden):
    block, width = parts[0].shape
    return pl.pallas_call(
        functools.partial(up_kernel, plan),
        in_specs=[pl.BlockSpec(memory_space=pltpu.SMEM)]
        + [pl.BlockSpec(memory_space=pltpu.VMEM)] * TP,
        out_shape=jax.ShapeDtypeStruct((block, hidden), f32),
        scratch_shapes=[pltpu.VMEM((TP, block, width), f32)],
        compiler_params=small_params(),
        cost_estimate=takes(1.7),
        name="join_up",
    )(idx, *parts)


def resid_kernel(r_ref, dm_ref, vec_ref, *refs):
    part_refs, (dr_ref, da_ref, sum_ref) = refs[:TP], refs[TP:]
    total = part_refs[0][...].astype(f32)
    for j in range(1, TP):
        total += part_refs[j][...].astype(f32)
    units, rstd = unit(r_ref[...])
    dm = dm_ref[...].astype(f32)
    dr = dm + unit_back(total * vec_ref[5:6, :], units, rstd)
    da = dr.astype(bf16)
    dr_ref[...] = dr
    da_ref[...] = da
    sum_ref[...] = jnp.zeros_like(sum_ref)
    sum_ref[0:1, :] = jnp.sum(da.astype(f32), axis=0, keepdims=True)
    sum_ref[1:2, :] = jnp.sum(dm, axis=0, keepdims=True)


def resid_back(parts, r_own, dm, vecs):
    rows, width = dm.shape
    return pl.pallas_call(
        resid_kernel,
        out_shape=[
            jax.ShapeDtypeStruct((rows, width), f32),
            jax.ShapeDtypeStruct((rows, width), bf16),
            jax.ShapeDtypeStruct((8, width), f32),
        ],
        compiler_params=small_params(),
        cost_estimate=takes(2.7),
        name="resid_back",
    )(r_own, dm, vecs, *parts)


def output_kernel(r_ref, vec_ref, *refs):
    total = r_ref[...] + vec_ref[7:8, :]
    for ref in refs[:TP]:
        total += ref[...].astype(f32)
    refs[TP][...] = total.astype(bf16)


def finish_output(parts, r_own, vecs):
    return pl.pallas_call(
        output_kernel,
        out_shape=jax.ShapeDtypeStruct(r_own.shape, bf16),
        cost_estimate=takes(2.1),
        name="finish_output",
    )(r_own, vecs, *parts)


def input_kernel(x_ref, dr_ref, vec_ref, *refs):
    total = refs[0][...].astype(f32)
    for ref in refs[1:TP]:
        total += ref[...].astype(f32)
    units, rstd = unit(x_ref[...].astype(f32))
    grad = dr_ref[...] + unit_back(total * vec_ref[3:4, :], units, rstd)
    refs[TP][...] = grad.astype(bf16)


def finish_input(parts, x, dr, vecs):
    return pl.pallas_call(
        input_kernel,
        out_shape=jax.ShapeDtypeStruct(x.shape, bf16),
        compiler_params=small_params(),
        cost_estimate=takes(2.4),
        name="finish_input",
    )(x, dr, vecs, *parts)


def normed_kernel(plan, n_recv, idx_ref, x_ref, dq_ref, own_ref, *refs):
    recv_refs, refs = refs[:n_recv], refs[n_recv:]
    w_ref, h_ref, o_ref, da_ref, own_sum_ref, two_ref = refs[:6]
    dh_refs, refs = refs[6 : 6 + TP], refs[6 + TP :]
    g_refs, (dh_now, low_ref, sum_ref, acc_ref, vec_ref) = refs[:-5], refs[-5:]
    step = pl.program_id(0)
    member, core = idx_ref[0], idx_ref[2]
    side = lax.rem(member, 2)
    cols = dq_ref.shape[1]
    rows, width = x_ref.shape

    @pl.when(step == 0)
    def _():
        sum_ref[...] = jnp.zeros_like(sum_ref)

    grad_k, grad_v = own_ref[0], own_ref[1]
    for ref in recv_refs:
        grad_k += ref[0].astype(f32)
        grad_v += ref[1].astype(f32)
    place = step ^ (member // 2)
    low_ref[place, :, :cols] = dq_ref[...]
    low_ref[place, :, cols : 2 * cols] = grad_k.astype(bf16)
    low_ref[place, :, 2 * cols : 3 * cols] = grad_v.astype(bf16)
    low_ref[place, :, 3 * cols :] = jnp.zeros((rows, SMALLS), bf16)
    low = low_ref[place]
    grad = dot(low, w_ref[...], 1, 1)
    dh_now[...] = grad.astype(bf16).reshape(dh_now.shape)
    for i in range(2):

        @pl.when(step == i)
        def _(i=i):
            for b in range(2):
                dh_refs[2 * i + b][...] = dh_now[side ^ b]

    units, _ = unit(x_ref[...].astype(f32))
    sum_ref[0:1, :width] += jnp.sum(grad * units, axis=0, keepdims=True)
    sum_ref[1:2, :width] += jnp.sum(grad, axis=0, keepdims=True)
    sum_ref[2:3, : low.shape[1]] += jnp.sum(low.astype(f32), axis=0, keepdims=True)

    @pl.when(step == 1)
    def _():
        wide = low_ref.shape[2]
        acc_ref[:, :wide] = dot(h_ref[...], low_ref[...].reshape(2 * rows, wide), 0, 0)
        da = da_ref[...].reshape(2 * rows, cols)
        for j in range(TP):
            at = j * cols
            acc_ref[at : at + cols, wide : wide + cols] = dot(o_ref[j], da, 0, 0)
        bias_q, bias_v = sum_ref[2:3, :cols], sum_ref[2:3, 2 * cols : 3 * cols]
        zero = jnp.zeros_like(bias_q)
        vec_ref[...] = jnp.zeros_like(vec_ref)
        vectors = [
            jnp.concatenate([jnp.where(member == j, b, zero) for j in range(TP)], axis=1)
            for b in (bias_q, bias_v)
        ]
        vectors += [
            own_sum_ref[0:1, :],
            sum_ref[0:1, :],
            sum_ref[1:2, :],
            two_ref[0:1, :],
            two_ref[1:2, :],
            own_sum_ref[1:2, :],
        ]
        for j, row in enumerate(vectors):
            vec_ref[SMALLS + j : SMALLS + j + 1, :] = row
        acc_ref[:, wide + cols :] = vec_ref[...].T[:, SMALLS:]
        if not plan.fast:
            g_refs[0][...] = acc_ref[...].astype(bf16)
            return
        near, block, _ = g_refs[0].shape
        span = near // plan.size["gx"]
        for ref, owner in ((g_refs[0], core), (g_refs[1], 1 - core)):
            for n in range(near):
                gx, rest = divmod(n, span)
                at = ((gx * 2 + owner) * span + rest) * block
                ref[n] = acc_ref[pl.ds(pl.multiple_of(at, 8), block), :].astype(bf16)


def normed_back(plan, idx, x_all, dq, own, recvs, w_qkv, low, o_all, da_cols, sum_own, sum_two):
    rows, width = x_all.shape
    cols = dq.shape[1]
    wide = w_qkv.shape[1]
    total = wide + cols + SMALLS
    step = rows // 2
    one = (rows // TP, width)
    near = plan.devices // 2

    def block(i, idx):
        return (i ^ (idx[0] // 2), 0)

    pairs = pl.BlockSpec((2, step, cols), lambda i, idx: (0, i ^ (idx[0] // 2), 0))
    if plan.fast:
        sums = [(near, width // plan.devices, total)] * 2
    else:
        sums = [(width, total)]
    constants = (w_qkv, low, o_all, da_cols, sum_own, sum_two)
    return pl.pallas_call(
        functools.partial(normed_kernel, plan, len(recvs)),
        grid_spec=pltpu.PrefetchScalarGridSpec(
            num_scalar_prefetch=1,
            grid=(2,),
            in_specs=[pl.BlockSpec((step, width), block), pl.BlockSpec((step, cols), block), pairs]
            + [pairs] * len(recvs)
            + [here(v.shape) for v in constants],
            out_specs=[here(one)] * TP + [here(shape) for shape in sums],
            scratch_shapes=[
                pltpu.VMEM((2, *one), bf16),
                pltpu.VMEM((2, step, wide), bf16),
                pltpu.VMEM((8, width), f32),
                pltpu.VMEM((width, total), f32),
                pltpu.VMEM((2 * SMALLS, width), f32),
            ],
        ),
        out_shape=[jax.ShapeDtypeStruct(one, bf16)] * TP
        + [jax.ShapeDtypeStruct(shape, bf16) for shape in sums],
        compiler_params=params(),
        cost_estimate=takes(NORMED),
        name="normed_back",
    )(idx, x_all, dq, own, *recvs, *constants)


def join_kernel(keep, cols, wide, in_ref, first_ref, second_ref, *refs):
    mats, vec_refs = refs[:4], refs[4:12]
    output_ref, input_ref, turn_ref = refs[12:]
    output_ref[...] = first_ref[...]
    input_ref[...] = second_ref[...]
    groups = {}
    for n in range(in_ref.shape[0]):
        value = in_ref[n].astype(f32)
        key = keep[n]
        groups[key] = value if key not in groups else groups[key] + value
    for j in range(TP):
        for ref, at in zip(mats, (0, cols, 2 * cols, wide)):
            ref[:, j * cols : (j + 1) * cols] = groups[j][:, at : at + cols]
    total = functools.reduce(jnp.add, [groups[j] for j in range(TP)])
    block = in_ref.shape[1]
    turn_ref[...] = jnp.zeros_like(turn_ref)
    turn_ref[:block, :SMALLS] = total[:, wide + cols :]
    turned = turn_ref[...].T
    for j, ref in enumerate(vec_refs):
        ref[...] = turned[j : j + 1, :block]


def join_grads(plan, got, first, second, cols, wide):
    near, block, _ = got.shape
    members = [plan.place(plan.same(n))[0] for n in range(near)]
    width = cols * TP
    return pl.pallas_call(
        functools.partial(join_kernel, members, cols, wide),
        out_shape=[jax.ShapeDtypeStruct((block, width), f32)] * 4
        + [jax.ShapeDtypeStruct((1, block), f32)] * 8
        + [jax.ShapeDtypeStruct(first.shape, bf16)] * 2,
        scratch_shapes=[pltpu.VMEM((128, 128), f32)],
        compiler_params=small_params(),
        cost_estimate=takes(2.2),
        name="join_grads",
    )(got, first, second)


def local(
    plan, inputs, segment_ids, padding, cotangent, w_query, b_query, w_key, w_value, b_value,
    w_out, b_out, ln1_gain, ln1_shift, ln2_gain, ln2_shift, w_up, b_up, w_down, b_down,
):
    x_own = inputs[0]
    rows, width = x_own.shape
    cols = width // TP
    length = segment_ids.shape[1]
    block = w_query.shape[0]
    hidden = w_up.shape[1]
    slab = b_up.shape[0]
    size = plan.size
    member = lax.axis_index(plan.tp)
    part = lax.axis_index(plan.half)
    core = lax.axis_index("c")
    idx = jnp.stack([member, part, core, lax.axis_index("sz")]).astype(jnp.int32)
    lines = plan.copies // 2
    fast = plan.fast

    id_rows = jnp.pad(segment_ids[0].astype(bf16), (0, 8 * width - length)).reshape(8, width)
    packed = jnp.concatenate([x_own, id_rows], axis=0)
    dm_own = (cotangent[0].astype(f32) * padding[0].astype(f32)[:, None]).astype(bf16)
    dm_mine = plan.move(dm_own, plan.route)

    small = [b_query, b_value, b_out, ln1_gain, ln1_shift, ln2_gain, ln2_shift, b_down]
    if fast:
        chunk = prepare(plan, w_query, w_key, w_value, small, w_up, w_out)
        got = lax.all_to_all(chunk, plan.tp, 0, 0, tiled=True)
        moved = plan.move(packed, plan.route)
        proj, shard = shards_of(got, w_down, b_up[None], 3 * cols + SMALLS, lines)
        moved, shard = lax.optimization_barrier((moved, shard))
        x_mine = moved[:rows]
        x_all = lax.all_gather(x_mine, plan.tp, axis=0, tiled=True)
        projs = [proj] + [plan.turn(proj, "sz", -j) for j in range(1, lines)]
        projs, x_all, shard, dm_mine = lax.optimization_barrier((projs, x_all, shard, dm_mine))
        shard = lax.all_to_all(shard, "sz", 0, 0, tiled=True)
        projs = jnp.stack(projs)
        low_one, query, kv, w_qkv, vecs = qkv(plan, idx, x_all, projs, plan.swap(projs))
    else:
        small = jnp.stack(small, axis=1)
        moved = plan.move(packed, plan.route)
        x_mine = moved[:rows]
        x_all = lax.all_gather(x_mine, plan.tp, axis=0, tiled=True)
        b_row = jnp.pad(b_up[None], ((0, 7), (0, width - slab)))
        table = [w_query, w_key, w_value, w_out, small]
        table = lax.all_gather(jnp.concatenate(table, axis=1), ALL, axis=0, tiled=True)
        vecs = table[:, 4 * width :].T.astype(f32)
        split = [lax.dynamic_slice(table, (0, i * width + member * cols), (width, cols)) for i in range(3)]
        w_qkv = jnp.concatenate([*split, jnp.zeros((width, SMALLS), bf16)], axis=1)
        out_full = table[:, 3 * width : 4 * width].reshape(TP, cols, width)
        low_one, query, kv = qkv(plan, idx, x_all, w_qkv, vecs)
        up_mine = lax.all_gather(w_up, ALL, axis=0, tiled=True)
        up_mine = up_mine.reshape(width, plan.devices, slab).transpose(1, 0, 2)
        up_mine = plan.shuffle(up_mine, ALL, plan.tp + plan.rep).reshape(TP, plan.copies, width, slab)
        up_mine = lax.dynamic_index_in_dim(up_mine, member, 0, keepdims=False)
        up_mine = up_mine.transpose(1, 0, 2).reshape(width, -1)
        downs = jnp.concatenate([w_down, b_row], axis=0)
        downs = lax.all_gather(downs, plan.rep, axis=0, tiled=False)
        down_mine = downs[:, :slab].reshape(-1, width)
        b_up_mine = downs[:, slab, :slab].reshape(1, -1).astype(f32)

    ids = moved[rows:].reshape(1, -1)[:, :length].astype(f32)

    parts = plan.parts
    kvs = [kv] + [plan.turn(kv, plan.half, -j) for j in range(1, parts)]
    mixed, lse = attend(idx, ids, query, kvs)
    o_all = lax.all_gather(mixed, plan.tp, axis=0, tiled=False)
    dms = plan.partners(dm_mine)
    if fast:
        shard, o_all, dms = lax.optimization_barrier((shard, o_all, dms))
        weights = [shard, plan.swap(shard)]
    else:
        weights = [out_full, up_mine, down_mine, b_up_mine]
    results = mlp(plan, idx, x_all, o_all, vecs, dms, weights, slab)
    r_own, low_two, act, grad_pre, dm_all, sum_two = results[:6]
    dh_two = results[6 : 6 + TP]
    if fast:
        out_mine, down_mine = results[6 + TP :]
    else:
        out_mine = lax.dynamic_index_in_dim(out_full, member, 0, keepdims=False)

    back_two = plan.reduce(dh_two)
    if fast:
        near_terms, far_terms, *out_terms = mlp_weight_grads(
            plan, idx, low_two, grad_pre, act, dm_all, down_mine
        )
        back_two, out_terms, far_terms = lax.optimization_barrier((back_two, out_terms, far_terms))
    else:
        up_terms = dot(low_two, grad_pre, 0, 0).astype(bf16)
        down_terms = dot(act, dm_all, 0, 0).astype(bf16)
        row = jnp.sum(grad_pre.astype(f32), axis=0).astype(bf16)
        out_terms = dot(act, down_mine).astype(bf16).reshape(TP, rows, width)
        out_terms = [
            lax.dynamic_index_in_dim(out_terms, member ^ j, 0, keepdims=False) for j in range(TP)
        ]
    dr, da, sum_own = resid_back(back_two, r_own, dm_mine, vecs)
    if fast:
        terms = add(near_terms, plan.swap(far_terms), after=(da,))
        das = plan.partners(da)
        after = [terms]
        terms = lax.all_to_all(terms, "sz", 0, 0, tiled=True)
        *ups, g_w_down, g_b_up = sum_rows(plan, idx, terms, block, slab)
    else:
        das = plan.partners(da)
        after = []
        row = jnp.pad(row.reshape(plan.copies, 1, slab), ((0, 0), (0, 7), (0, width - slab)))
        downs = jnp.concatenate([down_terms.reshape(plan.copies, slab, width), row], axis=1)
        downs = lax.psum_scatter(downs, plan.rep, scatter_dimension=0, tiled=False)
        g_w_down = downs[:slab].astype(f32)
        g_b_up = downs[slab, :slab].astype(f32)
        ups = plan.shuffle(up_terms.reshape(plan.devices, block, -1), ALL, plan.rep + plan.tp)
        ups = ups.reshape(plan.copies, TP * block, -1)
        ups = lax.psum_scatter(ups, plan.rep, scatter_dimension=0, tiled=False)
        ups = lax.all_to_all(ups.reshape(TP, block, -1), plan.tp, 0, 0, tiled=True).astype(f32)
    grad_query, kv_own, da_cols, *kv_others = attend_back(
        idx, ids, query, das, after, out_mine, lse, kvs
    )
    kv_others, out_parts = lax.optimization_barrier((kv_others, plan.reduce(out_terms)))
    recvs = [plan.turn(kv_others[j - 1], plan.half, j) for j in range(1, parts)]
    results = normed_back(
        plan, idx, x_all, grad_query, kv_own, recvs, w_qkv, low_one, o_all, da_cols, sum_own, sum_two
    )
    back_one, terms = plan.reduce(results[:TP]), results[TP:]
    output = plan.move(finish_output(out_parts, r_own, vecs), plan.back)
    if fast:
        keep, send = terms
        terms = add(keep, plan.swap(send))
        terms, ups, back_one = lax.optimization_barrier((terms, ups, back_one))
        got = lax.all_to_all(terms, SAME, 0, 0, tiled=True)
    else:
        terms = plan.shuffle(terms[0].reshape(plan.devices, block, -1), ALL, ("c",) + SAME)
        terms = terms.reshape(2, -1, *terms.shape[1:])
        keep, send = jnp.where(core == 0, terms, terms[::-1])
        got = lax.all_to_all(add(keep, plan.swap(send)), SAME, 0, 0, tiled=True)
    if fast:
        g_w_up = join_up(plan, idx, plan.reduce(ups), hidden)
        g_b_up = g_b_up[0]
    else:
        ups = ups.reshape(TP, block, plan.copies, slab).transpose(0, 2, 1, 3)
        ups = plan.shuffle(ups.reshape(plan.devices, block, slab), plan.tp + plan.rep, ALL)
        g_w_up = ups.transpose(1, 0, 2).reshape(block, hidden)
    grad_input = plan.move(finish_input(back_one, x_mine, dr, vecs), plan.back)
    joined = join_grads(plan, got, output, grad_input, cols, w_qkv.shape[1])
    g_query, g_key, g_value, g_out, *vec, output, grad_input = joined
    vec = [v[0] for v in vec]
    return (
        output[None],
        grad_input[None],
        g_query,
        vec[0],
        g_key,
        g_value,
        vec[1],
        g_out,
        vec[2],
        vec[3],
        vec[4],
        vec[5],
        vec[6],
        g_w_up,
        g_b_up,
        g_w_down,
        vec[7],
    )


def solution(mesh):
    groups, blocks = mesh.shape["grp"], mesh.shape["seq"]
    plan = Plan(groups, blocks)
    fine = Mesh(mesh.devices.reshape(plan.shape), ALL)
    grp, seq = ("gx", "c"), ("sz", "sy")
    matrix, vector = P(ALL, None), P(ALL)
    token = P(grp, seq, None)
    return jax.shard_map(
        functools.partial(local, plan),
        mesh=fine,
        in_specs=(
            token, P(grp, None), P(grp, seq), token,
            matrix, vector, matrix, matrix, vector, matrix, vector,
            vector, vector, vector, vector, matrix, vector, matrix, vector,
        ),
        out_specs=(
            token, token,
            matrix, vector, matrix, matrix, vector, matrix, vector,
            vector, vector, vector, vector, matrix, vector, matrix, vector,
        ),
        check_vma=False,
    )
```

```python
import functools

import jax
import jax.numpy as jnp
from jax import lax
from jax.experimental import pallas as pl
from jax.experimental.pallas import tpu as pltpu
from jax.sharding import Mesh, PartitionSpec as P

HEADS = 12
HEAD_DIM = 64
TP = 4
HEADS_TP = HEADS // TP
EPS = 1e-05
NEG = -1e30
SCALE = 0.125
ALL = ("gx", "c", "sz", "sy")
SAME = ("gx", "sz", "sy")
SMALLS = 64
NORMED = 13.0
f32 = jnp.float32
bf16 = jnp.bfloat16


class Plan:
    def __init__(self, groups, blocks):
        if (groups, blocks) == (4, 8):
            self.shape = (2, 2, 4, 2)
            self.tp, self.half, self.rep = ("gx", "sy"), "c", ("c", "sz")
            self.fast = True
        else:
            self.shape = (groups // 2, 2, blocks // TP, TP)
            self.tp, self.half, self.rep = ("sy",), "sz", ("gx", "c", "sz")
            self.fast = False
        self.size = dict(zip(ALL, self.shape))
        self.devices = groups * blocks
        self.parts = self.size[self.half]
        self.copies = self.devices // TP
        self.lines = tuple(a for a in self.rep if a != "c")
        self.route = []
        for src in range(self.devices):
            seq, block = divmod(src, blocks)
            part, member = divmod(block, TP)
            if self.tp == ("sy",):
                dst = src
            else:
                dst = (((member >> 1) * 2 + part) * 4 + seq) * 2 + (member & 1)
            self.route.append((src, dst))
        self.back = [(dst, src) for src, dst in self.route]

    def swap(self, value):
        return lax.ppermute(value, "c", [(0, 1), (1, 0)])

    def gather(self, value):
        return lax.all_to_all(
            jnp.broadcast_to(value, (TP, *value.shape)), self.tp, 0, 0, tiled=True
        )

    def partner(self, value, j):
        table = [(t, t ^ j) for t in range(TP)]
        return lax.ppermute(value, self.tp, table)

    def partners(self, value):
        return [value] + [self.partner(value, j) for j in range(1, TP)]

    def reduce(self, values):
        return [values[0]] + [self.partner(values[j], j) for j in range(1, TP)]

    def turn(self, value, axis, by):
        count = self.size[axis]
        return lax.ppermute(value, axis, [(i, (i + by) % count) for i in range(count)])

    def place(self, r):
        at, rest = {}, r
        for axis in reversed(ALL):
            rest, at[axis] = divmod(rest, self.size[axis])
        numbers = []
        for axes in (self.tp, self.rep):
            number = 0
            for axis in axes:
                number = number * self.size[axis] + at[axis]
            numbers.append(number)
        return tuple(numbers)

    def same(self, n):
        span = self.devices // 2 // self.size["gx"]
        gx, rest = divmod(n, span)
        return gx * 2 * span + rest

    def move(self, value, table):
        if all(a == b for a, b in table):
            return value
        return lax.ppermute(value, ALL, table)

    def shuffle(self, value, before, after):
        tail = value.shape[1:]
        dims = [self.size[a] for a in before]
        order = [before.index(a) for a in after]
        value = value.reshape(*dims, *tail)
        value = value.transpose(*order, *range(len(dims), len(dims) + len(tail)))
        return value.reshape(-1, *tail)


def dot(left, right, left_dim=1, right_dim=0):
    return lax.dot_general(
        left, right, (((left_dim,), (right_dim,)), ((), ())), preferred_element_type=f32
    )


def unit(values):
    center = values - jnp.mean(values, axis=-1, keepdims=True)
    variance = jnp.mean(center * center, axis=-1, keepdims=True)
    rstd = lax.rsqrt(variance + EPS)
    return center * rstd, rstd


def unit_back(grad_unit, units, rstd):
    first = jnp.mean(grad_unit, axis=-1, keepdims=True)
    second = jnp.mean(grad_unit * units, axis=-1, keepdims=True)
    return rstd * (grad_unit - first - units * second)


def params(limit=14 * 1024 * 1024, axes=1):
    return pltpu.CompilerParams(
        dimension_semantics=("arbitrary",) * axes, vmem_limit_bytes=limit
    )


def small_params():
    return pltpu.CompilerParams(vmem_limit_bytes=8 * 1024 * 1024)


def takes(microseconds):
    return pl.CostEstimate(
        flops=int(microseconds * 0.2 * 1.15e9),
        bytes_accessed=int(microseconds * 3.69e6),
        transcendentals=0,
    )


def whole(shape):
    zeros = (0,) * len(shape)
    return pl.BlockSpec(shape, lambda *_: zeros)


def here(shape):
    return pl.BlockSpec(memory_space=pltpu.VMEM)


def head_lanes(value, head):
    lane = lax.broadcasted_iota(jnp.int32, value.shape, 1)
    keep = (lane >= head * HEAD_DIM) & (lane < (head + 1) * HEAD_DIM)
    return jnp.where(keep, value, jnp.zeros_like(value))


def member_cols(row, member, cols):
    out = jnp.zeros((row.shape[0], cols), row.dtype)
    for j in range(TP):
        out = jnp.where(member == j, row[:, j * cols : (j + 1) * cols], out)
    return out


def prep_kernel(rep_of, q_ref, k_ref, v_ref, up_ref, out_ref, *refs):
    small_refs, chunk_ref, turn_ref = refs[:-2], refs[-2], refs[-1]
    block, width = q_ref.shape
    cols = width // TP
    wide = 3 * cols + SMALLS
    slab = up_ref.shape[1] // len(rep_of)
    turn_ref[...] = jnp.zeros_like(turn_ref)
    for j, ref in enumerate(small_refs):
        turn_ref[j : j + 1, :block] = ref[...].astype(f32)
    small = turn_ref[...].T[:block, :SMALLS]
    for j in range(TP):
        at = slice(j * cols, (j + 1) * cols)
        chunk_ref[j, :, :wide] = jnp.concatenate(
            [r[:, at].astype(f32) for r in (q_ref, k_ref, v_ref)] + [small], axis=1
        ).astype(bf16)
        chunk_ref[j, :, wide + width :] = out_ref[...]
    for r, (member, copy) in enumerate(rep_of):
        first = wide + copy * slab
        chunk_ref[member, :, first : first + slab] = up_ref[:, r * slab : (r + 1) * slab]


def prepare(plan, w_query, w_key, w_value, small, w_up, w_out):
    block, width = w_query.shape
    rep_of = [plan.place(r) for r in range(plan.devices)]
    wide = 3 * width // TP + SMALLS
    return pl.pallas_call(
        functools.partial(prep_kernel, rep_of),
        out_shape=jax.ShapeDtypeStruct((TP, block, wide + w_up.shape[1] // TP + width), bf16),
        scratch_shapes=[pltpu.VMEM((128, 128), f32)],
        cost_estimate=takes(1.9),
        name="prepare",
    )(w_query, w_key, w_value, w_up, w_out, *[v[None] for v in small])


def shards_kernel(wide, got_ref, down_ref, row_ref, proj_ref, shard_ref):
    block = got_ref.shape[1]
    slab, width = down_ref.shape
    first = TP * block
    for t in range(TP):
        at = t * block
        proj_ref[at : at + block, :] = got_ref[t, :, :wide]
        up = got_ref[t, :, wide : wide + width]
        out = got_ref[t, :, wide + width :]
        for n in range(shard_ref.shape[0]):
            shard_ref[n, at : at + block, :] = up
            shard_ref[n, first + at : first + at + block, :] = out
    row = jnp.concatenate([row_ref[...].astype(f32), jnp.zeros((1, width - slab), f32)], axis=1)
    row = jnp.broadcast_to(row, (8, width)).astype(bf16)
    for n in range(shard_ref.shape[0]):
        shard_ref[n, 2 * first : 2 * first + slab, :] = down_ref[...]
        shard_ref[n, 2 * first + slab :, :] = row


def shards_of(got, w_down, b_row, wide, lines):
    _, block, _ = got.shape
    slab, width = w_down.shape
    return pl.pallas_call(
        functools.partial(shards_kernel, wide),
        out_shape=[
            jax.ShapeDtypeStruct((TP * block, wide), bf16),
            jax.ShapeDtypeStruct((lines, 2 * TP * block + slab + 8, width), bf16),
        ],
        compiler_params=small_params(),
        cost_estimate=takes(2.4),
        name="shards_of",
    )(got, w_down, b_row)


def qkv_kernel(plan, idx_ref, x_ref, *refs):
    fast = plan.fast
    if fast:
        own_ref, other_ref, h_ref, q_ref, kv_ref, w_ref, vec_ref, wide_ref = refs
    else:
        w_ref, vec_ref, h_ref, q_ref, kv_ref = refs
    cols = q_ref.shape[1]
    if fast:

        @pl.when(pl.program_id(0) == 0)
        def _():
            core = idx_ref[2]
            line = idx_ref[3]
            lines, rows, _ = own_ref.shape
            pair = rows // plan.size["gx"]
            for ref, side in ((own_ref, core), (other_ref, 1 - core)):
                for j in range(lines):
                    z = lax.rem(line + j, lines)
                    value = ref[j].astype(f32)
                    for gx in range(plan.size["gx"]):
                        wide_ref[gx * 2 + side, z] = value[gx * pair : (gx + 1) * pair, :]
            table = wide_ref[...].reshape(w_ref.shape)
            w_ref[...] = table.astype(bf16)
            vec_ref[...] = table[:, 512:640].T[64:72, :]

    units, _ = unit(x_ref[...].astype(f32))
    low = (units * vec_ref[3:4, :] + vec_ref[4:5, :]).astype(bf16)
    h_ref[...] = low
    out = dot(low, w_ref[...])
    bias = member_cols(vec_ref[0:2, :], idx_ref[0], cols)
    query = (out[:, :cols] + bias[0:1, :]).astype(bf16)
    q_ref[...] = (query.astype(f32) * SCALE).astype(bf16)
    kv_ref[0] = out[:, cols : 2 * cols].astype(bf16)
    kv_ref[1] = (out[:, 2 * cols : 3 * cols] + bias[1:2, :]).astype(bf16)


def qkv(plan, idx, x_all, *operands):
    rows, width = x_all.shape
    cols = width // TP
    step = rows // 2
    wide = 3 * cols + SMALLS
    out_specs = [
        pl.BlockSpec((step, width), lambda i, *_: (i, 0)),
        pl.BlockSpec((step, cols), lambda i, *_: (i, 0)),
        pl.BlockSpec((2, step, cols), lambda i, *_: (0, i, 0)),
    ]
    out_shape = [
        jax.ShapeDtypeStruct((rows, width), bf16),
        jax.ShapeDtypeStruct((rows, cols), bf16),
        jax.ShapeDtypeStruct((2, rows, cols), bf16),
    ]
    scratch = []
    if plan.fast:
        out_specs += [here((width, wide)), here((8, width))]
        out_shape += [
            jax.ShapeDtypeStruct((width, wide), bf16),
            jax.ShapeDtypeStruct((8, width), f32),
        ]
        lines = plan.copies // 2
        scratch = [pltpu.VMEM((2 * plan.size["gx"], lines, width // (2 * plan.size["gx"] * lines), wide), f32)]
    return pl.pallas_call(
        functools.partial(qkv_kernel, plan),
        grid_spec=pltpu.PrefetchScalarGridSpec(
            num_scalar_prefetch=1,
            grid=(2,),
            in_specs=[pl.BlockSpec((step, width), lambda i, *_: (i, 0))]
            + [here(v.shape) for v in operands],
            out_specs=out_specs,
            scratch_shapes=scratch,
        ),
        out_shape=out_shape,
        compiler_params=params(),
        cost_estimate=takes(4.8),
        name="qkv",
    )(idx, x_all, *operands)


def fill_docs(ids_ref, part, parts, doc_ref):
    span, width = doc_ref.shape[1:]
    for j in range(parts):
        at = lax.rem(part + j, parts) * span
        row = ids_ref[0:1, pl.ds(pl.multiple_of(at, 512), span)]
        doc_ref[j] = jnp.broadcast_to(row, (width, span)).T


def fwd_kernel(parts, idx_ref, ids_ref, q_ref, *refs):
    kv_refs = refs[:parts]
    o_ref, lse_ref, turned, doc_ref = refs[parts:]
    step = pl.program_id(0)
    part = idx_ref[1]
    span = kv_refs[0].shape[1]
    width = q_ref.shape[0]

    @pl.when(step == 0)
    def _():
        fill_docs(ids_ref, part, parts, doc_ref)
        for j in range(parts):
            turned[j] = kv_refs[j][1].T

    at = part * span + step * width
    own = ids_ref[0:1, pl.ds(pl.multiple_of(at, 128), width)]
    query = q_ref[...]
    outs, lses = [], []
    for head in range(HEADS_TP):
        masked = head_lanes(query, head)
        scores = []
        for j in range(parts):
            raw = dot(kv_refs[j][0], masked, 1, 1)
            scores.append(jnp.where(doc_ref[j] == own, raw, NEG))
        peak = functools.reduce(
            jnp.maximum, [jnp.max(s, axis=0, keepdims=True) for s in scores]
        )
        exps = [jnp.exp(s - peak) for s in scores]
        total = functools.reduce(jnp.add, [jnp.sum(e, axis=0, keepdims=True) for e in exps])
        scale = 1.0 / total
        acc = None
        for j in range(parts):
            probs = (exps[j] * scale).astype(bf16)
            term = dot(turned[j, head * HEAD_DIM : (head + 1) * HEAD_DIM, :], probs)
            acc = term if acc is None else acc + term
        outs.append(acc)
        lses.append(peak + jnp.log(total))
    o_ref[...] = jnp.concatenate(outs, axis=0).T.astype(bf16)
    for head in range(HEADS_TP):
        lse_ref[head : head + 1, :] = lses[head]


def attend(idx, ids, q, kvs, width=256):
    rows, cols = q.shape
    parts = len(kvs)
    span = kvs[0].shape[1]
    return pl.pallas_call(
        functools.partial(fwd_kernel, parts),
        grid_spec=pltpu.PrefetchScalarGridSpec(
            num_scalar_prefetch=1,
            grid=(rows // width,),
            in_specs=[here(ids.shape), pl.BlockSpec((width, cols), lambda i, *_: (i, 0))]
            + [here(kv.shape) for kv in kvs],
            out_specs=[
                pl.BlockSpec((width, cols), lambda i, *_: (i, 0)),
                pl.BlockSpec((8, width), lambda i, *_: (0, i)),
            ],
            scratch_shapes=[
                pltpu.VMEM((parts, cols, span), bf16),
                pltpu.VMEM((parts, span, width), f32),
            ],
        ),
        out_shape=[
            jax.ShapeDtypeStruct((rows, cols), bf16),
            jax.ShapeDtypeStruct((8, rows), f32),
        ],
        compiler_params=params(),
        cost_estimate=takes(7.1),
        name="attend",
    )(idx, ids, q, *kvs)


def bwd_kernel(parts, waits, idx_ref, ids_ref, q_ref, w_ref, lse_ref, *refs):
    da_refs, refs = refs[:TP], refs[TP + waits :]
    kv_refs = refs[:parts]
    dq_ref, own_ref, cols_ref = refs[parts : parts + 3]
    other_refs = refs[parts + 3 : 2 * parts + 2]
    turned, doc_ref, key_acc, value_acc, mixed_ref = refs[2 * parts + 2 :]
    step = pl.program_id(0)
    part = idx_ref[1]
    span = kv_refs[0].shape[1]
    width, cols = q_ref.shape

    @pl.when(step == 0)
    def _():
        fill_docs(ids_ref, part, parts, doc_ref)
        for j in range(parts):
            turned[j] = kv_refs[j][0].T
        key_acc[...] = jnp.zeros_like(key_acc)
        value_acc[...] = jnp.zeros_like(value_acc)
        member = idx_ref[0]
        for j in range(TP):
            da = da_refs[j][...]
            mixed_ref[member ^ j] = dot(da, w_ref[...], 1, 1).astype(bf16)
            cols_ref[member ^ j] = member_cols(da, member, cols)

    at = part * span + step * width
    own = ids_ref[0:1, pl.ds(pl.multiple_of(at, 128), width)]
    query = q_ref[...]
    group = width // mixed_ref.shape[1]
    grad_mixed = mixed_ref[pl.ds(step * group, group)].reshape(width, cols)
    turned_grads = []
    for head in range(HEADS_TP):
        masked_q = head_lanes(query, head)
        masked_g = head_lanes(grad_mixed, head)
        lse = lse_ref[head : head + 1, :]
        probs, grads = [], []
        for j in range(parts):
            raw = dot(kv_refs[j][0], masked_q, 1, 1)
            probs.append(jnp.exp(jnp.where(doc_ref[j] == own, raw, NEG) - lse))
            grads.append(dot(kv_refs[j][1], masked_g, 1, 1))
        delta = functools.reduce(
            jnp.add,
            [jnp.sum(p * g, axis=0, keepdims=True) for p, g in zip(probs, grads)],
        )
        acc = None
        for j in range(parts):
            grad_scores = (probs[j] * (grads[j] - delta)).astype(bf16)
            value_acc[j] += dot(probs[j].astype(bf16), masked_g)
            key_acc[j] += dot(grad_scores, masked_q)
            term = dot(turned[j, head * HEAD_DIM : (head + 1) * HEAD_DIM, :], grad_scores)
            acc = term if acc is None else acc + term
        turned_grads.append(acc)
    dq_ref[...] = (jnp.concatenate(turned_grads, axis=0).T * SCALE).astype(bf16)

    @pl.when(step == pl.num_programs(0) - 1)
    def _():
        own_ref[0] = key_acc[0]
        own_ref[1] = value_acc[0]
        for j in range(1, parts):
            other_refs[j - 1][0] = key_acc[j].astype(bf16)
            other_refs[j - 1][1] = value_acc[j].astype(bf16)


def attend_back(idx, ids, q, das, after, w_out, lse, kvs, width=256):
    rows, cols = q.shape
    step, model = das[0].shape
    parts = len(kvs)
    span = kvs[0].shape[1]
    return pl.pallas_call(
        functools.partial(bwd_kernel, parts, len(after)),
        grid_spec=pltpu.PrefetchScalarGridSpec(
            num_scalar_prefetch=1,
            grid=(rows // width,),
            in_specs=[
                whole(ids.shape),
                pl.BlockSpec((width, cols), lambda i, *_: (i, 0)),
                whole((cols, model)),
                pl.BlockSpec((8, width), lambda i, *_: (0, i)),
            ]
            + [here((step, model))] * TP
            + [pl.BlockSpec(memory_space=pl.ANY)] * len(after)
            + [whole(kv.shape) for kv in kvs],
            out_specs=[
                pl.BlockSpec((width, cols), lambda i, *_: (i, 0)),
                here((2, span, cols)),
                here((TP, step, cols)),
            ]
            + [here((2, span, cols))] * (parts - 1),
            scratch_shapes=[
                pltpu.VMEM((parts, cols, span), bf16),
                pltpu.VMEM((parts, span, width), f32),
                pltpu.VMEM((parts, span, cols), f32),
                pltpu.VMEM((parts, span, cols), f32),
                pltpu.VMEM((TP, step, cols), bf16),
            ],
        ),
        out_shape=[
            jax.ShapeDtypeStruct((rows, cols), bf16),
            jax.ShapeDtypeStruct((2, span, cols), f32),
            jax.ShapeDtypeStruct((TP, step, cols), bf16),
        ]
        + [jax.ShapeDtypeStruct((2, span, cols), bf16)] * (parts - 1),
        compiler_params=params(),
        cost_estimate=takes(10.7),
        name="attend_back",
    )(idx, ids, q, w_out, lse, *das, *after, *kvs)


def mlp_kernel(plan, idx_ref, x_ref, o_ref, vec_ref, *refs):
    dm_refs, refs = refs[:TP], refs[TP:]
    step = pl.program_id(0)
    side = lax.rem(idx_ref[0], 2)
    if plan.fast:
        own_ref, other_ref, r_ref, h_ref, a_ref, du_ref, dm_ref, sum_ref = refs[:8]
        dh_refs = refs[8 : 8 + TP]
        out_ref, down_ref, dm_now, r_now, dh_now, held, held_down, held_row = refs[8 + TP :]

        @pl.when(step == 0)
        def _():
            core = idx_ref[2]
            first = held.shape[3] * plan.size["gx"]
            pair = held.shape[3]
            slab = held_down.shape[2]
            rows = []
            for z in range(held.shape[2]):
                for ref, owner in ((own_ref, core), (other_ref, 1 - core)):
                    for gx in range(plan.size["gx"]):
                        at = gx * pair
                        held[0, gx * 2 + owner, z] = ref[z, at : at + pair, :]
                        held[1, gx * 2 + owner, z] = ref[z, first + at : first + at + pair, :]
                    held_down[owner, z] = ref[z, 2 * first : 2 * first + slab, :]
            for owner in range(2):
                for z in range(held.shape[2]):
                    at = 2 * first + slab
                    row = jnp.where(
                        core == owner,
                        own_ref[z, at : at + 8, :].astype(f32),
                        other_ref[z, at : at + 8, :].astype(f32),
                    )
                    rows.append(row[0:1, :slab])
            held_row[...] = jnp.concatenate(rows, axis=1)
            out = held[1, idx_ref[0]]
            out_ref[...] = out.reshape(out_ref.shape)
            down_ref[...] = held_down[...].reshape(down_ref.shape)

        width = held.shape[-1]
        w_up = held[0].reshape(-1, width)
        outs = [held[1, j].reshape(-1, width) for j in range(TP)]
        w_down = held_down[...].reshape(-1, width)
        b_up = held_row[...]
    else:
        wo_ref, wu_ref, wd_ref, bup_ref, r_ref, h_ref, a_ref, du_ref, dm_ref, sum_ref = refs[:10]
        dh_refs, dm_now, r_now, dh_now = refs[10 : 10 + TP], refs[-3], refs[-2], refs[-1]
        w_up, w_down, b_up = wu_ref[...], wd_ref[...], bup_ref[...]
        outs = [wo_ref[j] for j in range(TP)]

    @pl.when(step == 0)
    def _():
        sum_ref[...] = jnp.zeros_like(sum_ref)

    attended = dot(o_ref[0], outs[0])
    for j in range(1, TP):
        attended += dot(o_ref[j], outs[j])
    residual = x_ref[...].astype(f32) + (attended + vec_ref[2:3, :])

    for i in range(2):

        @pl.when(step == i)
        def _(i=i):
            for b in range(2):
                dm_now[side ^ b] = dm_refs[2 * i + b][...]
            if i == 0:
                r_now[...] = residual.reshape(r_now.shape)
                r_ref[...] = r_now[side]

    units, _ = unit(residual)
    low = (units * vec_ref[5:6, :] + vec_ref[6:7, :]).astype(bf16)
    h_ref[...] = low
    pre = dot(low, w_up) + b_up
    normal = 0.5 * (1.0 + lax.erf(pre * 0.7071067811865476))
    act = (pre * normal).astype(bf16)
    a_ref[...] = act
    slope = normal + pre * (0.3989422804014327 * jnp.exp(-0.5 * pre * pre))
    dm = dm_now[...].reshape(x_ref.shape)
    dm_ref[...] = dm
    grad_pre = (dot(dm, w_down, 1, 1) * slope).astype(bf16)
    du_ref[...] = grad_pre
    grad = dot(grad_pre, w_up, 1, 1)
    sum_ref[0:1, :] += jnp.sum(grad * units, axis=0, keepdims=True)
    sum_ref[1:2, :] += jnp.sum(grad, axis=0, keepdims=True)
    dh_now[...] = grad.astype(bf16).reshape(dh_now.shape)
    for i in range(2):

        @pl.when(step == i)
        def _(i=i):
            for b in range(2):
                dh_refs[2 * i + b][...] = dh_now[side ^ b]


def mlp(plan, idx, x_all, o_all, vecs, dms, weights, slab):
    rows, width = x_all.shape
    hidden = plan.copies * slab
    cols = width // TP
    step = rows // 2

    def block(i, idx):
        return (i ^ (idx[0] // 2), 0)

    token = pl.BlockSpec((step, width), block)
    inner = pl.BlockSpec((step, hidden), block)
    one = here((rows // TP, width))
    now = (2, rows // TP, width)
    out_specs = [one, token, inner, inner, token, here((8, width))] + [one] * TP
    out_shape = [
        jax.ShapeDtypeStruct((rows // TP, width), f32),
        jax.ShapeDtypeStruct((rows, width), bf16),
        jax.ShapeDtypeStruct((rows, hidden), bf16),
        jax.ShapeDtypeStruct((rows, hidden), bf16),
        jax.ShapeDtypeStruct((rows, width), bf16),
        jax.ShapeDtypeStruct((8, width), f32),
    ] + [jax.ShapeDtypeStruct((rows // TP, width), bf16)] * TP
    scratch = [pltpu.VMEM(now, bf16), pltpu.VMEM(now, f32), pltpu.VMEM(now, bf16)]
    if plan.fast:
        lines = plan.copies // 2
        gx = plan.size["gx"]
        out_specs += [here((cols, width)), here((hidden, width))]
        out_shape += [
            jax.ShapeDtypeStruct((cols, width), bf16),
            jax.ShapeDtypeStruct((hidden, width), bf16),
        ]
        scratch += [
            pltpu.VMEM((2, 2 * gx, lines, width // (2 * gx * lines), width), bf16),
            pltpu.VMEM((2, lines, slab, width), bf16),
            pltpu.VMEM((1, hidden), f32),
        ]
    return pl.pallas_call(
        functools.partial(mlp_kernel, plan),
        grid_spec=pltpu.PrefetchScalarGridSpec(
            num_scalar_prefetch=1,
            grid=(2,),
            in_specs=[
                token,
                pl.BlockSpec((TP, step, cols), lambda i, idx: (0, i ^ (idx[0] // 2), 0)),
                here(vecs.shape),
            ]
            + [here(dms[0].shape)] * TP
            + [here(v.shape) for v in weights],
            out_specs=out_specs,
            scratch_shapes=scratch,
        ),
        out_shape=out_shape,
        compiler_params=params(),
        cost_estimate=takes(10.5),
        name="mlp",
    )(idx, x_all, o_all, vecs, *dms, *weights)


def pair_kernel(plan, idx_ref, h_ref, du_ref, a_ref, dm_ref, wd_ref, near_ref, far_ref, *refs):
    out_refs, acc_ref, wide_ref = refs[:TP], refs[TP], refs[TP + 1]
    lines = plan.copies // 2
    step = pl.program_id(0)
    member, core = idx_ref[0], idx_ref[2]
    half = step ^ core
    grad_pre = du_ref[...]
    act = a_ref[...]
    width = h_ref.shape[1]
    block = width // plan.devices
    size = act.shape[1]
    slab = size // lines
    first = TP * block
    up = dot(h_ref[...], grad_pre, 0, 0)
    down = dot(act, dm_ref[...], 0, 0)
    bias = jnp.sum(grad_pre.astype(f32), axis=0, keepdims=True)
    term = dot(act, wd_ref[...])

    @pl.when(step == 0)
    def _():
        acc_ref[...] = term.reshape(acc_ref.shape)
        wide_ref[:, :size] = up

    @pl.when(step == 1)
    def _():
        acc_ref[...] += term.reshape(acc_ref.shape)
        for j in range(TP):
            out_refs[j][...] = acc_ref[member ^ j].astype(bf16)
        wide_ref[:, size:] = up
        pair = plan.size["sy"] * block
        for ref, owner in ((near_ref, core), (far_ref, 1 - core)):
            for z in range(lines):
                for gx in range(plan.size["gx"]):
                    at = ((gx * 2 + owner) * lines + z) * pair
                    value = wide_ref[pl.ds(pl.multiple_of(at, 16), pair), :]
                    ref[z, gx * pair : (gx + 1) * pair, :] = value.astype(bf16)

    def put(ref):
        for k in range(lines):
            at = k * slab
            row = jnp.concatenate(
                [bias[:, at : at + slab], jnp.zeros((1, width - slab), f32)], axis=1
            )
            ref[k, first : first + slab, :] = down[at : at + slab, :].astype(bf16)
            ref[k, first + slab :, :] = jnp.broadcast_to(row, (8, width)).astype(bf16)

    @pl.when(half == 0)
    def _():
        put(near_ref)

    @pl.when(half == 1)
    def _():
        put(far_ref)


def mlp_weight_grads(plan, idx, low, grad_pre, act, dm_all, w_down):
    rows, width = low.shape
    hidden = act.shape[1]
    step = hidden // 2
    lines = plan.copies // 2
    block = width // plan.devices
    slab = hidden // plan.copies
    bundle = (lines, TP * block + slab + 8, width)
    token = (rows // TP, width)
    return pl.pallas_call(
        functools.partial(pair_kernel, plan),
        grid_spec=pltpu.PrefetchScalarGridSpec(
            num_scalar_prefetch=1,
            grid=(2,),
            in_specs=[
                here((rows, width)),
                pl.BlockSpec((rows, step), lambda i, idx: (0, i)),
                pl.BlockSpec((rows, step), lambda i, idx: (0, i)),
                here((rows, width)),
                pl.BlockSpec((step, width), lambda i, idx: (i, 0)),
            ],
            out_specs=[here(bundle)] * 2 + [here(token)] * TP,
            scratch_shapes=[
                pltpu.VMEM((TP, *token), f32),
                pltpu.VMEM((width, hidden), f32),
            ],
        ),
        out_shape=[jax.ShapeDtypeStruct(bundle, bf16)] * 2
        + [jax.ShapeDtypeStruct(token, bf16)] * TP,
        compiler_params=params(),
        cost_estimate=takes(7.6),
        name="mlp_weight_grads",
    )(idx, low, grad_pre, act, dm_all, w_down)


def add_kernel(count, *refs):
    total = refs[0][...].astype(f32)
    for ref in refs[1:count]:
        total += ref[...].astype(f32)
    refs[-1][...] = total.astype(bf16)


def add(*values, after=()):
    return pl.pallas_call(
        functools.partial(add_kernel, len(values)),
        in_specs=[pl.BlockSpec(memory_space=pltpu.VMEM)] * len(values)
        + [pl.BlockSpec(memory_space=pl.ANY)] * len(after),
        out_shape=jax.ShapeDtypeStruct(values[0].shape, bf16),
        compiler_params=small_params(),
        cost_estimate=takes(2.6),
        name="add",
    )(*values, *after)


def rows_kernel(plan, idx_ref, *refs):
    term_ref, up_refs = refs[0], refs[1 : 1 + TP]
    down_ref, row_ref, total_ref = refs[1 + TP :]
    member = idx_ref[0]
    total = term_ref[0].astype(f32)
    for z in range(1, term_ref.shape[0]):
        total += term_ref[z].astype(f32)
    block = up_refs[0].shape[0]
    first, slab = TP * block, down_ref.shape[0]
    total_ref[...] = total[:first].reshape(total_ref.shape)
    for j in range(TP):
        up_refs[j][...] = total_ref[member ^ j].astype(bf16)
    down_ref[...] = total[first : first + slab]
    row_ref[...] = total[first + slab : first + slab + 1, :slab]


def sum_rows(plan, idx, terms, block, slab):
    lines, rows, width = terms.shape
    return pl.pallas_call(
        functools.partial(rows_kernel, plan),
        in_specs=[pl.BlockSpec(memory_space=pltpu.SMEM), pl.BlockSpec(memory_space=pltpu.VMEM)],
        out_shape=[jax.ShapeDtypeStruct((block, width), bf16)] * TP
        + [jax.ShapeDtypeStruct((slab, width), f32), jax.ShapeDtypeStruct((1, slab), f32)],
        scratch_shapes=[pltpu.VMEM((TP, block, width), f32)],
        compiler_params=small_params(),
        cost_estimate=takes(2.2),
        name="sum_rows",
    )(idx, terms)


def up_kernel(plan, idx_ref, *refs):
    part_refs, out_ref, hold_ref = refs[:TP], refs[TP], refs[TP + 1]
    member = idx_ref[0]
    for j in range(TP):
        hold_ref[member ^ j] = part_refs[j][...].astype(f32)
    slab = out_ref.shape[1] // plan.devices
    for r in range(plan.devices):
        t, copy = plan.place(r)
        out_ref[:, r * slab : (r + 1) * slab] = hold_ref[t, :, copy * slab : (copy + 1) * slab]


def join_up(plan, idx, parts, hidden):
    block, width = parts[0].shape
    return pl.pallas_call(
        functools.partial(up_kernel, plan),
        in_specs=[pl.BlockSpec(memory_space=pltpu.SMEM)]
        + [pl.BlockSpec(memory_space=pltpu.VMEM)] * TP,
        out_shape=jax.ShapeDtypeStruct((block, hidden), f32),
        scratch_shapes=[pltpu.VMEM((TP, block, width), f32)],
        compiler_params=small_params(),
        cost_estimate=takes(40),
        name="join_up",
    )(idx, *parts)


def resid_kernel(r_ref, dm_ref, vec_ref, *refs):
    part_refs, (dr_ref, da_ref, sum_ref) = refs[:TP], refs[TP:]
    total = part_refs[0][...].astype(f32)
    for j in range(1, TP):
        total += part_refs[j][...].astype(f32)
    units, rstd = unit(r_ref[...])
    dm = dm_ref[...].astype(f32)
    dr = dm + unit_back(total * vec_ref[5:6, :], units, rstd)
    da = dr.astype(bf16)
    dr_ref[...] = dr
    da_ref[...] = da
    sum_ref[...] = jnp.zeros_like(sum_ref)
    sum_ref[0:1, :] = jnp.sum(da.astype(f32), axis=0, keepdims=True)
    sum_ref[1:2, :] = jnp.sum(dm, axis=0, keepdims=True)


def resid_back(parts, r_own, dm, vecs):
    rows, width = dm.shape
    return pl.pallas_call(
        resid_kernel,
        out_shape=[
            jax.ShapeDtypeStruct((rows, width), f32),
            jax.ShapeDtypeStruct((rows, width), bf16),
            jax.ShapeDtypeStruct((8, width), f32),
        ],
        compiler_params=small_params(),
        cost_estimate=takes(2.7),
        name="resid_back",
    )(r_own, dm, vecs, *parts)


def output_kernel(r_ref, vec_ref, *refs):
    total = r_ref[...] + vec_ref[7:8, :]
    for ref in refs[:TP]:
        total += ref[...].astype(f32)
    refs[TP][...] = total.astype(bf16)


def finish_output(parts, r_own, vecs):
    return pl.pallas_call(
        output_kernel,
        out_shape=jax.ShapeDtypeStruct(r_own.shape, bf16),
        cost_estimate=takes(2.1),
        name="finish_output",
    )(r_own, vecs, *parts)


def input_kernel(x_ref, dr_ref, vec_ref, *refs):
    total = refs[0][...].astype(f32)
    for ref in refs[1:TP]:
        total += ref[...].astype(f32)
    units, rstd = unit(x_ref[...].astype(f32))
    grad = dr_ref[...] + unit_back(total * vec_ref[3:4, :], units, rstd)
    refs[TP][...] = grad.astype(bf16)


def finish_input(parts, x, dr, vecs):
    return pl.pallas_call(
        input_kernel,
        out_shape=jax.ShapeDtypeStruct(x.shape, bf16),
        compiler_params=small_params(),
        cost_estimate=takes(40),
        name="finish_input",
    )(x, dr, vecs, *parts)


def normed_kernel(plan, n_recv, idx_ref, x_ref, dq_ref, own_ref, *refs):
    recv_refs, refs = refs[:n_recv], refs[n_recv:]
    w_ref, h_ref, o_ref, da_ref, own_sum_ref, two_ref = refs[:6]
    dh_refs, refs = refs[6 : 6 + TP], refs[6 + TP :]
    g_refs, (dh_now, low_ref, sum_ref, acc_ref, vec_ref) = refs[:-5], refs[-5:]
    step = pl.program_id(0)
    member, core = idx_ref[0], idx_ref[2]
    side = lax.rem(member, 2)
    cols = dq_ref.shape[1]
    rows, width = x_ref.shape

    @pl.when(step == 0)
    def _():
        sum_ref[...] = jnp.zeros_like(sum_ref)

    grad_k, grad_v = own_ref[0], own_ref[1]
    for ref in recv_refs:
        grad_k += ref[0].astype(f32)
        grad_v += ref[1].astype(f32)
    place = step ^ (member // 2)
    low_ref[place, :, :cols] = dq_ref[...]
    low_ref[place, :, cols : 2 * cols] = grad_k.astype(bf16)
    low_ref[place, :, 2 * cols : 3 * cols] = grad_v.astype(bf16)
    low_ref[place, :, 3 * cols :] = jnp.zeros((rows, SMALLS), bf16)
    low = low_ref[place]
    grad = dot(low, w_ref[...], 1, 1)
    dh_now[...] = grad.astype(bf16).reshape(dh_now.shape)
    for i in range(2):

        @pl.when(step == i)
        def _(i=i):
            for b in range(2):
                dh_refs[2 * i + b][...] = dh_now[side ^ b]

    units, _ = unit(x_ref[...].astype(f32))
    sum_ref[0:1, :width] += jnp.sum(grad * units, axis=0, keepdims=True)
    sum_ref[1:2, :width] += jnp.sum(grad, axis=0, keepdims=True)
    sum_ref[2:3, : low.shape[1]] += jnp.sum(low.astype(f32), axis=0, keepdims=True)

    @pl.when(step == 1)
    def _():
        wide = low_ref.shape[2]
        acc_ref[:, :wide] = dot(h_ref[...], low_ref[...].reshape(2 * rows, wide), 0, 0)
        da = da_ref[...].reshape(2 * rows, cols)
        for j in range(TP):
            at = j * cols
            acc_ref[at : at + cols, wide : wide + cols] = dot(o_ref[j], da, 0, 0)
        bias_q, bias_v = sum_ref[2:3, :cols], sum_ref[2:3, 2 * cols : 3 * cols]
        zero = jnp.zeros_like(bias_q)
        vec_ref[...] = jnp.zeros_like(vec_ref)
        vectors = [
            jnp.concatenate([jnp.where(member == j, b, zero) for j in range(TP)], axis=1)
            for b in (bias_q, bias_v)
        ]
        vectors += [
            own_sum_ref[0:1, :],
            sum_ref[0:1, :],
            sum_ref[1:2, :],
            two_ref[0:1, :],
            two_ref[1:2, :],
            own_sum_ref[1:2, :],
        ]
        for j, row in enumerate(vectors):
            vec_ref[SMALLS + j : SMALLS + j + 1, :] = row
        acc_ref[:, wide + cols :] = vec_ref[...].T[:, SMALLS:]
        if not plan.fast:
            g_refs[0][...] = acc_ref[...].astype(bf16)
            return
        near, block, _ = g_refs[0].shape
        span = near // plan.size["gx"]
        for ref, owner in ((g_refs[0], core), (g_refs[1], 1 - core)):
            for n in range(near):
                gx, rest = divmod(n, span)
                at = ((gx * 2 + owner) * span + rest) * block
                ref[n] = acc_ref[pl.ds(pl.multiple_of(at, 8), block), :].astype(bf16)


def normed_back(plan, idx, x_all, dq, own, recvs, w_qkv, low, o_all, da_cols, sum_own, sum_two):
    rows, width = x_all.shape
    cols = dq.shape[1]
    wide = w_qkv.shape[1]
    total = wide + cols + SMALLS
    step = rows // 2
    one = (rows // TP, width)
    near = plan.devices // 2

    def block(i, idx):
        return (i ^ (idx[0] // 2), 0)

    pairs = pl.BlockSpec((2, step, cols), lambda i, idx: (0, i ^ (idx[0] // 2), 0))
    if plan.fast:
        sums = [(near, width // plan.devices, total)] * 2
    else:
        sums = [(width, total)]
    constants = (w_qkv, low, o_all, da_cols, sum_own, sum_two)
    return pl.pallas_call(
        functools.partial(normed_kernel, plan, len(recvs)),
        grid_spec=pltpu.PrefetchScalarGridSpec(
            num_scalar_prefetch=1,
            grid=(2,),
            in_specs=[pl.BlockSpec((step, width), block), pl.BlockSpec((step, cols), block), pairs]
            + [pairs] * len(recvs)
            + [here(v.shape) for v in constants],
            out_specs=[here(one)] * TP + [here(shape) for shape in sums],
            scratch_shapes=[
                pltpu.VMEM((2, *one), bf16),
                pltpu.VMEM((2, step, wide), bf16),
                pltpu.VMEM((8, width), f32),
                pltpu.VMEM((width, total), f32),
                pltpu.VMEM((2 * SMALLS, width), f32),
            ],
        ),
        out_shape=[jax.ShapeDtypeStruct(one, bf16)] * TP
        + [jax.ShapeDtypeStruct(shape, bf16) for shape in sums],
        compiler_params=params(),
        cost_estimate=takes(NORMED),
        name="normed_back",
    )(idx, x_all, dq, own, *recvs, *constants)


def join_kernel(keep, cols, wide, in_ref, first_ref, second_ref, *refs):
    mats, vec_refs = refs[:4], refs[4:12]
    output_ref, input_ref, turn_ref = refs[12:]
    output_ref[...] = first_ref[...]
    input_ref[...] = second_ref[...]
    groups = {}
    for n in range(in_ref.shape[0]):
        value = in_ref[n].astype(f32)
        key = keep[n]
        groups[key] = value if key not in groups else groups[key] + value
    for j in range(TP):
        for ref, at in zip(mats, (0, cols, 2 * cols, wide)):
            ref[:, j * cols : (j + 1) * cols] = groups[j][:, at : at + cols]
    total = functools.reduce(jnp.add, [groups[j] for j in range(TP)])
    block = in_ref.shape[1]
    turn_ref[...] = jnp.zeros_like(turn_ref)
    turn_ref[:block, :SMALLS] = total[:, wide + cols :]
    turned = turn_ref[...].T
    for j, ref in enumerate(vec_refs):
        ref[...] = turned[j : j + 1, :block]


def join_grads(plan, got, first, second, cols, wide):
    near, block, _ = got.shape
    members = [plan.place(plan.same(n))[0] for n in range(near)]
    width = cols * TP
    return pl.pallas_call(
        functools.partial(join_kernel, members, cols, wide),
        out_shape=[jax.ShapeDtypeStruct((block, width), f32)] * 4
        + [jax.ShapeDtypeStruct((1, block), f32)] * 8
        + [jax.ShapeDtypeStruct(first.shape, bf16)] * 2,
        scratch_shapes=[pltpu.VMEM((128, 128), f32)],
        compiler_params=small_params(),
        cost_estimate=takes(2.2),
        name="join_grads",
    )(got, first, second)


def local(
    plan, inputs, segment_ids, padding, cotangent, w_query, b_query, w_key, w_value, b_value,
    w_out, b_out, ln1_gain, ln1_shift, ln2_gain, ln2_shift, w_up, b_up, w_down, b_down,
):
    x_own = inputs[0]
    rows, width = x_own.shape
    cols = width // TP
    length = segment_ids.shape[1]
    block = w_query.shape[0]
    hidden = w_up.shape[1]
    slab = b_up.shape[0]
    size = plan.size
    member = lax.axis_index(plan.tp)
    part = lax.axis_index(plan.half)
    core = lax.axis_index("c")
    idx = jnp.stack([member, part, core, lax.axis_index("sz")]).astype(jnp.int32)
    lines = plan.copies // 2
    fast = plan.fast

    id_rows = jnp.pad(segment_ids[0].astype(bf16), (0, 8 * width - length)).reshape(8, width)
    packed = jnp.concatenate([x_own, id_rows], axis=0)
    dm_own = (cotangent[0].astype(f32) * padding[0].astype(f32)[:, None]).astype(bf16)
    dm_mine = plan.move(dm_own, plan.route)

    small = [b_query, b_value, b_out, ln1_gain, ln1_shift, ln2_gain, ln2_shift, b_down]
    if fast:
        chunk = prepare(plan, w_query, w_key, w_value, small, w_up, w_out)
        got = lax.all_to_all(chunk, plan.tp, 0, 0, tiled=True)
        moved = plan.move(packed, plan.route)
        proj, shard = shards_of(got, w_down, b_up[None], 3 * cols + SMALLS, lines)
        projs = [proj] + [plan.turn(proj, "sz", -j) for j in range(1, lines)]
        projs, moved, shard, dm_mine = lax.optimization_barrier((projs, moved, shard, dm_mine))
        x_mine = moved[:rows]
        x_all = lax.all_gather(x_mine, plan.tp, axis=0, tiled=True)
        shard = lax.all_to_all(shard, "sz", 0, 0, tiled=True)
        projs = jnp.stack(projs)
        low_one, query, kv, w_qkv, vecs = qkv(plan, idx, x_all, projs, plan.swap(projs))
    else:
        small = jnp.stack(small, axis=1)
        moved = plan.move(packed, plan.route)
        x_mine = moved[:rows]
        x_all = lax.all_gather(x_mine, plan.tp, axis=0, tiled=True)
        b_row = jnp.pad(b_up[None], ((0, 7), (0, width - slab)))
        table = [w_query, w_key, w_value, w_out, small]
        table = lax.all_gather(jnp.concatenate(table, axis=1), ALL, axis=0, tiled=True)
        vecs = table[:, 4 * width :].T.astype(f32)
        split = [lax.dynamic_slice(table, (0, i * width + member * cols), (width, cols)) for i in range(3)]
        w_qkv = jnp.concatenate([*split, jnp.zeros((width, SMALLS), bf16)], axis=1)
        out_full = table[:, 3 * width : 4 * width].reshape(TP, cols, width)
        low_one, query, kv = qkv(plan, idx, x_all, w_qkv, vecs)
        up_mine = lax.all_gather(w_up, ALL, axis=0, tiled=True)
        up_mine = up_mine.reshape(width, plan.devices, slab).transpose(1, 0, 2)
        up_mine = plan.shuffle(up_mine, ALL, plan.tp + plan.rep).reshape(TP, plan.copies, width, slab)
        up_mine = lax.dynamic_index_in_dim(up_mine, member, 0, keepdims=False)
        up_mine = up_mine.transpose(1, 0, 2).reshape(width, -1)
        downs = jnp.concatenate([w_down, b_row], axis=0)
        downs = lax.all_gather(downs, plan.rep, axis=0, tiled=False)
        down_mine = downs[:, :slab].reshape(-1, width)
        b_up_mine = downs[:, slab, :slab].reshape(1, -1).astype(f32)

    ids = moved[rows:].reshape(1, -1)[:, :length].astype(f32)

    parts = plan.parts
    kv, dm_late = lax.optimization_barrier((kv, dm_mine))
    kvs = [kv] + [plan.turn(kv, plan.half, -j) for j in range(1, parts)]
    mixed, lse = attend(idx, ids, query, kvs)
    o_all = lax.all_gather(mixed, plan.tp, axis=0, tiled=False)
    dms = plan.partners(dm_late)
    if fast:
        shard, o_all, dms = lax.optimization_barrier((shard, o_all, dms))
        weights = [shard, plan.swap(shard)]
    else:
        weights = [out_full, up_mine, down_mine, b_up_mine]
    results = mlp(plan, idx, x_all, o_all, vecs, dms, weights, slab)
    r_own, low_two, act, grad_pre, dm_all, sum_two = results[:6]
    dh_two = results[6 : 6 + TP]
    if fast:
        out_mine, down_mine = results[6 + TP :]
    else:
        out_mine = lax.dynamic_index_in_dim(out_full, member, 0, keepdims=False)

    back_two = plan.reduce(dh_two)
    if fast:
        near_terms, far_terms, *out_terms = mlp_weight_grads(
            plan, idx, low_two, grad_pre, act, dm_all, down_mine
        )
        back_two, out_terms, far_terms = lax.optimization_barrier((back_two, out_terms, far_terms))
    else:
        up_terms = dot(low_two, grad_pre, 0, 0).astype(bf16)
        down_terms = dot(act, dm_all, 0, 0).astype(bf16)
        row = jnp.sum(grad_pre.astype(f32), axis=0).astype(bf16)
        out_terms = dot(act, down_mine).astype(bf16).reshape(TP, rows, width)
        out_terms = [
            lax.dynamic_index_in_dim(out_terms, member ^ j, 0, keepdims=False) for j in range(TP)
        ]
    dr, da, sum_own = resid_back(back_two, r_own, dm_mine, vecs)
    if fast:
        terms = add(near_terms, plan.swap(far_terms), after=(da,))
        das = plan.partners(da)
        after = [terms]
        terms = lax.all_to_all(terms, "sz", 0, 0, tiled=True)
        *ups, g_w_down, g_b_up = sum_rows(plan, idx, terms, block, slab)
    else:
        das = plan.partners(da)
        after = []
        row = jnp.pad(row.reshape(plan.copies, 1, slab), ((0, 0), (0, 7), (0, width - slab)))
        downs = jnp.concatenate([down_terms.reshape(plan.copies, slab, width), row], axis=1)
        downs = lax.psum_scatter(downs, plan.rep, scatter_dimension=0, tiled=False)
        g_w_down = downs[:slab].astype(f32)
        g_b_up = downs[slab, :slab].astype(f32)
        ups = plan.shuffle(up_terms.reshape(plan.devices, block, -1), ALL, plan.rep + plan.tp)
        ups = ups.reshape(plan.copies, TP * block, -1)
        ups = lax.psum_scatter(ups, plan.rep, scatter_dimension=0, tiled=False)
        ups = lax.all_to_all(ups.reshape(TP, block, -1), plan.tp, 0, 0, tiled=True).astype(f32)
    grad_query, kv_own, da_cols, *kv_others = attend_back(
        idx, ids, query, das, after, out_mine, lse, kvs
    )
    kv_others, out_parts = lax.optimization_barrier((kv_others, plan.reduce(out_terms)))
    recvs = [plan.turn(kv_others[j - 1], plan.half, j) for j in range(1, parts)]
    results = normed_back(
        plan, idx, x_all, grad_query, kv_own, recvs, w_qkv, low_one, o_all, da_cols, sum_own, sum_two
    )
    back_one, terms = plan.reduce(results[:TP]), results[TP:]
    if fast:
        keep, send = terms
        terms = add(keep, plan.swap(send))
        terms, ups = lax.optimization_barrier((terms, ups))
        got = lax.all_to_all(terms, SAME, 0, 0, tiled=True)
    else:
        terms = plan.shuffle(terms[0].reshape(plan.devices, block, -1), ALL, ("c",) + SAME)
        terms = terms.reshape(2, -1, *terms.shape[1:])
        keep, send = jnp.where(core == 0, terms, terms[::-1])
        got = lax.all_to_all(add(keep, plan.swap(send)), SAME, 0, 0, tiled=True)
    if fast:
        g_w_up = join_up(plan, idx, plan.reduce(ups), hidden)
        g_b_up = g_b_up[0]
    else:
        ups = ups.reshape(TP, block, plan.copies, slab).transpose(0, 2, 1, 3)
        ups = plan.shuffle(ups.reshape(plan.devices, block, slab), plan.tp + plan.rep, ALL)
        g_w_up = ups.transpose(1, 0, 2).reshape(block, hidden)
    g_w_down, out_parts = lax.optimization_barrier((g_w_down, out_parts))
    output = plan.move(finish_output(out_parts, r_own, vecs), plan.back)
    grad_input = plan.move(finish_input(back_one, x_mine, dr, vecs), plan.back)
    joined = join_grads(plan, got, output, grad_input, cols, w_qkv.shape[1])
    g_query, g_key, g_value, g_out, *vec, output, grad_input = joined
    vec = [v[0] for v in vec]
    return (
        output[None],
        grad_input[None],
        g_query,
        vec[0],
        g_key,
        g_value,
        vec[1],
        g_out,
        vec[2],
        vec[3],
        vec[4],
        vec[5],
        vec[6],
        g_w_up,
        g_b_up,
        g_w_down,
        vec[7],
    )


def solution(mesh):
    groups, blocks = mesh.shape["grp"], mesh.shape["seq"]
    plan = Plan(groups, blocks)
    fine = Mesh(mesh.devices.reshape(plan.shape), ALL)
    grp, seq = ("gx", "c"), ("sz", "sy")
    matrix, vector = P(ALL, None), P(ALL)
    token = P(grp, seq, None)
    return jax.shard_map(
        functools.partial(local, plan),
        mesh=fine,
        in_specs=(
            token, P(grp, None), P(grp, seq), token,
            matrix, vector, matrix, matrix, vector, matrix, vector,
            vector, vector, vector, vector, matrix, vector, matrix, vector,
        ),
        out_specs=(
            token, token,
            matrix, vector, matrix, matrix, vector, matrix, vector,
            vector, vector, vector, vector, matrix, vector, matrix, vector,
        ),
        check_vma=False,
    )
```

```python
import functools

import jax
import jax.numpy as jnp
from jax import lax
from jax.experimental import pallas as pl
from jax.experimental.pallas import tpu as pltpu
from jax.sharding import Mesh, PartitionSpec as P

HEADS = 12
HEAD_DIM = 64
TP = 4
HEADS_TP = HEADS // TP
EPS = 1e-05
NEG = -1e30
SCALE = 0.125
ALL = ("gx", "c", "sz", "sy")
SAME = ("gx", "sz", "sy")
SMALLS = 64
NORMED = 13.0
f32 = jnp.float32
bf16 = jnp.bfloat16


class Plan:
    def __init__(self, groups, blocks):
        if (groups, blocks) == (4, 8):
            self.shape = (2, 2, 4, 2)
            self.tp, self.half, self.rep = ("gx", "sy"), "c", ("c", "sz")
            self.fast = True
        else:
            self.shape = (groups // 2, 2, blocks // TP, TP)
            self.tp, self.half, self.rep = ("sy",), "sz", ("gx", "c", "sz")
            self.fast = False
        self.size = dict(zip(ALL, self.shape))
        self.devices = groups * blocks
        self.parts = self.size[self.half]
        self.copies = self.devices // TP
        self.lines = tuple(a for a in self.rep if a != "c")
        self.route = []
        for src in range(self.devices):
            seq, block = divmod(src, blocks)
            part, member = divmod(block, TP)
            if self.tp == ("sy",):
                dst = src
            else:
                dst = (((member >> 1) * 2 + part) * 4 + seq) * 2 + (member & 1)
            self.route.append((src, dst))
        self.back = [(dst, src) for src, dst in self.route]

    def swap(self, value):
        return lax.ppermute(value, "c", [(0, 1), (1, 0)])

    def gather(self, value):
        return lax.all_to_all(
            jnp.broadcast_to(value, (TP, *value.shape)), self.tp, 0, 0, tiled=True
        )

    def partner(self, value, j):
        table = [(t, t ^ j) for t in range(TP)]
        return lax.ppermute(value, self.tp, table)

    def partners(self, value):
        return [value] + [self.partner(value, j) for j in range(1, TP)]

    def reduce(self, values):
        return [values[0]] + [self.partner(values[j], j) for j in range(1, TP)]

    def turn(self, value, axis, by):
        count = self.size[axis]
        return lax.ppermute(value, axis, [(i, (i + by) % count) for i in range(count)])

    def place(self, r):
        at, rest = {}, r
        for axis in reversed(ALL):
            rest, at[axis] = divmod(rest, self.size[axis])
        numbers = []
        for axes in (self.tp, self.rep):
            number = 0
            for axis in axes:
                number = number * self.size[axis] + at[axis]
            numbers.append(number)
        return tuple(numbers)

    def same(self, n):
        span = self.devices // 2 // self.size["gx"]
        gx, rest = divmod(n, span)
        return gx * 2 * span + rest

    def move(self, value, table):
        if all(a == b for a, b in table):
            return value
        return lax.ppermute(value, ALL, table)

    def shuffle(self, value, before, after):
        tail = value.shape[1:]
        dims = [self.size[a] for a in before]
        order = [before.index(a) for a in after]
        value = value.reshape(*dims, *tail)
        value = value.transpose(*order, *range(len(dims), len(dims) + len(tail)))
        return value.reshape(-1, *tail)


def dot(left, right, left_dim=1, right_dim=0):
    return lax.dot_general(
        left, right, (((left_dim,), (right_dim,)), ((), ())), preferred_element_type=f32
    )


def unit(values):
    center = values - jnp.mean(values, axis=-1, keepdims=True)
    variance = jnp.mean(center * center, axis=-1, keepdims=True)
    rstd = lax.rsqrt(variance + EPS)
    return center * rstd, rstd


def unit_back(grad_unit, units, rstd):
    first = jnp.mean(grad_unit, axis=-1, keepdims=True)
    second = jnp.mean(grad_unit * units, axis=-1, keepdims=True)
    return rstd * (grad_unit - first - units * second)


def params(limit=14 * 1024 * 1024, axes=1):
    return pltpu.CompilerParams(
        dimension_semantics=("arbitrary",) * axes, vmem_limit_bytes=limit
    )


def small_params():
    return pltpu.CompilerParams(vmem_limit_bytes=8 * 1024 * 1024)


def takes(microseconds):
    return pl.CostEstimate(
        flops=int(microseconds * 0.2 * 1.15e9),
        bytes_accessed=int(microseconds * 3.69e6),
        transcendentals=0,
    )


def whole(shape):
    zeros = (0,) * len(shape)
    return pl.BlockSpec(shape, lambda *_: zeros)


def here(shape):
    return pl.BlockSpec(memory_space=pltpu.VMEM)


def head_lanes(value, head):
    lane = lax.broadcasted_iota(jnp.int32, value.shape, 1)
    keep = (lane >= head * HEAD_DIM) & (lane < (head + 1) * HEAD_DIM)
    return jnp.where(keep, value, jnp.zeros_like(value))


def member_cols(row, member, cols):
    out = jnp.zeros((row.shape[0], cols), row.dtype)
    for j in range(TP):
        out = jnp.where(member == j, row[:, j * cols : (j + 1) * cols], out)
    return out


def prep_kernel(rep_of, q_ref, k_ref, v_ref, up_ref, out_ref, *refs):
    small_refs, chunk_ref, turn_ref = refs[:-2], refs[-2], refs[-1]
    block, width = q_ref.shape
    cols = width // TP
    wide = 3 * cols + SMALLS
    slab = up_ref.shape[1] // len(rep_of)
    turn_ref[...] = jnp.zeros_like(turn_ref)
    for j, ref in enumerate(small_refs):
        turn_ref[j : j + 1, :block] = ref[...].astype(f32)
    small = turn_ref[...].T[:block, :SMALLS]
    for j in range(TP):
        at = slice(j * cols, (j + 1) * cols)
        chunk_ref[j, :, :wide] = jnp.concatenate(
            [r[:, at].astype(f32) for r in (q_ref, k_ref, v_ref)] + [small], axis=1
        ).astype(bf16)
        chunk_ref[j, :, wide + width :] = out_ref[...]
    for r, (member, copy) in enumerate(rep_of):
        first = wide + copy * slab
        chunk_ref[member, :, first : first + slab] = up_ref[:, r * slab : (r + 1) * slab]


def prepare(plan, w_query, w_key, w_value, small, w_up, w_out):
    block, width = w_query.shape
    rep_of = [plan.place(r) for r in range(plan.devices)]
    wide = 3 * width // TP + SMALLS
    return pl.pallas_call(
        functools.partial(prep_kernel, rep_of),
        out_shape=jax.ShapeDtypeStruct((TP, block, wide + w_up.shape[1] // TP + width), bf16),
        scratch_shapes=[pltpu.VMEM((128, 128), f32)],
        cost_estimate=takes(1.9),
        name="prepare",
    )(w_query, w_key, w_value, w_up, w_out, *[v[None] for v in small])


def shards_kernel(wide, got_ref, down_ref, row_ref, proj_ref, shard_ref):
    block = got_ref.shape[1]
    slab, width = down_ref.shape
    first = TP * block
    for t in range(TP):
        at = t * block
        proj_ref[at : at + block, :] = got_ref[t, :, :wide]
        up = got_ref[t, :, wide : wide + width]
        out = got_ref[t, :, wide + width :]
        for n in range(shard_ref.shape[0]):
            shard_ref[n, at : at + block, :] = up
            shard_ref[n, first + at : first + at + block, :] = out
    row = jnp.concatenate([row_ref[...].astype(f32), jnp.zeros((1, width - slab), f32)], axis=1)
    row = jnp.broadcast_to(row, (8, width)).astype(bf16)
    for n in range(shard_ref.shape[0]):
        shard_ref[n, 2 * first : 2 * first + slab, :] = down_ref[...]
        shard_ref[n, 2 * first + slab :, :] = row


def shards_of(got, w_down, b_row, wide, lines):
    _, block, _ = got.shape
    slab, width = w_down.shape
    return pl.pallas_call(
        functools.partial(shards_kernel, wide),
        out_shape=[
            jax.ShapeDtypeStruct((TP * block, wide), bf16),
            jax.ShapeDtypeStruct((lines, 2 * TP * block + slab + 8, width), bf16),
        ],
        compiler_params=small_params(),
        cost_estimate=takes(2.4),
        name="shards_of",
    )(got, w_down, b_row)


def qkv_kernel(plan, idx_ref, x_ref, *refs):
    fast = plan.fast
    if fast:
        own_ref, other_ref, h_ref, q_ref, kv_ref, w_ref, vec_ref, wide_ref = refs
    else:
        w_ref, vec_ref, h_ref, q_ref, kv_ref = refs
    cols = q_ref.shape[1]
    if fast:

        @pl.when(pl.program_id(0) == 0)
        def _():
            core = idx_ref[2]
            line = idx_ref[3]
            lines, rows, _ = own_ref.shape
            pair = rows // plan.size["gx"]
            for ref, side in ((own_ref, core), (other_ref, 1 - core)):
                for j in range(lines):
                    z = lax.rem(line + j, lines)
                    value = ref[j].astype(f32)
                    for gx in range(plan.size["gx"]):
                        wide_ref[gx * 2 + side, z] = value[gx * pair : (gx + 1) * pair, :]
            table = wide_ref[...].reshape(w_ref.shape)
            w_ref[...] = table.astype(bf16)
            vec_ref[...] = table[:, 512:640].T[64:72, :]

    units, _ = unit(x_ref[...].astype(f32))
    low = (units * vec_ref[3:4, :] + vec_ref[4:5, :]).astype(bf16)
    h_ref[...] = low
    out = dot(low, w_ref[...])
    bias = member_cols(vec_ref[0:2, :], idx_ref[0], cols)
    query = (out[:, :cols] + bias[0:1, :]).astype(bf16)
    q_ref[...] = (query.astype(f32) * SCALE).astype(bf16)
    kv_ref[0] = out[:, cols : 2 * cols].astype(bf16)
    kv_ref[1] = (out[:, 2 * cols : 3 * cols] + bias[1:2, :]).astype(bf16)


def qkv(plan, idx, x_all, *operands):
    rows, width = x_all.shape
    cols = width // TP
    step = rows // 2
    wide = 3 * cols + SMALLS
    out_specs = [
        pl.BlockSpec((step, width), lambda i, *_: (i, 0)),
        pl.BlockSpec((step, cols), lambda i, *_: (i, 0)),
        pl.BlockSpec((2, step, cols), lambda i, *_: (0, i, 0)),
    ]
    out_shape = [
        jax.ShapeDtypeStruct((rows, width), bf16),
        jax.ShapeDtypeStruct((rows, cols), bf16),
        jax.ShapeDtypeStruct((2, rows, cols), bf16),
    ]
    scratch = []
    if plan.fast:
        out_specs += [here((width, wide)), here((8, width))]
        out_shape += [
            jax.ShapeDtypeStruct((width, wide), bf16),
            jax.ShapeDtypeStruct((8, width), f32),
        ]
        lines = plan.copies // 2
        scratch = [pltpu.VMEM((2 * plan.size["gx"], lines, width // (2 * plan.size["gx"] * lines), wide), f32)]
    return pl.pallas_call(
        functools.partial(qkv_kernel, plan),
        grid_spec=pltpu.PrefetchScalarGridSpec(
            num_scalar_prefetch=1,
            grid=(2,),
            in_specs=[pl.BlockSpec((step, width), lambda i, *_: (i, 0))]
            + [here(v.shape) for v in operands],
            out_specs=out_specs,
            scratch_shapes=scratch,
        ),
        out_shape=out_shape,
        compiler_params=params(),
        cost_estimate=takes(4.8),
        name="qkv",
    )(idx, x_all, *operands)


def fill_docs(ids_ref, part, parts, doc_ref):
    span, width = doc_ref.shape[1:]
    for j in range(parts):
        at = lax.rem(part + j, parts) * span
        row = ids_ref[0:1, pl.ds(pl.multiple_of(at, 512), span)]
        doc_ref[j] = jnp.broadcast_to(row, (width, span)).T


def fwd_kernel(parts, idx_ref, ids_ref, q_ref, *refs):
    kv_refs = refs[:parts]
    o_ref, lse_ref, turned, doc_ref = refs[parts:]
    step = pl.program_id(0)
    part = idx_ref[1]
    span = kv_refs[0].shape[1]
    width = q_ref.shape[0]

    @pl.when(step == 0)
    def _():
        fill_docs(ids_ref, part, parts, doc_ref)
        for j in range(parts):
            turned[j] = kv_refs[j][1].T

    at = part * span + step * width
    own = ids_ref[0:1, pl.ds(pl.multiple_of(at, 128), width)]
    query = q_ref[...]
    outs, lses = [], []
    for head in range(HEADS_TP):
        masked = head_lanes(query, head)
        scores = []
        for j in range(parts):
            raw = dot(kv_refs[j][0], masked, 1, 1)
            scores.append(jnp.where(doc_ref[j] == own, raw, NEG))
        peak = functools.reduce(
            jnp.maximum, [jnp.max(s, axis=0, keepdims=True) for s in scores]
        )
        exps = [jnp.exp(s - peak) for s in scores]
        total = functools.reduce(jnp.add, [jnp.sum(e, axis=0, keepdims=True) for e in exps])
        scale = 1.0 / total
        acc = None
        for j in range(parts):
            probs = (exps[j] * scale).astype(bf16)
            term = dot(turned[j, head * HEAD_DIM : (head + 1) * HEAD_DIM, :], probs)
            acc = term if acc is None else acc + term
        outs.append(acc)
        lses.append(peak + jnp.log(total))
    o_ref[...] = jnp.concatenate(outs, axis=0).T.astype(bf16)
    for head in range(HEADS_TP):
        lse_ref[head : head + 1, :] = lses[head]


def attend(idx, ids, q, kvs, width=256):
    rows, cols = q.shape
    parts = len(kvs)
    span = kvs[0].shape[1]
    return pl.pallas_call(
        functools.partial(fwd_kernel, parts),
        grid_spec=pltpu.PrefetchScalarGridSpec(
            num_scalar_prefetch=1,
            grid=(rows // width,),
            in_specs=[here(ids.shape), pl.BlockSpec((width, cols), lambda i, *_: (i, 0))]
            + [here(kv.shape) for kv in kvs],
            out_specs=[
                pl.BlockSpec((width, cols), lambda i, *_: (i, 0)),
                pl.BlockSpec((8, width), lambda i, *_: (0, i)),
            ],
            scratch_shapes=[
                pltpu.VMEM((parts, cols, span), bf16),
                pltpu.VMEM((parts, span, width), f32),
            ],
        ),
        out_shape=[
            jax.ShapeDtypeStruct((rows, cols), bf16),
            jax.ShapeDtypeStruct((8, rows), f32),
        ],
        compiler_params=params(parts * 7 * 1024 * 1024),
        cost_estimate=takes(7.1),
        name="attend",
    )(idx, ids, q, *kvs)


def bwd_kernel(parts, waits, idx_ref, ids_ref, q_ref, w_ref, lse_ref, *refs):
    da_refs, refs = refs[:TP], refs[TP + waits :]
    kv_refs = refs[:parts]
    dq_ref, own_ref, cols_ref = refs[parts : parts + 3]
    other_refs = refs[parts + 3 : 2 * parts + 2]
    turned, doc_ref, key_acc, value_acc, mixed_ref = refs[2 * parts + 2 :]
    step = pl.program_id(0)
    part = idx_ref[1]
    span = kv_refs[0].shape[1]
    width, cols = q_ref.shape

    @pl.when(step == 0)
    def _():
        fill_docs(ids_ref, part, parts, doc_ref)
        for j in range(parts):
            turned[j] = kv_refs[j][0].T
        key_acc[...] = jnp.zeros_like(key_acc)
        value_acc[...] = jnp.zeros_like(value_acc)
        member = idx_ref[0]
        for j in range(TP):
            da = da_refs[j][...]
            mixed_ref[member ^ j] = dot(da, w_ref[...], 1, 1).astype(bf16)
            cols_ref[member ^ j] = member_cols(da, member, cols)

    at = part * span + step * width
    own = ids_ref[0:1, pl.ds(pl.multiple_of(at, 128), width)]
    query = q_ref[...]
    group = width // mixed_ref.shape[1]
    grad_mixed = mixed_ref[pl.ds(step * group, group)].reshape(width, cols)
    turned_grads = []
    for head in range(HEADS_TP):
        masked_q = head_lanes(query, head)
        masked_g = head_lanes(grad_mixed, head)
        lse = lse_ref[head : head + 1, :]
        probs, grads = [], []
        for j in range(parts):
            raw = dot(kv_refs[j][0], masked_q, 1, 1)
            probs.append(jnp.exp(jnp.where(doc_ref[j] == own, raw, NEG) - lse))
            grads.append(dot(kv_refs[j][1], masked_g, 1, 1))
        delta = functools.reduce(
            jnp.add,
            [jnp.sum(p * g, axis=0, keepdims=True) for p, g in zip(probs, grads)],
        )
        acc = None
        for j in range(parts):
            grad_scores = (probs[j] * (grads[j] - delta)).astype(bf16)
            value_acc[j] += dot(probs[j].astype(bf16), masked_g)
            key_acc[j] += dot(grad_scores, masked_q)
            term = dot(turned[j, head * HEAD_DIM : (head + 1) * HEAD_DIM, :], grad_scores)
            acc = term if acc is None else acc + term
        turned_grads.append(acc)
    dq_ref[...] = (jnp.concatenate(turned_grads, axis=0).T * SCALE).astype(bf16)

    @pl.when(step == pl.num_programs(0) - 1)
    def _():
        own_ref[0] = key_acc[0]
        own_ref[1] = value_acc[0]
        for j in range(1, parts):
            other_refs[j - 1][0] = key_acc[j].astype(bf16)
            other_refs[j - 1][1] = value_acc[j].astype(bf16)


def attend_back(idx, ids, q, das, after, w_out, lse, kvs, width=256):
    rows, cols = q.shape
    step, model = das[0].shape
    parts = len(kvs)
    span = kvs[0].shape[1]
    return pl.pallas_call(
        functools.partial(bwd_kernel, parts, len(after)),
        grid_spec=pltpu.PrefetchScalarGridSpec(
            num_scalar_prefetch=1,
            grid=(rows // width,),
            in_specs=[
                whole(ids.shape),
                pl.BlockSpec((width, cols), lambda i, *_: (i, 0)),
                whole((cols, model)),
                pl.BlockSpec((8, width), lambda i, *_: (0, i)),
            ]
            + [here((step, model))] * TP
            + [pl.BlockSpec(memory_space=pl.ANY)] * len(after)
            + [whole(kv.shape) for kv in kvs],
            out_specs=[
                pl.BlockSpec((width, cols), lambda i, *_: (i, 0)),
                here((2, span, cols)),
                here((TP, step, cols)),
            ]
            + [here((2, span, cols))] * (parts - 1),
            scratch_shapes=[
                pltpu.VMEM((parts, cols, span), bf16),
                pltpu.VMEM((parts, span, width), f32),
                pltpu.VMEM((parts, span, cols), f32),
                pltpu.VMEM((parts, span, cols), f32),
                pltpu.VMEM((TP, step, cols), bf16),
            ],
        ),
        out_shape=[
            jax.ShapeDtypeStruct((rows, cols), bf16),
            jax.ShapeDtypeStruct((2, span, cols), f32),
            jax.ShapeDtypeStruct((TP, step, cols), bf16),
        ]
        + [jax.ShapeDtypeStruct((2, span, cols), bf16)] * (parts - 1),
        compiler_params=params(parts * 7 * 1024 * 1024),
        cost_estimate=takes(10.7),
        name="attend_back",
    )(idx, ids, q, w_out, lse, *das, *after, *kvs)


def stage_kernel(idx_ref, x_ref, *refs):
    same_ref, dm_ref = refs[TP:]
    same_ref[...] = x_ref[...]
    for j in range(TP):
        dm_ref[idx_ref[0] ^ j] = refs[j][...]


def stage(idx, x_all, dms):
    return pl.pallas_call(
        stage_kernel,
        in_specs=[pl.BlockSpec(memory_space=pltpu.SMEM)]
        + [pl.BlockSpec(memory_space=pltpu.VMEM)] * (1 + TP),
        out_shape=[
            jax.ShapeDtypeStruct(x_all.shape, bf16),
            jax.ShapeDtypeStruct((TP, *dms[0].shape), bf16),
        ],
        compiler_params=small_params(),
        cost_estimate=takes(1.5),
        name="stage",
    )(idx, x_all, *dms)


def mlp_kernel(plan, idx_ref, x_ref, o_ref, vec_ref, dm_ref, *refs):
    step = pl.program_id(0)
    side = lax.rem(idx_ref[0], 2)
    if plan.fast:
        own_ref, other_ref, r_ref, h_ref, a_ref, du_ref, sum_ref = refs[:7]
        dh_refs = refs[7 : 7 + TP]
        out_ref, down_ref, r_now, dh_now, held, held_down, held_row = refs[7 + TP :]

        @pl.when(step == 0)
        def _():
            core = idx_ref[2]
            first = held.shape[3] * plan.size["gx"]
            pair = held.shape[3]
            slab = held_down.shape[2]
            rows = []
            for z in range(held.shape[2]):
                for ref, owner in ((own_ref, core), (other_ref, 1 - core)):
                    for gx in range(plan.size["gx"]):
                        at = gx * pair
                        held[0, gx * 2 + owner, z] = ref[z, at : at + pair, :]
                        held[1, gx * 2 + owner, z] = ref[z, first + at : first + at + pair, :]
                    held_down[owner, z] = ref[z, 2 * first : 2 * first + slab, :]
            for owner in range(2):
                for z in range(held.shape[2]):
                    at = 2 * first + slab
                    row = jnp.where(
                        core == owner,
                        own_ref[z, at : at + 8, :].astype(f32),
                        other_ref[z, at : at + 8, :].astype(f32),
                    )
                    rows.append(row[0:1, :slab])
            held_row[...] = jnp.concatenate(rows, axis=1)
            out = held[1, idx_ref[0]]
            out_ref[...] = out.reshape(out_ref.shape)
            down_ref[...] = held_down[...].reshape(down_ref.shape)

        width = held.shape[-1]
        w_up = held[0].reshape(-1, width)
        outs = [held[1, j].reshape(-1, width) for j in range(TP)]
        w_down = held_down[...].reshape(-1, width)
        b_up = held_row[...]
    else:
        wo_ref, wu_ref, wd_ref, bup_ref, r_ref, h_ref, a_ref, du_ref, sum_ref = refs[:9]
        dh_refs, r_now, dh_now = refs[9 : 9 + TP], refs[-2], refs[-1]
        w_up, w_down, b_up = wu_ref[...], wd_ref[...], bup_ref[...]
        outs = [wo_ref[j] for j in range(TP)]

    @pl.when(step == 0)
    def _():
        sum_ref[...] = jnp.zeros_like(sum_ref)

    attended = dot(o_ref[0], outs[0])
    for j in range(1, TP):
        attended += dot(o_ref[j], outs[j])
    residual = x_ref[...].astype(f32) + (attended + vec_ref[2:3, :])

    @pl.when(step == 0)
    def _():
        r_now[...] = residual.reshape(r_now.shape)
        r_ref[...] = r_now[side]

    units, _ = unit(residual)
    low = (units * vec_ref[5:6, :] + vec_ref[6:7, :]).astype(bf16)
    h_ref[...] = low
    pre = dot(low, w_up) + b_up
    normal = 0.5 * (1.0 + lax.erf(pre * 0.7071067811865476))
    act = (pre * normal).astype(bf16)
    a_ref[...] = act
    slope = normal + pre * (0.3989422804014327 * jnp.exp(-0.5 * pre * pre))
    dm = dm_ref[...]
    grad_pre = (dot(dm, w_down, 1, 1) * slope).astype(bf16)
    du_ref[...] = grad_pre
    grad = dot(grad_pre, w_up, 1, 1)
    sum_ref[0:1, :] += jnp.sum(grad * units, axis=0, keepdims=True)
    sum_ref[1:2, :] += jnp.sum(grad, axis=0, keepdims=True)
    dh_now[...] = grad.astype(bf16).reshape(dh_now.shape)
    for i in range(2):

        @pl.when(step == i)
        def _(i=i):
            for b in range(2):
                dh_refs[2 * i + b][...] = dh_now[side ^ b]


def mlp(plan, idx, x_all, o_all, vecs, dm_all, weights, slab):
    rows, width = x_all.shape
    hidden = plan.copies * slab
    cols = width // TP
    step = rows // 2

    def block(i, idx):
        return (i ^ (idx[0] // 2), 0)

    token = pl.BlockSpec((step, width), block)
    inner = pl.BlockSpec((step, hidden), block)
    one = here((rows // TP, width))
    now = (2, rows // TP, width)
    out_specs = [one, token, inner, inner, here((8, width))] + [one] * TP
    out_shape = [
        jax.ShapeDtypeStruct((rows // TP, width), f32),
        jax.ShapeDtypeStruct((rows, width), bf16),
        jax.ShapeDtypeStruct((rows, hidden), bf16),
        jax.ShapeDtypeStruct((rows, hidden), bf16),
        jax.ShapeDtypeStruct((8, width), f32),
    ] + [jax.ShapeDtypeStruct((rows // TP, width), bf16)] * TP
    scratch = [pltpu.VMEM(now, f32), pltpu.VMEM(now, bf16)]
    if plan.fast:
        lines = plan.copies // 2
        gx = plan.size["gx"]
        out_specs += [here((cols, width)), here((hidden, width))]
        out_shape += [
            jax.ShapeDtypeStruct((cols, width), bf16),
            jax.ShapeDtypeStruct((hidden, width), bf16),
        ]
        scratch += [
            pltpu.VMEM((2, 2 * gx, lines, width // (2 * gx * lines), width), bf16),
            pltpu.VMEM((2, lines, slab, width), bf16),
            pltpu.VMEM((1, hidden), f32),
        ]
    return pl.pallas_call(
        functools.partial(mlp_kernel, plan),
        grid_spec=pltpu.PrefetchScalarGridSpec(
            num_scalar_prefetch=1,
            grid=(2,),
            in_specs=[
                token,
                pl.BlockSpec((TP, step, cols), lambda i, idx: (0, i ^ (idx[0] // 2), 0)),
                here(vecs.shape),
                token,
            ]
            + [here(v.shape) for v in weights],
            out_specs=out_specs,
            scratch_shapes=scratch,
        ),
        out_shape=out_shape,
        compiler_params=params(),
        cost_estimate=takes(10.5),
        name="mlp",
    )(idx, x_all, o_all, vecs, dm_all, *weights)


def pair_kernel(plan, idx_ref, h_ref, du_ref, a_ref, dm_ref, wd_ref, near_ref, far_ref, *refs):
    out_refs, acc_ref, wide_ref = refs[:TP], refs[TP], refs[TP + 1]
    lines = plan.copies // 2
    step = pl.program_id(0)
    member, core = idx_ref[0], idx_ref[2]
    half = step ^ core
    grad_pre = du_ref[...]
    act = a_ref[...]
    width = h_ref.shape[1]
    block = width // plan.devices
    size = act.shape[1]
    slab = size // lines
    first = TP * block
    up = dot(h_ref[...], grad_pre, 0, 0)
    down = dot(act, dm_ref[...], 0, 0)
    bias = jnp.sum(grad_pre.astype(f32), axis=0, keepdims=True)
    term = dot(act, wd_ref[...])

    @pl.when(step == 0)
    def _():
        acc_ref[...] = term.reshape(acc_ref.shape)
        wide_ref[:, :size] = up

    @pl.when(step == 1)
    def _():
        acc_ref[...] += term.reshape(acc_ref.shape)
        for j in range(TP):
            out_refs[j][...] = acc_ref[member ^ j].astype(bf16)
        wide_ref[:, size:] = up
        pair = plan.size["sy"] * block
        for ref, owner in ((near_ref, core), (far_ref, 1 - core)):
            for z in range(lines):
                for gx in range(plan.size["gx"]):
                    at = ((gx * 2 + owner) * lines + z) * pair
                    value = wide_ref[pl.ds(pl.multiple_of(at, 16), pair), :]
                    ref[z, gx * pair : (gx + 1) * pair, :] = value.astype(bf16)

    def put(ref):
        for k in range(lines):
            at = k * slab
            row = jnp.concatenate(
                [bias[:, at : at + slab], jnp.zeros((1, width - slab), f32)], axis=1
            )
            ref[k, first : first + slab, :] = down[at : at + slab, :].astype(bf16)
            ref[k, first + slab :, :] = jnp.broadcast_to(row, (8, width)).astype(bf16)

    @pl.when(half == 0)
    def _():
        put(near_ref)

    @pl.when(half == 1)
    def _():
        put(far_ref)


def mlp_weight_grads(plan, idx, low, grad_pre, act, dm_all, w_down):
    rows, width = low.shape
    hidden = act.shape[1]
    step = hidden // 2
    lines = plan.copies // 2
    block = width // plan.devices
    slab = hidden // plan.copies
    bundle = (lines, TP * block + slab + 8, width)
    token = (rows // TP, width)
    return pl.pallas_call(
        functools.partial(pair_kernel, plan),
        grid_spec=pltpu.PrefetchScalarGridSpec(
            num_scalar_prefetch=1,
            grid=(2,),
            in_specs=[
                here((rows, width)),
                pl.BlockSpec((rows, step), lambda i, idx: (0, i)),
                pl.BlockSpec((rows, step), lambda i, idx: (0, i)),
                here((rows, width)),
                pl.BlockSpec((step, width), lambda i, idx: (i, 0)),
            ],
            out_specs=[here(bundle)] * 2 + [here(token)] * TP,
            scratch_shapes=[
                pltpu.VMEM((TP, *token), f32),
                pltpu.VMEM((width, hidden), f32),
            ],
        ),
        out_shape=[jax.ShapeDtypeStruct(bundle, bf16)] * 2
        + [jax.ShapeDtypeStruct(token, bf16)] * TP,
        compiler_params=params(),
        cost_estimate=takes(7.6),
        name="mlp_weight_grads",
    )(idx, low, grad_pre, act, dm_all, w_down)


def add_kernel(count, *refs):
    total = refs[0][...].astype(f32)
    for ref in refs[1:count]:
        total += ref[...].astype(f32)
    refs[-1][...] = total.astype(bf16)


def add(*values, after=()):
    return pl.pallas_call(
        functools.partial(add_kernel, len(values)),
        in_specs=[pl.BlockSpec(memory_space=pltpu.VMEM)] * len(values)
        + [pl.BlockSpec(memory_space=pl.ANY)] * len(after),
        out_shape=jax.ShapeDtypeStruct(values[0].shape, bf16),
        compiler_params=small_params(),
        cost_estimate=takes(2.6),
        name="add",
    )(*values, *after)


def rows_kernel(plan, idx_ref, *refs):
    term_ref, up_refs = refs[0], refs[1 : 1 + TP]
    down_ref, row_ref, total_ref = refs[1 + TP :]
    member = idx_ref[0]
    total = term_ref[0].astype(f32)
    for z in range(1, term_ref.shape[0]):
        total += term_ref[z].astype(f32)
    block = up_refs[0].shape[0]
    first, slab = TP * block, down_ref.shape[0]
    total_ref[...] = total[:first].reshape(total_ref.shape)
    for j in range(TP):
        up_refs[j][...] = total_ref[member ^ j].astype(bf16)
    down_ref[...] = total[first : first + slab]
    row_ref[...] = total[first + slab : first + slab + 1, :slab]


def sum_rows(plan, idx, terms, block, slab):
    lines, rows, width = terms.shape
    return pl.pallas_call(
        functools.partial(rows_kernel, plan),
        in_specs=[pl.BlockSpec(memory_space=pltpu.SMEM), pl.BlockSpec(memory_space=pltpu.VMEM)],
        out_shape=[jax.ShapeDtypeStruct((block, width), bf16)] * TP
        + [jax.ShapeDtypeStruct((slab, width), f32), jax.ShapeDtypeStruct((1, slab), f32)],
        scratch_shapes=[pltpu.VMEM((TP, block, width), f32)],
        compiler_params=small_params(),
        cost_estimate=takes(2.2),
        name="sum_rows",
    )(idx, terms)


def up_kernel(plan, idx_ref, *refs):
    part_refs, out_ref, hold_ref = refs[:TP], refs[TP], refs[TP + 1]
    member = idx_ref[0]
    for j in range(TP):
        hold_ref[member ^ j] = part_refs[j][...].astype(f32)
    slab = out_ref.shape[1] // plan.devices
    for r in range(plan.devices):
        t, copy = plan.place(r)
        out_ref[:, r * slab : (r + 1) * slab] = hold_ref[t, :, copy * slab : (copy + 1) * slab]


def join_up(plan, idx, parts, hidden):
    block, width = parts[0].shape
    return pl.pallas_call(
        functools.partial(up_kernel, plan),
        in_specs=[pl.BlockSpec(memory_space=pltpu.SMEM)]
        + [pl.BlockSpec(memory_space=pltpu.VMEM)] * TP,
        out_shape=jax.ShapeDtypeStruct((block, hidden), f32),
        scratch_shapes=[pltpu.VMEM((TP, block, width), f32)],
        compiler_params=small_params(),
        cost_estimate=takes(40),
        name="join_up",
    )(idx, *parts)


def resid_kernel(r_ref, dm_ref, vec_ref, *refs):
    part_refs, (dr_ref, da_ref, sum_ref) = refs[:TP], refs[TP:]
    total = part_refs[0][...].astype(f32)
    for j in range(1, TP):
        total += part_refs[j][...].astype(f32)
    units, rstd = unit(r_ref[...])
    dm = dm_ref[...].astype(f32)
    dr = dm + unit_back(total * vec_ref[5:6, :], units, rstd)
    da = dr.astype(bf16)
    dr_ref[...] = dr
    da_ref[...] = da
    sum_ref[...] = jnp.zeros_like(sum_ref)
    sum_ref[0:1, :] = jnp.sum(da.astype(f32), axis=0, keepdims=True)
    sum_ref[1:2, :] = jnp.sum(dm, axis=0, keepdims=True)


def resid_back(parts, r_own, dm, vecs):
    rows, width = dm.shape
    return pl.pallas_call(
        resid_kernel,
        out_shape=[
            jax.ShapeDtypeStruct((rows, width), f32),
            jax.ShapeDtypeStruct((rows, width), bf16),
            jax.ShapeDtypeStruct((8, width), f32),
        ],
        compiler_params=small_params(),
        cost_estimate=takes(2.7),
        name="resid_back",
    )(r_own, dm, vecs, *parts)


def output_kernel(r_ref, vec_ref, *refs):
    total = r_ref[...] + vec_ref[7:8, :]
    for ref in refs[:TP]:
        total += ref[...].astype(f32)
    refs[TP][...] = total.astype(bf16)


def finish_output(parts, r_own, vecs):
    return pl.pallas_call(
        output_kernel,
        out_shape=jax.ShapeDtypeStruct(r_own.shape, bf16),
        cost_estimate=takes(2.1),
        name="finish_output",
    )(r_own, vecs, *parts)


def input_kernel(x_ref, dr_ref, vec_ref, *refs):
    total = refs[0][...].astype(f32)
    for ref in refs[1:TP]:
        total += ref[...].astype(f32)
    units, rstd = unit(x_ref[...].astype(f32))
    grad = dr_ref[...] + unit_back(total * vec_ref[3:4, :], units, rstd)
    refs[TP][...] = grad.astype(bf16)


def finish_input(parts, x, dr, vecs):
    return pl.pallas_call(
        input_kernel,
        out_shape=jax.ShapeDtypeStruct(x.shape, bf16),
        compiler_params=small_params(),
        cost_estimate=takes(40),
        name="finish_input",
    )(x, dr, vecs, *parts)


def normed_kernel(plan, n_recv, idx_ref, x_ref, dq_ref, own_ref, *refs):
    recv_refs, refs = refs[:n_recv], refs[n_recv:]
    w_ref, h_ref, o_ref, da_ref, own_sum_ref, two_ref = refs[:6]
    dh_refs, refs = refs[6 : 6 + TP], refs[6 + TP :]
    g_refs, (dh_now, low_ref, sum_ref, acc_ref, vec_ref) = refs[:-5], refs[-5:]
    step = pl.program_id(0)
    member, core = idx_ref[0], idx_ref[2]
    side = lax.rem(member, 2)
    cols = dq_ref.shape[1]
    rows, width = x_ref.shape

    @pl.when(step == 0)
    def _():
        sum_ref[...] = jnp.zeros_like(sum_ref)

    grad_k, grad_v = own_ref[0], own_ref[1]
    for ref in recv_refs:
        grad_k += ref[0].astype(f32)
        grad_v += ref[1].astype(f32)
    place = step ^ (member // 2)
    low_ref[place, :, :cols] = dq_ref[...]
    low_ref[place, :, cols : 2 * cols] = grad_k.astype(bf16)
    low_ref[place, :, 2 * cols : 3 * cols] = grad_v.astype(bf16)
    low_ref[place, :, 3 * cols :] = jnp.zeros((rows, SMALLS), bf16)
    low = low_ref[place]
    grad = dot(low, w_ref[...], 1, 1)
    dh_now[...] = grad.astype(bf16).reshape(dh_now.shape)
    for i in range(2):

        @pl.when(step == i)
        def _(i=i):
            for b in range(2):
                dh_refs[2 * i + b][...] = dh_now[side ^ b]

    units, _ = unit(x_ref[...].astype(f32))
    sum_ref[0:1, :width] += jnp.sum(grad * units, axis=0, keepdims=True)
    sum_ref[1:2, :width] += jnp.sum(grad, axis=0, keepdims=True)
    sum_ref[2:3, : low.shape[1]] += jnp.sum(low.astype(f32), axis=0, keepdims=True)

    @pl.when(step == 1)
    def _():
        wide = low_ref.shape[2]
        acc_ref[:, :wide] = dot(h_ref[...], low_ref[...].reshape(2 * rows, wide), 0, 0)
        da = da_ref[...].reshape(2 * rows, cols)
        for j in range(TP):
            at = j * cols
            acc_ref[at : at + cols, wide : wide + cols] = dot(o_ref[j], da, 0, 0)
        bias_q, bias_v = sum_ref[2:3, :cols], sum_ref[2:3, 2 * cols : 3 * cols]
        zero = jnp.zeros_like(bias_q)
        vec_ref[...] = jnp.zeros_like(vec_ref)
        vectors = [
            jnp.concatenate([jnp.where(member == j, b, zero) for j in range(TP)], axis=1)
            for b in (bias_q, bias_v)
        ]
        vectors += [
            own_sum_ref[0:1, :],
            sum_ref[0:1, :],
            sum_ref[1:2, :],
            two_ref[0:1, :],
            two_ref[1:2, :],
            own_sum_ref[1:2, :],
        ]
        for j, row in enumerate(vectors):
            vec_ref[SMALLS + j : SMALLS + j + 1, :] = row
        acc_ref[:, wide + cols :] = vec_ref[...].T[:, SMALLS:]
        if not plan.fast:
            g_refs[0][...] = acc_ref[...].astype(bf16)
            return
        near, block, _ = g_refs[0].shape
        span = near // plan.size["gx"]
        for ref, owner in ((g_refs[0], core), (g_refs[1], 1 - core)):
            for n in range(near):
                gx, rest = divmod(n, span)
                at = ((gx * 2 + owner) * span + rest) * block
                ref[n] = acc_ref[pl.ds(pl.multiple_of(at, 8), block), :].astype(bf16)


def normed_back(plan, idx, x_all, dq, own, recvs, w_qkv, low, o_all, da_cols, sum_own, sum_two):
    rows, width = x_all.shape
    cols = dq.shape[1]
    wide = w_qkv.shape[1]
    total = wide + cols + SMALLS
    step = rows // 2
    one = (rows // TP, width)
    near = plan.devices // 2

    def block(i, idx):
        return (i ^ (idx[0] // 2), 0)

    pairs = pl.BlockSpec((2, step, cols), lambda i, idx: (0, i ^ (idx[0] // 2), 0))
    if plan.fast:
        sums = [(near, width // plan.devices, total)] * 2
    else:
        sums = [(width, total)]
    constants = (w_qkv, low, o_all, da_cols, sum_own, sum_two)
    return pl.pallas_call(
        functools.partial(normed_kernel, plan, len(recvs)),
        grid_spec=pltpu.PrefetchScalarGridSpec(
            num_scalar_prefetch=1,
            grid=(2,),
            in_specs=[pl.BlockSpec((step, width), block), pl.BlockSpec((step, cols), block), pairs]
            + [pairs] * len(recvs)
            + [here(v.shape) for v in constants],
            out_specs=[here(one)] * TP + [here(shape) for shape in sums],
            scratch_shapes=[
                pltpu.VMEM((2, *one), bf16),
                pltpu.VMEM((2, step, wide), bf16),
                pltpu.VMEM((8, width), f32),
                pltpu.VMEM((width, total), f32),
                pltpu.VMEM((2 * SMALLS, width), f32),
            ],
        ),
        out_shape=[jax.ShapeDtypeStruct(one, bf16)] * TP
        + [jax.ShapeDtypeStruct(shape, bf16) for shape in sums],
        compiler_params=params(),
        cost_estimate=takes(NORMED),
        name="normed_back",
    )(idx, x_all, dq, own, *recvs, *constants)


def join_kernel(keep, cols, wide, in_ref, first_ref, second_ref, *refs):
    mats, vec_refs = refs[:4], refs[4:12]
    output_ref, input_ref, turn_ref = refs[12:]
    output_ref[...] = first_ref[...]
    input_ref[...] = second_ref[...]
    groups = {}
    for n in range(in_ref.shape[0]):
        value = in_ref[n].astype(f32)
        key = keep[n]
        groups[key] = value if key not in groups else groups[key] + value
    for j in range(TP):
        for ref, at in zip(mats, (0, cols, 2 * cols, wide)):
            ref[:, j * cols : (j + 1) * cols] = groups[j][:, at : at + cols]
    total = functools.reduce(jnp.add, [groups[j] for j in range(TP)])
    block = in_ref.shape[1]
    turn_ref[...] = jnp.zeros_like(turn_ref)
    turn_ref[:block, :SMALLS] = total[:, wide + cols :]
    turned = turn_ref[...].T
    for j, ref in enumerate(vec_refs):
        ref[...] = turned[j : j + 1, :block]


def join_grads(plan, got, first, second, cols, wide):
    near, block, _ = got.shape
    members = [plan.place(plan.same(n))[0] for n in range(near)]
    width = cols * TP
    return pl.pallas_call(
        functools.partial(join_kernel, members, cols, wide),
        out_shape=[jax.ShapeDtypeStruct((block, width), f32)] * 4
        + [jax.ShapeDtypeStruct((1, block), f32)] * 8
        + [jax.ShapeDtypeStruct(first.shape, bf16)] * 2,
        scratch_shapes=[pltpu.VMEM((128, 128), f32)],
        compiler_params=small_params(),
        cost_estimate=takes(2.2),
        name="join_grads",
    )(got, first, second)


def local(
    plan, inputs, segment_ids, padding, cotangent, w_query, b_query, w_key, w_value, b_value,
    w_out, b_out, ln1_gain, ln1_shift, ln2_gain, ln2_shift, w_up, b_up, w_down, b_down,
):
    x_own = inputs[0]
    rows, width = x_own.shape
    cols = width // TP
    length = segment_ids.shape[1]
    block = w_query.shape[0]
    hidden = w_up.shape[1]
    slab = b_up.shape[0]
    size = plan.size
    member = lax.axis_index(plan.tp)
    part = lax.axis_index(plan.half)
    core = lax.axis_index("c")
    idx = jnp.stack([member, part, core, lax.axis_index("sz")]).astype(jnp.int32)
    lines = plan.copies // 2
    fast = plan.fast

    id_rows = jnp.pad(segment_ids[0].astype(bf16), (0, 8 * width - length)).reshape(8, width)
    packed = jnp.concatenate([x_own, id_rows], axis=0)
    dm_own = (cotangent[0].astype(f32) * padding[0].astype(f32)[:, None]).astype(bf16)
    dm_mine = plan.move(dm_own, plan.route)

    small = [b_query, b_value, b_out, ln1_gain, ln1_shift, ln2_gain, ln2_shift, b_down]
    if fast:
        chunk = prepare(plan, w_query, w_key, w_value, small, w_up, w_out)
        got = lax.all_to_all(chunk, plan.tp, 0, 0, tiled=True)
        moved = plan.move(packed, plan.route)
        proj, shard = shards_of(got, w_down, b_up[None], 3 * cols + SMALLS, lines)
        projs = [proj] + [plan.turn(proj, "sz", -j) for j in range(1, lines)]
        projs, moved, shard, dm_mine = lax.optimization_barrier((projs, moved, shard, dm_mine))
        x_mine = moved[:rows]
        x_all = lax.all_gather(x_mine, plan.tp, axis=0, tiled=True)
        shard = lax.all_to_all(shard, "sz", 0, 0, tiled=True)
        projs = jnp.stack(projs)
        low_one, query, kv, w_qkv, vecs = qkv(plan, idx, x_all, projs, plan.swap(projs))
    else:
        small = jnp.stack(small, axis=1)
        moved = plan.move(packed, plan.route)
        x_mine = moved[:rows]
        x_all = lax.all_gather(x_mine, plan.tp, axis=0, tiled=True)
        b_row = jnp.pad(b_up[None], ((0, 7), (0, width - slab)))
        table = [w_query, w_key, w_value, w_out, small]
        table = lax.all_gather(jnp.concatenate(table, axis=1), ALL, axis=0, tiled=True)
        vecs = table[:, 4 * width :].T.astype(f32)
        split = [lax.dynamic_slice(table, (0, i * width + member * cols), (width, cols)) for i in range(3)]
        w_qkv = jnp.concatenate([*split, jnp.zeros((width, SMALLS), bf16)], axis=1)
        out_full = table[:, 3 * width : 4 * width].reshape(TP, cols, width)
        low_one, query, kv = qkv(plan, idx, x_all, w_qkv, vecs)
        up_mine = lax.all_gather(w_up, ALL, axis=0, tiled=True)
        up_mine = up_mine.reshape(width, plan.devices, slab).transpose(1, 0, 2)
        up_mine = plan.shuffle(up_mine, ALL, plan.tp + plan.rep).reshape(TP, plan.copies, width, slab)
        up_mine = lax.dynamic_index_in_dim(up_mine, member, 0, keepdims=False)
        up_mine = up_mine.transpose(1, 0, 2).reshape(width, -1)
        downs = jnp.concatenate([w_down, b_row], axis=0)
        downs = lax.all_gather(downs, plan.rep, axis=0, tiled=False)
        down_mine = downs[:, :slab].reshape(-1, width)
        b_up_mine = downs[:, slab, :slab].reshape(1, -1).astype(f32)

    ids = moved[rows:].reshape(1, -1)[:, :length].astype(f32)

    parts = plan.parts
    kv, dm_late = lax.optimization_barrier((kv, dm_mine))
    kvs = [kv] + [plan.turn(kv, plan.half, -j) for j in range(1, parts)]
    mixed, lse = attend(idx, ids, query, kvs)
    o_all = lax.all_gather(mixed, plan.tp, axis=0, tiled=False)
    dms = plan.partners(dm_late)
    if fast:
        shard, o_all, dms = lax.optimization_barrier((shard, o_all, dms))
        weights = [shard, plan.swap(shard)]
    else:
        weights = [out_full, up_mine, down_mine, b_up_mine]
    x_same, dm_all = stage(idx, x_all, dms)
    dm_all = dm_all.reshape(TP * rows, width)
    results = mlp(plan, idx, x_same, o_all, vecs, dm_all, weights, slab)
    r_own, low_two, act, grad_pre, sum_two = results[:5]
    dh_two = results[5 : 5 + TP]
    if fast:
        out_mine, down_mine = results[5 + TP :]
    else:
        out_mine = lax.dynamic_index_in_dim(out_full, member, 0, keepdims=False)

    back_two = plan.reduce(dh_two)
    if fast:
        near_terms, far_terms, *out_terms = mlp_weight_grads(
            plan, idx, low_two, grad_pre, act, dm_all, down_mine
        )
        back_two, out_terms, far_terms = lax.optimization_barrier((back_two, out_terms, far_terms))
    else:
        up_terms = dot(low_two, grad_pre, 0, 0).astype(bf16)
        down_terms = dot(act, dm_all, 0, 0).astype(bf16)
        row = jnp.sum(grad_pre.astype(f32), axis=0).astype(bf16)
        out_terms = dot(act, down_mine).astype(bf16).reshape(TP, rows, width)
        out_terms = [
            lax.dynamic_index_in_dim(out_terms, member ^ j, 0, keepdims=False) for j in range(TP)
        ]
    dr, da, sum_own = resid_back(back_two, r_own, dm_mine, vecs)
    if fast:
        terms = add(near_terms, plan.swap(far_terms), after=(da,))
        das = plan.partners(da)
        after = [terms]
        terms = lax.all_to_all(terms, "sz", 0, 0, tiled=True)
        *ups, g_w_down, g_b_up = sum_rows(plan, idx, terms, block, slab)
    else:
        das = plan.partners(da)
        after = []
        row = jnp.pad(row.reshape(plan.copies, 1, slab), ((0, 0), (0, 7), (0, width - slab)))
        downs = jnp.concatenate([down_terms.reshape(plan.copies, slab, width), row], axis=1)
        downs = lax.psum_scatter(downs, plan.rep, scatter_dimension=0, tiled=False)
        g_w_down = downs[:slab].astype(f32)
        g_b_up = downs[slab, :slab].astype(f32)
        ups = plan.shuffle(up_terms.reshape(plan.devices, block, -1), ALL, plan.rep + plan.tp)
        ups = ups.reshape(plan.copies, TP * block, -1)
        ups = lax.psum_scatter(ups, plan.rep, scatter_dimension=0, tiled=False)
        ups = lax.all_to_all(ups.reshape(TP, block, -1), plan.tp, 0, 0, tiled=True).astype(f32)
    grad_query, kv_own, da_cols, *kv_others = attend_back(
        idx, ids, query, das, after, out_mine, lse, kvs
    )
    kv_others, out_parts = lax.optimization_barrier((kv_others, plan.reduce(out_terms)))
    recvs = [plan.turn(kv_others[j - 1], plan.half, j) for j in range(1, parts)]
    results = normed_back(
        plan, idx, x_all, grad_query, kv_own, recvs, w_qkv, low_one, o_all, da_cols, sum_own, sum_two
    )
    back_one, terms = plan.reduce(results[:TP]), results[TP:]
    if fast:
        keep, send = terms
        terms = add(keep, plan.swap(send))
        terms, ups = lax.optimization_barrier((terms, ups))
        got = lax.all_to_all(terms, SAME, 0, 0, tiled=True)
    else:
        terms = plan.shuffle(terms[0].reshape(plan.devices, block, -1), ALL, ("c",) + SAME)
        terms = terms.reshape(2, -1, *terms.shape[1:])
        keep, send = jnp.where(core == 0, terms, terms[::-1])
        got = lax.all_to_all(add(keep, plan.swap(send)), SAME, 0, 0, tiled=True)
    if fast:
        g_w_up = join_up(plan, idx, plan.reduce(ups), hidden)
        g_b_up = g_b_up[0]
    else:
        ups = ups.reshape(TP, block, plan.copies, slab).transpose(0, 2, 1, 3)
        ups = plan.shuffle(ups.reshape(plan.devices, block, slab), plan.tp + plan.rep, ALL)
        g_w_up = ups.transpose(1, 0, 2).reshape(block, hidden)
    g_w_down, out_parts = lax.optimization_barrier((g_w_down, out_parts))
    output = plan.move(finish_output(out_parts, r_own, vecs), plan.back)
    grad_input = plan.move(finish_input(back_one, x_mine, dr, vecs), plan.back)
    joined = join_grads(plan, got, output, grad_input, cols, w_qkv.shape[1])
    g_query, g_key, g_value, g_out, *vec, output, grad_input = joined
    vec = [v[0] for v in vec]
    return (
        output[None],
        grad_input[None],
        g_query,
        vec[0],
        g_key,
        g_value,
        vec[1],
        g_out,
        vec[2],
        vec[3],
        vec[4],
        vec[5],
        vec[6],
        g_w_up,
        g_b_up,
        g_w_down,
        vec[7],
    )


def solution(mesh):
    groups, blocks = mesh.shape["grp"], mesh.shape["seq"]
    plan = Plan(groups, blocks)
    fine = Mesh(mesh.devices.reshape(plan.shape), ALL)
    grp, seq = ("gx", "c"), ("sz", "sy")
    matrix, vector = P(ALL, None), P(ALL)
    token = P(grp, seq, None)
    return jax.shard_map(
        functools.partial(local, plan),
        mesh=fine,
        in_specs=(
            token, P(grp, None), P(grp, seq), token,
            matrix, vector, matrix, matrix, vector, matrix, vector,
            vector, vector, vector, vector, matrix, vector, matrix, vector,
        ),
        out_specs=(
            token, token,
            matrix, vector, matrix, matrix, vector, matrix, vector,
            vector, vector, vector, vector, matrix, vector, matrix, vector,
        ),
        check_vma=False,
    )
```

```python
import functools

import jax
import jax.numpy as jnp
from jax import lax
from jax.experimental import pallas as pl
from jax.experimental.pallas import tpu as pltpu
from jax.sharding import Mesh, PartitionSpec as P

HEADS = 12
HEAD_DIM = 64
TP = 4
HEADS_TP = HEADS // TP
EPS = 1e-05
NEG = -1e30
SCALE = 0.125
ALL = ("gx", "c", "sz", "sy")
SAME = ("gx", "sz", "sy")
SMALLS = 64
NORMED = 13.0
f32 = jnp.float32
bf16 = jnp.bfloat16


class Plan:
    def __init__(self, groups, blocks):
        if (groups, blocks) == (4, 8):
            self.shape = (2, 2, 4, 2)
            self.tp, self.half, self.rep = ("gx", "sy"), "c", ("c", "sz")
            self.fast = True
        else:
            self.shape = (groups // 2, 2, blocks // TP, TP)
            self.tp, self.half, self.rep = ("sy",), "sz", ("gx", "c", "sz")
            self.fast = False
        self.size = dict(zip(ALL, self.shape))
        self.devices = groups * blocks
        self.parts = self.size[self.half]
        self.copies = self.devices // TP
        self.lines = tuple(a for a in self.rep if a != "c")
        self.route = []
        for src in range(self.devices):
            seq, block = divmod(src, blocks)
            part, member = divmod(block, TP)
            if self.tp == ("sy",):
                dst = src
            else:
                dst = (((member >> 1) * 2 + part) * 4 + seq) * 2 + (member & 1)
            self.route.append((src, dst))
        self.back = [(dst, src) for src, dst in self.route]

    def swap(self, value):
        return lax.ppermute(value, "c", [(0, 1), (1, 0)])

    def gather(self, value):
        return lax.all_to_all(
            jnp.broadcast_to(value, (TP, *value.shape)), self.tp, 0, 0, tiled=True
        )

    def partner(self, value, j):
        table = [(t, t ^ j) for t in range(TP)]
        return lax.ppermute(value, self.tp, table)

    def partners(self, value):
        return [value] + [self.partner(value, j) for j in range(1, TP)]

    def reduce(self, values):
        return [values[0]] + [self.partner(values[j], j) for j in range(1, TP)]

    def turn(self, value, axis, by):
        count = self.size[axis]
        return lax.ppermute(value, axis, [(i, (i + by) % count) for i in range(count)])

    def place(self, r):
        at, rest = {}, r
        for axis in reversed(ALL):
            rest, at[axis] = divmod(rest, self.size[axis])
        numbers = []
        for axes in (self.tp, self.rep):
            number = 0
            for axis in axes:
                number = number * self.size[axis] + at[axis]
            numbers.append(number)
        return tuple(numbers)

    def same(self, n):
        span = self.devices // 2 // self.size["gx"]
        gx, rest = divmod(n, span)
        return gx * 2 * span + rest

    def move(self, value, table):
        if all(a == b for a, b in table):
            return value
        return lax.ppermute(value, ALL, table)

    def shuffle(self, value, before, after):
        tail = value.shape[1:]
        dims = [self.size[a] for a in before]
        order = [before.index(a) for a in after]
        value = value.reshape(*dims, *tail)
        value = value.transpose(*order, *range(len(dims), len(dims) + len(tail)))
        return value.reshape(-1, *tail)


def dot(left, right, left_dim=1, right_dim=0):
    return lax.dot_general(
        left, right, (((left_dim,), (right_dim,)), ((), ())), preferred_element_type=f32
    )


def unit(values):
    center = values - jnp.mean(values, axis=-1, keepdims=True)
    variance = jnp.mean(center * center, axis=-1, keepdims=True)
    rstd = lax.rsqrt(variance + EPS)
    return center * rstd, rstd


def unit_back(grad_unit, units, rstd):
    first = jnp.mean(grad_unit, axis=-1, keepdims=True)
    second = jnp.mean(grad_unit * units, axis=-1, keepdims=True)
    return rstd * (grad_unit - first - units * second)


def params(limit=14 * 1024 * 1024, axes=1):
    return pltpu.CompilerParams(
        dimension_semantics=("arbitrary",) * axes, vmem_limit_bytes=limit
    )


def small_params():
    return pltpu.CompilerParams(vmem_limit_bytes=8 * 1024 * 1024)


def takes(microseconds):
    return pl.CostEstimate(
        flops=int(microseconds * 0.2 * 1.15e9),
        bytes_accessed=int(microseconds * 3.69e6),
        transcendentals=0,
    )


def whole(shape):
    zeros = (0,) * len(shape)
    return pl.BlockSpec(shape, lambda *_: zeros)


def here(shape):
    return pl.BlockSpec(memory_space=pltpu.VMEM)


def head_lanes(value, head):
    lane = lax.broadcasted_iota(jnp.int32, value.shape, 1)
    keep = (lane >= head * HEAD_DIM) & (lane < (head + 1) * HEAD_DIM)
    return jnp.where(keep, value, jnp.zeros_like(value))


def member_cols(row, member, cols):
    out = jnp.zeros((row.shape[0], cols), row.dtype)
    for j in range(TP):
        out = jnp.where(member == j, row[:, j * cols : (j + 1) * cols], out)
    return out


def prep_kernel(rep_of, q_ref, k_ref, v_ref, up_ref, out_ref, *refs):
    small_refs, chunk_ref, turn_ref = refs[:-2], refs[-2], refs[-1]
    block, width = q_ref.shape
    cols = width // TP
    wide = 3 * cols + SMALLS
    slab = up_ref.shape[1] // len(rep_of)
    turn_ref[...] = jnp.zeros_like(turn_ref)
    for j, ref in enumerate(small_refs):
        turn_ref[j : j + 1, :block] = ref[...].astype(f32)
    small = turn_ref[...].T[:block, :SMALLS]
    for j in range(TP):
        at = slice(j * cols, (j + 1) * cols)
        chunk_ref[j, :, :wide] = jnp.concatenate(
            [r[:, at].astype(f32) for r in (q_ref, k_ref, v_ref)] + [small], axis=1
        ).astype(bf16)
        chunk_ref[j, :, wide + width :] = out_ref[...]
    for r, (member, copy) in enumerate(rep_of):
        first = wide + copy * slab
        chunk_ref[member, :, first : first + slab] = up_ref[:, r * slab : (r + 1) * slab]


def prepare(plan, w_query, w_key, w_value, small, w_up, w_out):
    block, width = w_query.shape
    rep_of = [plan.place(r) for r in range(plan.devices)]
    wide = 3 * width // TP + SMALLS
    return pl.pallas_call(
        functools.partial(prep_kernel, rep_of),
        out_shape=jax.ShapeDtypeStruct((TP, block, wide + w_up.shape[1] // TP + width), bf16),
        scratch_shapes=[pltpu.VMEM((128, 128), f32)],
        cost_estimate=takes(1.9),
        name="prepare",
    )(w_query, w_key, w_value, w_up, w_out, *[v[None] for v in small])


def shards_kernel(wide, got_ref, down_ref, row_ref, proj_ref, shard_ref):
    block = got_ref.shape[1]
    slab, width = down_ref.shape
    first = TP * block
    for t in range(TP):
        at = t * block
        proj_ref[at : at + block, :] = got_ref[t, :, :wide]
        up = got_ref[t, :, wide : wide + width]
        out = got_ref[t, :, wide + width :]
        for n in range(shard_ref.shape[0]):
            shard_ref[n, at : at + block, :] = up
            shard_ref[n, first + at : first + at + block, :] = out
    row = jnp.concatenate([row_ref[...].astype(f32), jnp.zeros((1, width - slab), f32)], axis=1)
    row = jnp.broadcast_to(row, (8, width)).astype(bf16)
    for n in range(shard_ref.shape[0]):
        shard_ref[n, 2 * first : 2 * first + slab, :] = down_ref[...]
        shard_ref[n, 2 * first + slab :, :] = row


def shards_of(got, w_down, b_row, wide, lines):
    _, block, _ = got.shape
    slab, width = w_down.shape
    return pl.pallas_call(
        functools.partial(shards_kernel, wide),
        out_shape=[
            jax.ShapeDtypeStruct((TP * block, wide), bf16),
            jax.ShapeDtypeStruct((lines, 2 * TP * block + slab + 8, width), bf16),
        ],
        compiler_params=small_params(),
        cost_estimate=takes(2.4),
        name="shards_of",
    )(got, w_down, b_row)


def qkv_kernel(plan, idx_ref, x_ref, *refs):
    fast = plan.fast
    if fast:
        own_ref, other_ref, h_ref, q_ref, kv_ref, w_ref, vec_ref, wide_ref = refs
    else:
        w_ref, vec_ref, h_ref, q_ref, kv_ref = refs
    cols = q_ref.shape[1]
    if fast:

        @pl.when(pl.program_id(0) == 0)
        def _():
            core = idx_ref[2]
            line = idx_ref[3]
            lines, rows, _ = own_ref.shape
            pair = rows // plan.size["gx"]
            for ref, side in ((own_ref, core), (other_ref, 1 - core)):
                for j in range(lines):
                    z = lax.rem(line + j, lines)
                    value = ref[j].astype(f32)
                    for gx in range(plan.size["gx"]):
                        wide_ref[gx * 2 + side, z] = value[gx * pair : (gx + 1) * pair, :]
            table = wide_ref[...].reshape(w_ref.shape)
            w_ref[...] = table.astype(bf16)
            vec_ref[...] = table[:, 512:640].T[64:72, :]

    units, _ = unit(x_ref[...].astype(f32))
    low = (units * vec_ref[3:4, :] + vec_ref[4:5, :]).astype(bf16)
    h_ref[...] = low
    out = dot(low, w_ref[...])
    bias = member_cols(vec_ref[0:2, :], idx_ref[0], cols)
    query = (out[:, :cols] + bias[0:1, :]).astype(bf16)
    q_ref[...] = (query.astype(f32) * SCALE).astype(bf16)
    kv_ref[0] = out[:, cols : 2 * cols].astype(bf16)
    kv_ref[1] = (out[:, 2 * cols : 3 * cols] + bias[1:2, :]).astype(bf16)


def qkv(plan, idx, x_all, *operands):
    rows, width = x_all.shape
    cols = width // TP
    step = rows // 2
    wide = 3 * cols + SMALLS
    out_specs = [
        pl.BlockSpec((step, width), lambda i, *_: (i, 0)),
        pl.BlockSpec((step, cols), lambda i, *_: (i, 0)),
        pl.BlockSpec((2, step, cols), lambda i, *_: (0, i, 0)),
    ]
    out_shape = [
        jax.ShapeDtypeStruct((rows, width), bf16),
        jax.ShapeDtypeStruct((rows, cols), bf16),
        jax.ShapeDtypeStruct((2, rows, cols), bf16),
    ]
    scratch = []
    if plan.fast:
        out_specs += [here((width, wide)), here((8, width))]
        out_shape += [
            jax.ShapeDtypeStruct((width, wide), bf16),
            jax.ShapeDtypeStruct((8, width), f32),
        ]
        lines = plan.copies // 2
        scratch = [pltpu.VMEM((2 * plan.size["gx"], lines, width // (2 * plan.size["gx"] * lines), wide), f32)]
    return pl.pallas_call(
        functools.partial(qkv_kernel, plan),
        grid_spec=pltpu.PrefetchScalarGridSpec(
            num_scalar_prefetch=1,
            grid=(2,),
            in_specs=[pl.BlockSpec((step, width), lambda i, *_: (i, 0))]
            + [here(v.shape) for v in operands],
            out_specs=out_specs,
            scratch_shapes=scratch,
        ),
        out_shape=out_shape,
        compiler_params=params(),
        cost_estimate=takes(4.8),
        name="qkv",
    )(idx, x_all, *operands)


def fill_docs(ids_ref, part, parts, doc_ref):
    span, width = doc_ref.shape[1:]
    for j in range(parts):
        at = lax.rem(part + j, parts) * span
        row = ids_ref[0:1, pl.ds(pl.multiple_of(at, 512), span)]
        doc_ref[j] = jnp.broadcast_to(row, (width, span)).T


def fwd_kernel(parts, idx_ref, ids_ref, q_ref, *refs):
    kv_refs = refs[:parts]
    o_ref, lse_ref, turned, doc_ref = refs[parts:]
    step = pl.program_id(0)
    part = idx_ref[1]
    span = kv_refs[0].shape[1]
    width = q_ref.shape[0]

    @pl.when(step == 0)
    def _():
        fill_docs(ids_ref, part, parts, doc_ref)
        for j in range(parts):
            turned[j] = kv_refs[j][1].T

    at = part * span + step * width
    own = ids_ref[0:1, pl.ds(pl.multiple_of(at, 128), width)]
    query = q_ref[...]
    outs, lses = [], []
    for head in range(HEADS_TP):
        masked = head_lanes(query, head)
        scores = []
        for j in range(parts):
            raw = dot(kv_refs[j][0], masked, 1, 1)
            scores.append(jnp.where(doc_ref[j] == own, raw, NEG))
        peak = functools.reduce(
            jnp.maximum, [jnp.max(s, axis=0, keepdims=True) for s in scores]
        )
        exps = [jnp.exp(s - peak) for s in scores]
        total = functools.reduce(jnp.add, [jnp.sum(e, axis=0, keepdims=True) for e in exps])
        scale = 1.0 / total
        acc = None
        for j in range(parts):
            probs = (exps[j] * scale).astype(bf16)
            term = dot(turned[j, head * HEAD_DIM : (head + 1) * HEAD_DIM, :], probs)
            acc = term if acc is None else acc + term
        outs.append(acc)
        lses.append(peak + jnp.log(total))
    o_ref[...] = jnp.concatenate(outs, axis=0).T.astype(bf16)
    for head in range(HEADS_TP):
        lse_ref[head : head + 1, :] = lses[head]


def attend(idx, ids, q, kvs, width=512):
    rows, cols = q.shape
    parts = len(kvs)
    span = kvs[0].shape[1]
    return pl.pallas_call(
        functools.partial(fwd_kernel, parts),
        grid_spec=pltpu.PrefetchScalarGridSpec(
            num_scalar_prefetch=1,
            grid=(rows // width,),
            in_specs=[here(ids.shape), pl.BlockSpec((width, cols), lambda i, *_: (i, 0))]
            + [here(kv.shape) for kv in kvs],
            out_specs=[
                pl.BlockSpec((width, cols), lambda i, *_: (i, 0)),
                pl.BlockSpec((8, width), lambda i, *_: (0, i)),
            ],
            scratch_shapes=[
                pltpu.VMEM((parts, cols, span), bf16),
                pltpu.VMEM((parts, span, width), f32),
            ],
        ),
        out_shape=[
            jax.ShapeDtypeStruct((rows, cols), bf16),
            jax.ShapeDtypeStruct((8, rows), f32),
        ],
        compiler_params=params(parts * 10 * 1024 * 1024),
        cost_estimate=takes(7.1),
        name="attend",
    )(idx, ids, q, *kvs)


def bwd_kernel(parts, waits, idx_ref, ids_ref, q_ref, w_ref, lse_ref, *refs):
    da_refs, refs = refs[:TP], refs[TP + waits :]
    kv_refs = refs[:parts]
    dq_ref, own_ref, cols_ref = refs[parts : parts + 3]
    other_refs = refs[parts + 3 : 2 * parts + 2]
    turned, doc_ref, key_acc, value_acc, mixed_ref = refs[2 * parts + 2 :]
    step = pl.program_id(0)
    part = idx_ref[1]
    span = kv_refs[0].shape[1]
    width, cols = q_ref.shape

    @pl.when(step == 0)
    def _():
        fill_docs(ids_ref, part, parts, doc_ref)
        for j in range(parts):
            turned[j] = kv_refs[j][0].T
        key_acc[...] = jnp.zeros_like(key_acc)
        value_acc[...] = jnp.zeros_like(value_acc)
        member = idx_ref[0]
        for j in range(TP):
            da = da_refs[j][...]
            mixed_ref[member ^ j] = dot(da, w_ref[...], 1, 1).astype(bf16)
            cols_ref[member ^ j] = member_cols(da, member, cols)

    at = part * span + step * width
    own = ids_ref[0:1, pl.ds(pl.multiple_of(at, 128), width)]
    query = q_ref[...]
    group = width // mixed_ref.shape[1]
    grad_mixed = mixed_ref[pl.ds(step * group, group)].reshape(width, cols)
    turned_grads = []
    for head in range(HEADS_TP):
        masked_q = head_lanes(query, head)
        masked_g = head_lanes(grad_mixed, head)
        lse = lse_ref[head : head + 1, :]
        probs, grads = [], []
        for j in range(parts):
            raw = dot(kv_refs[j][0], masked_q, 1, 1)
            probs.append(jnp.exp(jnp.where(doc_ref[j] == own, raw, NEG) - lse))
            grads.append(dot(kv_refs[j][1], masked_g, 1, 1))
        delta = functools.reduce(
            jnp.add,
            [jnp.sum(p * g, axis=0, keepdims=True) for p, g in zip(probs, grads)],
        )
        acc = None
        for j in range(parts):
            grad_scores = (probs[j] * (grads[j] - delta)).astype(bf16)
            value_acc[j] += dot(probs[j].astype(bf16), masked_g)
            key_acc[j] += dot(grad_scores, masked_q)
            term = dot(turned[j, head * HEAD_DIM : (head + 1) * HEAD_DIM, :], grad_scores)
            acc = term if acc is None else acc + term
        turned_grads.append(acc)
    dq_ref[...] = (jnp.concatenate(turned_grads, axis=0).T * SCALE).astype(bf16)

    @pl.when(step == pl.num_programs(0) - 1)
    def _():
        own_ref[0] = key_acc[0]
        own_ref[1] = value_acc[0]
        for j in range(1, parts):
            other_refs[j - 1][0] = key_acc[j].astype(bf16)
            other_refs[j - 1][1] = value_acc[j].astype(bf16)


def attend_back(idx, ids, q, das, after, w_out, lse, kvs, width=512):
    rows, cols = q.shape
    step, model = das[0].shape
    parts = len(kvs)
    span = kvs[0].shape[1]
    return pl.pallas_call(
        functools.partial(bwd_kernel, parts, len(after)),
        grid_spec=pltpu.PrefetchScalarGridSpec(
            num_scalar_prefetch=1,
            grid=(rows // width,),
            in_specs=[
                whole(ids.shape),
                pl.BlockSpec((width, cols), lambda i, *_: (i, 0)),
                whole((cols, model)),
                pl.BlockSpec((8, width), lambda i, *_: (0, i)),
            ]
            + [here((step, model))] * TP
            + [pl.BlockSpec(memory_space=pl.ANY)] * len(after)
            + [whole(kv.shape) for kv in kvs],
            out_specs=[
                pl.BlockSpec((width, cols), lambda i, *_: (i, 0)),
                here((2, span, cols)),
                here((TP, step, cols)),
            ]
            + [here((2, span, cols))] * (parts - 1),
            scratch_shapes=[
                pltpu.VMEM((parts, cols, span), bf16),
                pltpu.VMEM((parts, span, width), f32),
                pltpu.VMEM((parts, span, cols), f32),
                pltpu.VMEM((parts, span, cols), f32),
                pltpu.VMEM((TP, step, cols), bf16),
            ],
        ),
        out_shape=[
            jax.ShapeDtypeStruct((rows, cols), bf16),
            jax.ShapeDtypeStruct((2, span, cols), f32),
            jax.ShapeDtypeStruct((TP, step, cols), bf16),
        ]
        + [jax.ShapeDtypeStruct((2, span, cols), bf16)] * (parts - 1),
        compiler_params=params(parts * 12 * 1024 * 1024),
        cost_estimate=takes(10.7),
        name="attend_back",
    )(idx, ids, q, w_out, lse, *das, *after, *kvs)


def stage_kernel(idx_ref, x_ref, *refs):
    same_ref, dm_ref = refs[TP:]
    same_ref[...] = x_ref[...]
    for j in range(TP):
        dm_ref[idx_ref[0] ^ j] = refs[j][...]


def stage(idx, x_all, dms):
    return pl.pallas_call(
        stage_kernel,
        in_specs=[pl.BlockSpec(memory_space=pltpu.SMEM)]
        + [pl.BlockSpec(memory_space=pltpu.VMEM)] * (1 + TP),
        out_shape=[
            jax.ShapeDtypeStruct(x_all.shape, bf16),
            jax.ShapeDtypeStruct((TP, *dms[0].shape), bf16),
        ],
        compiler_params=small_params(),
        cost_estimate=takes(1.5),
        name="stage",
    )(idx, x_all, *dms)


def mlp_kernel(plan, idx_ref, x_ref, o_ref, vec_ref, dm_ref, *refs):
    step = pl.program_id(0)
    side = lax.rem(idx_ref[0], 2)
    if plan.fast:
        own_ref, other_ref, r_ref, h_ref, a_ref, du_ref, sum_ref = refs[:7]
        dh_refs = refs[7 : 7 + TP]
        out_ref, down_ref, r_now, dh_now, held, held_down, held_row = refs[7 + TP :]

        @pl.when(step == 0)
        def _():
            core = idx_ref[2]
            first = held.shape[3] * plan.size["gx"]
            pair = held.shape[3]
            slab = held_down.shape[2]
            rows = []
            for z in range(held.shape[2]):
                for ref, owner in ((own_ref, core), (other_ref, 1 - core)):
                    for gx in range(plan.size["gx"]):
                        at = gx * pair
                        held[0, gx * 2 + owner, z] = ref[z, at : at + pair, :]
                        held[1, gx * 2 + owner, z] = ref[z, first + at : first + at + pair, :]
                    held_down[owner, z] = ref[z, 2 * first : 2 * first + slab, :]
            for owner in range(2):
                for z in range(held.shape[2]):
                    at = 2 * first + slab
                    row = jnp.where(
                        core == owner,
                        own_ref[z, at : at + 8, :].astype(f32),
                        other_ref[z, at : at + 8, :].astype(f32),
                    )
                    rows.append(row[0:1, :slab])
            held_row[...] = jnp.concatenate(rows, axis=1)
            out = held[1, idx_ref[0]]
            out_ref[...] = out.reshape(out_ref.shape)
            down_ref[...] = held_down[...].reshape(down_ref.shape)

        width = held.shape[-1]
        w_up = held[0].reshape(-1, width)
        outs = [held[1, j].reshape(-1, width) for j in range(TP)]
        w_down = held_down[...].reshape(-1, width)
        b_up = held_row[...]
    else:
        wo_ref, wu_ref, wd_ref, bup_ref, r_ref, h_ref, a_ref, du_ref, sum_ref = refs[:9]
        dh_refs, r_now, dh_now = refs[9 : 9 + TP], refs[-2], refs[-1]
        w_up, w_down, b_up = wu_ref[...], wd_ref[...], bup_ref[...]
        outs = [wo_ref[j] for j in range(TP)]

    @pl.when(step == 0)
    def _():
        sum_ref[...] = jnp.zeros_like(sum_ref)

    attended = dot(o_ref[0], outs[0])
    for j in range(1, TP):
        attended += dot(o_ref[j], outs[j])
    residual = x_ref[...].astype(f32) + (attended + vec_ref[2:3, :])

    @pl.when(step == 0)
    def _():
        r_now[...] = residual.reshape(r_now.shape)
        r_ref[...] = r_now[side]

    units, _ = unit(residual)
    low = (units * vec_ref[5:6, :] + vec_ref[6:7, :]).astype(bf16)
    h_ref[...] = low
    pre = dot(low, w_up) + b_up
    normal = 0.5 * (1.0 + lax.erf(pre * 0.7071067811865476))
    act = (pre * normal).astype(bf16)
    a_ref[...] = act
    slope = normal + pre * (0.3989422804014327 * jnp.exp(-0.5 * pre * pre))
    dm = dm_ref[...]
    grad_pre = (dot(dm, w_down, 1, 1) * slope).astype(bf16)
    du_ref[...] = grad_pre
    grad = dot(grad_pre, w_up, 1, 1)
    sum_ref[0:1, :] += jnp.sum(grad * units, axis=0, keepdims=True)
    sum_ref[1:2, :] += jnp.sum(grad, axis=0, keepdims=True)
    dh_now[...] = grad.astype(bf16).reshape(dh_now.shape)
    for i in range(2):

        @pl.when(step == i)
        def _(i=i):
            for b in range(2):
                dh_refs[2 * i + b][...] = dh_now[side ^ b]


def mlp(plan, idx, x_all, o_all, vecs, dm_all, weights, slab):
    rows, width = x_all.shape
    hidden = plan.copies * slab
    cols = width // TP
    step = rows // 2

    def block(i, idx):
        return (i ^ (idx[0] // 2), 0)

    token = pl.BlockSpec((step, width), block)
    inner = pl.BlockSpec((step, hidden), block)
    one = here((rows // TP, width))
    now = (2, rows // TP, width)
    out_specs = [one, token, inner, inner, here((8, width))] + [one] * TP
    out_shape = [
        jax.ShapeDtypeStruct((rows // TP, width), f32),
        jax.ShapeDtypeStruct((rows, width), bf16),
        jax.ShapeDtypeStruct((rows, hidden), bf16),
        jax.ShapeDtypeStruct((rows, hidden), bf16),
        jax.ShapeDtypeStruct((8, width), f32),
    ] + [jax.ShapeDtypeStruct((rows // TP, width), bf16)] * TP
    scratch = [pltpu.VMEM(now, f32), pltpu.VMEM(now, bf16)]
    if plan.fast:
        lines = plan.copies // 2
        gx = plan.size["gx"]
        out_specs += [here((cols, width)), here((hidden, width))]
        out_shape += [
            jax.ShapeDtypeStruct((cols, width), bf16),
            jax.ShapeDtypeStruct((hidden, width), bf16),
        ]
        scratch += [
            pltpu.VMEM((2, 2 * gx, lines, width // (2 * gx * lines), width), bf16),
            pltpu.VMEM((2, lines, slab, width), bf16),
            pltpu.VMEM((1, hidden), f32),
        ]
    return pl.pallas_call(
        functools.partial(mlp_kernel, plan),
        grid_spec=pltpu.PrefetchScalarGridSpec(
            num_scalar_prefetch=1,
            grid=(2,),
            in_specs=[
                token,
                pl.BlockSpec((TP, step, cols), lambda i, idx: (0, i ^ (idx[0] // 2), 0)),
                here(vecs.shape),
                token,
            ]
            + [here(v.shape) for v in weights],
            out_specs=out_specs,
            scratch_shapes=scratch,
        ),
        out_shape=out_shape,
        compiler_params=params(),
        cost_estimate=takes(10.5),
        name="mlp",
    )(idx, x_all, o_all, vecs, dm_all, *weights)


def pair_kernel(plan, idx_ref, h_ref, du_ref, a_ref, dm_ref, wd_ref, near_ref, far_ref, *refs):
    out_refs, acc_ref, wide_ref = refs[:TP], refs[TP], refs[TP + 1]
    lines = plan.copies // 2
    step = pl.program_id(0)
    member, core = idx_ref[0], idx_ref[2]
    half = step ^ core
    grad_pre = du_ref[...]
    act = a_ref[...]
    width = h_ref.shape[1]
    block = width // plan.devices
    size = act.shape[1]
    slab = size // lines
    first = TP * block
    up = dot(h_ref[...], grad_pre, 0, 0)
    down = dot(act, dm_ref[...], 0, 0)
    bias = jnp.sum(grad_pre.astype(f32), axis=0, keepdims=True)
    term = dot(act, wd_ref[...])

    @pl.when(step == 0)
    def _():
        acc_ref[...] = term.reshape(acc_ref.shape)
        wide_ref[:, :size] = up

    @pl.when(step == 1)
    def _():
        acc_ref[...] += term.reshape(acc_ref.shape)
        for j in range(TP):
            out_refs[j][...] = acc_ref[member ^ j].astype(bf16)
        wide_ref[:, size:] = up
        pair = plan.size["sy"] * block
        for ref, owner in ((near_ref, core), (far_ref, 1 - core)):
            for z in range(lines):
                for gx in range(plan.size["gx"]):
                    at = ((gx * 2 + owner) * lines + z) * pair
                    value = wide_ref[pl.ds(pl.multiple_of(at, 16), pair), :]
                    ref[z, gx * pair : (gx + 1) * pair, :] = value.astype(bf16)

    def put(ref):
        for k in range(lines):
            at = k * slab
            row = jnp.concatenate(
                [bias[:, at : at + slab], jnp.zeros((1, width - slab), f32)], axis=1
            )
            ref[k, first : first + slab, :] = down[at : at + slab, :].astype(bf16)
            ref[k, first + slab :, :] = jnp.broadcast_to(row, (8, width)).astype(bf16)

    @pl.when(half == 0)
    def _():
        put(near_ref)

    @pl.when(half == 1)
    def _():
        put(far_ref)


def mlp_weight_grads(plan, idx, low, grad_pre, act, dm_all, w_down):
    rows, width = low.shape
    hidden = act.shape[1]
    step = hidden // 2
    lines = plan.copies // 2
    block = width // plan.devices
    slab = hidden // plan.copies
    bundle = (lines, TP * block + slab + 8, width)
    token = (rows // TP, width)
    return pl.pallas_call(
        functools.partial(pair_kernel, plan),
        grid_spec=pltpu.PrefetchScalarGridSpec(
            num_scalar_prefetch=1,
            grid=(2,),
            in_specs=[
                here((rows, width)),
                pl.BlockSpec((rows, step), lambda i, idx: (0, i)),
                pl.BlockSpec((rows, step), lambda i, idx: (0, i)),
                here((rows, width)),
                pl.BlockSpec((step, width), lambda i, idx: (i, 0)),
            ],
            out_specs=[here(bundle)] * 2 + [here(token)] * TP,
            scratch_shapes=[
                pltpu.VMEM((TP, *token), f32),
                pltpu.VMEM((width, hidden), f32),
            ],
        ),
        out_shape=[jax.ShapeDtypeStruct(bundle, bf16)] * 2
        + [jax.ShapeDtypeStruct(token, bf16)] * TP,
        compiler_params=params(),
        cost_estimate=takes(7.6),
        name="mlp_weight_grads",
    )(idx, low, grad_pre, act, dm_all, w_down)


def add_kernel(count, *refs):
    total = refs[0][...].astype(f32)
    for ref in refs[1:count]:
        total += ref[...].astype(f32)
    refs[-1][...] = total.astype(bf16)


def add(*values, after=()):
    return pl.pallas_call(
        functools.partial(add_kernel, len(values)),
        in_specs=[pl.BlockSpec(memory_space=pltpu.VMEM)] * len(values)
        + [pl.BlockSpec(memory_space=pl.ANY)] * len(after),
        out_shape=jax.ShapeDtypeStruct(values[0].shape, bf16),
        compiler_params=small_params(),
        cost_estimate=takes(2.6),
        name="add",
    )(*values, *after)


def rows_kernel(plan, idx_ref, *refs):
    term_ref, up_refs = refs[0], refs[1 : 1 + TP]
    down_ref, row_ref, total_ref = refs[1 + TP :]
    member = idx_ref[0]
    total = term_ref[0].astype(f32)
    for z in range(1, term_ref.shape[0]):
        total += term_ref[z].astype(f32)
    block = up_refs[0].shape[0]
    first, slab = TP * block, down_ref.shape[0]
    total_ref[...] = total[:first].reshape(total_ref.shape)
    for j in range(TP):
        up_refs[j][...] = total_ref[member ^ j].astype(bf16)
    down_ref[...] = total[first : first + slab]
    row_ref[...] = total[first + slab : first + slab + 1, :slab]


def sum_rows(plan, idx, terms, block, slab):
    lines, rows, width = terms.shape
    return pl.pallas_call(
        functools.partial(rows_kernel, plan),
        in_specs=[pl.BlockSpec(memory_space=pltpu.SMEM), pl.BlockSpec(memory_space=pltpu.VMEM)],
        out_shape=[jax.ShapeDtypeStruct((block, width), bf16)] * TP
        + [jax.ShapeDtypeStruct((slab, width), f32), jax.ShapeDtypeStruct((1, slab), f32)],
        scratch_shapes=[pltpu.VMEM((TP, block, width), f32)],
        compiler_params=small_params(),
        cost_estimate=takes(2.2),
        name="sum_rows",
    )(idx, terms)


def up_kernel(plan, idx_ref, *refs):
    part_refs, out_ref, hold_ref = refs[:TP], refs[TP], refs[TP + 1]
    member = idx_ref[0]
    for j in range(TP):
        hold_ref[member ^ j] = part_refs[j][...].astype(f32)
    slab = out_ref.shape[1] // plan.devices
    for r in range(plan.devices):
        t, copy = plan.place(r)
        out_ref[:, r * slab : (r + 1) * slab] = hold_ref[t, :, copy * slab : (copy + 1) * slab]


def join_up(plan, idx, parts, hidden):
    block, width = parts[0].shape
    return pl.pallas_call(
        functools.partial(up_kernel, plan),
        in_specs=[pl.BlockSpec(memory_space=pltpu.SMEM)]
        + [pl.BlockSpec(memory_space=pltpu.VMEM)] * TP,
        out_shape=jax.ShapeDtypeStruct((block, hidden), f32),
        scratch_shapes=[pltpu.VMEM((TP, block, width), f32)],
        compiler_params=small_params(),
        cost_estimate=takes(40),
        name="join_up",
    )(idx, *parts)


def resid_kernel(r_ref, dm_ref, vec_ref, *refs):
    part_refs, (dr_ref, da_ref, sum_ref) = refs[:TP], refs[TP:]
    total = part_refs[0][...].astype(f32)
    for j in range(1, TP):
        total += part_refs[j][...].astype(f32)
    units, rstd = unit(r_ref[...])
    dm = dm_ref[...].astype(f32)
    dr = dm + unit_back(total * vec_ref[5:6, :], units, rstd)
    da = dr.astype(bf16)
    dr_ref[...] = dr
    da_ref[...] = da
    sum_ref[...] = jnp.zeros_like(sum_ref)
    sum_ref[0:1, :] = jnp.sum(da.astype(f32), axis=0, keepdims=True)
    sum_ref[1:2, :] = jnp.sum(dm, axis=0, keepdims=True)


def resid_back(parts, r_own, dm, vecs):
    rows, width = dm.shape
    return pl.pallas_call(
        resid_kernel,
        out_shape=[
            jax.ShapeDtypeStruct((rows, width), f32),
            jax.ShapeDtypeStruct((rows, width), bf16),
            jax.ShapeDtypeStruct((8, width), f32),
        ],
        compiler_params=small_params(),
        cost_estimate=takes(2.7),
        name="resid_back",
    )(r_own, dm, vecs, *parts)


def output_kernel(r_ref, vec_ref, *refs):
    total = r_ref[...] + vec_ref[7:8, :]
    for ref in refs[:TP]:
        total += ref[...].astype(f32)
    refs[TP][...] = total.astype(bf16)


def finish_output(parts, r_own, vecs):
    return pl.pallas_call(
        output_kernel,
        out_shape=jax.ShapeDtypeStruct(r_own.shape, bf16),
        cost_estimate=takes(2.1),
        name="finish_output",
    )(r_own, vecs, *parts)


def input_kernel(x_ref, dr_ref, vec_ref, *refs):
    total = refs[0][...].astype(f32)
    for ref in refs[1:TP]:
        total += ref[...].astype(f32)
    units, rstd = unit(x_ref[...].astype(f32))
    grad = dr_ref[...] + unit_back(total * vec_ref[3:4, :], units, rstd)
    refs[TP][...] = grad.astype(bf16)


def finish_input(parts, x, dr, vecs):
    return pl.pallas_call(
        input_kernel,
        out_shape=jax.ShapeDtypeStruct(x.shape, bf16),
        compiler_params=small_params(),
        cost_estimate=takes(40),
        name="finish_input",
    )(x, dr, vecs, *parts)


def normed_kernel(plan, n_recv, idx_ref, x_ref, dq_ref, own_ref, *refs):
    recv_refs, refs = refs[:n_recv], refs[n_recv:]
    w_ref, h_ref, o_ref, da_ref, own_sum_ref, two_ref = refs[:6]
    dh_refs, refs = refs[6 : 6 + TP], refs[6 + TP :]
    g_refs, (dh_now, low_ref, sum_ref, acc_ref, vec_ref) = refs[:-5], refs[-5:]
    step = pl.program_id(0)
    member, core = idx_ref[0], idx_ref[2]
    side = lax.rem(member, 2)
    cols = dq_ref.shape[1]
    rows, width = x_ref.shape

    @pl.when(step == 0)
    def _():
        sum_ref[...] = jnp.zeros_like(sum_ref)

    grad_k, grad_v = own_ref[0], own_ref[1]
    for ref in recv_refs:
        grad_k += ref[0].astype(f32)
        grad_v += ref[1].astype(f32)
    place = step ^ (member // 2)
    low_ref[place, :, :cols] = dq_ref[...]
    low_ref[place, :, cols : 2 * cols] = grad_k.astype(bf16)
    low_ref[place, :, 2 * cols : 3 * cols] = grad_v.astype(bf16)
    low_ref[place, :, 3 * cols :] = jnp.zeros((rows, SMALLS), bf16)
    low = low_ref[place]
    grad = dot(low, w_ref[...], 1, 1)
    dh_now[...] = grad.astype(bf16).reshape(dh_now.shape)
    for i in range(2):

        @pl.when(step == i)
        def _(i=i):
            for b in range(2):
                dh_refs[2 * i + b][...] = dh_now[side ^ b]

    units, _ = unit(x_ref[...].astype(f32))
    sum_ref[0:1, :width] += jnp.sum(grad * units, axis=0, keepdims=True)
    sum_ref[1:2, :width] += jnp.sum(grad, axis=0, keepdims=True)
    sum_ref[2:3, : low.shape[1]] += jnp.sum(low.astype(f32), axis=0, keepdims=True)

    @pl.when(step == 1)
    def _():
        wide = low_ref.shape[2]
        acc_ref[:, :wide] = dot(h_ref[...], low_ref[...].reshape(2 * rows, wide), 0, 0)
        da = da_ref[...].reshape(2 * rows, cols)
        for j in range(TP):
            at = j * cols
            acc_ref[at : at + cols, wide : wide + cols] = dot(o_ref[j], da, 0, 0)
        bias_q, bias_v = sum_ref[2:3, :cols], sum_ref[2:3, 2 * cols : 3 * cols]
        zero = jnp.zeros_like(bias_q)
        vec_ref[...] = jnp.zeros_like(vec_ref)
        vectors = [
            jnp.concatenate([jnp.where(member == j, b, zero) for j in range(TP)], axis=1)
            for b in (bias_q, bias_v)
        ]
        vectors += [
            own_sum_ref[0:1, :],
            sum_ref[0:1, :],
            sum_ref[1:2, :],
            two_ref[0:1, :],
            two_ref[1:2, :],
            own_sum_ref[1:2, :],
        ]
        for j, row in enumerate(vectors):
            vec_ref[SMALLS + j : SMALLS + j + 1, :] = row
        acc_ref[:, wide + cols :] = vec_ref[...].T[:, SMALLS:]
        if not plan.fast:
            g_refs[0][...] = acc_ref[...].astype(bf16)
            return
        near, block, _ = g_refs[0].shape
        span = near // plan.size["gx"]
        for ref, owner in ((g_refs[0], core), (g_refs[1], 1 - core)):
            for n in range(near):
                gx, rest = divmod(n, span)
                at = ((gx * 2 + owner) * span + rest) * block
                ref[n] = acc_ref[pl.ds(pl.multiple_of(at, 8), block), :].astype(bf16)


def normed_back(plan, idx, x_all, dq, own, recvs, w_qkv, low, o_all, da_cols, sum_own, sum_two):
    rows, width = x_all.shape
    cols = dq.shape[1]
    wide = w_qkv.shape[1]
    total = wide + cols + SMALLS
    step = rows // 2
    one = (rows // TP, width)
    near = plan.devices // 2

    def block(i, idx):
        return (i ^ (idx[0] // 2), 0)

    pairs = pl.BlockSpec((2, step, cols), lambda i, idx: (0, i ^ (idx[0] // 2), 0))
    if plan.fast:
        sums = [(near, width // plan.devices, total)] * 2
    else:
        sums = [(width, total)]
    constants = (w_qkv, low, o_all, da_cols, sum_own, sum_two)
    return pl.pallas_call(
        functools.partial(normed_kernel, plan, len(recvs)),
        grid_spec=pltpu.PrefetchScalarGridSpec(
            num_scalar_prefetch=1,
            grid=(2,),
            in_specs=[pl.BlockSpec((step, width), block), pl.BlockSpec((step, cols), block), pairs]
            + [pairs] * len(recvs)
            + [here(v.shape) for v in constants],
            out_specs=[here(one)] * TP + [here(shape) for shape in sums],
            scratch_shapes=[
                pltpu.VMEM((2, *one), bf16),
                pltpu.VMEM((2, step, wide), bf16),
                pltpu.VMEM((8, width), f32),
                pltpu.VMEM((width, total), f32),
                pltpu.VMEM((2 * SMALLS, width), f32),
            ],
        ),
        out_shape=[jax.ShapeDtypeStruct(one, bf16)] * TP
        + [jax.ShapeDtypeStruct(shape, bf16) for shape in sums],
        compiler_params=params(),
        cost_estimate=takes(NORMED),
        name="normed_back",
    )(idx, x_all, dq, own, *recvs, *constants)


def join_kernel(keep, cols, wide, in_ref, first_ref, second_ref, *refs):
    mats, vec_refs = refs[:4], refs[4:12]
    output_ref, input_ref, turn_ref = refs[12:]
    output_ref[...] = first_ref[...]
    input_ref[...] = second_ref[...]
    groups = {}
    for n in range(in_ref.shape[0]):
        value = in_ref[n].astype(f32)
        key = keep[n]
        groups[key] = value if key not in groups else groups[key] + value
    for j in range(TP):
        for ref, at in zip(mats, (0, cols, 2 * cols, wide)):
            ref[:, j * cols : (j + 1) * cols] = groups[j][:, at : at + cols]
    total = functools.reduce(jnp.add, [groups[j] for j in range(TP)])
    block = in_ref.shape[1]
    turn_ref[...] = jnp.zeros_like(turn_ref)
    turn_ref[:block, :SMALLS] = total[:, wide + cols :]
    turned = turn_ref[...].T
    for j, ref in enumerate(vec_refs):
        ref[...] = turned[j : j + 1, :block]


def join_grads(plan, got, first, second, cols, wide):
    near, block, _ = got.shape
    members = [plan.place(plan.same(n))[0] for n in range(near)]
    width = cols * TP
    return pl.pallas_call(
        functools.partial(join_kernel, members, cols, wide),
        out_shape=[jax.ShapeDtypeStruct((block, width), f32)] * 4
        + [jax.ShapeDtypeStruct((1, block), f32)] * 8
        + [jax.ShapeDtypeStruct(first.shape, bf16)] * 2,
        scratch_shapes=[pltpu.VMEM((128, 128), f32)],
        compiler_params=small_params(),
        cost_estimate=takes(2.2),
        name="join_grads",
    )(got, first, second)


def local(
    plan, inputs, segment_ids, padding, cotangent, w_query, b_query, w_key, w_value, b_value,
    w_out, b_out, ln1_gain, ln1_shift, ln2_gain, ln2_shift, w_up, b_up, w_down, b_down,
):
    x_own = inputs[0]
    rows, width = x_own.shape
    cols = width // TP
    length = segment_ids.shape[1]
    block = w_query.shape[0]
    hidden = w_up.shape[1]
    slab = b_up.shape[0]
    size = plan.size
    member = lax.axis_index(plan.tp)
    part = lax.axis_index(plan.half)
    core = lax.axis_index("c")
    idx = jnp.stack([member, part, core, lax.axis_index("sz")]).astype(jnp.int32)
    lines = plan.copies // 2
    fast = plan.fast

    id_rows = jnp.pad(segment_ids[0].astype(bf16), (0, 8 * width - length)).reshape(8, width)
    packed = jnp.concatenate([x_own, id_rows], axis=0)
    dm_own = (cotangent[0].astype(f32) * padding[0].astype(f32)[:, None]).astype(bf16)
    dm_mine = plan.move(dm_own, plan.route)

    small = [b_query, b_value, b_out, ln1_gain, ln1_shift, ln2_gain, ln2_shift, b_down]
    if fast:
        chunk = prepare(plan, w_query, w_key, w_value, small, w_up, w_out)
        got = lax.all_to_all(chunk, plan.tp, 0, 0, tiled=True)
        moved = plan.move(packed, plan.route)
        proj, shard = shards_of(got, w_down, b_up[None], 3 * cols + SMALLS, lines)
        projs = [proj] + [plan.turn(proj, "sz", -j) for j in range(1, lines)]
        projs, moved, shard, dm_mine = lax.optimization_barrier((projs, moved, shard, dm_mine))
        x_mine = moved[:rows]
        x_all = lax.all_gather(x_mine, plan.tp, axis=0, tiled=True)
        shard = lax.all_to_all(shard, "sz", 0, 0, tiled=True)
        projs = jnp.stack(projs)
        low_one, query, kv, w_qkv, vecs = qkv(plan, idx, x_all, projs, plan.swap(projs))
    else:
        small = jnp.stack(small, axis=1)
        moved = plan.move(packed, plan.route)
        x_mine = moved[:rows]
        x_all = lax.all_gather(x_mine, plan.tp, axis=0, tiled=True)
        b_row = jnp.pad(b_up[None], ((0, 7), (0, width - slab)))
        table = [w_query, w_key, w_value, w_out, small]
        table = lax.all_gather(jnp.concatenate(table, axis=1), ALL, axis=0, tiled=True)
        vecs = table[:, 4 * width :].T.astype(f32)
        split = [lax.dynamic_slice(table, (0, i * width + member * cols), (width, cols)) for i in range(3)]
        w_qkv = jnp.concatenate([*split, jnp.zeros((width, SMALLS), bf16)], axis=1)
        out_full = table[:, 3 * width : 4 * width].reshape(TP, cols, width)
        low_one, query, kv = qkv(plan, idx, x_all, w_qkv, vecs)
        up_mine = lax.all_gather(w_up, ALL, axis=0, tiled=True)
        up_mine = up_mine.reshape(width, plan.devices, slab).transpose(1, 0, 2)
        up_mine = plan.shuffle(up_mine, ALL, plan.tp + plan.rep).reshape(TP, plan.copies, width, slab)
        up_mine = lax.dynamic_index_in_dim(up_mine, member, 0, keepdims=False)
        up_mine = up_mine.transpose(1, 0, 2).reshape(width, -1)
        downs = jnp.concatenate([w_down, b_row], axis=0)
        downs = lax.all_gather(downs, plan.rep, axis=0, tiled=False)
        down_mine = downs[:, :slab].reshape(-1, width)
        b_up_mine = downs[:, slab, :slab].reshape(1, -1).astype(f32)

    ids = moved[rows:].reshape(1, -1)[:, :length].astype(f32)

    parts = plan.parts
    kv, dm_late = lax.optimization_barrier((kv, dm_mine))
    kvs = [kv] + [plan.turn(kv, plan.half, -j) for j in range(1, parts)]
    mixed, lse = attend(idx, ids, query, kvs)
    o_all = lax.all_gather(mixed, plan.tp, axis=0, tiled=False)
    dms = plan.partners(dm_late)
    if fast:
        shard, o_all, dms = lax.optimization_barrier((shard, o_all, dms))
        weights = [shard, plan.swap(shard)]
    else:
        weights = [out_full, up_mine, down_mine, b_up_mine]
    x_same, dm_all = stage(idx, x_all, dms)
    dm_all = dm_all.reshape(TP * rows, width)
    results = mlp(plan, idx, x_same, o_all, vecs, dm_all, weights, slab)
    r_own, low_two, act, grad_pre, sum_two = results[:5]
    dh_two = results[5 : 5 + TP]
    if fast:
        out_mine, down_mine = results[5 + TP :]
    else:
        out_mine = lax.dynamic_index_in_dim(out_full, member, 0, keepdims=False)

    back_two = plan.reduce(dh_two)
    if fast:
        near_terms, far_terms, *out_terms = mlp_weight_grads(
            plan, idx, low_two, grad_pre, act, dm_all, down_mine
        )
        back_two, out_terms, far_terms = lax.optimization_barrier((back_two, out_terms, far_terms))
    else:
        up_terms = dot(low_two, grad_pre, 0, 0).astype(bf16)
        down_terms = dot(act, dm_all, 0, 0).astype(bf16)
        row = jnp.sum(grad_pre.astype(f32), axis=0).astype(bf16)
        out_terms = dot(act, down_mine).astype(bf16).reshape(TP, rows, width)
        out_terms = [
            lax.dynamic_index_in_dim(out_terms, member ^ j, 0, keepdims=False) for j in range(TP)
        ]
    dr, da, sum_own = resid_back(back_two, r_own, dm_mine, vecs)
    if fast:
        terms = add(near_terms, plan.swap(far_terms), after=(da,))
        das = plan.partners(da)
        after = [terms]
        terms = lax.all_to_all(terms, "sz", 0, 0, tiled=True)
        *ups, g_w_down, g_b_up = sum_rows(plan, idx, terms, block, slab)
    else:
        das = plan.partners(da)
        after = []
        row = jnp.pad(row.reshape(plan.copies, 1, slab), ((0, 0), (0, 7), (0, width - slab)))
        downs = jnp.concatenate([down_terms.reshape(plan.copies, slab, width), row], axis=1)
        downs = lax.psum_scatter(downs, plan.rep, scatter_dimension=0, tiled=False)
        g_w_down = downs[:slab].astype(f32)
        g_b_up = downs[slab, :slab].astype(f32)
        ups = plan.shuffle(up_terms.reshape(plan.devices, block, -1), ALL, plan.rep + plan.tp)
        ups = ups.reshape(plan.copies, TP * block, -1)
        ups = lax.psum_scatter(ups, plan.rep, scatter_dimension=0, tiled=False)
        ups = lax.all_to_all(ups.reshape(TP, block, -1), plan.tp, 0, 0, tiled=True).astype(f32)
    grad_query, kv_own, da_cols, *kv_others = attend_back(
        idx, ids, query, das, after, out_mine, lse, kvs
    )
    kv_others, out_parts = lax.optimization_barrier((kv_others, plan.reduce(out_terms)))
    recvs = [plan.turn(kv_others[j - 1], plan.half, j) for j in range(1, parts)]
    results = normed_back(
        plan, idx, x_all, grad_query, kv_own, recvs, w_qkv, low_one, o_all, da_cols, sum_own, sum_two
    )
    back_one, terms = plan.reduce(results[:TP]), results[TP:]
    if fast:
        keep, send = terms
        terms = add(keep, plan.swap(send))
        terms, ups = lax.optimization_barrier((terms, ups))
        got = lax.all_to_all(terms, SAME, 0, 0, tiled=True)
    else:
        terms = plan.shuffle(terms[0].reshape(plan.devices, block, -1), ALL, ("c",) + SAME)
        terms = terms.reshape(2, -1, *terms.shape[1:])
        keep, send = jnp.where(core == 0, terms, terms[::-1])
        got = lax.all_to_all(add(keep, plan.swap(send)), SAME, 0, 0, tiled=True)
    if fast:
        g_w_up = join_up(plan, idx, plan.reduce(ups), hidden)
        g_b_up = g_b_up[0]
    else:
        ups = ups.reshape(TP, block, plan.copies, slab).transpose(0, 2, 1, 3)
        ups = plan.shuffle(ups.reshape(plan.devices, block, slab), plan.tp + plan.rep, ALL)
        g_w_up = ups.transpose(1, 0, 2).reshape(block, hidden)
    g_w_down, out_parts = lax.optimization_barrier((g_w_down, out_parts))
    output = plan.move(finish_output(out_parts, r_own, vecs), plan.back)
    grad_input = plan.move(finish_input(back_one, x_mine, dr, vecs), plan.back)
    joined = join_grads(plan, got, output, grad_input, cols, w_qkv.shape[1])
    g_query, g_key, g_value, g_out, *vec, output, grad_input = joined
    vec = [v[0] for v in vec]
    return (
        output[None],
        grad_input[None],
        g_query,
        vec[0],
        g_key,
        g_value,
        vec[1],
        g_out,
        vec[2],
        vec[3],
        vec[4],
        vec[5],
        vec[6],
        g_w_up,
        g_b_up,
        g_w_down,
        vec[7],
    )


def solution(mesh):
    groups, blocks = mesh.shape["grp"], mesh.shape["seq"]
    plan = Plan(groups, blocks)
    fine = Mesh(mesh.devices.reshape(plan.shape), ALL)
    grp, seq = ("gx", "c"), ("sz", "sy")
    matrix, vector = P(ALL, None), P(ALL)
    token = P(grp, seq, None)
    return jax.shard_map(
        functools.partial(local, plan),
        mesh=fine,
        in_specs=(
            token, P(grp, None), P(grp, seq), token,
            matrix, vector, matrix, matrix, vector, matrix, vector,
            vector, vector, vector, vector, matrix, vector, matrix, vector,
        ),
        out_specs=(
            token, token,
            matrix, vector, matrix, matrix, vector, matrix, vector,
            vector, vector, vector, vector, matrix, vector, matrix, vector,
        ),
        check_vma=False,
    )
```
